32 devices in a mesh: tm: 8 (over z, x), freq: 4 (over y, core).
Axes of the slice: x: 2, y: 2, z: 4, core: 2. Of those that a mesh axis runs over, the one named last changes fastest.
Arguments:
- latent: bfloat16 [4096, 8, 256], P('tm', 'freq'), may hold values from -6 to 6
- condition: float32 [64, 512], replicated, may hold values from -6 to 6
- lengths: int32 [64], replicated, may hold values from 1 to 128, 4096 in all
- cotangent: bfloat16 [4096, 8, 256], P('tm', 'freq'), may hold values from -6 to 6
- conv_weight: float32 [2, 2304, 256], P(None, 'freq'), may hold values from -0.125 to 0.125
- conv_moment: float32 [2, 2304, 256], P(None, 'freq'), may hold values from -56 to 56
- conv_second: float32 [2, 2304, 256], P(None, 'freq'), may hold values from 6.5536 to 65.536
- proj_weight: float32 [6, 256, 256], P(None, 'freq'), may hold values from -0.375 to 0.375
- proj_moment: float32 [6, 256, 256], P(None, 'freq'), may hold values from -56 to 56
- proj_second: float32 [6, 256, 256], P(None, 'freq'), may hold values from 6.5536 to 65.536
- mlp_weight: float32 [2, 1024, 256], P(None, 'freq'), may hold values from -0.25 to 0.25
- mlp_moment: float32 [2, 1024, 256], P(None, 'freq'), may hold values from -56 to 56
- mlp_second: float32 [2, 1024, 256], P(None, 'freq'), may hold values from 6.5536 to 65.536
- emb_weight: float32 [512, 256], P('freq'), may hold values from -0.25 to 0.25
- emb_moment: float32 [512, 256], P('freq'), may hold values from -56 to 56
- emb_second: float32 [512, 256], P('freq'), may hold values from 6.5536 to 65.536
- small_weight: float32 [17, 256], P(None, 'freq'), may hold values from -1.2 to 2.2
- small_moment: float32 [17, 256], P(None, 'freq'), may hold values from -56 to 56
- small_second: float32 [17, 256], P(None, 'freq'), may hold values from 6.5536 to 65.536
Outputs:
- output: bfloat16 [4096, 8, 256], P('tm', 'freq')
- latent_grad: bfloat16 [4096, 8, 256], P('tm', 'freq')
- conv_weight_new: float32 [2, 2304, 256], P(None, 'freq')
- conv_moment_new: float32 [2, 2304, 256], P(None, 'freq')
- conv_second_new: float32 [2, 2304, 256], P(None, 'freq')
- proj_weight_new: float32 [6, 256, 256], P(None, 'freq')
- proj_moment_new: float32 [6, 256, 256], P(None, 'freq')
- proj_second_new: float32 [6, 256, 256], P(None, 'freq')
- mlp_weight_new: float32 [2, 1024, 256], P(None, 'freq')
- mlp_moment_new: float32 [2, 1024, 256], P(None, 'freq')
- mlp_second_new: float32 [2, 1024, 256], P(None, 'freq')
- emb_weight_new: float32 [512, 256], P('freq')
- emb_moment_new: float32 [512, 256], P('freq')
- emb_second_new: float32 [512, 256], P('freq')
- small_weight_new: float32 [17, 256], P(None, 'freq')
- small_moment_new: float32 [17, 256], P(None, 'freq')
- small_second_new: float32 [17, 256], P(None, 'freq')
- out_bias_grad: float32 [256], P('freq')
The draws below stay inside these ranges and needn't reach their ends.
Inputs may be any that keep to these rules, and one draw needn't show every extreme that they name: `lengths`: clips lie end to end along time and fill all 4096 rows; the longest clip has exactly 128 rows.
All inputs are finite; a program needn't handle non-finite values.
Results may differ from the reference program's by a relative error of at most 0.035.
The reference program's roundings to bfloat16 on the way count: a program that leaves them out, or rounds other values in their place, can miss the bound.
Values may be sent and summed in bfloat16 or wider, within the bound.
A program may use at most 192 MiB of HBM per device.

```python
import math
import jax
import jax.numpy as jnp
import numpy as np
from jax import lax

C = 256
G = 32
E = 512
H = 8
HD = 32
FF = 1024
F = 8
TR = 512
MAXLEN = 128
STEP = 10
ROWS = 4096
CLIPS = 64
PIX = 32768
NSMALL = 17


def draw_proj_weight(key, part):
    own_key = jax.random.fold_in(key, 1301)
    matrix_scales = jnp.array([1.0, 1.5, 1.5, 1.5, 1.5, 1.0], jnp.float32) * C ** (-0.5)
    base_values = jnp.clip(jax.random.normal(own_key, (6, C, C), jnp.float32), -4.0, 4.0)
    return base_values * matrix_scales[:, None, None]


def draw_small_weight(key, part):
    own_key = jax.random.fold_in(key, 2707)
    row_index = jnp.arange(NSMALL)
    is_gain = (row_index == 0) | (row_index == 4) | (row_index == 7)
    base_values = jnp.clip(0.3 * jax.random.normal(own_key, (NSMALL, C), jnp.float32), -1.2, 1.2)
    return jnp.where(is_gain[:, None], 1.0 + base_values, base_values)


def block_levels(key, shape, split, low, largest):
    level, own = 1.0, jax.random.fold_in(key, 6)
    for axis_at, parts in split:
        heights = jnp.exp(jax.random.uniform(jax.random.fold_in(own, axis_at), (parts,), jnp.float32, low / len(split), largest / len(split)))
        level = level * jnp.repeat(heights, shape[axis_at] // parts).reshape([-1 if axis == axis_at else 1 for axis in range(len(shape))])
    return level


def length_profile(count, total, most, lean):
    loads = [(1 << 20) // math.isqrt(rank ** lean) + 1 for rank in range(2, count + 1)]
    surplus, counts = total - most - (count - 1), [1] * (count - 1)
    while surplus > 0:
        candidates = [i for i in range(count - 1) if counts[i] < most]
        pool, remaining = sum([loads[i] for i in candidates]), surplus
        for i in candidates:
            addition = min(most - counts[i], max(1, remaining * loads[i] // pool), surplus)
            counts[i] = counts[i] + addition
            surplus = surplus - addition
    return np.array([most] + counts)


def ragged_sizes(key, count, total, bound, slope):
    if count == 2:
        one = jax.random.randint(key, (), max(1, total - bound), min(bound, total - 1) + 1)
        return jnp.stack([one, total - one])
    sizes = jnp.asarray(length_profile(count, total, bound, slope), jnp.int32)
    pairs = (count - 1) // 2
    giver, sink = sizes[1:1 + 2 * pairs:2], sizes[2:2 + 2 * pairs:2]
    room = jnp.minimum(giver - 1, bound - sink)
    moved = jax.random.randint(jax.random.fold_in(key, 1), (pairs,), 0, 1 << 20) % (room + 1)
    sizes = sizes.at[1:1 + 2 * pairs:2].set(giver - moved).at[2:2 + 2 * pairs:2].set(sink + moved)
    return sizes[jax.random.permutation(jax.random.fold_in(key, 2), count)]


def noise(rng, shape, spread, bound, cuts=(), kind=jnp.bfloat16):
    values = jax.random.normal(rng, shape, jnp.float32) * spread
    if len(cuts) > 0:
        values = block_levels(rng, shape, cuts, -0.22, 0.18) * values
    return jnp.clip(values, min=-bound, max=bound).astype(kind)


def setup_inputs(seed: int = 0) -> dict:
    streams_of = jax.random.split(jax.random.key(seed), 20)
    latent = noise(streams_of[0], (ROWS, F, C), 1.0, 6.0, ((0, 8), (1, 4)))
    condition = noise(streams_of[1], (CLIPS, E), 1.0, 6.0, (), jnp.float32)
    lengths = ragged_sizes(streams_of[2], CLIPS, ROWS, MAXLEN, 1).astype(jnp.int32)
    cotangent = noise(streams_of[3], (ROWS, F, C), 1.0, 6.0, ((0, 8), (1, 4)))
    conv_weight = noise(streams_of[4], (2, 9 * C, C), (9 * C) ** -0.5, 0.125, ((1, 4),), jnp.float32)
    conv_moment = noise(streams_of[5], (2, 9 * C, C), (0.05 * PIX ** 0.5), 56.0, ((1, 4),), jnp.float32)
    conv_second = jnp.clip(jnp.exp(math.log(65.536) - 2.3025852 * jax.random.uniform(streams_of[6], (2, 9 * C, C), jnp.float32) ** block_levels(streams_of[6], (2, 9 * C, C), ((1, 4),), -0.2, 0.2)), 6.5536, 65.536)
    proj_weight = draw_proj_weight(jax.random.fold_in(streams_of[19], 71), 0)
    proj_moment = noise(streams_of[8], (6, C, C), (0.05 * PIX ** 0.5), 56.0, ((1, 4),), jnp.float32)
    proj_second = jnp.clip(jnp.exp(math.log(65.536) - 2.3025852 * jax.random.uniform(streams_of[9], (6, C, C), jnp.float32) ** block_levels(streams_of[9], (6, C, C), ((1, 4),), -0.2, 0.2)), 6.5536, 65.536)
    mlp_weight = noise(streams_of[10], (2, FF, C), (2 * C) ** -0.5, 0.25, ((1, 4),), jnp.float32)
    mlp_moment = noise(streams_of[11], (2, FF, C), (0.05 * PIX ** 0.5), 56.0, ((1, 4),), jnp.float32)
    mlp_second = jnp.clip(jnp.exp(math.log(65.536) - 2.3025852 * jax.random.uniform(streams_of[12], (2, FF, C), jnp.float32) ** block_levels(streams_of[12], (2, FF, C), ((1, 4),), -0.2, 0.2)), 6.5536, 65.536)
    emb_weight = noise(streams_of[13], (E, C), E ** -0.5, 0.25, ((0, 4),), jnp.float32)
    emb_moment = noise(streams_of[14], (E, C), (0.05 * PIX ** 0.5), 56.0, ((0, 4),), jnp.float32)
    emb_second = jnp.clip(jnp.exp(math.log(65.536) - 2.3025852 * jax.random.uniform(streams_of[15], (E, C), jnp.float32) ** block_levels(streams_of[15], (E, C), ((0, 4),), -0.2, 0.2)), 6.5536, 65.536)
    small_weight = draw_small_weight(jax.random.fold_in(streams_of[19], 71), 0)
    small_moment = noise(streams_of[17], (NSMALL, C), (0.05 * PIX ** 0.5), 56.0, ((1, 4),), jnp.float32)
    small_second = jnp.clip(jnp.exp(math.log(65.536) - 2.3025852 * jax.random.uniform(streams_of[18], (NSMALL, C), jnp.float32) ** block_levels(streams_of[18], (NSMALL, C), ((1, 4),), -0.2, 0.2)), 6.5536, 65.536)
    return dict(latent=latent, condition=condition, lengths=lengths, cotangent=cotangent, conv_weight=conv_weight, conv_moment=conv_moment, conv_second=conv_second, proj_weight=proj_weight, proj_moment=proj_moment, proj_second=proj_second, mlp_weight=mlp_weight, mlp_moment=mlp_moment, mlp_second=mlp_second, emb_weight=emb_weight, emb_moment=emb_moment, emb_second=emb_second, small_weight=small_weight, small_moment=small_moment, small_second=small_second)


@jax.custom_vjp
def low(v):
    return lax.optimization_barrier(v.astype(jnp.bfloat16)).astype(jnp.float32)

@jax.custom_vjp
def low_back(v):
    return v

def low_keep(v):
    return (low(v), None)

def low_pass(kept, grad):
    return (grad,)

def back_keep(v):
    return (v, None)

def back_low(kept, grad):
    return (low(grad),)
low.defvjp(low_keep, low_pass)
low_back.defvjp(back_keep, back_low)
HIGHEST = lax.Precision.HIGHEST
norm_eps = 1e-05
beta_first = 0.9
beta_second = 0.999
learn_rate = 0.5
weight_decay = 0.01
adam_eps = 1e-08
masked_score = -1e+30

def segment_ids(lengths):
    clip_ends = jnp.cumsum(lengths)
    row_index = jnp.arange(ROWS, dtype=jnp.int32)
    return lax.optimization_barrier(jnp.sum((clip_ends[None, :] <= row_index[:, None]).astype(jnp.int32), axis=1))

def group_norm(source, seg_ids, clip_counts, gain_vec, shift_vec):
    grouped = source.reshape(ROWS, F, G, C // G)
    row_sums = lax.optimization_barrier(jnp.sum(grouped, axis=(1, 3)))
    row_squares = lax.optimization_barrier(jnp.sum(grouped * grouped, axis=(1, 3)))
    clip_mean = jax.ops.segment_sum(row_sums, seg_ids, CLIPS) / clip_counts[:, None]
    clip_square = jax.ops.segment_sum(row_squares, seg_ids, CLIPS) / clip_counts[:, None]
    clip_inv = lax.rsqrt(clip_square - clip_mean * clip_mean + norm_eps)
    normed = (grouped - clip_mean[seg_ids][:, None, :, None]) * clip_inv[seg_ids][:, None, :, None]
    return normed.reshape(ROWS, F, C) * gain_vec + shift_vec

def conv_apply(source, kernel, seg_ids):
    padded = jnp.pad(source, ((1, 1), (1, 1), (0, 0)))
    seg_pad = jnp.pad(seg_ids, 1, constant_values=-1)
    pieces = []
    for row_offset in range(3):
        keep_rows = (seg_pad[row_offset:row_offset + ROWS] == seg_ids).astype(source.dtype)[:, None, None]
        for col_offset in range(3):
            pieces.append(padded[row_offset:row_offset + ROWS, col_offset:col_offset + F] * keep_rows)
    patches = jnp.concatenate(pieces, axis=2).reshape(ROWS * F, 9 * C)
    return jnp.dot(patches, kernel, precision=HIGHEST).reshape(ROWS, F, C)

def attention(query_all, key_all, value_all, seg_ids):
    block_rows = math.gcd(TR, 64)
    key_rows = block_rows + 2 * MAXLEN
    key_pad = jnp.pad(key_all, ((MAXLEN, MAXLEN), (0, 0), (0, 0)))
    value_pad = jnp.pad(value_all, ((MAXLEN, MAXLEN), (0, 0), (0, 0)))
    seg_pad = jnp.pad(seg_ids, MAXLEN, constant_values=-1)
    score_scale = HD ** (-0.5)

    def one_block(block_index):
        start_row = block_index * block_rows
        query_blk = lax.dynamic_slice_in_dim(query_all, start_row, block_rows, 0).reshape(block_rows * F, H, HD)
        key_blk = lax.dynamic_slice_in_dim(key_pad, start_row, key_rows, 0).reshape(key_rows * F, H, HD)
        value_blk = lax.dynamic_slice_in_dim(value_pad, start_row, key_rows, 0).reshape(key_rows * F, H, HD)
        seg_query = jnp.repeat(lax.dynamic_slice_in_dim(seg_ids, start_row, block_rows, 0), F)
        seg_key = jnp.repeat(lax.dynamic_slice_in_dim(seg_pad, start_row, key_rows, 0), F)
        same_clip = seg_query[:, None] == seg_key[None, :]
        scores = low_back(jnp.einsum('phd,khd->hpk', query_blk, key_blk, precision=HIGHEST)) * score_scale
        scores = jnp.where(same_clip[None], scores, masked_score)
        probs_low = low(jax.nn.softmax(scores, axis=-1))
        mixed_blk = low(low_back(jnp.einsum('hpk,khd->phd', probs_low, value_blk, precision=HIGHEST)))
        return mixed_blk.reshape(block_rows, F, C)
    blocks = lax.map(jax.checkpoint(one_block), jnp.arange(ROWS // block_rows, dtype=jnp.int32))
    return blocks.reshape(ROWS, F, C)

def forward(latent_f, condition, seg_ids, clip_counts, conv_weight, proj_weight, mlp_weight, emb_weight, small_weight):
    conv_low = low(conv_weight)
    proj_low = low(proj_weight)
    mlp_low_w = low(mlp_weight)
    emb_low = low(emb_weight)
    vectors = low(small_weight)
    tail = 11 + FF // C
    cond_low = low(jax.nn.silu(condition))
    film_bias = jnp.dot(cond_low, emb_low, precision=HIGHEST) + vectors[3]
    act_one = low(jax.nn.silu(group_norm(latent_f, seg_ids, clip_counts, vectors[0], vectors[1])))
    hidden_one = low_back(conv_apply(act_one, conv_low[0], seg_ids)) + vectors[2] + film_bias[seg_ids][:, None, :]
    act_two = low(jax.nn.silu(group_norm(hidden_one, seg_ids, clip_counts, vectors[4], vectors[5])))
    resid = latent_f + low_back(conv_apply(act_two, conv_low[1], seg_ids)) + vectors[6]
    normed_low = low(group_norm(resid, seg_ids, clip_counts, vectors[7], vectors[8])).reshape(ROWS * F, C)
    inner = low_back(jnp.dot(normed_low, proj_low[0], precision=HIGHEST)) + vectors[9]
    inner_low = low(inner)
    query_all = low(low_back(jnp.dot(inner_low, proj_low[1], precision=HIGHEST)))
    key_all = low(low_back(jnp.dot(inner_low, proj_low[2], precision=HIGHEST)))
    value_all = low(low_back(jnp.dot(inner_low, proj_low[3], precision=HIGHEST)))
    mixed = attention(query_all.reshape(ROWS, F, C), key_all.reshape(ROWS, F, C), value_all.reshape(ROWS, F, C), seg_ids).reshape(ROWS * F, C)
    after_attn = inner + low_back(jnp.dot(mixed, proj_low[4], precision=HIGHEST)) + vectors[10]
    pre_act = low_back(jnp.dot(low(after_attn), mlp_low_w[0].T, precision=HIGHEST)) + vectors[11:tail].reshape(FF)
    act_mlp = low(jax.nn.gelu(pre_act, approximate=False))
    after_mlp = after_attn + low_back(jnp.dot(act_mlp, mlp_low_w[1], precision=HIGHEST)) + vectors[tail]
    result = resid.reshape(ROWS * F, C) + low_back(jnp.dot(low(after_mlp), proj_low[5], precision=HIGHEST)) + vectors[tail + 1]
    return result.reshape(ROWS, F, C)

def adamw_step(weight, moment, second, grad, decay_rate):
    moment_new = beta_first * moment + (1.0 - beta_first) * grad
    second_new = beta_second * second + (1.0 - beta_second) * grad * grad
    moment_hat = moment_new / (1.0 - beta_first ** STEP)
    second_hat = second_new / (1.0 - beta_second ** STEP)
    weight_new = weight - learn_rate * (moment_hat / (jnp.sqrt(second_hat) + adam_eps) + decay_rate * weight)
    return (weight_new, moment_new, second_new)

def reference(latent, condition, lengths, cotangent, conv_weight, conv_moment, conv_second, proj_weight, proj_moment, proj_second, mlp_weight, mlp_moment, mlp_second, emb_weight, emb_moment, emb_second, small_weight, small_moment, small_second):
    seg_ids = segment_ids(lengths)
    clip_counts = lengths.astype(jnp.float32) * (F * (C // G))
    latent_f = latent.astype(jnp.float32)

    def whole(latent_in, conv_in, proj_in, mlp_in, emb_in, small_in):
        return forward(latent_in, condition, seg_ids, clip_counts, conv_in, proj_in, mlp_in, emb_in, small_in)
    output, pullback = jax.vjp(whole, latent_f, conv_weight, proj_weight, mlp_weight, emb_weight, small_weight)
    grad_latent, grad_conv, grad_proj, grad_mlp, grad_emb, grad_small = pullback(cotangent.astype(jnp.float32))
    conv_new = adamw_step(conv_weight, conv_moment, conv_second, grad_conv, weight_decay)
    proj_new = adamw_step(proj_weight, proj_moment, proj_second, grad_proj, weight_decay)
    mlp_new = adamw_step(mlp_weight, mlp_moment, mlp_second, grad_mlp, weight_decay)
    emb_new = adamw_step(emb_weight, emb_moment, emb_second, grad_emb, weight_decay)
    small_new = adamw_step(small_weight, small_moment, small_second, grad_small, 0.0)
    return (output.astype(jnp.bfloat16), grad_latent.astype(jnp.bfloat16), conv_new[0], conv_new[1], conv_new[2], proj_new[0], proj_new[1], proj_new[2], mlp_new[0], mlp_new[1], mlp_new[2], emb_new[0], emb_new[1], emb_new[2], small_new[0], small_new[1], small_new[2], grad_small[12 + FF // C])
```

```python
from functools import partial

import jax
import jax.numpy as jnp
from jax import lax
from jax.experimental import pallas as pl
from jax.experimental.pallas import tpu as pltpu
from jax.sharding import PartitionSpec as P

C = 256
G = 32
GW = C // G
HD = 32
H = C // HD
FF = 1024
F = 8
MAXLEN = 128
STEP = 10
TAPS = 9
CH = 256
CR = CH // F

HIGHEST = lax.Precision.HIGHEST
norm_eps = 1e-05
beta_first = 0.9
beta_second = 0.999
learn_rate = 0.5
weight_decay = 0.01
adam_eps = 1e-08
masked_score = -1e30
score_scale = HD**-0.5
LOG2E = 1.4426950408889634
MESH = pltpu.DeviceIdType.MESH if hasattr(pltpu, "DeviceIdType") else pl.DeviceIdType.MESH
VMEM_LIMIT = 64 * 1024 * 1024 - 65536
BF = jnp.bfloat16
F32 = jnp.float32


def mm(a, b):
    return jnp.dot(a, b, preferred_element_type=F32)


def mm_nt(a, b):
    return lax.dot_general(a, b, (((1,), (1,)), ((), ())), preferred_element_type=F32)


def mm_tn(a, b):
    return lax.dot_general(a, b, (((0,), (0,)), ((), ())), preferred_element_type=F32)


def hdot(a, b):
    return jnp.dot(a, b, precision=HIGHEST, preferred_element_type=F32)


def place(nt, nf):
    t = lax.axis_index("tm")
    f = lax.axis_index("freq")
    odd = lax.rem(t, 2)
    s = f + odd * (nf - 1 - 2 * f)
    turn = 1 - 2 * odd
    at_end = (s + 1) // nf
    at_start = 1 - (s + nf - 1) // nf
    right = {"tm": t + at_end, "freq": f + (1 - at_end) * turn}
    left = {"tm": t - at_start, "freq": f - (1 - at_start) * turn}
    return t * nf + s, left, right


def enter(spot, count, left, right):
    barrier = pltpu.get_barrier_semaphore()

    @pl.when(spot > 0)
    def _():
        pl.semaphore_signal(barrier, inc=1, device_id=left, device_id_type=MESH)

    @pl.when(spot < count - 1)
    def _():
        pl.semaphore_signal(barrier, inc=1, device_id=right, device_id_type=MESH)

    inside = (spot > 0) & (spot < count - 1)

    @pl.when(inside)
    def _():
        pl.semaphore_wait(barrier, 2)

    @pl.when(jnp.logical_not(inside))
    def _():
        pl.semaphore_wait(barrier, 1)


class Swap:
    def __init__(self, where, to_left, to_right, from_left, from_right, sems):
        self.spot, self.count, left, right = where
        self.go_left = pltpu.make_async_remote_copy(
            src_ref=to_left,
            dst_ref=from_right,
            send_sem=sems.at[0],
            recv_sem=sems.at[1],
            device_id=left,
            device_id_type=MESH,
        )
        self.go_right = pltpu.make_async_remote_copy(
            src_ref=to_right,
            dst_ref=from_left,
            send_sem=sems.at[2],
            recv_sem=sems.at[3],
            device_id=right,
            device_id_type=MESH,
        )

    def start(self):
        @pl.when(self.spot > 0)
        def _():
            self.go_left.start()

        @pl.when(self.spot < self.count - 1)
        def _():
            self.go_right.start()

    def wait(self):
        @pl.when(self.spot > 0)
        def _():
            self.go_left.wait_send()
            self.go_right.wait_recv()

        @pl.when(self.spot < self.count - 1)
        def _():
            self.go_right.wait_send()
            self.go_left.wait_recv()


def clear_ends(spot, count, from_left, from_right):
    @pl.when(spot == 0)
    def _():
        from_left[...] = jnp.zeros_like(from_left)

    @pl.when(spot == count - 1)
    def _():
        from_right[...] = jnp.zeros_like(from_right)


def group_matrix():
    i = lax.broadcasted_iota(jnp.int32, (C, C), 0) // GW
    j = lax.broadcasted_iota(jnp.int32, (C, C), 1) // GW
    return (i == j).astype(F32)


def spread(rows, count):
    return jnp.broadcast_to(rows[:, None, :], (count, F, C))


def column_index(count):
    return lax.broadcasted_iota(jnp.int32, (count, F, C), 1)


def column_shifts(act, count):
    col = column_index(count)
    before = jnp.where(col == 0, 0.0, pltpu.roll(act, 1, 1))
    after = jnp.where(col == F - 1, 0.0, pltpu.roll(act, F - 1, 1))
    return before, after


def store_shifts(xc, at, act, count):
    before, after = column_shifts(act, count)
    size = count * F
    xc[pl.ds(at, size), 0:C] = before.reshape(size, C).astype(BF)
    xc[pl.ds(at, size), C : 2 * C] = act.reshape(size, C).astype(BF)
    xc[pl.ds(at, size), 2 * C : 3 * C] = after.reshape(size, C).astype(BF)


def loop(count, body):
    def step(i, carry):
        body(i)
        return carry

    lax.fori_loop(0, count, step, 0)


def chunk_at(i, size=CH):
    return pl.multiple_of(i * size, size)


class Clip:
    def __init__(self, same, rowtab, edge, gmat):
        self.same, self.rowtab, self.edge, self.gmat = same, rowtab, edge, gmat

    def pack(self, rs, rq, to_left, to_right):
        first = hdot(self.edge[...], rs[...])
        second = hdot(self.edge[...], rq[...])
        to_left[0:1] = first[0:1]
        to_left[1:2] = second[0:1]
        to_right[0:1] = first[1:2]
        to_right[1:2] = second[1:2]

    def means(self, rs, rq, gain, from_left, from_right):
        at_left = self.rowtab[:, 1:2] > 0.0
        at_right = self.rowtab[:, 2:3] > 0.0
        inverse = self.rowtab[:, 0:1]
        results = []
        for index, table in ((0, rs), (1, rq)):
            total = hdot(self.same[...], table[...])
            total = total + jnp.where(at_left, from_left[index : index + 1], 0.0)
            total = total + jnp.where(at_right, from_right[index : index + 1], 0.0)
            total = total * inverse
            if gain is not None:
                total = total * gain
            results.append(hdot(total, self.gmat[...]))
        return results


def row_masks(rowtab, prev_mask, next_mask, rows):
    prev_mask[...] = jnp.broadcast_to(rowtab[0:rows, 3:4], (rows, C))
    next_mask[...] = jnp.broadcast_to(rowtab[0:rows, 4:5], (rows, C))


def front_kernel(
    nt,
    nf,
    lat,
    film,
    conv,
    proj,
    vec,
    same,
    rowtab,
    edge,
    zhat1,
    zhat2,
    zhat3,
    rstd1,
    rstd2,
    rstd3,
    resid,
    inner,
    query,
    kext,
    vext,
    gmat,
    rs,
    rq,
    mean,
    prev_mask,
    next_mask,
    xc,
    z_prev,
    z_here,
    z_next,
    hidden,
    to_left,
    to_right,
    from_left,
    from_right,
    msg_sems,
    kv_sems,
):
    px = lat.shape[0]
    rows = px // F
    chunks = px // CH
    spot, left, right = place(nt, nf)
    count = nt * nf
    where = (spot, count, left, right)
    enter(spot, count, left, right)
    clear_ends(spot, count, from_left, from_right)

    @pl.when(spot == 0)
    def _():
        kext[0:px] = jnp.zeros((px, C), BF)
        vext[0:px] = jnp.zeros((px, C), BF)

    @pl.when(spot == count - 1)
    def _():
        kext[2 * px : 3 * px] = jnp.zeros((px, C), BF)
        vext[2 * px : 3 * px] = jnp.zeros((px, C), BF)

    gmat[...] = group_matrix()
    row_masks(rowtab, prev_mask, next_mask, rows)
    clip = Clip(same, rowtab, edge, gmat)

    def v(i):
        return vec[i : i + 1]

    def norm_stage(step, load, zhat, rstd, rim):
        def sums(c):
            x3 = load(c).reshape(CR, F, C)
            rs[pl.ds(chunk_at(c, CR), CR)] = jnp.sum(x3, axis=1)
            rq[pl.ds(chunk_at(c, CR), CR)] = jnp.sum(x3 * x3, axis=1)

        loop(chunks, sums)
        clip.pack(rs, rq, to_left.at[step], to_right.at[step])
        first, last = rim()
        to_left[step, 8:16] = first
        to_right[step, 8:16] = last
        swap = Swap(
            where,
            to_left.at[step],
            to_right.at[step],
            from_left.at[step],
            from_right.at[step],
            msg_sems.at[step],
        )
        swap.start()
        swap.wait()
        mean_rows, square_rows = clip.means(rs, rq, None, from_left.at[step], from_right.at[step])
        mean[...] = mean_rows
        rstd[...] = lax.rsqrt(square_rows - mean_rows * mean_rows + norm_eps)
        rim_raw = jnp.concatenate([from_left[step, 8:16], from_right[step, 8:16]], axis=0)
        rim3 = rim_raw.reshape(2, F, C)
        rim_hat = (rim3 - spread(mean[rows : rows + 2], 2)) * spread(rstd[rows : rows + 2], 2)
        if zhat.shape[0] > px:
            zhat[px : px + 16] = rim_hat.reshape(16, C)
        return rim_hat

    def normed(load, zhat, rstd, c):
        r0 = chunk_at(c, CR)
        x3 = load(c).reshape(CR, F, C)
        hat = (x3 - spread(mean[pl.ds(r0, CR)], CR)) * spread(rstd[pl.ds(r0, CR)], CR)
        zhat[pl.ds(chunk_at(c), CH)] = hat.reshape(CH, C)
        return hat

    def conv_stage(rim_hat, load, zhat, rstd, gain, shift, kernel, finish):
        pre = rim_hat * gain + shift
        store_shifts(xc, px, (pre * jax.nn.sigmoid(pre)).astype(BF).astype(F32), 2)

        def build(c):
            pre = normed(load, zhat, rstd, c) * gain + shift
            act = (pre * jax.nn.sigmoid(pre)).astype(BF).astype(F32)
            store_shifts(xc, chunk_at(c), act, CR)

        loop(chunks, build)

        def product(c):
            p0 = chunk_at(c)
            part = xc[pl.ds(p0, CH)]
            z_prev[pl.ds(pl.multiple_of(p0 + 8, 8), CH)] = mm(part, kernel[0 : 3 * C])
            z_here[pl.ds(p0, CH)] = mm(part, kernel[3 * C : 6 * C])
            z_next[pl.ds(p0, CH)] = mm(part, kernel[6 * C : 9 * C])

        loop(chunks, product)
        part = xc[px : px + 16]
        z_prev[0:8] = mm(part, kernel[0 : 3 * C])[0:8]
        z_next[px : px + 8] = mm(part, kernel[6 * C : 9 * C])[8:16]

        def join(c):
            p0 = chunk_at(c)
            r0 = chunk_at(c, CR)
            keep_prev = spread(prev_mask[pl.ds(r0, CR)], CR) > 0.0
            keep_next = spread(next_mask[pl.ds(r0, CR)], CR) > 0.0
            out = z_here[pl.ds(p0, CH)].reshape(CR, F, C)
            out = out + jnp.where(keep_prev, z_prev[pl.ds(p0, CH)].reshape(CR, F, C), 0.0)
            after = z_next[pl.ds(pl.multiple_of(p0 + 8, 8), CH)].reshape(CR, F, C)
            finish(c, out + jnp.where(keep_next, after, 0.0))

        loop(chunks, join)

    def load_latent(c):
        return lat[pl.ds(chunk_at(c), CH)].astype(F32)

    def load_hidden(c):
        return hidden[pl.ds(chunk_at(c), CH)]

    def load_resid(c):
        return resid[pl.ds(chunk_at(c), CH)]

    rim_hat = norm_stage(
        0,
        load_latent,
        zhat1,
        rstd1,
        lambda: (lat[0:16].astype(F32)[0:8], lat[px - 16 : px].astype(F32)[8:16]),
    )

    def finish_one(c, out):
        r0 = chunk_at(c, CR)
        out = out + v(2) + spread(film[pl.ds(r0, CR)], CR)
        hidden[pl.ds(chunk_at(c), CH)] = out.reshape(CH, C)

    conv_stage(rim_hat, load_latent, zhat1, rstd1, v(0), v(1), conv.at[0], finish_one)

    rim_hat = norm_stage(
        1, load_hidden, zhat2, rstd2, lambda: (hidden[0:8], hidden[px - 8 : px])
    )

    def finish_two(c, out):
        p0 = chunk_at(c)
        total = lat[pl.ds(p0, CH)].astype(F32) + out.reshape(CH, C) + v(6)
        resid[pl.ds(p0, CH)] = total

    conv_stage(rim_hat, load_hidden, zhat2, rstd2, v(4), v(5), conv.at[1], finish_two)

    norm_stage(2, load_resid, zhat3, rstd3, lambda: (resid[0:8], resid[px - 8 : px]))

    def project(c):
        p0 = chunk_at(c)
        hat = normed(load_resid, zhat3, rstd3, c).reshape(CH, C)
        low = (hat * v(7) + v(8)).astype(BF)
        value = mm(low, proj[0]) + v(9)
        inner[pl.ds(p0, CH)] = value
        inner_low = value.astype(BF)
        query[pl.ds(p0, CH)] = mm(inner_low, proj[1]).astype(BF)
        kext[pl.ds(pl.multiple_of(px + p0, CH), CH)] = mm(inner_low, proj[2]).astype(BF)
        vext[pl.ds(pl.multiple_of(px + p0, CH), CH)] = mm(inner_low, proj[3]).astype(BF)

    loop(chunks, project)
    swaps = []
    for index, ext in enumerate((kext, vext)):
        swaps.append(
            Swap(
                where,
                ext.at[px : 2 * px],
                ext.at[px : 2 * px],
                ext.at[0:px],
                ext.at[2 * px : 3 * px],
                kv_sems.at[index],
            )
        )
    for swap in swaps:
        swap.start()
    for swap in swaps:
        swap.wait()


def vmem(count):
    return [pl.BlockSpec(memory_space=pltpu.VMEM)] * count


def front(nt, nf, lat, film, conv, proj, vec, same, rowtab, edge):
    px = lat.shape[0]
    rows = px // F
    tab = rowtab.shape[0]
    shapes = (
        ((px, C), F32),
        ((px + 16, C), F32),
        ((px + 16, C), F32),
        ((tab, C), F32),
        ((tab, C), F32),
        ((tab, C), F32),
        ((px, C), F32),
        ((px, C), F32),
        ((px, C), BF),
        ((3 * px, C), BF),
        ((3 * px, C), BF),
    )
    return pl.pallas_call(
        partial(front_kernel, nt, nf),
        out_shape=[jax.ShapeDtypeStruct(s, d) for s, d in shapes],
        in_specs=vmem(8),
        out_specs=vmem(len(shapes)),
        scratch_shapes=[
            pltpu.VMEM((C, C), F32),
            pltpu.VMEM((rows, C), F32),
            pltpu.VMEM((rows, C), F32),
            pltpu.VMEM((tab, C), F32),
            pltpu.VMEM((rows, C), F32),
            pltpu.VMEM((rows, C), F32),
            pltpu.VMEM((px + 16, 3 * C), BF),
            pltpu.VMEM((px + 16, C), F32),
            pltpu.VMEM((px, C), F32),
            pltpu.VMEM((px + 16, C), F32),
            pltpu.VMEM((px, C), F32),
            pltpu.VMEM((3, 16, C), F32),
            pltpu.VMEM((3, 16, C), F32),
            pltpu.VMEM((3, 16, C), F32),
            pltpu.VMEM((3, 16, C), F32),
            pltpu.SemaphoreType.DMA((3, 4)),
            pltpu.SemaphoreType.DMA((2, 4)),
        ],
        compiler_params=pltpu.CompilerParams(
            collective_id=1, has_side_effects=True, vmem_limit_bytes=VMEM_LIMIT
        ),
        name="front",
    )(lat, film, conv, proj, vec, same, rowtab, edge)


def head_mask(h):
    lane = lax.broadcasted_iota(jnp.int32, (CH, C), 1)
    return (lane >= h * HD) & (lane < (h + 1) * HD)


def head_rows(h):
    return slice(h * HD, (h + 1) * HD)


def turned(block):
    return block.astype(F32).T


def score_bias(segk, segq, key_row, q0):
    keys = jnp.broadcast_to(segk[pl.ds(key_row, CR), 0:1], (CR, C))
    keys = spread(keys, CR).reshape(CH, C)
    return jnp.where(keys == segq[0:1, pl.ds(q0, CH)], 0.0, masked_score)


def attend_kernel(meta, query, kext, vext, segq, segk, mixed, mixed_t, lse, vt, qm, bias, top, tot, acc):
    px = query.shape[0]
    factor = score_scale * LOG2E

    def turn(i):
        k0 = chunk_at(i)
        vt[:, pl.ds(k0, CH)] = turned(vext[pl.ds(k0, CH)]).astype(BF)

    loop(vext.shape[0] // CH, turn)

    def tile(t):
        q0 = chunk_at(t)
        block = query[pl.ds(q0, CH)].astype(F32)
        for h in range(H):
            qm[h] = jnp.where(head_mask(h), block, 0.0).astype(BF)
        top[...] = jnp.full((H, CH), masked_score, F32)
        tot[...] = jnp.zeros((H, CH), F32)
        acc[...] = jnp.zeros((C, CH), F32)

        def keys(i):
            row = meta[0, t] * 16 + i * CR
            base = pl.multiple_of(row * F, 128)
            bias[...] = score_bias(segk, segq, pl.multiple_of(row, 16), q0)
            key = kext[pl.ds(base, CH)]
            for h in range(H):
                raw = mm_nt(key, qm[h]) + bias[...]
                old = top[h : h + 1]
                new = jnp.maximum(old, jnp.max(raw, axis=0, keepdims=True))
                fade = jnp.exp2((old - new) * factor)
                weight = jnp.exp2((raw - new) * factor)
                top[h : h + 1] = new
                tot[h : h + 1] = tot[h : h + 1] * fade + jnp.sum(weight, axis=0, keepdims=True)
                part = mm(vt[head_rows(h), pl.ds(base, CH)], weight.astype(BF))
                acc[head_rows(h)] = acc[head_rows(h)] * fade + part

        loop(meta[1, t], keys)
        for h in range(H):
            acc[head_rows(h)] = acc[head_rows(h)] / tot[h : h + 1]
        lse[:, pl.ds(q0, CH)] = top[...] * factor + jnp.log2(tot[...])
        mixed_t[:, pl.ds(q0, CH)] = acc[...].astype(BF)
        mixed[pl.ds(q0, CH)] = acc[...].T.astype(BF)

    loop(px // CH, tile)


def attend(meta, query, kext, vext, segq, segk):
    px = query.shape[0]
    ext = kext.shape[0]
    return pl.pallas_call(
        attend_kernel,
        out_shape=[
            jax.ShapeDtypeStruct((px, C), BF),
            jax.ShapeDtypeStruct((C, px), BF),
            jax.ShapeDtypeStruct((H, px), F32),
        ],
        in_specs=[pl.BlockSpec(memory_space=pltpu.SMEM)] + vmem(5),
        out_specs=vmem(3),
        scratch_shapes=[
            pltpu.VMEM((C, ext), BF),
            pltpu.VMEM((H, CH, C), BF),
            pltpu.VMEM((CH, CH), F32),
            pltpu.VMEM((H, CH), F32),
            pltpu.VMEM((H, CH), F32),
            pltpu.VMEM((C, CH), F32),
        ],
        compiler_params=pltpu.CompilerParams(vmem_limit_bytes=VMEM_LIMIT),
        name="attend",
    )(meta, query, kext, vext, segq, segk)


def attend_back_kernel(
    meta,
    query,
    kext,
    vext,
    segq,
    segk,
    gmix,
    mixed_t,
    lse,
    dq,
    dk_own,
    dv_own,
    dk_rim,
    dv_rim,
    kt,
    qm,
    gm,
    qt,
    gt,
    inner_rows,
    bias,
    dqt,
    dkt,
    dvt,
):
    px = query.shape[0]
    ext = kext.shape[0]
    factor = score_scale * LOG2E

    def turn(i):
        k0 = chunk_at(i)
        kt[:, pl.ds(k0, CH)] = turned(kext[pl.ds(k0, CH)]).astype(BF)
        dkt[:, pl.ds(k0, CH)] = jnp.zeros((C, CH), F32)
        dvt[:, pl.ds(k0, CH)] = jnp.zeros((C, CH), F32)

    loop(ext // CH, turn)

    def tile(t):
        q0 = chunk_at(t)
        block = query[pl.ds(q0, CH)].astype(F32)
        grad = gmix[pl.ds(q0, CH)].astype(F32)
        for h in range(H):
            qm[h] = jnp.where(head_mask(h), block, 0.0).astype(BF)
            gm[h] = jnp.where(head_mask(h), grad, 0.0).astype(BF)
        qt[...] = block.T.astype(BF)
        grad_t = grad.T
        gt[...] = grad_t.astype(BF)
        crossed = grad_t * mixed_t[:, pl.ds(q0, CH)].astype(F32)
        inner_rows[...] = jnp.sum(crossed.reshape(H, HD, CH), axis=1)
        dqt[...] = jnp.zeros((C, CH), F32)

        def keys(i):
            row = meta[0, t] * 16 + i * CR
            base = pl.multiple_of(row * F, 128)
            bias[...] = score_bias(segk, segq, pl.multiple_of(row, 16), q0)
            key = kext[pl.ds(base, CH)]
            val = vext[pl.ds(base, CH)]
            for h in range(H):
                raw = mm_nt(key, qm[h]) + bias[...]
                probs = jnp.exp2(raw * factor - lse[h : h + 1, pl.ds(q0, CH)])
                gprob = mm_nt(val, gm[h])
                gscore = (probs * (gprob - inner_rows[h : h + 1]) * score_scale).astype(BF)
                dvt[head_rows(h), pl.ds(base, CH)] += mm_nt(gt[head_rows(h)], probs.astype(BF))
                dkt[head_rows(h), pl.ds(base, CH)] += mm_nt(qt[head_rows(h)], gscore)
                dqt[head_rows(h)] += mm(kt[head_rows(h), pl.ds(base, CH)], gscore)

        loop(meta[1, t], keys)
        dq[pl.ds(q0, CH)] = dqt[...].T.astype(BF)

    loop(px // CH, tile)

    def own(i):
        k0 = chunk_at(i)
        k1 = pl.multiple_of(px + k0, CH)
        dk_own[pl.ds(k0, CH)] = dkt[:, pl.ds(k1, CH)].T
        dv_own[pl.ds(k0, CH)] = dvt[:, pl.ds(k1, CH)].T
        k2 = pl.multiple_of(2 * px + k0, CH)
        dk_rim[0, pl.ds(k0, CH)] = dkt[:, pl.ds(k0, CH)].T.astype(BF)
        dv_rim[0, pl.ds(k0, CH)] = dvt[:, pl.ds(k0, CH)].T.astype(BF)
        dk_rim[1, pl.ds(k0, CH)] = dkt[:, pl.ds(k2, CH)].T.astype(BF)
        dv_rim[1, pl.ds(k0, CH)] = dvt[:, pl.ds(k2, CH)].T.astype(BF)

    loop(px // CH, own)


def attend_back(meta, query, kext, vext, segq, segk, gmix, mixed_t, lse):
    px = query.shape[0]
    ext = kext.shape[0]
    return pl.pallas_call(
        attend_back_kernel,
        out_shape=[
            jax.ShapeDtypeStruct((px, C), BF),
            jax.ShapeDtypeStruct((px, C), F32),
            jax.ShapeDtypeStruct((px, C), F32),
            jax.ShapeDtypeStruct((2, px, C), BF),
            jax.ShapeDtypeStruct((2, px, C), BF),
        ],
        in_specs=[pl.BlockSpec(memory_space=pltpu.SMEM)] + vmem(8),
        out_specs=vmem(5),
        scratch_shapes=[
            pltpu.VMEM((C, ext), BF),
            pltpu.VMEM((H, CH, C), BF),
            pltpu.VMEM((H, CH, C), BF),
            pltpu.VMEM((C, CH), BF),
            pltpu.VMEM((C, CH), BF),
            pltpu.VMEM((H, CH), F32),
            pltpu.VMEM((CH, CH), F32),
            pltpu.VMEM((C, CH), F32),
            pltpu.VMEM((C, ext), F32),
            pltpu.VMEM((C, ext), F32),
        ],
        compiler_params=pltpu.CompilerParams(vmem_limit_bytes=VMEM_LIMIT),
        name="attend_back",
    )(meta, query, kext, vext, segq, segk, gmix, mixed_t, lse)


def middle_kernel(
    inner,
    mixed,
    resid,
    cot,
    proj,
    mlp,
    vec,
    output,
    gafter,
    gmix,
    gw_out,
    gw_down,
    gw_up,
    gw_attn,
    sums,
    after_low,
    act_low,
    pre_low,
    down_low,
    mlp_low,
    after_grad_low,
    ubias,
):
    px = inner.shape[0]
    tail = 11 + FF // C
    sums[...] = jnp.zeros_like(sums)
    for j in range(FF // C):
        ubias[:, j * C : (j + 1) * C] = vec[11 + j : 12 + j]

    def step(c):
        p0 = chunk_at(c)
        after = inner[pl.ds(p0, CH)] + mm(mixed[pl.ds(p0, CH)], proj[4]) + vec[10:11]
        low = after.astype(BF)
        after_low[pl.ds(p0, CH)] = low
        grad_out = cot[pl.ds(p0, CH)]
        grad_mlp = mm_nt(grad_out, proj[5])
        down = grad_mlp.astype(BF)
        down_low[pl.ds(p0, CH)] = down
        total = after
        grad_after = grad_mlp
        for j in range(FF // C):
            part = slice(j * C, (j + 1) * C)
            pre = mm_nt(low, mlp[0, part]) + ubias[:, part]
            cdf = 0.5 + 0.5 * lax.erf(pre * (0.5**0.5))
            act = (pre * cdf).astype(BF)
            act_low[pl.ds(p0, CH), part] = act
            total = total + mm(act, mlp[1, part])
            density = jnp.exp(pre * pre * -0.5) * 0.3989422804014327
            grad_pre = mm_nt(down, mlp[1, part]) * (cdf + pre * density)
            sums[3 + j : 4 + j] += jnp.sum(grad_pre, axis=0, keepdims=True)
            grad_low = grad_pre.astype(BF)
            pre_low[pl.ds(p0, CH), part] = grad_low
            grad_after = grad_after + mm(grad_low, mlp[0, part])
        total = (total + vec[tail : tail + 1]).astype(BF)
        mlp_low[pl.ds(p0, CH)] = total
        branch = mm(total, proj[5]) + vec[tail + 1 : tail + 2]
        output[pl.ds(p0, CH)] = (resid[pl.ds(p0, CH)] + branch).astype(BF)
        gafter[pl.ds(p0, CH)] = grad_after
        grad_low = grad_after.astype(BF)
        after_grad_low[pl.ds(p0, CH)] = grad_low
        gmix[pl.ds(p0, CH)] = mm_nt(grad_low, proj[4]).astype(BF)
        sums[0:1] += jnp.sum(grad_out.astype(F32), axis=0, keepdims=True)
        sums[1:2] += jnp.sum(grad_mlp, axis=0, keepdims=True)
        sums[2:3] += jnp.sum(grad_after, axis=0, keepdims=True)

    loop(px // CH, step)
    gw_out[...] = mm_tn(mlp_low[...], cot[...])
    gw_attn[...] = mm_tn(mixed[...], after_grad_low[...])
    for j in range(FF // C):
        part = slice(j * C, (j + 1) * C)
        gw_down[part] = mm_tn(act_low[:, part], down_low[...])
        gw_up[part] = mm_tn(pre_low[:, part], after_low[...])


def middle(inner, mixed, resid, cot, proj, mlp, vec):
    px = inner.shape[0]
    return pl.pallas_call(
        middle_kernel,
        out_shape=[
            jax.ShapeDtypeStruct((px, C), BF),
            jax.ShapeDtypeStruct((px, C), F32),
            jax.ShapeDtypeStruct((px, C), BF),
            jax.ShapeDtypeStruct((C, C), F32),
            jax.ShapeDtypeStruct((FF, C), F32),
            jax.ShapeDtypeStruct((FF, C), F32),
            jax.ShapeDtypeStruct((C, C), F32),
            jax.ShapeDtypeStruct((8, C), F32),
        ],
        in_specs=vmem(7),
        out_specs=vmem(8),
        scratch_shapes=[
            pltpu.VMEM((px, C), BF),
            pltpu.VMEM((px, FF), BF),
            pltpu.VMEM((px, FF), BF),
            pltpu.VMEM((px, C), BF),
            pltpu.VMEM((px, C), BF),
            pltpu.VMEM((px, C), BF),
            pltpu.VMEM((1, FF), F32),
        ],
        compiler_params=pltpu.CompilerParams(vmem_limit_bytes=VMEM_LIMIT),
        name="middle",
    )(inner, mixed, resid, cot, proj, mlp, vec)


def back_kernel(
    nt,
    nf,
    dq,
    dk_own,
    dv_own,
    dk_rim,
    dv_rim,
    gafter,
    inner,
    zhat1,
    zhat2,
    zhat3,
    rstd1,
    rstd2,
    rstd3,
    cot,
    conv,
    proj,
    vec,
    same,
    rowtab,
    edge,
    glat,
    gproj,
    gconv,
    sums,
    film_rows,
    gmat,
    rs,
    rq,
    mean_e,
    mean_ez,
    prev_mask,
    next_mask,
    inner_low,
    normed_low,
    grad_low,
    dk_low,
    dv_low,
    gresid,
    dgrad,
    two,
    xc,
    shifted,
    dk_got,
    dv_got,
    to_left,
    to_right,
    from_left,
    from_right,
    msg_sems,
    kv_sems,
):
    px = dq.shape[0]
    rows = px // F
    chunks = px // CH
    spot, left, right = place(nt, nf)
    count = nt * nf
    where = (spot, count, left, right)
    enter(spot, count, left, right)
    swaps = []
    for index, (rim, got) in enumerate(((dk_rim, dk_got), (dv_rim, dv_got))):
        swaps.append(
            Swap(where, rim.at[0], rim.at[1], got.at[0], got.at[1], kv_sems.at[index])
        )
    for swap in swaps:
        swap.start()
    clear_ends(spot, count, from_left, from_right)
    clear_ends(spot, count, dk_got.at[0], dk_got.at[1])
    clear_ends(spot, count, dv_got.at[0], dv_got.at[1])
    gmat[...] = group_matrix()
    row_masks(rowtab, prev_mask, next_mask, rows)
    clip = Clip(same, rowtab, edge, gmat)
    sums[...] = jnp.zeros_like(sums)

    def v(i):
        return vec[i : i + 1]

    def first(c):
        p0 = chunk_at(c)
        inner_low[pl.ds(p0, CH)] = inner[pl.ds(p0, CH)].astype(BF)
        hat = zhat3[pl.ds(p0, CH)]
        normed_low[pl.ds(p0, CH)] = (hat * v(7) + v(8)).astype(BF)
        gresid[pl.ds(p0, CH)] = gafter[pl.ds(p0, CH)] + mm_nt(dq[pl.ds(p0, CH)], proj[1])

    loop(chunks, first)
    gproj[1] = mm_tn(inner_low[...], dq[...])
    for swap in swaps:
        swap.wait()

    def row_sums(c, grad3, hat3):
        rs[pl.ds(chunk_at(c, CR), CR)] = jnp.sum(grad3, axis=1)
        rq[pl.ds(chunk_at(c, CR), CR)] = jnp.sum(grad3 * hat3, axis=1)

    def second(c):
        p0 = chunk_at(c)
        part = pl.ds(p0, CH)
        dk = (dk_own[part] + dk_got[0, part].astype(F32) + dk_got[1, part].astype(F32)).astype(BF)
        dv = (dv_own[part] + dv_got[0, part].astype(F32) + dv_got[1, part].astype(F32)).astype(BF)
        dk_low[part] = dk
        dv_low[part] = dv
        grad = gresid[part] + mm_nt(dk, proj[2]) + mm_nt(dv, proj[3])
        sums[9:10] += jnp.sum(grad, axis=0, keepdims=True)
        low = grad.astype(BF)
        grad_low[part] = low
        d3 = mm_nt(low, proj[0])
        dgrad[part] = d3
        row_sums(c, d3.reshape(CR, F, C), zhat3[part].reshape(CR, F, C))

    loop(chunks, second)

    def swap_step(step, rim_first, rim_last):
        clip.pack(rs, rq, to_left.at[step], to_right.at[step])
        if rim_first is not None:
            to_left[step, 8 : 8 + rim_first.shape[0]] = rim_first
            to_right[step, 8 : 8 + rim_last.shape[0]] = rim_last
        swap = Swap(
            where,
            to_left.at[step],
            to_right.at[step],
            from_left.at[step],
            from_right.at[step],
            msg_sems.at[step],
        )
        swap.start()
        return swap

    def set_means(step, gain):
        mean_e[...], mean_ez[...] = clip.means(
            rs, rq, gain, from_left.at[step], from_right.at[step]
        )

    def back_norm(grad3, hat3, rstd, gain, r0, size):
        value = grad3 * gain - spread(mean_e[pl.ds(r0, size)], size)
        value = value - hat3 * spread(mean_ez[pl.ds(r0, size)], size)
        return value * spread(rstd[pl.ds(r0, size)], size)

    def rim_grad(step, at):
        both = jnp.concatenate([from_left[step, at : at + 8], from_right[step, at : at + 8]], axis=0)
        return both.reshape(2, F, C)

    sums[7:8] = jnp.sum(rq[...], axis=0, keepdims=True)
    sums[8:9] = jnp.sum(rs[...], axis=0, keepdims=True)
    cot_first = cot[0:16].astype(F32)[0:8]
    cot_last = cot[px - 16 : px].astype(F32)[8:16]
    swap = swap_step(
        0,
        jnp.concatenate([dgrad[0:8], cot_first], axis=0),
        jnp.concatenate([dgrad[px - 8 : px], cot_last], axis=0),
    )
    gproj[2] = mm_tn(inner_low[...], dk_low[...])
    gproj[3] = mm_tn(inner_low[...], dv_low[...])
    gproj[0] = mm_tn(normed_low[...], grad_low[...])
    swap.wait()
    set_means(0, v(7))

    def set_rims(value):
        low = value.astype(BF).astype(F32)
        two[0:8] = low[0]
        two[px + 8 : px + 16] = low[1]

    rim = rim_grad(0, 8)
    rim_hat = zhat3[px : px + 16].reshape(2, F, C)
    set_rims(rim_grad(0, 16) + back_norm(rim, rim_hat, rstd3, v(7), rows, 2))

    def third(c):
        p0 = chunk_at(c)
        part = pl.ds(p0, CH)
        grad3 = dgrad[part].reshape(CR, F, C)
        hat3 = zhat3[part].reshape(CR, F, C)
        value = back_norm(grad3, hat3, rstd3, v(7), chunk_at(c, CR), CR).reshape(CH, C)
        value = cot[part].astype(F32) + value
        gresid[part] = value
        sums[6:7] += jnp.sum(value, axis=0, keepdims=True)
        two[pl.ds(pl.multiple_of(p0 + 8, 8), CH)] = value.astype(BF).astype(F32)

    loop(chunks, third)

    def conv_back(kernel, zhat, gain, shift):
        def step(c):
            p0 = chunk_at(c)
            part = pl.ds(p0, CH)
            r0 = chunk_at(c, CR)
            keep_prev = spread(prev_mask[pl.ds(r0, CR)], CR).reshape(CH, C) > 0.0
            keep_next = spread(next_mask[pl.ds(r0, CR)], CR).reshape(CH, C) > 0.0
            after = two[pl.ds(pl.multiple_of(p0 + 16, 16), CH)]
            here = two[pl.ds(pl.multiple_of(p0 + 8, 8), CH)]
            low0 = jnp.where(keep_next, after, 0.0).astype(BF)
            low1 = here.astype(BF)
            low2 = jnp.where(keep_prev, two[part], 0.0).astype(BF)
            shifted[part, 0:C] = low0
            shifted[part, C : 2 * C] = low1
            shifted[part, 2 * C : 3 * C] = low2
            hat = zhat[part]
            pre = hat * gain + shift
            sig = jax.nn.sigmoid(pre)
            act = (pre * sig).astype(BF).astype(F32).reshape(CR, F, C)
            store_shifts(xc, p0, act, CR)

            def columns(j):
                piece = slice(j * C, (j + 1) * C)
                value = mm_nt(low0, kernel[0 : 3 * C][piece])
                value = value + mm_nt(low1, kernel[3 * C : 6 * C][piece])
                value = value + mm_nt(low2, kernel[6 * C : 9 * C][piece])
                return value.reshape(CR, F, C)

            col = column_index(CR)
            back = columns(1)
            back = back + jnp.where(col == F - 1, 0.0, pltpu.roll(columns(0), F - 1, 1))
            back = back + jnp.where(col == 0, 0.0, pltpu.roll(columns(2), 1, 1))
            grad = back.reshape(CH, C) * sig * (1.0 + pre * (1.0 - sig))
            dgrad[part] = grad
            row_sums(c, grad.reshape(CR, F, C), hat.reshape(CR, F, C))

        loop(chunks, step)

    def kernel_grad(which):
        for d in range(3):
            for j in range(3):
                gconv[which, d * 3 * C + j * C : d * 3 * C + (j + 1) * C] = mm_tn(
                    xc[:, j * C : (j + 1) * C], shifted[:, d * C : (d + 1) * C]
                )

    conv_back(conv.at[1], zhat2, v(4), v(5))
    sums[4:5] = jnp.sum(rq[...], axis=0, keepdims=True)
    sums[5:6] = jnp.sum(rs[...], axis=0, keepdims=True)
    swap = swap_step(1, dgrad[0:8], dgrad[px - 8 : px])
    kernel_grad(1)
    swap.wait()
    set_means(1, v(4))
    rim_hat = zhat2[px : px + 16].reshape(2, F, C)
    set_rims(back_norm(rim_grad(1, 8), rim_hat, rstd2, v(4), rows, 2))

    def fourth(c):
        p0 = chunk_at(c)
        part = pl.ds(p0, CH)
        grad3 = dgrad[part].reshape(CR, F, C)
        hat3 = zhat2[part].reshape(CR, F, C)
        value3 = back_norm(grad3, hat3, rstd2, v(4), chunk_at(c, CR), CR)
        film_rows[pl.ds(chunk_at(c, CR), CR)] = jnp.sum(value3, axis=1)
        low = value3.reshape(CH, C).astype(BF).astype(F32)
        two[pl.ds(pl.multiple_of(p0 + 8, 8), CH)] = low

    loop(chunks, fourth)
    total = jnp.sum(film_rows[...], axis=0, keepdims=True)
    sums[2:3] = total
    sums[3:4] = total
    conv_back(conv.at[0], zhat1, v(0), v(1))
    sums[0:1] = jnp.sum(rq[...], axis=0, keepdims=True)
    sums[1:2] = jnp.sum(rs[...], axis=0, keepdims=True)
    swap = swap_step(2, None, None)
    kernel_grad(0)
    swap.wait()
    set_means(2, v(0))

    def fifth(c):
        p0 = chunk_at(c)
        part = pl.ds(p0, CH)
        grad3 = dgrad[part].reshape(CR, F, C)
        hat3 = zhat1[part].reshape(CR, F, C)
        value = back_norm(grad3, hat3, rstd1, v(0), chunk_at(c, CR), CR).reshape(CH, C)
        glat[part] = (gresid[part] + value).astype(BF)

    loop(chunks, fifth)


def back(nt, nf, *args):
    px = args[0].shape[0]
    rows = px // F
    tab = args[-2].shape[0]
    big = pltpu.VMEM((px, C), F32)
    low = pltpu.VMEM((px, C), BF)
    table = pltpu.VMEM((rows, C), F32)
    return pl.pallas_call(
        partial(back_kernel, nt, nf),
        out_shape=[
            jax.ShapeDtypeStruct((px, C), BF),
            jax.ShapeDtypeStruct((4, C, C), F32),
            jax.ShapeDtypeStruct((2, TAPS * C, C), F32),
            jax.ShapeDtypeStruct((16, C), F32),
            jax.ShapeDtypeStruct((rows, C), F32),
        ],
        in_specs=vmem(len(args)),
        out_specs=vmem(5),
        scratch_shapes=[
            pltpu.VMEM((C, C), F32),
            table,
            table,
            pltpu.VMEM((tab, C), F32),
            pltpu.VMEM((tab, C), F32),
            table,
            table,
            low,
            low,
            low,
            low,
            low,
            big,
            big,
            pltpu.VMEM((px + 16, C), F32),
            pltpu.VMEM((px, 3 * C), BF),
            pltpu.VMEM((px, 3 * C), BF),
            pltpu.VMEM((2, px, C), BF),
            pltpu.VMEM((2, px, C), BF),
            pltpu.VMEM((3, 24, C), F32),
            pltpu.VMEM((3, 24, C), F32),
            pltpu.VMEM((3, 24, C), F32),
            pltpu.VMEM((3, 24, C), F32),
            pltpu.SemaphoreType.DMA((3, 4)),
            pltpu.SemaphoreType.DMA((2, 4)),
        ],
        compiler_params=pltpu.CompilerParams(
            collective_id=2, has_side_effects=True, vmem_limit_bytes=VMEM_LIMIT
        ),
        name="back",
    )(*args)


def adamw_step(weight, moment, second, grad, decay_rate):
    moment_new = beta_first * moment + (1.0 - beta_first) * grad
    second_new = beta_second * second + (1.0 - beta_second) * grad * grad
    moment_hat = moment_new / (1.0 - beta_first**STEP)
    second_hat = second_new / (1.0 - beta_second**STEP)
    weight_new = weight - learn_rate * (
        moment_hat / (jnp.sqrt(second_hat) + adam_eps) + decay_rate * weight
    )
    return (weight_new, moment_new, second_new)


def turn_blocks(array, nf, odd):
    rows = array.shape[0]
    blocks = array.reshape((nf, rows // nf) + array.shape[1:])
    return jnp.where(odd, blocks[::-1], blocks).reshape(array.shape)


def to_time(array, nf, odd):
    turned_rows = turn_blocks(array, nf, odd)
    whole = lax.all_to_all(turned_rows, "freq", split_axis=0, concat_axis=1, tiled=True)
    return whole.reshape(-1, C)


def from_time(array, nf, odd):
    whole = array.reshape(-1, F, C)
    back_rows = lax.all_to_all(whole, "freq", split_axis=1, concat_axis=0, tiled=True)
    return turn_blocks(back_rows, nf, odd)


def layout_of(lengths, spot, count, rows):
    clips = lengths.shape[0]
    clip_index = jnp.arange(clips, dtype=jnp.int32)
    upto = clip_index[:, None] >= clip_index[None, :]
    clip_ends = jnp.sum(jnp.where(upto, lengths[None, :], 0), axis=1)
    first_row = spot * rows
    total_rows = count * rows
    row = first_row - rows + jnp.arange(3 * rows, dtype=jnp.int32)
    seg_ext = jnp.sum((clip_ends[None, :] <= row[:, None]).astype(jnp.int32), axis=1)
    seg_ext = jnp.where((row >= 0) & (row < total_rows), seg_ext, -1)
    seg = seg_ext[rows : 2 * rows]
    seg_left = seg_ext[rows - 1]
    seg_right = seg_ext[2 * rows]
    pad = jnp.full((6,), -2, jnp.int32)
    seg_tab = jnp.concatenate([seg, seg_ext[rows - 1 : rows], seg_ext[2 * rows : 2 * rows + 1], pad])
    onehot = (seg_tab[:, None] == clip_index[None, :]).astype(F32)
    row_len = jnp.sum(onehot * lengths[None, :].astype(F32), axis=1)
    inverse = 1.0 / jnp.maximum(row_len * (F * GW), 1.0)
    beside_prev = jnp.concatenate([(seg_ext[rows - 1 : 2 * rows - 1] == seg).astype(F32), jnp.zeros((8,), F32)])
    beside_next = jnp.concatenate([(seg_ext[rows + 1 : 2 * rows + 1] == seg).astype(F32), jnp.zeros((8,), F32)])
    fields = (
        inverse,
        (seg_tab == seg_left).astype(F32),
        (seg_tab == seg_right).astype(F32),
        beside_prev,
        beside_next,
    )
    lane = jnp.arange(128, dtype=jnp.int32)[None, :]
    rowtab = jnp.zeros((rows + 8, 128), F32)
    for index, field in enumerate(fields):
        rowtab = jnp.where(lane == index, field[:, None], rowtab)
    same = (seg_tab[:, None] == seg[None, :]).astype(F32)
    which = jnp.arange(8, dtype=jnp.int32)[:, None]
    edge = jnp.where(which == 0, seg[None, :] == seg[0], seg[None, :] == seg[rows - 1])
    edge = jnp.where(which < 2, edge, False).astype(F32)
    segk = jnp.broadcast_to(seg_ext.astype(F32)[:, None], (3 * rows, 128))
    segq = jnp.broadcast_to(jnp.repeat(seg.astype(F32), F)[None, :], (8, rows * F))
    tiles = rows // CR
    starts = clip_ends - lengths
    low_clip = seg[::CR]
    high_clip = seg[CR - 1 :: CR]
    low_row = jnp.sum(jnp.where(low_clip[:, None] == clip_index[None, :], starts[None, :], 0), axis=1)
    high_row = jnp.sum(
        jnp.where(high_clip[:, None] == clip_index[None, :], clip_ends[None, :], 0), axis=1
    )
    low_row = low_row - first_row + rows
    high_row = high_row - first_row + rows
    low = low_row // 16
    number = (high_row - low * 16 + CR - 1) // CR
    low = jnp.minimum(low, (3 * rows - number * CR) // 16)
    meta = jnp.stack([low, number]).astype(jnp.int32)
    return same, rowtab, edge, segk, segq, meta, onehot[:rows]


def on_device(
    nt,
    nf,
    latent,
    condition,
    lengths,
    cotangent,
    conv_weight,
    conv_moment,
    conv_second,
    proj_weight,
    proj_moment,
    proj_second,
    mlp_weight,
    mlp_moment,
    mlp_second,
    emb_weight,
    emb_moment,
    emb_second,
    small_weight,
    small_moment,
    small_second,
):
    masters = (conv_weight, proj_weight, mlp_weight, emb_weight, small_weight)
    conv_full = lax.all_gather(conv_weight.astype(BF), "freq", axis=1, tiled=True)
    proj_full = lax.all_gather(proj_weight.astype(BF), "freq", axis=1, tiled=True)
    mlp_full = lax.all_gather(mlp_weight.astype(BF), "freq", axis=1, tiled=True)
    emb_full = lax.all_gather(emb_weight.astype(BF), "freq", axis=0, tiled=True)
    small_full = lax.all_gather(small_weight.astype(BF), "freq", axis=1, tiled=True)
    nsmall = small_weight.shape[0]
    vec = jnp.pad(small_full.astype(F32), ((0, 24 - nsmall), (0, 0)))
    t = lax.axis_index("tm")
    f = lax.axis_index("freq")
    odd = lax.rem(t, 2)
    spot = t * nf + f + odd * (nf - 1 - 2 * f)
    rows = latent.shape[0] // nf
    same, rowtab, edge, segk, segq, meta, onehot = layout_of(lengths, spot, nt * nf, rows)
    lat = to_time(latent, nf, odd == 1)
    cot = to_time(cotangent, nf, odd == 1)
    cond_low = jax.nn.silu(condition).astype(BF)
    film = hdot(onehot, mm(cond_low, emb_full) + vec[3])
    (zhat1, zhat2, zhat3, rstd1, rstd2, rstd3, resid, inner, query, kext, vext) = front(
        nt, nf, lat, film, conv_full, proj_full, vec, same, rowtab, edge
    )
    mixed, mixed_t, lse = attend(meta, query, kext, vext, segq, segk)
    (output, gafter, gmix, gw_out, gw_down, gw_up, gw_attn, mid_sums) = middle(
        inner, mixed, resid, cot, proj_full, mlp_full, vec
    )
    dq, dk_own, dv_own, dk_rim, dv_rim = attend_back(
        meta, query, kext, vext, segq, segk, gmix, mixed_t, lse
    )
    glat, gproj, gconv, sums, film_rows = back(
        nt,
        nf,
        dq,
        dk_own,
        dv_own,
        dk_rim,
        dv_rim,
        gafter,
        inner,
        zhat1,
        zhat2,
        zhat3,
        rstd1,
        rstd2,
        rstd3,
        cot,
        conv_full,
        proj_full,
        vec,
        same,
        rowtab,
        edge,
    )
    grad_film = lax.dot_general(
        onehot, film_rows, (((0,), (0,)), ((), ())), precision=HIGHEST
    )
    gemb = lax.dot_general(
        cond_low.astype(F32), grad_film, (((0,), (0,)), ((), ())), precision=HIGHEST
    )
    small_grad = jnp.concatenate(
        [sums[:10], mid_sums[2:3], mid_sums[3 : 3 + FF // C], mid_sums[1:2], mid_sums[0:1]], axis=0
    )
    proj_grad = jnp.concatenate([gproj, gw_attn[None], gw_out[None]], axis=0)
    mlp_grad = jnp.stack([gw_up, gw_down])
    pieces = []
    for grad in (gconv, proj_grad, mlp_grad, gemb[None]):
        stack, depth, _ = grad.shape
        cut = grad.reshape(stack, nf, depth // nf, C)
        pieces.append(jnp.transpose(cut, (1, 0, 2, 3)).reshape(nf, -1, C))
    width = C // nf
    small_cut = jnp.transpose(small_grad.reshape(nsmall, nf, width), (1, 0, 2))
    small_cut = jnp.pad(small_cut, ((0, 0), (0, 32 - nsmall), (0, C - width)))
    pieces.append(small_cut)
    flat = jnp.concatenate(pieces, axis=1).astype(BF)
    part = lax.psum_scatter(flat, "freq", scatter_dimension=0, tiled=True)[0]
    total = lax.psum(part.astype(F32), "tm")
    shares = []
    start = 0
    for master in masters[:4]:
        size = master.size // C
        shares.append(total[start : start + size].reshape(master.shape))
        start += size
    shares.append(total[start : start + nsmall, :width])
    moments = (conv_moment, proj_moment, mlp_moment, emb_moment, small_moment)
    seconds = (conv_second, proj_second, mlp_second, emb_second, small_second)
    decays = (weight_decay, weight_decay, weight_decay, weight_decay, 0.0)
    updated = []
    for position in range(5):
        updated.extend(
            adamw_step(
                masters[position],
                moments[position],
                seconds[position],
                shares[position],
                decays[position],
            )
        )
    bias_share = shares[4][nsmall - 1]
    return (
        from_time(output, nf, odd == 1),
        from_time(glat, nf, odd == 1),
        *updated,
        bias_share,
    )


def solution(mesh):
    nt, nf = mesh.shape["tm"], mesh.shape["freq"]
    rows_spec = P("tm", "freq", None)
    middle_spec = P(None, "freq", None)
    params = (middle_spec,) * 9 + (P("freq", None),) * 3 + (P(None, "freq"),) * 3
    return jax.shard_map(
        partial(on_device, nt, nf),
        mesh=mesh,
        in_specs=(rows_spec, P(), P(), rows_spec) + params,
        out_specs=(rows_spec, rows_spec) + params + (P("freq"),),
        check_vma=False,
    )
```

```python
from functools import partial

import jax
import jax.numpy as jnp
from jax import lax
from jax.experimental import pallas as pl
from jax.experimental.pallas import tpu as pltpu
from jax.sharding import PartitionSpec as P

C = 256
G = 32
GW = C // G
HD = 32
H = C // HD
FF = 1024
F = 8
MAXLEN = 128
STEP = 10
TAPS = 9
CH = 256
CR = CH // F

HIGHEST = lax.Precision.HIGHEST
norm_eps = 1e-05
beta_first = 0.9
beta_second = 0.999
learn_rate = 0.5
weight_decay = 0.01
adam_eps = 1e-08
masked_score = -1e30
score_scale = HD**-0.5
LOG2E = 1.4426950408889634
MESH = pltpu.DeviceIdType.MESH if hasattr(pltpu, "DeviceIdType") else pl.DeviceIdType.MESH
VMEM_LIMIT = 64 * 1024 * 1024 - 65536
BF = jnp.bfloat16
F32 = jnp.float32


def mm(a, b):
    return jnp.dot(a, b, preferred_element_type=F32)


def mm_nt(a, b):
    return lax.dot_general(a, b, (((1,), (1,)), ((), ())), preferred_element_type=F32)


def mm_tn(a, b):
    return lax.dot_general(a, b, (((0,), (0,)), ((), ())), preferred_element_type=F32)


def hdot(a, b):
    return jnp.dot(a, b, precision=HIGHEST, preferred_element_type=F32)


def hdot_tn(a, b):
    return lax.dot_general(
        a, b, (((0,), (0,)), ((), ())), precision=HIGHEST, preferred_element_type=F32
    )


def place(nt, nf):
    t = lax.axis_index("tm")
    f = lax.axis_index("freq")
    odd = lax.rem(t, 2)
    s = f + odd * (nf - 1 - 2 * f)
    turn = 1 - 2 * odd
    at_end = (s + 1) // nf
    at_start = 1 - (s + nf - 1) // nf
    right = {"tm": t + at_end, "freq": f + (1 - at_end) * turn}
    left = {"tm": t - at_start, "freq": f - (1 - at_start) * turn}
    return t * nf + s, left, right


def flip(x, bit):
    return x + bit - 2 * bit * lax.rem(x // bit, 2)


def flip_by(x, mask):
    bit = 1
    while bit <= mask:
        if mask & bit:
            x = flip(x, bit)
        bit *= 2
    return x


def bits_of(count):
    bits = []
    bit = 1
    while bit < count:
        bits.append(bit)
        bit *= 2
    return bits


def snake(f, t, nf):
    return f + lax.rem(t, 2) * (nf - 1 - 2 * f)


def enter(spot, count, left, right, partners):
    barrier = pltpu.get_barrier_semaphore()
    for partner in partners:
        pl.semaphore_signal(barrier, inc=1, device_id=partner, device_id_type=MESH)

    @pl.when(spot > 0)
    def _():
        pl.semaphore_signal(barrier, inc=1, device_id=left, device_id_type=MESH)

    @pl.when(spot < count - 1)
    def _():
        pl.semaphore_signal(barrier, inc=1, device_id=right, device_id_type=MESH)

    inside = (spot > 0) & (spot < count - 1)

    @pl.when(inside)
    def _():
        pl.semaphore_wait(barrier, len(partners) + 2)

    @pl.when(jnp.logical_not(inside))
    def _():
        pl.semaphore_wait(barrier, len(partners) + 1)


class Swap:
    def __init__(self, where, to_left, to_right, from_left, from_right, sems):
        self.spot, self.count, left, right = where
        self.go_left = pltpu.make_async_remote_copy(
            src_ref=to_left,
            dst_ref=from_right,
            send_sem=sems.at[0],
            recv_sem=sems.at[1],
            device_id=left,
            device_id_type=MESH,
        )
        self.go_right = pltpu.make_async_remote_copy(
            src_ref=to_right,
            dst_ref=from_left,
            send_sem=sems.at[2],
            recv_sem=sems.at[3],
            device_id=right,
            device_id_type=MESH,
        )

    def start(self):
        @pl.when(self.spot > 0)
        def _():
            self.go_left.start()

        @pl.when(self.spot < self.count - 1)
        def _():
            self.go_right.start()

    def wait(self):
        @pl.when(self.spot > 0)
        def _():
            self.go_left.wait_send()
            self.go_right.wait_recv()

        @pl.when(self.spot < self.count - 1)
        def _():
            self.go_right.wait_send()
            self.go_left.wait_recv()


def remote(src, dst, sems, device):
    return pltpu.make_async_remote_copy(
        src_ref=src,
        dst_ref=dst,
        send_sem=sems.at[0],
        recv_sem=sems.at[1],
        device_id=device,
        device_id_type=MESH,
    )


class Exchange:
    def __init__(self, source, target, own_source, own_target, f, nf, sems):
        self.copies = []
        for mask in range(1, nf):
            peer = flip_by(f, mask)
            self.copies.append(
                remote(source(peer), target(peer), sems.at[mask - 1], {"freq": peer})
            )
        self.own_source, self.own_target = own_source, own_target

    def start(self):
        for copy in self.copies[::-1]:
            copy.start()
        self.own_target[...] = self.own_source[...]

    def wait(self):
        for copy in self.copies:
            copy.wait()


class Gather:
    def __init__(self, view, f, sems):
        near = {"freq": flip(f, 1)}
        self.far = remote(view(f), view(f), sems.at[0], {"freq": flip(f, 2)})
        self.near = remote(view(f), view(f), sems.at[1], near)
        self.forward = remote(view(flip(f, 2)), view(flip(f, 2)), sems.at[2], near)

    def start(self):
        self.far.start()
        self.near.start()

    def collect(self):
        self.far.wait_recv()
        self.forward.start()
        self.near.wait_recv()
        self.forward.wait_recv()

    def finish(self):
        self.far.wait_send()
        self.near.wait_send()
        self.forward.wait_send()


def rows_at(start, size):
    return pl.ds(pl.multiple_of(start, 16), size)


def piece_of(n):
    for size in (128, 80, 64, 48, 32):
        if n % size == 0:
            return size
    return 16


def add_rows(dst, to, a, a_at, b, b_at, n):
    size = piece_of(n)

    def step(i):
        left = a[rows_at(a_at + i * size, size)].astype(F32)
        right = b[rows_at(b_at + i * size, size)].astype(F32)
        dst[rows_at(to + i * size, size)] = (left + right).astype(BF)

    loop(n // size, step)


class Reduce:
    def __init__(self, pack, got, acc, far, red, rs, out, sems, t, f, nt):
        u = far.shape[0]
        near = {"freq": flip(f, 1)}
        one = remote(pack.at[flip_by(f, 1)], got.at[0], sems.at[0], near)
        two = remote(pack.at[flip_by(f, 3)], got.at[1], sems.at[1], near)
        across = remote(acc.at[1], far, sems.at[2], {"freq": flip(f, 2)})

        def add_near():
            add_rows(acc.at[1], 0, pack.at[flip(f, 2)], 0, got.at[1], 0, u)
            add_rows(acc.at[0], 0, pack.at[f], 0, got.at[0], 0, u)

        def add_far():
            add_rows(red, 0, acc.at[0], 0, far, 0, u)

        self.stages = [((two, one), add_near), ((across,), add_far)]
        spread_stages = []
        n, at, base, place_at = u, 0, 0, 3
        bits = bits_of(nt)
        for bit in bits:
            peer = {"tm": flip(t, bit)}
            upper = lax.rem(t // bit, 2)
            half = n % 32 == 0
            if half:
                n = n // 2
                keep, give = at + upper * n, at + (1 - upper) * n
            else:
                keep, give = at, at
            copy = remote(
                red.at[rows_at(give, n)], rs.at[base : base + n], sems.at[place_at], peer
            )
            target = out if bit == bits[-1] else red
            self.stages.append(
                ((copy,), partial(add_rows, target, keep, red, keep, rs, base, n))
            )
            if half:
                share = out.at[rows_at(keep, n)]
                back_copy = remote(share, share, sems.at[place_at + 1], peer)
                spread_stages.append(((back_copy,), None))
            at, base, place_at = keep, base + n, place_at + 2
        self.stages.extend(spread_stages[::-1])
        self.now = -1

    def done(self):
        return self.now >= len(self.stages)

    def advance(self):
        if self.done():
            return
        if self.now >= 0:
            copies, finish = self.stages[self.now]
            for copy in copies:
                copy.wait()
            if finish is not None:
                finish()
        self.now += 1
        if not self.done():
            for copy in self.stages[self.now][0]:
                copy.start()


def stage_count(nt):
    return 3 + 2 * len(bits_of(nt))


def padded(rows):
    return (rows + 127) // 128 * 128


def chunk_order(nf):
    width = F // nf
    row = lax.broadcasted_iota(jnp.int32, (CH, CH), 0)
    source = lax.broadcasted_iota(jnp.int32, (CH, CH), 1)
    col = lax.rem(row, F)
    wanted = (col // width) * (CR * width) + (row // F) * width + lax.rem(col, width)
    return jnp.where(source == wanted, 1.0, 0.0).astype(BF)


def clear_ends(spot, count, from_left, from_right):
    @pl.when(spot == 0)
    def _():
        from_left[...] = jnp.zeros_like(from_left)

    @pl.when(spot == count - 1)
    def _():
        from_right[...] = jnp.zeros_like(from_right)


def group_matrix():
    i = lax.broadcasted_iota(jnp.int32, (C, C), 0) // GW
    j = lax.broadcasted_iota(jnp.int32, (C, C), 1) // GW
    return (i == j).astype(F32)


def spread(rows, count):
    return jnp.broadcast_to(rows[:, None, :], (count, F, C))


def column_index(count):
    return lax.broadcasted_iota(jnp.int32, (count, F, C), 1)


def column_shifts(act, count):
    col = column_index(count)
    before = jnp.where(col == 0, 0.0, pltpu.roll(act, 1, 1))
    after = jnp.where(col == F - 1, 0.0, pltpu.roll(act, F - 1, 1))
    return before, after


def store_shifts(xc, at, act, count):
    before, after = column_shifts(act, count)
    size = count * F
    xc[pl.ds(at, size), 0:C] = before.reshape(size, C).astype(BF)
    xc[pl.ds(at, size), C : 2 * C] = act.reshape(size, C).astype(BF)
    xc[pl.ds(at, size), 2 * C : 3 * C] = after.reshape(size, C).astype(BF)


def loop(count, body):
    def step(i, carry):
        body(i)
        return carry

    lax.fori_loop(0, count, step, 0)


def chunk_at(i, size=CH):
    return pl.multiple_of(i * size, size)


class Clip:
    def __init__(self, same, rowtab, edge, gmat):
        self.same, self.rowtab, self.edge, self.gmat = same, rowtab, edge, gmat

    def pack(self, rs, rq, to_left, to_right):
        first = hdot(self.edge[...], rs[...])
        second = hdot(self.edge[...], rq[...])
        to_left[0:1] = first[0:1]
        to_left[1:2] = second[0:1]
        to_right[0:1] = first[1:2]
        to_right[1:2] = second[1:2]

    def means(self, rs, rq, gain, from_left, from_right):
        at_left = self.rowtab[:, 1:2] > 0.0
        at_right = self.rowtab[:, 2:3] > 0.0
        inverse = self.rowtab[:, 0:1]
        results = []
        for index, table in ((0, rs), (1, rq)):
            total = hdot(self.same[...], table[...])
            total = total + jnp.where(at_left, from_left[index : index + 1], 0.0)
            total = total + jnp.where(at_right, from_right[index : index + 1], 0.0)
            total = total * inverse
            if gain is not None:
                total = total * gain
            results.append(hdot(total, self.gmat[...]))
        return results


def row_masks(rowtab, prev_mask, next_mask, rows):
    prev_mask[...] = jnp.broadcast_to(rowtab[0:rows, 3:4], (rows, C))
    next_mask[...] = jnp.broadcast_to(rowtab[0:rows, 4:5], (rows, C))


def front_kernel(
    nt,
    nf,
    lat_local,
    cot_local,
    wconv,
    wproj,
    wmlp,
    wemb,
    wsmall,
    cond,
    onehot,
    same,
    rowtab,
    edge,
    conv,
    proj,
    mlp,
    vec,
    cot,
    zhat1,
    zhat2,
    zhat3,
    rstd1,
    rstd2,
    rstd3,
    resid,
    inner,
    query,
    kext,
    vext,
    gmat,
    rs,
    rq,
    mean,
    prev_mask,
    next_mask,
    xc,
    z_prev,
    z_here,
    z_next,
    hidden,
    to_left,
    to_right,
    from_left,
    from_right,
    emb,
    small,
    lat,
    lat_in,
    cot_in,
    order,
    film,
    msg_sems,
    kv_sems,
    block_sems,
    gather_sems,
):
    px = lat.shape[0]
    rows = px // F
    chunks = px // CH
    blk = px // nf
    seg = CH // nf
    spot, left, right = place(nt, nf)
    count = nt * nf
    where = (spot, count, left, right)
    f = lax.axis_index("freq")
    t = lax.axis_index("tm")
    s = snake(f, t, nf)
    enter(spot, count, left, right, [{"freq": flip_by(f, mask)} for mask in range(1, nf)])
    blocks = []
    for index, (local, landed) in enumerate(((lat_local, lat_in), (cot_local, cot_in))):
        blocks.append(
            Exchange(
                lambda peer, local=local: local.at[rows_at(snake(peer, t, nf) * blk, blk)],
                lambda peer, landed=landed: landed.at[f],
                local.at[rows_at(s * blk, blk)],
                landed.at[f],
                f,
                nf,
                block_sems.at[index],
            )
        )
    blocks[0].start()

    def cast(src, dst, base):
        size = 32 if src.shape[0] % 64 else 64

        def step(i):
            dst[rows_at(base + i * size, size)] = src[rows_at(i * size, size)].astype(BF)

        loop(src.shape[0] // size, step)

    cdepth, pdepth, mdepth, edepth = (
        wconv.shape[1],
        wproj.shape[1],
        wmlp.shape[1],
        wemb.shape[0],
    )
    views = (
        lambda i: conv.at[0, rows_at(i * cdepth, cdepth)],
        lambda i: conv.at[1, rows_at(i * cdepth, cdepth)],
        lambda i: proj.at[:, rows_at(i * pdepth, pdepth)],
        lambda i: mlp.at[:, rows_at(i * mdepth, mdepth)],
        lambda i: emb.at[rows_at(i * edepth, edepth)],
        lambda i: small.at[i],
    )
    gathers = [Gather(view, f, gather_sems.at[i]) for i, view in enumerate(views)]
    get_first, get_second, get_proj, get_mlp, get_emb, get_small = gathers
    cast(wsmall, small.at[f], 0)
    cast(wconv.at[0], conv.at[0], f * cdepth)
    get_small.start()
    get_first.start()
    cast(wemb, emb, f * edepth)
    cast(wconv.at[1], conv.at[1], f * cdepth)
    for i in range(wproj.shape[0]):
        cast(wproj.at[i], proj.at[i], f * pdepth)
    for i in range(wmlp.shape[0]):
        cast(wmlp.at[i], mlp.at[i], f * mdepth)
    order[...] = chunk_order(nf)

    def arrange(landed, target):
        def step(c):
            parts = [landed[k, rows_at(c * seg, seg)] for k in range(nf)]
            moved = mm(order[...], jnp.concatenate(parts, axis=0))
            target[pl.ds(chunk_at(c), CH)] = moved.astype(BF)

        loop(chunks, step)

    clear_ends(spot, count, from_left, from_right)

    @pl.when(spot == 0)
    def _():
        kext[0:px] = jnp.zeros((px, C), BF)
        vext[0:px] = jnp.zeros((px, C), BF)

    @pl.when(spot == count - 1)
    def _():
        kext[2 * px : 3 * px] = jnp.zeros((px, C), BF)
        vext[2 * px : 3 * px] = jnp.zeros((px, C), BF)

    gmat[...] = group_matrix()
    row_masks(rowtab, prev_mask, next_mask, rows)
    clip = Clip(same, rowtab, edge, gmat)

    def v(i):
        return vec[i : i + 1]

    def norm_stage(step, load, zhat, rstd, rim, beside):
        def sums(c):
            x3 = load(c).reshape(CR, F, C)
            rs[pl.ds(chunk_at(c, CR), CR)] = jnp.sum(x3, axis=1)
            rq[pl.ds(chunk_at(c, CR), CR)] = jnp.sum(x3 * x3, axis=1)

        loop(chunks, sums)
        clip.pack(rs, rq, to_left.at[step], to_right.at[step])
        first, last = rim()
        to_left[step, 8:16] = first
        to_right[step, 8:16] = last
        swap = Swap(
            where,
            to_left.at[step],
            to_right.at[step],
            from_left.at[step],
            from_right.at[step],
            msg_sems.at[step],
        )
        swap.start()
        beside()
        swap.wait()
        mean_rows, square_rows = clip.means(rs, rq, None, from_left.at[step], from_right.at[step])
        mean[...] = mean_rows
        rstd[...] = lax.rsqrt(square_rows - mean_rows * mean_rows + norm_eps)
        rim_raw = jnp.concatenate([from_left[step, 8:16], from_right[step, 8:16]], axis=0)
        rim3 = rim_raw.reshape(2, F, C)
        rim_hat = (rim3 - spread(mean[rows : rows + 2], 2)) * spread(rstd[rows : rows + 2], 2)
        if zhat.shape[0] > px:
            zhat[px : px + 16] = rim_hat.reshape(16, C)
        return rim_hat

    def normed(load, zhat, rstd, c):
        r0 = chunk_at(c, CR)
        x3 = load(c).reshape(CR, F, C)
        hat = (x3 - spread(mean[pl.ds(r0, CR)], CR)) * spread(rstd[pl.ds(r0, CR)], CR)
        zhat[pl.ds(chunk_at(c), CH)] = hat.reshape(CH, C)
        return hat

    def conv_stage(rim_hat, load, zhat, rstd, gain, shift, kernel, ready, finish):
        pre = rim_hat * gain + shift
        store_shifts(xc, px, (pre * jax.nn.sigmoid(pre)).astype(BF).astype(F32), 2)

        def build(c):
            pre = normed(load, zhat, rstd, c) * gain + shift
            act = (pre * jax.nn.sigmoid(pre)).astype(BF).astype(F32)
            store_shifts(xc, chunk_at(c), act, CR)

        loop(chunks, build)
        ready()

        def product(c):
            p0 = chunk_at(c)
            part = xc[pl.ds(p0, CH)]
            z_prev[pl.ds(pl.multiple_of(p0 + 8, 8), CH)] = mm(part, kernel[0 : 3 * C])
            z_here[pl.ds(p0, CH)] = mm(part, kernel[3 * C : 6 * C])
            z_next[pl.ds(p0, CH)] = mm(part, kernel[6 * C : 9 * C])

        loop(chunks, product)
        part = xc[px : px + 16]
        z_prev[0:8] = mm(part, kernel[0 : 3 * C])[0:8]
        z_next[px : px + 8] = mm(part, kernel[6 * C : 9 * C])[8:16]

        def join(c):
            p0 = chunk_at(c)
            r0 = chunk_at(c, CR)
            keep_prev = spread(prev_mask[pl.ds(r0, CR)], CR) > 0.0
            keep_next = spread(next_mask[pl.ds(r0, CR)], CR) > 0.0
            out = z_here[pl.ds(p0, CH)].reshape(CR, F, C)
            out = out + jnp.where(keep_prev, z_prev[pl.ds(p0, CH)].reshape(CR, F, C), 0.0)
            after = z_next[pl.ds(pl.multiple_of(p0 + 8, 8), CH)].reshape(CR, F, C)
            finish(c, out + jnp.where(keep_next, after, 0.0))

        loop(chunks, join)

    def load_latent(c):
        return lat[pl.ds(chunk_at(c), CH)].astype(F32)

    def load_hidden(c):
        return hidden[pl.ds(chunk_at(c), CH)]

    def load_resid(c):
        return resid[pl.ds(chunk_at(c), CH)]

    def send_second():
        get_emb.start()
        get_second.start()
        get_small.collect()
        total = small[0].astype(F32)
        for k in range(1, nf):
            total = total + small[k].astype(F32)
        vec[...] = total

    blocks[0].wait()
    arrange(lat_in, lat)
    rim_hat = norm_stage(
        0,
        load_latent,
        zhat1,
        rstd1,
        lambda: (lat[0:16].astype(F32)[0:8], lat[px - 16 : px].astype(F32)[8:16]),
        send_second,
    )

    def ready_first():
        get_first.collect()
        get_emb.collect()
        table = mm(cond[...], emb[...]) + v(3)
        film[...] = hdot(onehot[...], table)

    def finish_one(c, out):
        r0 = chunk_at(c, CR)
        out = out + v(2) + spread(film[pl.ds(r0, CR)], CR)
        hidden[pl.ds(chunk_at(c), CH)] = out.reshape(CH, C)

    conv_stage(rim_hat, load_latent, zhat1, rstd1, v(0), v(1), conv.at[0], ready_first, finish_one)

    def send_proj():
        get_proj.start()
        blocks[1].start()

    rim_hat = norm_stage(
        1, load_hidden, zhat2, rstd2, lambda: (hidden[0:8], hidden[px - 8 : px]), send_proj
    )

    def finish_two(c, out):
        p0 = chunk_at(c)
        total = lat[pl.ds(p0, CH)].astype(F32) + out.reshape(CH, C) + v(6)
        resid[pl.ds(p0, CH)] = total

    conv_stage(rim_hat, load_hidden, zhat2, rstd2, v(4), v(5), conv.at[1], get_second.collect, finish_two)

    norm_stage(2, load_resid, zhat3, rstd3, lambda: (resid[0:8], resid[px - 8 : px]), get_proj.collect)

    def project(c):
        p0 = chunk_at(c)
        hat = normed(load_resid, zhat3, rstd3, c).reshape(CH, C)
        low = (hat * v(7) + v(8)).astype(BF)
        value = mm(low, proj[0]) + v(9)
        inner[pl.ds(p0, CH)] = value
        inner_low = value.astype(BF)
        query[pl.ds(p0, CH)] = mm(inner_low, proj[1]).astype(BF)
        kext[pl.ds(pl.multiple_of(px + p0, CH), CH)] = mm(inner_low, proj[2]).astype(BF)
        vext[pl.ds(pl.multiple_of(px + p0, CH), CH)] = mm(inner_low, proj[3]).astype(BF)

    loop(chunks, project)
    swaps = []
    for index, ext in enumerate((kext, vext)):
        swaps.append(
            Swap(
                where,
                ext.at[px : 2 * px],
                ext.at[px : 2 * px],
                ext.at[0:px],
                ext.at[2 * px : 3 * px],
                kv_sems.at[index],
            )
        )
    for swap in swaps:
        swap.start()
    get_mlp.start()
    blocks[1].wait()
    arrange(cot_in, cot)
    for swap in swaps:
        swap.wait()
    get_mlp.collect()
    for gather in gathers:
        gather.finish()


def vmem(count):
    return [pl.BlockSpec(memory_space=pltpu.VMEM)] * count


def front(nt, nf, lat, cot, wconv, wproj, wmlp, wemb, wsmall, cond, onehot, same, rowtab, edge):
    px = lat.shape[0]
    rows = px // F
    tab = rowtab.shape[0]

    def whole(share, axis):
        shape = list(share.shape)
        shape[axis] *= nf
        return tuple(shape)

    shapes = (
        (whole(wconv, 1), BF),
        (whole(wproj, 1), BF),
        (whole(wmlp, 1), BF),
        (wsmall.shape, F32),
        ((px, C), BF),
        ((px, C), F32),
        ((px + 16, C), F32),
        ((px + 16, C), F32),
        ((tab, C), F32),
        ((tab, C), F32),
        ((tab, C), F32),
        ((px, C), F32),
        ((px, C), F32),
        ((px, C), BF),
        ((3 * px, C), BF),
        ((3 * px, C), BF),
    )
    return pl.pallas_call(
        partial(front_kernel, nt, nf),
        out_shape=[jax.ShapeDtypeStruct(s, d) for s, d in shapes],
        in_specs=vmem(12),
        out_specs=vmem(len(shapes)),
        scratch_shapes=[
            pltpu.VMEM((C, C), F32),
            pltpu.VMEM((rows, C), F32),
            pltpu.VMEM((rows, C), F32),
            pltpu.VMEM((tab, C), F32),
            pltpu.VMEM((rows, C), F32),
            pltpu.VMEM((rows, C), F32),
            pltpu.VMEM((px + 16, 3 * C), BF),
            pltpu.VMEM((px + 16, C), F32),
            pltpu.VMEM((px, C), F32),
            pltpu.VMEM((px + 16, C), F32),
            pltpu.VMEM((px, C), F32),
            pltpu.VMEM((3, 16, C), F32),
            pltpu.VMEM((3, 16, C), F32),
            pltpu.VMEM((3, 16, C), F32),
            pltpu.VMEM((3, 16, C), F32),
            pltpu.VMEM(whole(wemb, 0), BF),
            pltpu.VMEM((nf,) + wsmall.shape, BF),
            pltpu.VMEM((px, C), BF),
            pltpu.VMEM((nf, px // nf, C), BF),
            pltpu.VMEM((nf, px // nf, C), BF),
            pltpu.VMEM((CH, CH), BF),
            pltpu.VMEM((rows, C), F32),
            pltpu.SemaphoreType.DMA((3, 4)),
            pltpu.SemaphoreType.DMA((2, 4)),
            pltpu.SemaphoreType.DMA((2, nf - 1, 2)),
            pltpu.SemaphoreType.DMA((6, 3, 2)),
        ],
        compiler_params=pltpu.CompilerParams(
            collective_id=1, has_side_effects=True, vmem_limit_bytes=VMEM_LIMIT
        ),
        name="front",
    )(lat, cot, wconv, wproj, wmlp, wemb, wsmall, cond, onehot, same, rowtab, edge)


def head_mask(h):
    lane = lax.broadcasted_iota(jnp.int32, (CH, C), 1)
    return (lane >= h * HD) & (lane < (h + 1) * HD)


def head_rows(h):
    return slice(h * HD, (h + 1) * HD)


def turned(block):
    return block.astype(F32).T


def score_bias(segk, segq, key_row, q0):
    keys = jnp.broadcast_to(segk[pl.ds(key_row, CR), 0:1], (CR, C))
    keys = spread(keys, CR).reshape(CH, C)
    return jnp.where(keys == segq[0:1, pl.ds(q0, CH)], 0.0, masked_score)


def attend_kernel(meta, query, kext, vext, segq, segk, mixed, mixed_t, lse, vt, qm, bias, top, tot, acc):
    px = query.shape[0]
    factor = score_scale * LOG2E

    def turn(i):
        k0 = chunk_at(i)
        vt[:, pl.ds(k0, CH)] = turned(vext[pl.ds(k0, CH)]).astype(BF)

    loop(vext.shape[0] // CH, turn)

    def tile(t):
        q0 = chunk_at(t)
        block = query[pl.ds(q0, CH)].astype(F32)
        for h in range(H):
            qm[h] = jnp.where(head_mask(h), block, 0.0).astype(BF)
        top[...] = jnp.full((H, CH), masked_score, F32)
        tot[...] = jnp.zeros((H, CH), F32)
        acc[...] = jnp.zeros((C, CH), F32)

        def keys(i):
            row = meta[0, t] * 16 + i * CR
            base = pl.multiple_of(row * F, 128)
            bias[...] = score_bias(segk, segq, pl.multiple_of(row, 16), q0)
            key = kext[pl.ds(base, CH)]
            for h in range(H):
                raw = mm_nt(key, qm[h]) + bias[...]
                old = top[h : h + 1]
                new = jnp.maximum(old, jnp.max(raw, axis=0, keepdims=True))
                fade = jnp.exp2((old - new) * factor)
                weight = jnp.exp2((raw - new) * factor)
                top[h : h + 1] = new
                tot[h : h + 1] = tot[h : h + 1] * fade + jnp.sum(weight, axis=0, keepdims=True)
                part = mm(vt[head_rows(h), pl.ds(base, CH)], weight.astype(BF))
                acc[head_rows(h)] = acc[head_rows(h)] * fade + part

        loop(meta[1, t], keys)
        for h in range(H):
            acc[head_rows(h)] = acc[head_rows(h)] / tot[h : h + 1]
        lse[:, pl.ds(q0, CH)] = top[...] * factor + jnp.log2(tot[...])
        mixed_t[:, pl.ds(q0, CH)] = acc[...].astype(BF)
        mixed[pl.ds(q0, CH)] = acc[...].T.astype(BF)

    loop(px // CH, tile)


def attend(meta, query, kext, vext, segq, segk):
    px = query.shape[0]
    ext = kext.shape[0]
    return pl.pallas_call(
        attend_kernel,
        out_shape=[
            jax.ShapeDtypeStruct((px, C), BF),
            jax.ShapeDtypeStruct((C, px), BF),
            jax.ShapeDtypeStruct((H, px), F32),
        ],
        in_specs=[pl.BlockSpec(memory_space=pltpu.SMEM)] + vmem(5),
        out_specs=vmem(3),
        scratch_shapes=[
            pltpu.VMEM((C, ext), BF),
            pltpu.VMEM((H, CH, C), BF),
            pltpu.VMEM((CH, CH), F32),
            pltpu.VMEM((H, CH), F32),
            pltpu.VMEM((H, CH), F32),
            pltpu.VMEM((C, CH), F32),
        ],
        compiler_params=pltpu.CompilerParams(vmem_limit_bytes=VMEM_LIMIT),
        name="attend",
    )(meta, query, kext, vext, segq, segk)


def attend_back_kernel(
    meta,
    query,
    kext,
    vext,
    segq,
    segk,
    gmix,
    mixed_t,
    lse,
    dq,
    dk_own,
    dv_own,
    dk_rim,
    dv_rim,
    kt,
    qm,
    gm,
    qt,
    gt,
    inner_rows,
    bias,
    dqt,
    dkt,
    dvt,
):
    px = query.shape[0]
    ext = kext.shape[0]
    factor = score_scale * LOG2E

    def turn(i):
        k0 = chunk_at(i)
        kt[:, pl.ds(k0, CH)] = turned(kext[pl.ds(k0, CH)]).astype(BF)
        dkt[:, pl.ds(k0, CH)] = jnp.zeros((C, CH), F32)
        dvt[:, pl.ds(k0, CH)] = jnp.zeros((C, CH), F32)

    loop(ext // CH, turn)

    def tile(t):
        q0 = chunk_at(t)
        block = query[pl.ds(q0, CH)].astype(F32)
        grad = gmix[pl.ds(q0, CH)].astype(F32)
        for h in range(H):
            qm[h] = jnp.where(head_mask(h), block, 0.0).astype(BF)
            gm[h] = jnp.where(head_mask(h), grad, 0.0).astype(BF)
        qt[...] = block.T.astype(BF)
        grad_t = grad.T
        gt[...] = grad_t.astype(BF)
        crossed = grad_t * mixed_t[:, pl.ds(q0, CH)].astype(F32)
        inner_rows[...] = jnp.sum(crossed.reshape(H, HD, CH), axis=1)
        dqt[...] = jnp.zeros((C, CH), F32)

        def keys(i):
            row = meta[0, t] * 16 + i * CR
            base = pl.multiple_of(row * F, 128)
            bias[...] = score_bias(segk, segq, pl.multiple_of(row, 16), q0)
            key = kext[pl.ds(base, CH)]
            val = vext[pl.ds(base, CH)]
            for h in range(H):
                raw = mm_nt(key, qm[h]) + bias[...]
                probs = jnp.exp2(raw * factor - lse[h : h + 1, pl.ds(q0, CH)])
                gprob = mm_nt(val, gm[h])
                gscore = (probs * (gprob - inner_rows[h : h + 1]) * score_scale).astype(BF)
                dvt[head_rows(h), pl.ds(base, CH)] += mm_nt(gt[head_rows(h)], probs.astype(BF))
                dkt[head_rows(h), pl.ds(base, CH)] += mm_nt(qt[head_rows(h)], gscore)
                dqt[head_rows(h)] += mm(kt[head_rows(h), pl.ds(base, CH)], gscore)

        loop(meta[1, t], keys)
        dq[pl.ds(q0, CH)] = dqt[...].T.astype(BF)

    loop(px // CH, tile)

    def own(i):
        k0 = chunk_at(i)
        k1 = pl.multiple_of(px + k0, CH)
        dk_own[pl.ds(k0, CH)] = dkt[:, pl.ds(k1, CH)].T
        dv_own[pl.ds(k0, CH)] = dvt[:, pl.ds(k1, CH)].T
        k2 = pl.multiple_of(2 * px + k0, CH)
        dk_rim[0, pl.ds(k0, CH)] = dkt[:, pl.ds(k0, CH)].T.astype(BF)
        dv_rim[0, pl.ds(k0, CH)] = dvt[:, pl.ds(k0, CH)].T.astype(BF)
        dk_rim[1, pl.ds(k0, CH)] = dkt[:, pl.ds(k2, CH)].T.astype(BF)
        dv_rim[1, pl.ds(k0, CH)] = dvt[:, pl.ds(k2, CH)].T.astype(BF)

    loop(px // CH, own)


def attend_back(meta, query, kext, vext, segq, segk, gmix, mixed_t, lse):
    px = query.shape[0]
    ext = kext.shape[0]
    return pl.pallas_call(
        attend_back_kernel,
        out_shape=[
            jax.ShapeDtypeStruct((px, C), BF),
            jax.ShapeDtypeStruct((px, C), F32),
            jax.ShapeDtypeStruct((px, C), F32),
            jax.ShapeDtypeStruct((2, px, C), BF),
            jax.ShapeDtypeStruct((2, px, C), BF),
        ],
        in_specs=[pl.BlockSpec(memory_space=pltpu.SMEM)] + vmem(8),
        out_specs=vmem(5),
        scratch_shapes=[
            pltpu.VMEM((C, ext), BF),
            pltpu.VMEM((H, CH, C), BF),
            pltpu.VMEM((H, CH, C), BF),
            pltpu.VMEM((C, CH), BF),
            pltpu.VMEM((C, CH), BF),
            pltpu.VMEM((H, CH), F32),
            pltpu.VMEM((CH, CH), F32),
            pltpu.VMEM((C, CH), F32),
            pltpu.VMEM((C, ext), F32),
            pltpu.VMEM((C, ext), F32),
        ],
        compiler_params=pltpu.CompilerParams(vmem_limit_bytes=VMEM_LIMIT),
        name="attend_back",
    )(meta, query, kext, vext, segq, segk, gmix, mixed_t, lse)


def middle_kernel(
    nf,
    inner,
    mixed,
    resid,
    cot,
    proj,
    mlp,
    vec,
    output,
    gafter,
    gmix,
    pack,
    sums,
    after_low,
    act_low,
    pre_low,
    down_low,
    mlp_low,
    after_grad_low,
    ubias,
    order,
):
    px = inner.shape[0]
    seg = CH // nf
    tail = 11 + FF // C
    order[...] = chunk_order(nf)
    sums[...] = jnp.zeros_like(sums)
    for j in range(FF // C):
        ubias[:, j * C : (j + 1) * C] = vec[11 + j : 12 + j]

    def step(c):
        p0 = chunk_at(c)
        after = inner[pl.ds(p0, CH)] + mm(mixed[pl.ds(p0, CH)], proj[4]) + vec[10:11]
        low = after.astype(BF)
        after_low[pl.ds(p0, CH)] = low
        grad_out = cot[pl.ds(p0, CH)]
        grad_mlp = mm_nt(grad_out, proj[5])
        down = grad_mlp.astype(BF)
        down_low[pl.ds(p0, CH)] = down
        total = after
        grad_after = grad_mlp
        for j in range(FF // C):
            part = slice(j * C, (j + 1) * C)
            pre = mm_nt(low, mlp[0, part]) + ubias[:, part]
            cdf = 0.5 + 0.5 * lax.erf(pre * (0.5**0.5))
            act = (pre * cdf).astype(BF)
            act_low[pl.ds(p0, CH), part] = act
            total = total + mm(act, mlp[1, part])
            density = jnp.exp(pre * pre * -0.5) * 0.3989422804014327
            grad_pre = mm_nt(down, mlp[1, part]) * (cdf + pre * density)
            sums[3 + j : 4 + j] += jnp.sum(grad_pre, axis=0, keepdims=True)
            grad_low = grad_pre.astype(BF)
            pre_low[pl.ds(p0, CH), part] = grad_low
            grad_after = grad_after + mm(grad_low, mlp[0, part])
        total = (total + vec[tail : tail + 1]).astype(BF)
        mlp_low[pl.ds(p0, CH)] = total
        branch = mm(total, proj[5]) + vec[tail + 1 : tail + 2]
        moved = mm_tn(order[...], (resid[pl.ds(p0, CH)] + branch).astype(BF)).astype(BF)
        for k in range(nf):
            output[k, rows_at(c * seg, seg)] = moved[k * seg : (k + 1) * seg]
        gafter[pl.ds(p0, CH)] = grad_after
        grad_low = grad_after.astype(BF)
        after_grad_low[pl.ds(p0, CH)] = grad_low
        gmix[pl.ds(p0, CH)] = mm_nt(grad_low, proj[4]).astype(BF)
        sums[0:1] += jnp.sum(grad_out.astype(F32), axis=0, keepdims=True)
        sums[1:2] += jnp.sum(grad_mlp, axis=0, keepdims=True)
        sums[2:3] += jnp.sum(grad_after, axis=0, keepdims=True)

    loop(px // CH, step)
    width = FF // nf
    for k in range(nf):
        part = slice(k * width, (k + 1) * width)
        pack[k, 0:width] = mm_tn(pre_low[:, part], after_low[...]).astype(BF)
        pack[k, width : 2 * width] = mm_tn(act_low[:, part], down_low[...]).astype(BF)
    depth = C // nf
    gw_attn = mm_tn(mixed[...], after_grad_low[...]).astype(BF)
    gw_out = mm_tn(mlp_low[...], cot[...]).astype(BF)
    for k in range(nf):
        part = slice(k * depth, (k + 1) * depth)
        pack[k, 2 * width : 2 * width + depth] = gw_attn[part]
        pack[k, 2 * width + depth : 2 * width + 2 * depth] = gw_out[part]


def middle(nf, inner, mixed, resid, cot, proj, mlp, vec):
    px = inner.shape[0]
    return pl.pallas_call(
        partial(middle_kernel, nf),
        out_shape=[
            jax.ShapeDtypeStruct((nf, px // nf, C), BF),
            jax.ShapeDtypeStruct((px, C), F32),
            jax.ShapeDtypeStruct((px, C), BF),
            jax.ShapeDtypeStruct((nf, 2 * (FF + C) // nf, C), BF),
            jax.ShapeDtypeStruct((8, C), F32),
        ],
        in_specs=vmem(7),
        out_specs=vmem(5),
        scratch_shapes=[
            pltpu.VMEM((px, C), BF),
            pltpu.VMEM((px, FF), BF),
            pltpu.VMEM((px, FF), BF),
            pltpu.VMEM((px, C), BF),
            pltpu.VMEM((px, C), BF),
            pltpu.VMEM((px, C), BF),
            pltpu.VMEM((1, FF), F32),
            pltpu.VMEM((CH, CH), BF),
        ],
        compiler_params=pltpu.CompilerParams(vmem_limit_bytes=VMEM_LIMIT),
        name="middle",
    )(inner, mixed, resid, cot, proj, mlp, vec)


def back_kernel(
    nt,
    nf,
    dq,
    dk_own,
    dv_own,
    dk_rim,
    dv_rim,
    gafter,
    inner,
    zhat1,
    zhat2,
    zhat3,
    rstd1,
    rstd2,
    rstd3,
    cot,
    conv,
    proj,
    vec,
    same,
    rowtab,
    edge,
    cond,
    onehot,
    mid_sums,
    pack_a,
    out_blocks,
    output,
    glat,
    out_a,
    out_b,
    out_c,
    out_d,
    out_e,
    sums,
    film_rows,
    gmat,
    rs,
    rq,
    mean_e,
    mean_ez,
    prev_mask,
    next_mask,
    inner_low,
    normed_low,
    grad_low,
    dk_low,
    dv_low,
    gresid,
    dgrad,
    two,
    xc,
    shifted,
    dk_got,
    dv_got,
    to_left,
    to_right,
    from_left,
    from_right,
    order,
    glat_blocks,
    *rest,
):
    pieces = rest[:29]
    msg_sems, kv_sems, block_sems, reduce_sems = rest[29:33]
    px = dq.shape[0]
    rows = px // F
    chunks = px // CH
    blk = px // nf
    seg = CH // nf
    spot, left, right = place(nt, nf)
    count = nt * nf
    where = (spot, count, left, right)
    f = lax.axis_index("freq")
    t = lax.axis_index("tm")
    s = snake(f, t, nf)
    partners = [{"freq": flip_by(f, mask)} for mask in range(1, nf)]
    partners = partners + [{"tm": flip(t, bit)} for bit in bits_of(nt)]
    enter(spot, count, left, right, partners)
    packs = [pack_a, *pieces[0:4]]
    outs = (out_a, out_b, out_c, out_d, out_e)
    jobs = []
    for index in range(5):
        room = pieces[4 + 5 * index : 9 + 5 * index]
        sems = reduce_sems.at[index]
        jobs.append(Reduce(packs[index], *room, outs[index], sems, t, f, nt))
    job_a, job_b, job_c, job_d, job_e = jobs
    pack_b, pack_c, pack_d, pack_e = packs[1:]
    blocks = []
    for index, (source, landed) in enumerate(((out_blocks, output), (glat_blocks, glat))):
        blocks.append(
            Exchange(
                lambda peer, source=source: source.at[peer],
                lambda peer, landed=landed: landed.at[rows_at(s * blk, blk)],
                source.at[f],
                landed.at[rows_at(s * blk, blk)],
                f,
                nf,
                block_sems.at[index],
            )
        )
    swaps = []
    for index, (rim, got) in enumerate(((dk_rim, dk_got), (dv_rim, dv_got))):
        swaps.append(
            Swap(where, rim.at[0], rim.at[1], got.at[0], got.at[1], kv_sems.at[index])
        )
    for swap in swaps:
        swap.start()
    job_a.advance()
    order[...] = chunk_order(nf)
    clear_ends(spot, count, from_left, from_right)
    clear_ends(spot, count, dk_got.at[0], dk_got.at[1])
    clear_ends(spot, count, dv_got.at[0], dv_got.at[1])
    gmat[...] = group_matrix()
    row_masks(rowtab, prev_mask, next_mask, rows)
    clip = Clip(same, rowtab, edge, gmat)
    sums[...] = jnp.zeros_like(sums)

    def v(i):
        return vec[i : i + 1]

    def first(c):
        p0 = chunk_at(c)
        inner_low[pl.ds(p0, CH)] = inner[pl.ds(p0, CH)].astype(BF)
        hat = zhat3[pl.ds(p0, CH)]
        normed_low[pl.ds(p0, CH)] = (hat * v(7) + v(8)).astype(BF)
        gresid[pl.ds(p0, CH)] = gafter[pl.ds(p0, CH)] + mm_nt(dq[pl.ds(p0, CH)], proj[1])

    loop(chunks, first)
    depth = C // nf

    def proj_grad(which, grad):
        low = grad.astype(BF)
        for k in range(nf):
            pack_b[k, which * depth : (which + 1) * depth] = low[k * depth : (k + 1) * depth]

    proj_grad(1, mm_tn(inner_low[...], dq[...]))
    job_a.advance()
    for swap in swaps:
        swap.wait()

    def row_sums(c, grad3, hat3):
        rs[pl.ds(chunk_at(c, CR), CR)] = jnp.sum(grad3, axis=1)
        rq[pl.ds(chunk_at(c, CR), CR)] = jnp.sum(grad3 * hat3, axis=1)

    def second(c):
        p0 = chunk_at(c)
        part = pl.ds(p0, CH)
        dk = (dk_own[part] + dk_got[0, part].astype(F32) + dk_got[1, part].astype(F32)).astype(BF)
        dv = (dv_own[part] + dv_got[0, part].astype(F32) + dv_got[1, part].astype(F32)).astype(BF)
        dk_low[part] = dk
        dv_low[part] = dv
        grad = gresid[part] + mm_nt(dk, proj[2]) + mm_nt(dv, proj[3])
        sums[9:10] += jnp.sum(grad, axis=0, keepdims=True)
        low = grad.astype(BF)
        grad_low[part] = low
        d3 = mm_nt(low, proj[0])
        dgrad[part] = d3
        row_sums(c, d3.reshape(CR, F, C), zhat3[part].reshape(CR, F, C))

    loop(chunks, second)

    def swap_step(step, rim_first, rim_last):
        clip.pack(rs, rq, to_left.at[step], to_right.at[step])
        if rim_first is not None:
            to_left[step, 8 : 8 + rim_first.shape[0]] = rim_first
            to_right[step, 8 : 8 + rim_last.shape[0]] = rim_last
        swap = Swap(
            where,
            to_left.at[step],
            to_right.at[step],
            from_left.at[step],
            from_right.at[step],
            msg_sems.at[step],
        )
        swap.start()
        return swap

    def set_means(step, gain):
        mean_e[...], mean_ez[...] = clip.means(
            rs, rq, gain, from_left.at[step], from_right.at[step]
        )

    def back_norm(grad3, hat3, rstd, gain, r0, size):
        value = grad3 * gain - spread(mean_e[pl.ds(r0, size)], size)
        value = value - hat3 * spread(mean_ez[pl.ds(r0, size)], size)
        return value * spread(rstd[pl.ds(r0, size)], size)

    def rim_grad(step, at):
        both = jnp.concatenate([from_left[step, at : at + 8], from_right[step, at : at + 8]], axis=0)
        return both.reshape(2, F, C)

    sums[7:8] = jnp.sum(rq[...], axis=0, keepdims=True)
    sums[8:9] = jnp.sum(rs[...], axis=0, keepdims=True)
    cot_first = cot[0:16].astype(F32)[0:8]
    cot_last = cot[px - 16 : px].astype(F32)[8:16]
    swap = swap_step(
        0,
        jnp.concatenate([dgrad[0:8], cot_first], axis=0),
        jnp.concatenate([dgrad[px - 8 : px], cot_last], axis=0),
    )
    job_a.advance()
    proj_grad(2, mm_tn(inner_low[...], dk_low[...]))
    proj_grad(3, mm_tn(inner_low[...], dv_low[...]))
    proj_grad(0, mm_tn(normed_low[...], grad_low[...]))
    job_b.advance()
    blocks[0].start()
    swap.wait()
    set_means(0, v(7))

    def set_rims(value):
        low = value.astype(BF).astype(F32)
        two[0:8] = low[0]
        two[px + 8 : px + 16] = low[1]

    rim = rim_grad(0, 8)
    rim_hat = zhat3[px : px + 16].reshape(2, F, C)
    set_rims(rim_grad(0, 16) + back_norm(rim, rim_hat, rstd3, v(7), rows, 2))

    def third(c):
        p0 = chunk_at(c)
        part = pl.ds(p0, CH)
        grad3 = dgrad[part].reshape(CR, F, C)
        hat3 = zhat3[part].reshape(CR, F, C)
        value = back_norm(grad3, hat3, rstd3, v(7), chunk_at(c, CR), CR).reshape(CH, C)
        value = cot[part].astype(F32) + value
        gresid[part] = value
        sums[6:7] += jnp.sum(value, axis=0, keepdims=True)
        two[pl.ds(pl.multiple_of(p0 + 8, 8), CH)] = value.astype(BF).astype(F32)

    loop(chunks, third)

    def conv_back(kernel, zhat, gain, shift):
        def step(c):
            p0 = chunk_at(c)
            part = pl.ds(p0, CH)
            r0 = chunk_at(c, CR)
            keep_prev = spread(prev_mask[pl.ds(r0, CR)], CR).reshape(CH, C) > 0.0
            keep_next = spread(next_mask[pl.ds(r0, CR)], CR).reshape(CH, C) > 0.0
            after = two[pl.ds(pl.multiple_of(p0 + 16, 16), CH)]
            here = two[pl.ds(pl.multiple_of(p0 + 8, 8), CH)]
            low0 = jnp.where(keep_next, after, 0.0).astype(BF)
            low1 = here.astype(BF)
            low2 = jnp.where(keep_prev, two[part], 0.0).astype(BF)
            shifted[part, 0:C] = low0
            shifted[part, C : 2 * C] = low1
            shifted[part, 2 * C : 3 * C] = low2
            hat = zhat[part]
            pre = hat * gain + shift
            sig = jax.nn.sigmoid(pre)
            act = (pre * sig).astype(BF).astype(F32).reshape(CR, F, C)
            store_shifts(xc, p0, act, CR)

            def columns(j):
                piece = slice(j * C, (j + 1) * C)
                value = mm_nt(low0, kernel[0 : 3 * C][piece])
                value = value + mm_nt(low1, kernel[3 * C : 6 * C][piece])
                value = value + mm_nt(low2, kernel[6 * C : 9 * C][piece])
                return value.reshape(CR, F, C)

            col = column_index(CR)
            back = columns(1)
            back = back + jnp.where(col == F - 1, 0.0, pltpu.roll(columns(0), F - 1, 1))
            back = back + jnp.where(col == 0, 0.0, pltpu.roll(columns(2), 1, 1))
            grad = back.reshape(CH, C) * sig * (1.0 + pre * (1.0 - sig))
            dgrad[part] = grad
            row_sums(c, grad.reshape(CR, F, C), hat.reshape(CR, F, C))

        loop(chunks, step)

    share = TAPS * C // nf

    def kernel_grad(pack):
        for k in range(nf):
            if pack.shape[1] > share:
                pack[k, share:] = jnp.zeros((pack.shape[1] - share, C), BF)
        for d in range(3):
            for j in range(3):
                grad = mm_tn(xc[:, j * C : (j + 1) * C], shifted[:, d * C : (d + 1) * C])
                low = grad.astype(BF)
                start = (d * 3 + j) * C
                end = start + C
                at = start
                while at < end:
                    k = at // share
                    upto = min(end, (k + 1) * share)
                    pack[k, at - k * share : upto - k * share] = low[at - start : upto - start]
                    at = upto

    job_a.advance()
    conv_back(conv.at[1], zhat2, v(4), v(5))
    job_a.advance()
    job_b.advance()
    sums[4:5] = jnp.sum(rq[...], axis=0, keepdims=True)
    sums[5:6] = jnp.sum(rs[...], axis=0, keepdims=True)
    swap = swap_step(1, dgrad[0:8], dgrad[px - 8 : px])
    kernel_grad(pack_c)
    job_c.advance()
    job_a.advance()
    job_b.advance()
    swap.wait()
    set_means(1, v(4))
    rim_hat = zhat2[px : px + 16].reshape(2, F, C)
    set_rims(back_norm(rim_grad(1, 8), rim_hat, rstd2, v(4), rows, 2))

    def fourth(c):
        p0 = chunk_at(c)
        part = pl.ds(p0, CH)
        grad3 = dgrad[part].reshape(CR, F, C)
        hat3 = zhat2[part].reshape(CR, F, C)
        value3 = back_norm(grad3, hat3, rstd2, v(4), chunk_at(c, CR), CR)
        film_rows[pl.ds(chunk_at(c, CR), CR)] = jnp.sum(value3, axis=1)
        low = value3.reshape(CH, C).astype(BF).astype(F32)
        two[pl.ds(pl.multiple_of(p0 + 8, 8), CH)] = low

    loop(chunks, fourth)
    job_c.advance()
    job_a.advance()
    job_b.advance()
    total = jnp.sum(film_rows[...], axis=0, keepdims=True)
    sums[2:3] = total
    sums[3:4] = total
    grad_film = hdot_tn(onehot[...], film_rows[...])
    gemb = hdot_tn(cond[...].astype(F32), grad_film).astype(BF)
    edepth = gemb.shape[0] // nf
    conv_back(conv.at[0], zhat1, v(0), v(1))
    sums[0:1] = jnp.sum(rq[...], axis=0, keepdims=True)
    sums[1:2] = jnp.sum(rs[...], axis=0, keepdims=True)
    swap = swap_step(2, None, None)
    for k in range(nf):
        pack_e[k, 0:edepth] = gemb[k * edepth : (k + 1) * edepth]
        pack_e[k, edepth:] = jnp.zeros((pack_e.shape[1] - edepth, C), BF)
        tail = jnp.concatenate(
            [
                sums[0:10],
                mid_sums[2:3],
                mid_sums[3 : 3 + FF // C],
                mid_sums[1:2],
                mid_sums[0:1],
                jnp.zeros((32 - 13 - FF // C, C), F32),
            ],
            axis=0,
        )
        pack_e[k, edepth : edepth + 32] = tail.astype(BF)
    job_e.advance()
    kernel_grad(pack_d)
    job_d.advance()
    for job in (job_c, job_a, job_b):
        job.advance()
    swap.wait()
    set_means(2, v(0))

    def fifth(c):
        p0 = chunk_at(c)
        part = pl.ds(p0, CH)
        grad3 = dgrad[part].reshape(CR, F, C)
        hat3 = zhat1[part].reshape(CR, F, C)
        value = back_norm(grad3, hat3, rstd1, v(0), chunk_at(c, CR), CR).reshape(CH, C)
        moved = mm_tn(order[...], (gresid[part] + value).astype(BF)).astype(BF)
        for k in range(nf):
            glat_blocks[k, rows_at(c * seg, seg)] = moved[k * seg : (k + 1) * seg]

    loop(chunks, fifth)
    while not all(job.done() for job in jobs):
        for job in (job_d, job_c, job_e, job_b, job_a):
            job.advance()
        if job_d.now == 1:
            blocks[1].start()
    for block in blocks:
        block.wait()


def back(nt, nf, *args):
    px = args[0].shape[0]
    rows = px // F
    tab = args[-7].shape[0]
    pack_rows = args[-2].shape[1]
    edepth = args[-5].shape[1] // nf
    heights = (
        pack_rows,
        padded(4 * C // nf),
        padded(TAPS * C // nf),
        padded(TAPS * C // nf),
        padded(edepth + 32),
    )
    buffers = [pltpu.VMEM((nf, u, C), BF) for u in heights[1:]]
    for u in heights:
        buffers.extend(
            [
                pltpu.VMEM((2, u, C), BF),
                pltpu.VMEM((2, u, C), BF),
                pltpu.VMEM((u, C), BF),
                pltpu.VMEM((u, C), BF),
                pltpu.VMEM((2 * u, C), BF),
            ]
        )
    big = pltpu.VMEM((px, C), F32)
    low = pltpu.VMEM((px, C), BF)
    table = pltpu.VMEM((rows, C), F32)
    return pl.pallas_call(
        partial(back_kernel, nt, nf),
        out_shape=[
            jax.ShapeDtypeStruct((px, C), BF),
            jax.ShapeDtypeStruct((px, C), BF),
        ]
        + [jax.ShapeDtypeStruct((u, C), BF) for u in heights],
        in_specs=vmem(len(args)),
        out_specs=vmem(7),
        scratch_shapes=[
            pltpu.VMEM((16, C), F32),
            pltpu.VMEM((rows, C), F32),
            pltpu.VMEM((C, C), F32),
            table,
            table,
            pltpu.VMEM((tab, C), F32),
            pltpu.VMEM((tab, C), F32),
            table,
            table,
            low,
            low,
            low,
            low,
            low,
            big,
            big,
            pltpu.VMEM((px + 16, C), F32),
            pltpu.VMEM((px, 3 * C), BF),
            pltpu.VMEM((px, 3 * C), BF),
            pltpu.VMEM((2, px, C), BF),
            pltpu.VMEM((2, px, C), BF),
            pltpu.VMEM((3, 24, C), F32),
            pltpu.VMEM((3, 24, C), F32),
            pltpu.VMEM((3, 24, C), F32),
            pltpu.VMEM((3, 24, C), F32),
            pltpu.VMEM((CH, CH), BF),
            pltpu.VMEM((nf, px // nf, C), BF),
            *buffers,
            pltpu.SemaphoreType.DMA((3, 4)),
            pltpu.SemaphoreType.DMA((2, 4)),
            pltpu.SemaphoreType.DMA((2, nf - 1, 2)),
            pltpu.SemaphoreType.DMA((5, stage_count(nt), 2)),
        ],
        compiler_params=pltpu.CompilerParams(
            collective_id=2, has_side_effects=True, vmem_limit_bytes=VMEM_LIMIT
        ),
        name="back",
    )(*args)


def adamw_step(weight, moment, second, grad, decay_rate):
    moment_new = beta_first * moment + (1.0 - beta_first) * grad
    second_new = beta_second * second + (1.0 - beta_second) * grad * grad
    moment_hat = moment_new / (1.0 - beta_first**STEP)
    second_hat = second_new / (1.0 - beta_second**STEP)
    weight_new = weight - learn_rate * (
        moment_hat / (jnp.sqrt(second_hat) + adam_eps) + decay_rate * weight
    )
    return (weight_new, moment_new, second_new)


def layout_of(lengths, spot, count, rows):
    clips = lengths.shape[0]
    clip_index = jnp.arange(clips, dtype=jnp.int32)
    upto = clip_index[:, None] >= clip_index[None, :]
    clip_ends = jnp.sum(jnp.where(upto, lengths[None, :], 0), axis=1)
    first_row = spot * rows
    total_rows = count * rows
    row = first_row - rows + jnp.arange(3 * rows, dtype=jnp.int32)
    seg_ext = jnp.sum((clip_ends[None, :] <= row[:, None]).astype(jnp.int32), axis=1)
    seg_ext = jnp.where((row >= 0) & (row < total_rows), seg_ext, -1)
    seg = seg_ext[rows : 2 * rows]
    seg_left = seg_ext[rows - 1]
    seg_right = seg_ext[2 * rows]
    pad = jnp.full((6,), -2, jnp.int32)
    seg_tab = jnp.concatenate([seg, seg_ext[rows - 1 : rows], seg_ext[2 * rows : 2 * rows + 1], pad])
    onehot = (seg_tab[:, None] == clip_index[None, :]).astype(F32)
    row_len = jnp.sum(onehot * lengths[None, :].astype(F32), axis=1)
    inverse = 1.0 / jnp.maximum(row_len * (F * GW), 1.0)
    beside_prev = jnp.concatenate([(seg_ext[rows - 1 : 2 * rows - 1] == seg).astype(F32), jnp.zeros((8,), F32)])
    beside_next = jnp.concatenate([(seg_ext[rows + 1 : 2 * rows + 1] == seg).astype(F32), jnp.zeros((8,), F32)])
    fields = (
        inverse,
        (seg_tab == seg_left).astype(F32),
        (seg_tab == seg_right).astype(F32),
        beside_prev,
        beside_next,
    )
    lane = jnp.arange(128, dtype=jnp.int32)[None, :]
    rowtab = jnp.zeros((rows + 8, 128), F32)
    for index, field in enumerate(fields):
        rowtab = jnp.where(lane == index, field[:, None], rowtab)
    same = (seg_tab[:, None] == seg[None, :]).astype(F32)
    which = jnp.arange(8, dtype=jnp.int32)[:, None]
    edge = jnp.where(which == 0, seg[None, :] == seg[0], seg[None, :] == seg[rows - 1])
    edge = jnp.where(which < 2, edge, False).astype(F32)
    segk = jnp.broadcast_to(seg_ext.astype(F32)[:, None], (3 * rows, 128))
    segq = jnp.broadcast_to(jnp.repeat(seg.astype(F32), F)[None, :], (8, rows * F))
    tiles = rows // CR
    starts = clip_ends - lengths
    low_clip = seg[::CR]
    high_clip = seg[CR - 1 :: CR]
    low_row = jnp.sum(jnp.where(low_clip[:, None] == clip_index[None, :], starts[None, :], 0), axis=1)
    high_row = jnp.sum(
        jnp.where(high_clip[:, None] == clip_index[None, :], clip_ends[None, :], 0), axis=1
    )
    low_row = low_row - first_row + rows
    high_row = high_row - first_row + rows
    low = low_row // 16
    number = (high_row - low * 16 + CR - 1) // CR
    low = jnp.minimum(low, (3 * rows - number * CR) // 16)
    meta = jnp.stack([low, number]).astype(jnp.int32)
    return same, rowtab, edge, segk, segq, meta, onehot[:rows]


def on_device(
    nt,
    nf,
    latent,
    condition,
    lengths,
    cotangent,
    conv_weight,
    conv_moment,
    conv_second,
    proj_weight,
    proj_moment,
    proj_second,
    mlp_weight,
    mlp_moment,
    mlp_second,
    emb_weight,
    emb_moment,
    emb_second,
    small_weight,
    small_moment,
    small_second,
):
    masters = (conv_weight, proj_weight, mlp_weight, emb_weight, small_weight)
    nsmall, width = small_weight.shape
    t = lax.axis_index("tm")
    f = lax.axis_index("freq")
    lane_share = jnp.arange(C, dtype=jnp.int32)[None, :] // width
    wsmall = jnp.where(lane_share == f, jnp.tile(small_weight, (1, nf)), 0.0)
    wsmall = jnp.pad(wsmall, ((0, 32 - nsmall), (0, 0)))
    spot = t * nf + snake(f, t, nf)
    rows = latent.shape[0] // nf
    same, rowtab, edge, segk, segq, meta, onehot = layout_of(lengths, spot, nt * nf, rows)
    cond_low = jax.nn.silu(condition).astype(BF)
    (
        conv_full,
        proj_full,
        mlp_full,
        vec,
        cot,
        zhat1,
        zhat2,
        zhat3,
        rstd1,
        rstd2,
        rstd3,
        resid,
        inner,
        query,
        kext,
        vext,
    ) = front(
        nt,
        nf,
        latent.reshape(-1, C),
        cotangent.reshape(-1, C),
        conv_weight,
        proj_weight,
        mlp_weight,
        emb_weight,
        wsmall,
        cond_low,
        onehot,
        same,
        rowtab,
        edge,
    )
    mixed, mixed_t, lse = attend(meta, query, kext, vext, segq, segk)
    out_blocks, gafter, gmix, pack_a, mid_sums = middle(
        nf, inner, mixed, resid, cot, proj_full, mlp_full, vec
    )
    dq, dk_own, dv_own, dk_rim, dv_rim = attend_back(
        meta, query, kext, vext, segq, segk, gmix, mixed_t, lse
    )
    output, glat, sum_a, sum_b, sum_c, sum_d, sum_e = back(
        nt,
        nf,
        dq,
        dk_own,
        dv_own,
        dk_rim,
        dv_rim,
        gafter,
        inner,
        zhat1,
        zhat2,
        zhat3,
        rstd1,
        rstd2,
        rstd3,
        cot,
        conv_full,
        proj_full,
        vec,
        same,
        rowtab,
        edge,
        cond_low,
        onehot,
        mid_sums,
        pack_a,
        out_blocks,
    )
    cdepth, pdepth, mdepth, edepth = (
        conv_weight.shape[1],
        proj_weight.shape[1],
        mlp_weight.shape[1],
        emb_weight.shape[0],
    )
    grad_conv = jnp.stack([sum_d[:cdepth], sum_c[:cdepth]])
    first_four = sum_b[: 4 * pdepth].reshape(4, pdepth, C)
    last_two = sum_a[2 * mdepth :].reshape(2, pdepth, C)
    grad_small = lax.dynamic_slice(sum_e, (edepth, f * width), (nsmall, width))
    shares = [
        grad_conv.astype(F32),
        jnp.concatenate([first_four, last_two], axis=0).astype(F32),
        sum_a[: 2 * mdepth].reshape(2, mdepth, C).astype(F32),
        sum_e[:edepth].astype(F32),
        grad_small.astype(F32),
    ]
    moments = (conv_moment, proj_moment, mlp_moment, emb_moment, small_moment)
    seconds = (conv_second, proj_second, mlp_second, emb_second, small_second)
    decays = (weight_decay, weight_decay, weight_decay, weight_decay, 0.0)
    updated = []
    for position in range(5):
        updated.extend(
            adamw_step(
                masters[position],
                moments[position],
                seconds[position],
                shares[position],
                decays[position],
            )
        )
    bias_share = shares[4][nsmall - 1]
    return (
        output.reshape(latent.shape),
        glat.reshape(latent.shape),
        *updated,
        bias_share,
    )


def solution(mesh):
    nt, nf = mesh.shape["tm"], mesh.shape["freq"]
    rows_spec = P("tm", "freq", None)
    middle_spec = P(None, "freq", None)
    params = (middle_spec,) * 9 + (P("freq", None),) * 3 + (P(None, "freq"),) * 3
    return jax.shard_map(
        partial(on_device, nt, nf),
        mesh=mesh,
        in_specs=(rows_spec, P(), P(), rows_spec) + params,
        out_specs=(rows_spec, rows_spec) + params + (P("freq"),),
        check_vma=False,
    )
```

```python
from functools import partial

import jax
import jax.numpy as jnp
from jax import lax
from jax.experimental import pallas as pl
from jax.experimental.pallas import tpu as pltpu
from jax.sharding import PartitionSpec as P

C = 256
G = 32
GW = C // G
HD = 32
H = C // HD
FF = 1024
F = 8
MAXLEN = 128
STEP = 10
TAPS = 9
CH = 256
CR = CH // F

HIGHEST = lax.Precision.HIGHEST
norm_eps = 1e-05
beta_first = 0.9
beta_second = 0.999
learn_rate = 0.5
weight_decay = 0.01
adam_eps = 1e-08
masked_score = -1e30
score_scale = HD**-0.5
LOG2E = 1.4426950408889634
MESH = pltpu.DeviceIdType.MESH if hasattr(pltpu, "DeviceIdType") else pl.DeviceIdType.MESH
VMEM_LIMIT = 64 * 1024 * 1024 - 65536
BF = jnp.bfloat16
F32 = jnp.float32


def mm(a, b):
    return jnp.dot(a, b, preferred_element_type=F32)


def mm_nt(a, b):
    return lax.dot_general(a, b, (((1,), (1,)), ((), ())), preferred_element_type=F32)


def mm_tn(a, b):
    return lax.dot_general(a, b, (((0,), (0,)), ((), ())), preferred_element_type=F32)


def hdot(a, b):
    return jnp.dot(a, b, precision=HIGHEST, preferred_element_type=F32)


def hdot_tn(a, b):
    return lax.dot_general(
        a, b, (((0,), (0,)), ((), ())), precision=HIGHEST, preferred_element_type=F32
    )


def place(nt, nf):
    t = lax.axis_index("tm")
    f = lax.axis_index("freq")
    odd = lax.rem(t, 2)
    s = f + odd * (nf - 1 - 2 * f)
    turn = 1 - 2 * odd
    at_end = (s + 1) // nf
    at_start = 1 - (s + nf - 1) // nf
    right = {"tm": t + at_end, "freq": f + (1 - at_end) * turn}
    left = {"tm": t - at_start, "freq": f - (1 - at_start) * turn}
    return t * nf + s, left, right


def flip(x, bit):
    return x + bit - 2 * bit * lax.rem(x // bit, 2)


def flip_by(x, mask):
    bit = 1
    while bit <= mask:
        if mask & bit:
            x = flip(x, bit)
        bit *= 2
    return x


def bits_of(count):
    bits = []
    bit = 1
    while bit < count:
        bits.append(bit)
        bit *= 2
    return bits


def snake(f, t, nf):
    return f + lax.rem(t, 2) * (nf - 1 - 2 * f)


def enter(spot, count, left, right, partners):
    barrier = pltpu.get_barrier_semaphore()
    for partner in partners:
        pl.semaphore_signal(barrier, inc=1, device_id=partner, device_id_type=MESH)

    @pl.when(spot > 0)
    def _():
        pl.semaphore_signal(barrier, inc=1, device_id=left, device_id_type=MESH)

    @pl.when(spot < count - 1)
    def _():
        pl.semaphore_signal(barrier, inc=1, device_id=right, device_id_type=MESH)

    inside = (spot > 0) & (spot < count - 1)

    @pl.when(inside)
    def _():
        pl.semaphore_wait(barrier, len(partners) + 2)

    @pl.when(jnp.logical_not(inside))
    def _():
        pl.semaphore_wait(barrier, len(partners) + 1)


class Swap:
    def __init__(self, where, to_left, to_right, from_left, from_right, sems):
        self.spot, self.count, left, right = where
        self.go_left = pltpu.make_async_remote_copy(
            src_ref=to_left,
            dst_ref=from_right,
            send_sem=sems.at[0],
            recv_sem=sems.at[1],
            device_id=left,
            device_id_type=MESH,
        )
        self.go_right = pltpu.make_async_remote_copy(
            src_ref=to_right,
            dst_ref=from_left,
            send_sem=sems.at[2],
            recv_sem=sems.at[3],
            device_id=right,
            device_id_type=MESH,
        )

    def start(self):
        @pl.when(self.spot > 0)
        def _():
            self.go_left.start()

        @pl.when(self.spot < self.count - 1)
        def _():
            self.go_right.start()

    def wait(self):
        @pl.when(self.spot > 0)
        def _():
            self.go_left.wait_send()
            self.go_right.wait_recv()

        @pl.when(self.spot < self.count - 1)
        def _():
            self.go_right.wait_send()
            self.go_left.wait_recv()


def remote(src, dst, sems, device):
    return pltpu.make_async_remote_copy(
        src_ref=src,
        dst_ref=dst,
        send_sem=sems.at[0],
        recv_sem=sems.at[1],
        device_id=device,
        device_id_type=MESH,
    )


class Exchange:
    def __init__(self, source, target, own_source, own_target, f, nf, sems):
        self.copies = []
        for mask in range(1, nf):
            peer = flip_by(f, mask)
            self.copies.append(
                remote(source(peer), target(peer), sems.at[mask - 1], {"freq": peer})
            )
        self.own_source, self.own_target = own_source, own_target

    def start(self):
        for copy in self.copies[::-1]:
            copy.start()
        self.own_target[...] = self.own_source[...]

    def wait(self):
        for copy in self.copies:
            copy.wait()


class Gather:
    def __init__(self, view, f, t, sems, size=None):
        near = {"freq": flip(f, 1)}
        far = flip(f, 2)
        self.halves = size is not None
        if self.halves:
            side = lax.rem(t, 2)
            mine, other = (side, size // 2), (1 - side, size // 2)
        else:
            mine = (0, None)
        beside = {"tm": flip(t, 1)}
        self.far = remote(view(f, mine), view(f, mine), sems.at[0], {"freq": far})
        self.near = remote(view(f, (0, None)), view(f, (0, None)), sems.at[1], near)
        self.forward = remote(view(far, mine), view(far, mine), sems.at[2], near)
        if self.halves:
            self.cross = remote(view(far, mine), view(far, mine), sems.at[3], beside)
            self.second = remote(view(far, other), view(far, other), sems.at[4], near)

    def start(self):
        self.far.start()
        self.near.start()

    def relay(self):
        self.far.wait_recv()
        if self.halves:
            self.cross.start()
        self.forward.start()

    def collect(self):
        if self.halves:
            self.cross.wait_recv()
            self.second.start()
        self.near.wait_recv()
        self.forward.wait_recv()
        if self.halves:
            self.second.wait_recv()

    def finish(self):
        self.far.wait_send()
        self.near.wait_send()
        self.forward.wait_send()
        if self.halves:
            self.cross.wait_send()
            self.second.wait_send()


def share_view(ref, depth, lead):
    def view(i, part):
        which, size = part
        start = i * depth if size is None else i * depth + which * size
        rows = rows_at(start, depth if size is None else size)
        return ref.at[lead, rows] if lead is not None else ref.at[rows]

    return view


def rows_at(start, size):
    return pl.ds(pl.multiple_of(start, 16), size)


def piece_of(n):
    for size in (128, 96, 80, 64, 48, 32):
        if n % size == 0:
            return size
    return 16


def add_rows(dst, to, a, a_at, b, b_at, n):
    size = piece_of(n)

    def step(i):
        left = a[rows_at(a_at + i * size, size)].astype(F32)
        right = b[rows_at(b_at + i * size, size)].astype(F32)
        dst[rows_at(to + i * size, size)] = (left + right).astype(BF)

    loop(n // size, step)


class Reduce:
    def __init__(self, order, pack, got, acc, far, rs, out, sems, t, f):
        u = far.shape[0]
        near = {"freq": flip(f, 1)}
        one = remote(pack(flip_by(f, 1)), got.at[0], sems.at[0], near)
        two = remote(pack(flip_by(f, 3)), got.at[1], sems.at[1], near)

        def add_near():
            add_rows(acc.at[1], 0, pack(flip(f, 2)), 0, got.at[1], 0, u)
            add_rows(acc.at[0], 0, pack(f), 0, got.at[0], 0, u)

        self.stages = [((two, one), add_near)]
        gathers = []
        n, at, base, place_at = u, 0, 0, 2
        slots = 2
        for bit in order:
            last = bit == order[-1]
            if bit == 0:
                rows = rows_at(at, n)
                copy = remote(
                    acc.at[1, rows], far.at[0:n], sems.at[place_at], {"freq": flip(f, 2)}
                )
                finish = partial(add_rows, acc.at[0], at, acc.at[0], at, far, 0, n)
                self.stages.append(((copy,), finish))
                slots, place_at = 1, place_at + 1
                continue
            peer = {"tm": flip(t, bit)}
            half = n % 32 == 0 and not last
            if half:
                upper = lax.rem(t // bit, 2)
                n = n // 2
                keep, give = at + upper * n, at + (1 - upper) * n
            else:
                keep, give = at, at
            copy = remote(
                acc.at[0:slots, rows_at(give, n)],
                rs.at[0:slots, base : base + n],
                sems.at[place_at],
                peer,
            )

            def finish(slots=slots, keep=keep, base=base, n=n, last=last):
                for slot in range(slots):
                    target = out if last else acc.at[slot]
                    add_rows(target, keep, acc.at[slot], keep, rs.at[slot], base, n)

            self.stages.append(((copy,), finish))
            if half:
                share = out.at[rows_at(keep, n)]
                gathers.append(((remote(share, share, sems.at[place_at + 1], peer),), None))
            at, base, place_at = keep, base + n, place_at + 2
        self.stages.extend(gathers[::-1])
        self.now = -1

    def done(self):
        return self.now >= len(self.stages)

    def advance(self):
        if self.done():
            return
        if self.now >= 0:
            copies, finish = self.stages[self.now]
            for copy in copies:
                copy.wait()
            if finish is not None:
                finish()
        self.now += 1
        if not self.done():
            for copy in self.stages[self.now][0]:
                copy.start()


def orders_of(nt):
    bits = bits_of(nt)
    far_first = [0] + bits
    if len(bits) < 2:
        return far_first, far_first
    return far_first, [bits[1], 0, bits[0]] + bits[2:]


def stage_count(nt):
    return 3 + 2 * len(bits_of(nt))


def padded(rows):
    return (rows + 63) // 64 * 64


def chunk_order(nf):
    width = F // nf
    row = lax.broadcasted_iota(jnp.int32, (CH, CH), 0)
    source = lax.broadcasted_iota(jnp.int32, (CH, CH), 1)
    col = lax.rem(row, F)
    wanted = (col // width) * (CR * width) + (row // F) * width + lax.rem(col, width)
    return jnp.where(source == wanted, 1.0, 0.0).astype(BF)


def clear_ends(spot, count, from_left, from_right):
    @pl.when(spot == 0)
    def _():
        from_left[...] = jnp.zeros_like(from_left)

    @pl.when(spot == count - 1)
    def _():
        from_right[...] = jnp.zeros_like(from_right)


def group_matrix():
    i = lax.broadcasted_iota(jnp.int32, (C, C), 0) // GW
    j = lax.broadcasted_iota(jnp.int32, (C, C), 1) // GW
    return (i == j).astype(F32)


def spread(rows, count):
    return jnp.broadcast_to(rows[:, None, :], (count, F, C))


def column_index(count):
    return lax.broadcasted_iota(jnp.int32, (count, F, C), 1)


def column_shifts(act, count):
    col = column_index(count)
    before = jnp.where(col == 0, 0.0, pltpu.roll(act, 1, 1))
    after = jnp.where(col == F - 1, 0.0, pltpu.roll(act, F - 1, 1))
    return before, after


def store_shifts(xc, at, act, count):
    before, after = column_shifts(act, count)
    size = count * F
    xc[pl.ds(at, size), 0:C] = before.reshape(size, C).astype(BF)
    xc[pl.ds(at, size), C : 2 * C] = act.reshape(size, C).astype(BF)
    xc[pl.ds(at, size), 2 * C : 3 * C] = after.reshape(size, C).astype(BF)


def loop(count, body):
    def step(i, carry):
        body(i)
        return carry

    lax.fori_loop(0, count, step, 0)


def chunk_at(i, size=CH):
    return pl.multiple_of(i * size, size)


class Clip:
    def __init__(self, same, rowtab, edge, gmat):
        self.same, self.rowtab, self.edge, self.gmat = same, rowtab, edge, gmat

    def pack(self, rs, rq, to_left, to_right):
        first = hdot(self.edge[...], rs[...])
        second = hdot(self.edge[...], rq[...])
        to_left[0:1] = first[0:1]
        to_left[1:2] = second[0:1]
        to_right[0:1] = first[1:2]
        to_right[1:2] = second[1:2]

    def means(self, rs, rq, gain, from_left, from_right):
        at_left = self.rowtab[:, 1:2] > 0.0
        at_right = self.rowtab[:, 2:3] > 0.0
        inverse = self.rowtab[:, 0:1]
        results = []
        for index, table in ((0, rs), (1, rq)):
            total = hdot(self.same[...], table[...])
            total = total + jnp.where(at_left, from_left[index : index + 1], 0.0)
            total = total + jnp.where(at_right, from_right[index : index + 1], 0.0)
            total = total * inverse
            if gain is not None:
                total = total * gain
            results.append(hdot(total, self.gmat[...]))
        return results


def row_masks(rowtab, prev_mask, next_mask, rows):
    prev_mask[...] = jnp.broadcast_to(rowtab[0:rows, 3:4], (rows, C))
    next_mask[...] = jnp.broadcast_to(rowtab[0:rows, 4:5], (rows, C))


def front_kernel(
    nt,
    nf,
    lat_local,
    cot_local,
    wconv,
    wproj,
    wmlp,
    wemb,
    wsmall,
    cond,
    onehot,
    same,
    rowtab,
    edge,
    conv,
    proj,
    mlp,
    vec,
    cot,
    zhat1,
    zhat2,
    zhat3,
    rstd1,
    rstd2,
    rstd3,
    resid,
    inner,
    query,
    kext,
    vext,
    inext,
    gmat,
    rs,
    rq,
    mean,
    prev_mask,
    next_mask,
    xc,
    z_prev,
    z_here,
    z_next,
    hidden,
    to_left,
    to_right,
    from_left,
    from_right,
    emb,
    small,
    lat,
    lat_in,
    cot_in,
    order,
    film,
    msg_sems,
    kv_sems,
    block_sems,
    gather_sems,
):
    px = lat.shape[0]
    rows = px // F
    chunks = px // CH
    blk = px // nf
    seg = CH // nf
    spot, left, right = place(nt, nf)
    count = nt * nf
    where = (spot, count, left, right)
    f = lax.axis_index("freq")
    t = lax.axis_index("tm")
    s = snake(f, t, nf)
    partners = [{"freq": flip_by(f, mask)} for mask in range(1, nf)] + [{"tm": flip(t, 1)}]
    enter(spot, count, left, right, partners)
    blocks = []
    for index, (local, landed) in enumerate(((lat_local, lat_in), (cot_local, cot_in))):
        blocks.append(
            Exchange(
                lambda peer, local=local: local.at[rows_at(snake(peer, t, nf) * blk, blk)],
                lambda peer, landed=landed: landed.at[f],
                local.at[rows_at(s * blk, blk)],
                landed.at[f],
                f,
                nf,
                block_sems.at[index],
            )
        )
    blocks[0].start()

    def cast(src, dst, base):
        size = 32 if src.shape[0] % 64 else 64

        def step(i):
            dst[rows_at(base + i * size, size)] = src[rows_at(i * size, size)].astype(BF)

        loop(src.shape[0] // size, step)

    cdepth, pdepth, mdepth, edepth = (
        wconv.shape[1],
        wproj.shape[1],
        wmlp.shape[1],
        wemb.shape[0],
    )
    views = (
        (share_view(conv, cdepth, 0), None),
        (share_view(conv, cdepth, 1), cdepth),
        (share_view(proj, pdepth, slice(None)), pdepth),
        (share_view(mlp, mdepth, slice(None)), mdepth),
        (share_view(emb, edepth, None), edepth),
        (share_view(small, wsmall.shape[0], None), None),
    )
    gathers = []
    for i, (view, size) in enumerate(views):
        gathers.append(Gather(view, f, t, gather_sems.at[i], size))
    get_first, get_second, get_proj, get_mlp, get_emb, get_small = gathers
    cast(wsmall, small, f * wsmall.shape[0])
    cast(wconv.at[0], conv.at[0], f * cdepth)
    get_small.start()
    get_first.start()
    cast(wemb, emb, f * edepth)
    cast(wconv.at[1], conv.at[1], f * cdepth)
    for i in range(wproj.shape[0]):
        cast(wproj.at[i], proj.at[i], f * pdepth)
    for i in range(wmlp.shape[0]):
        cast(wmlp.at[i], mlp.at[i], f * mdepth)
    order[...] = chunk_order(nf)

    def arrange(landed, target):
        def step(c):
            parts = [landed[k, rows_at(c * seg, seg)] for k in range(nf)]
            moved = mm(order[...], jnp.concatenate(parts, axis=0))
            target[pl.ds(chunk_at(c), CH)] = moved.astype(BF)

        loop(chunks, step)

    clear_ends(spot, count, from_left, from_right)

    @pl.when(spot == 0)
    def _():
        inext[0:px] = jnp.zeros((px, C), BF)

    @pl.when(spot == count - 1)
    def _():
        inext[2 * px : 3 * px] = jnp.zeros((px, C), BF)

    gmat[...] = group_matrix()
    row_masks(rowtab, prev_mask, next_mask, rows)
    clip = Clip(same, rowtab, edge, gmat)

    def v(i):
        return vec[i : i + 1]

    def norm_stage(step, load, zhat, rstd, rim, beside):
        def sums(c):
            x3 = load(c).reshape(CR, F, C)
            rs[pl.ds(chunk_at(c, CR), CR)] = jnp.sum(x3, axis=1)
            rq[pl.ds(chunk_at(c, CR), CR)] = jnp.sum(x3 * x3, axis=1)

        loop(chunks, sums)
        clip.pack(rs, rq, to_left.at[step], to_right.at[step])
        first, last = rim()
        to_left[step, 8:16] = first
        to_right[step, 8:16] = last
        swap = Swap(
            where,
            to_left.at[step],
            to_right.at[step],
            from_left.at[step],
            from_right.at[step],
            msg_sems.at[step],
        )
        swap.start()
        beside()
        swap.wait()
        mean_rows, square_rows = clip.means(rs, rq, None, from_left.at[step], from_right.at[step])
        mean[...] = mean_rows
        rstd[...] = lax.rsqrt(square_rows - mean_rows * mean_rows + norm_eps)
        rim_raw = jnp.concatenate([from_left[step, 8:16], from_right[step, 8:16]], axis=0)
        rim3 = rim_raw.reshape(2, F, C)
        rim_hat = (rim3 - spread(mean[rows : rows + 2], 2)) * spread(rstd[rows : rows + 2], 2)
        if zhat.shape[0] > px:
            zhat[px : px + 16] = rim_hat.reshape(16, C)
        return rim_hat

    def normed(load, zhat, rstd, c):
        r0 = chunk_at(c, CR)
        x3 = load(c).reshape(CR, F, C)
        hat = (x3 - spread(mean[pl.ds(r0, CR)], CR)) * spread(rstd[pl.ds(r0, CR)], CR)
        zhat[pl.ds(chunk_at(c), CH)] = hat.reshape(CH, C)
        return hat

    def conv_stage(rim_hat, load, zhat, rstd, gain, shift, kernel, ready, finish):
        pre = rim_hat * gain + shift
        store_shifts(xc, px, (pre * jax.nn.sigmoid(pre)).astype(BF).astype(F32), 2)

        def build(c):
            pre = normed(load, zhat, rstd, c) * gain + shift
            act = (pre * jax.nn.sigmoid(pre)).astype(BF).astype(F32)
            store_shifts(xc, chunk_at(c), act, CR)

        loop(chunks, build)
        ready()

        def product(c):
            p0 = chunk_at(c)
            part = xc[pl.ds(p0, CH)]
            z_prev[pl.ds(pl.multiple_of(p0 + 8, 8), CH)] = mm(part, kernel[0 : 3 * C])
            z_here[pl.ds(p0, CH)] = mm(part, kernel[3 * C : 6 * C])
            z_next[pl.ds(p0, CH)] = mm(part, kernel[6 * C : 9 * C])

        loop(chunks, product)
        part = xc[px : px + 16]
        z_prev[0:8] = mm(part, kernel[0 : 3 * C])[0:8]
        z_next[px : px + 8] = mm(part, kernel[6 * C : 9 * C])[8:16]

        def join(c):
            p0 = chunk_at(c)
            r0 = chunk_at(c, CR)
            keep_prev = spread(prev_mask[pl.ds(r0, CR)], CR) > 0.0
            keep_next = spread(next_mask[pl.ds(r0, CR)], CR) > 0.0
            out = z_here[pl.ds(p0, CH)].reshape(CR, F, C)
            out = out + jnp.where(keep_prev, z_prev[pl.ds(p0, CH)].reshape(CR, F, C), 0.0)
            after = z_next[pl.ds(pl.multiple_of(p0 + 8, 8), CH)].reshape(CR, F, C)
            finish(c, out + jnp.where(keep_next, after, 0.0))

        loop(chunks, join)

    def load_latent(c):
        return lat[pl.ds(chunk_at(c), CH)].astype(F32)

    def load_hidden(c):
        return hidden[pl.ds(chunk_at(c), CH)]

    def load_resid(c):
        return resid[pl.ds(chunk_at(c), CH)]

    def send_second():
        get_emb.start()
        get_second.start()
        blocks[1].start()
        get_small.relay()
        get_small.collect()
        total = small[0 : wsmall.shape[0]].astype(F32)
        for k in range(1, nf):
            at = k * wsmall.shape[0]
            total = total + small[at : at + wsmall.shape[0]].astype(F32)
        vec[...] = total

    blocks[0].wait()
    arrange(lat_in, lat)
    rim_hat = norm_stage(
        0,
        load_latent,
        zhat1,
        rstd1,
        lambda: (lat[0:16].astype(F32)[0:8], lat[px - 16 : px].astype(F32)[8:16]),
        send_second,
    )

    def ready_first():
        get_first.relay()
        get_emb.relay()
        get_second.relay()
        get_first.collect()
        get_emb.collect()
        table = mm(cond[...], emb[...]) + v(3)
        film[...] = hdot(onehot[...], table)

    def finish_one(c, out):
        r0 = chunk_at(c, CR)
        out = out + v(2) + spread(film[pl.ds(r0, CR)], CR)
        hidden[pl.ds(chunk_at(c), CH)] = out.reshape(CH, C)

    conv_stage(rim_hat, load_latent, zhat1, rstd1, v(0), v(1), conv.at[0], ready_first, finish_one)

    def send_proj():
        get_proj.start()
        get_mlp.start()
        blocks[1].wait()
        arrange(cot_in, cot)

    def ready_second():
        get_second.collect()
        get_proj.relay()
        get_mlp.relay()

    rim_hat = norm_stage(
        1, load_hidden, zhat2, rstd2, lambda: (hidden[0:8], hidden[px - 8 : px]), send_proj
    )

    def finish_two(c, out):
        p0 = chunk_at(c)
        total = lat[pl.ds(p0, CH)].astype(F32) + out.reshape(CH, C) + v(6)
        resid[pl.ds(p0, CH)] = total

    conv_stage(rim_hat, load_hidden, zhat2, rstd2, v(4), v(5), conv.at[1], ready_second, finish_two)

    def ready_proj():
        get_proj.collect()
        get_mlp.collect()

    norm_stage(
        2, load_resid, zhat3, rstd3, lambda: (resid[0:8], resid[px - 8 : px]), ready_proj
    )

    def project(c):
        p0 = chunk_at(c)
        hat = normed(load_resid, zhat3, rstd3, c).reshape(CH, C)
        low = (hat * v(7) + v(8)).astype(BF)
        value = mm(low, proj[0]) + v(9)
        inner[pl.ds(p0, CH)] = value
        inext[pl.ds(pl.multiple_of(px + p0, CH), CH)] = value.astype(BF)

    loop(chunks, project)
    swap = Swap(
        where,
        inext.at[px : 2 * px],
        inext.at[px : 2 * px],
        inext.at[0:px],
        inext.at[2 * px : 3 * px],
        kv_sems.at[0],
    )
    swap.start()

    def keys_values(part):
        low = inext[part]
        kext[part] = mm(low, proj[2]).astype(BF)
        vext[part] = mm(low, proj[3]).astype(BF)

    def heads(c):
        part = pl.ds(pl.multiple_of(px + chunk_at(c), CH), CH)
        query[pl.ds(chunk_at(c), CH)] = mm(inext[part], proj[1]).astype(BF)
        keys_values(part)

    loop(chunks, heads)
    swap.wait()

    def rims(c):
        keys_values(pl.ds(chunk_at(c), CH))
        keys_values(pl.ds(pl.multiple_of(2 * px + chunk_at(c), CH), CH))

    loop(chunks, rims)
    for gather in gathers:
        gather.finish()


def vmem(count):
    return [pl.BlockSpec(memory_space=pltpu.VMEM)] * count


def front(nt, nf, lat, cot, wconv, wproj, wmlp, wemb, wsmall, cond, onehot, same, rowtab, edge):
    px = lat.shape[0]
    rows = px // F
    tab = rowtab.shape[0]

    def whole(share, axis):
        shape = list(share.shape)
        shape[axis] *= nf
        return tuple(shape)

    shapes = (
        (whole(wconv, 1), BF),
        (whole(wproj, 1), BF),
        (whole(wmlp, 1), BF),
        (wsmall.shape, F32),
        ((px, C), BF),
        ((px, C), F32),
        ((px + 16, C), F32),
        ((px + 16, C), F32),
        ((tab, C), F32),
        ((tab, C), F32),
        ((tab, C), F32),
        ((px, C), F32),
        ((px, C), F32),
        ((px, C), BF),
        ((3 * px, C), BF),
        ((3 * px, C), BF),
        ((3 * px, C), BF),
    )
    return pl.pallas_call(
        partial(front_kernel, nt, nf),
        out_shape=[jax.ShapeDtypeStruct(s, d) for s, d in shapes],
        in_specs=vmem(12),
        out_specs=vmem(len(shapes)),
        scratch_shapes=[
            pltpu.VMEM((C, C), F32),
            pltpu.VMEM((rows, C), F32),
            pltpu.VMEM((rows, C), F32),
            pltpu.VMEM((tab, C), F32),
            pltpu.VMEM((rows, C), F32),
            pltpu.VMEM((rows, C), F32),
            pltpu.VMEM((px + 16, 3 * C), BF),
            pltpu.VMEM((px + 16, C), F32),
            pltpu.VMEM((px, C), F32),
            pltpu.VMEM((px + 16, C), F32),
            pltpu.VMEM((px, C), F32),
            pltpu.VMEM((3, 16, C), F32),
            pltpu.VMEM((3, 16, C), F32),
            pltpu.VMEM((3, 16, C), F32),
            pltpu.VMEM((3, 16, C), F32),
            pltpu.VMEM(whole(wemb, 0), BF),
            pltpu.VMEM((nf * wsmall.shape[0], C), BF),
            pltpu.VMEM((px, C), BF),
            pltpu.VMEM((nf, px // nf, C), BF),
            pltpu.VMEM((nf, px // nf, C), BF),
            pltpu.VMEM((CH, CH), BF),
            pltpu.VMEM((rows, C), F32),
            pltpu.SemaphoreType.DMA((3, 4)),
            pltpu.SemaphoreType.DMA((2, 4)),
            pltpu.SemaphoreType.DMA((2, nf - 1, 2)),
            pltpu.SemaphoreType.DMA((6, 5, 2)),
        ],
        compiler_params=pltpu.CompilerParams(
            collective_id=1, has_side_effects=True, vmem_limit_bytes=VMEM_LIMIT
        ),
        name="front",
    )(lat, cot, wconv, wproj, wmlp, wemb, wsmall, cond, onehot, same, rowtab, edge)


def head_mask(h):
    lane = lax.broadcasted_iota(jnp.int32, (CH, C), 1)
    return (lane >= h * HD) & (lane < (h + 1) * HD)


def head_rows(h):
    return slice(h * HD, (h + 1) * HD)


def turned(block):
    return block.astype(F32).T


def score_bias(segk, segq, key_row, q0):
    keys = jnp.broadcast_to(segk[pl.ds(key_row, CR), 0:1], (CR, C))
    keys = spread(keys, CR).reshape(CH, C)
    return jnp.where(keys == segq[0:1, pl.ds(q0, CH)], 0.0, masked_score)


def attend_kernel(meta, query, kext, vext, segq, segk, mixed, mixed_t, lse, vt, qm, bias, top, tot, acc):
    px = query.shape[0]
    factor = score_scale * LOG2E

    def turn(i):
        k0 = chunk_at(i)
        vt[:, pl.ds(k0, CH)] = turned(vext[pl.ds(k0, CH)]).astype(BF)

    loop(vext.shape[0] // CH, turn)

    def tile(t):
        q0 = chunk_at(t)
        block = query[pl.ds(q0, CH)].astype(F32)
        for h in range(H):
            qm[h] = jnp.where(head_mask(h), block, 0.0).astype(BF)
        top[...] = jnp.full((H, CH), masked_score, F32)
        tot[...] = jnp.zeros((H, CH), F32)
        acc[...] = jnp.zeros((C, CH), F32)

        def keys(i):
            row = meta[0, t] * 16 + i * CR
            base = pl.multiple_of(row * F, 128)
            bias[...] = score_bias(segk, segq, pl.multiple_of(row, 16), q0)
            key = kext[pl.ds(base, CH)]
            for h in range(H):
                raw = mm_nt(key, qm[h]) + bias[...]
                old = top[h : h + 1]
                new = jnp.maximum(old, jnp.max(raw, axis=0, keepdims=True))
                fade = jnp.exp2((old - new) * factor)
                weight = jnp.exp2((raw - new) * factor)
                top[h : h + 1] = new
                tot[h : h + 1] = tot[h : h + 1] * fade + jnp.sum(weight, axis=0, keepdims=True)
                part = mm(vt[head_rows(h), pl.ds(base, CH)], weight.astype(BF))
                acc[head_rows(h)] = acc[head_rows(h)] * fade + part

        loop(meta[1, t], keys)
        for h in range(H):
            acc[head_rows(h)] = acc[head_rows(h)] / tot[h : h + 1]
        lse[:, pl.ds(q0, CH)] = top[...] * factor + jnp.log2(tot[...])
        mixed_t[:, pl.ds(q0, CH)] = acc[...].astype(BF)
        mixed[pl.ds(q0, CH)] = acc[...].T.astype(BF)

    loop(px // CH, tile)


def attend(meta, query, kext, vext, segq, segk):
    px = query.shape[0]
    ext = kext.shape[0]
    return pl.pallas_call(
        attend_kernel,
        out_shape=[
            jax.ShapeDtypeStruct((px, C), BF),
            jax.ShapeDtypeStruct((C, px), BF),
            jax.ShapeDtypeStruct((H, px), F32),
        ],
        in_specs=[pl.BlockSpec(memory_space=pltpu.SMEM)] + vmem(5),
        out_specs=vmem(3),
        scratch_shapes=[
            pltpu.VMEM((C, ext), BF),
            pltpu.VMEM((H, CH, C), BF),
            pltpu.VMEM((CH, CH), F32),
            pltpu.VMEM((H, CH), F32),
            pltpu.VMEM((H, CH), F32),
            pltpu.VMEM((C, CH), F32),
        ],
        compiler_params=pltpu.CompilerParams(vmem_limit_bytes=VMEM_LIMIT),
        name="attend",
    )(meta, query, kext, vext, segq, segk)


def attend_back_kernel(
    meta,
    query,
    kext,
    vext,
    segq,
    segk,
    gmix,
    mixed_t,
    lse,
    dq,
    dk,
    dv,
    kt,
    qm,
    gm,
    qt,
    gt,
    inner_rows,
    bias,
    dqt,
    dkt,
    dvt,
):
    px = query.shape[0]
    ext = kext.shape[0]
    factor = score_scale * LOG2E

    def turn(i):
        k0 = chunk_at(i)
        kt[:, pl.ds(k0, CH)] = turned(kext[pl.ds(k0, CH)]).astype(BF)
        dkt[:, pl.ds(k0, CH)] = jnp.zeros((C, CH), F32)
        dvt[:, pl.ds(k0, CH)] = jnp.zeros((C, CH), F32)

    loop(ext // CH, turn)

    def tile(t):
        q0 = chunk_at(t)
        block = query[pl.ds(q0, CH)].astype(F32)
        grad = gmix[pl.ds(q0, CH)].astype(F32)
        for h in range(H):
            qm[h] = jnp.where(head_mask(h), block, 0.0).astype(BF)
            gm[h] = jnp.where(head_mask(h), grad, 0.0).astype(BF)
        qt[...] = block.T.astype(BF)
        grad_t = grad.T
        gt[...] = grad_t.astype(BF)
        crossed = grad_t * mixed_t[:, pl.ds(q0, CH)].astype(F32)
        inner_rows[...] = jnp.sum(crossed.reshape(H, HD, CH), axis=1)
        dqt[...] = jnp.zeros((C, CH), F32)

        def keys(i):
            row = meta[0, t] * 16 + i * CR
            base = pl.multiple_of(row * F, 128)
            bias[...] = score_bias(segk, segq, pl.multiple_of(row, 16), q0)
            key = kext[pl.ds(base, CH)]
            val = vext[pl.ds(base, CH)]
            for h in range(H):
                raw = mm_nt(key, qm[h]) + bias[...]
                probs = jnp.exp2(raw * factor - lse[h : h + 1, pl.ds(q0, CH)])
                gprob = mm_nt(val, gm[h])
                gscore = (probs * (gprob - inner_rows[h : h + 1]) * score_scale).astype(BF)
                dvt[head_rows(h), pl.ds(base, CH)] += mm_nt(gt[head_rows(h)], probs.astype(BF))
                dkt[head_rows(h), pl.ds(base, CH)] += mm_nt(qt[head_rows(h)], gscore)
                dqt[head_rows(h)] += mm(kt[head_rows(h), pl.ds(base, CH)], gscore)

        loop(meta[1, t], keys)
        dq[pl.ds(q0, CH)] = dqt[...].T.astype(BF)

    loop(px // CH, tile)

    def settle(i):
        k0 = chunk_at(i)
        dk[pl.ds(k0, CH)] = dkt[:, pl.ds(k0, CH)].T.astype(BF)
        dv[pl.ds(k0, CH)] = dvt[:, pl.ds(k0, CH)].T.astype(BF)

    loop(ext // CH, settle)


def attend_back(meta, query, kext, vext, segq, segk, gmix, mixed_t, lse):
    px = query.shape[0]
    ext = kext.shape[0]
    return pl.pallas_call(
        attend_back_kernel,
        out_shape=[
            jax.ShapeDtypeStruct((px, C), BF),
            jax.ShapeDtypeStruct((ext, C), BF),
            jax.ShapeDtypeStruct((ext, C), BF),
        ],
        in_specs=[pl.BlockSpec(memory_space=pltpu.SMEM)] + vmem(8),
        out_specs=vmem(3),
        scratch_shapes=[
            pltpu.VMEM((C, ext), BF),
            pltpu.VMEM((H, CH, C), BF),
            pltpu.VMEM((H, CH, C), BF),
            pltpu.VMEM((C, CH), BF),
            pltpu.VMEM((C, CH), BF),
            pltpu.VMEM((H, CH), F32),
            pltpu.VMEM((CH, CH), F32),
            pltpu.VMEM((C, CH), F32),
            pltpu.VMEM((C, ext), F32),
            pltpu.VMEM((C, ext), F32),
        ],
        compiler_params=pltpu.CompilerParams(vmem_limit_bytes=VMEM_LIMIT),
        name="attend_back",
    )(meta, query, kext, vext, segq, segk, gmix, mixed_t, lse)


def middle_kernel(
    nf,
    inner,
    mixed,
    resid,
    cot,
    proj,
    mlp,
    vec,
    output,
    gafter,
    gmix,
    pack,
    sums,
    after_low,
    act_low,
    pre_low,
    down_low,
    mlp_low,
    after_grad_low,
    ubias,
    order,
):
    px = inner.shape[0]
    seg = CH // nf
    tail = 11 + FF // C
    order[...] = chunk_order(nf)
    sums[...] = jnp.zeros_like(sums)
    for j in range(FF // C):
        ubias[:, j * C : (j + 1) * C] = vec[11 + j : 12 + j]

    def step(c):
        p0 = chunk_at(c)
        after = inner[pl.ds(p0, CH)] + mm(mixed[pl.ds(p0, CH)], proj[4]) + vec[10:11]
        low = after.astype(BF)
        after_low[pl.ds(p0, CH)] = low
        grad_out = cot[pl.ds(p0, CH)]
        grad_mlp = mm_nt(grad_out, proj[5])
        down = grad_mlp.astype(BF)
        down_low[pl.ds(p0, CH)] = down
        total = after
        grad_after = grad_mlp
        for j in range(FF // C):
            part = slice(j * C, (j + 1) * C)
            pre = mm_nt(low, mlp[0, part]) + ubias[:, part]
            cdf = 0.5 + 0.5 * lax.erf(pre * (0.5**0.5))
            act = (pre * cdf).astype(BF)
            act_low[pl.ds(p0, CH), part] = act
            total = total + mm(act, mlp[1, part])
            density = jnp.exp(pre * pre * -0.5) * 0.3989422804014327
            grad_pre = mm_nt(down, mlp[1, part]) * (cdf + pre * density)
            sums[3 + j : 4 + j] += jnp.sum(grad_pre, axis=0, keepdims=True)
            grad_low = grad_pre.astype(BF)
            pre_low[pl.ds(p0, CH), part] = grad_low
            grad_after = grad_after + mm(grad_low, mlp[0, part])
        total = (total + vec[tail : tail + 1]).astype(BF)
        mlp_low[pl.ds(p0, CH)] = total
        branch = mm(total, proj[5]) + vec[tail + 1 : tail + 2]
        moved = mm_tn(order[...], (resid[pl.ds(p0, CH)] + branch).astype(BF)).astype(BF)
        for k in range(nf):
            output[k, rows_at(c * seg, seg)] = moved[k * seg : (k + 1) * seg]
        gafter[pl.ds(p0, CH)] = grad_after
        grad_low = grad_after.astype(BF)
        after_grad_low[pl.ds(p0, CH)] = grad_low
        gmix[pl.ds(p0, CH)] = mm_nt(grad_low, proj[4]).astype(BF)
        sums[0:1] += jnp.sum(grad_out.astype(F32), axis=0, keepdims=True)
        sums[1:2] += jnp.sum(grad_mlp, axis=0, keepdims=True)
        sums[2:3] += jnp.sum(grad_after, axis=0, keepdims=True)

    loop(px // CH, step)
    width = FF // nf
    for k in range(nf):
        part = slice(k * width, (k + 1) * width)
        pack[k, 0:width] = mm_tn(pre_low[:, part], after_low[...]).astype(BF)
        pack[k, width : 2 * width] = mm_tn(act_low[:, part], down_low[...]).astype(BF)
    depth = C // nf
    gw_attn = mm_tn(mixed[...], after_grad_low[...]).astype(BF)
    gw_out = mm_tn(mlp_low[...], cot[...]).astype(BF)
    for k in range(nf):
        part = slice(k * depth, (k + 1) * depth)
        pack[k, 2 * width : 2 * width + depth] = gw_attn[part]
        pack[k, 2 * width + depth : 2 * width + 2 * depth] = gw_out[part]


def middle(nf, inner, mixed, resid, cot, proj, mlp, vec):
    px = inner.shape[0]
    return pl.pallas_call(
        partial(middle_kernel, nf),
        out_shape=[
            jax.ShapeDtypeStruct((nf, px // nf, C), BF),
            jax.ShapeDtypeStruct((px, C), F32),
            jax.ShapeDtypeStruct((px, C), BF),
            jax.ShapeDtypeStruct((nf, 2 * (FF + C) // nf, C), BF),
            jax.ShapeDtypeStruct((8, C), F32),
        ],
        in_specs=vmem(7),
        out_specs=vmem(5),
        scratch_shapes=[
            pltpu.VMEM((px, C), BF),
            pltpu.VMEM((px, FF), BF),
            pltpu.VMEM((px, FF), BF),
            pltpu.VMEM((px, C), BF),
            pltpu.VMEM((px, C), BF),
            pltpu.VMEM((px, C), BF),
            pltpu.VMEM((1, FF), F32),
            pltpu.VMEM((CH, CH), BF),
        ],
        compiler_params=pltpu.CompilerParams(vmem_limit_bytes=VMEM_LIMIT),
        name="middle",
    )(inner, mixed, resid, cot, proj, mlp, vec)


def back_kernel(
    nt,
    nf,
    dq,
    dk,
    dv,
    gafter,
    inext,
    zhat1,
    zhat2,
    zhat3,
    rstd1,
    rstd2,
    rstd3,
    cot,
    conv,
    proj,
    vec,
    same,
    rowtab,
    edge,
    cond,
    onehot,
    mid_sums,
    pack_a,
    out_blocks,
    output,
    glat,
    out_a,
    out_b,
    out_c,
    out_d,
    out_e,
    sums,
    film_rows,
    gmat,
    rs,
    rq,
    mean_e,
    mean_ez,
    prev_mask,
    next_mask,
    normed_low,
    grad_low,
    gresid,
    dgrad,
    two,
    xc,
    shifted,
    rim_out,
    rim_got,
    to_left,
    to_right,
    from_left,
    from_right,
    order,
    glat_blocks,
    *rest,
):
    pack_b, pack_c, pack_d, pack_e = rest[:4]
    pieces = rest[4:28]
    msg_sems, kv_sems, block_sems, reduce_sems = rest[28:32]
    px = dq.shape[0]
    rows = px // F
    chunks = px // CH
    blk = px // nf
    seg = CH // nf
    spot, left, right = place(nt, nf)
    count = nt * nf
    where = (spot, count, left, right)
    f = lax.axis_index("freq")
    t = lax.axis_index("tm")
    s = snake(f, t, nf)
    partners = [{"freq": flip_by(f, mask)} for mask in range(1, nf)]
    partners = partners + [{"tm": flip(t, bit)} for bit in bits_of(nt)]
    enter(spot, count, left, right, partners)
    far_first, far_later = orders_of(nt)
    whole_d = out_d.shape[0]
    half = padded(whole_d // 2)
    plans = (
        (far_later, lambda i: pack_a.at[i], out_a),
        (far_first, lambda i: pack_b.at[i], out_b),
        (far_later, lambda i: pack_c.at[i], out_c),
        (far_first, lambda i: pack_d.at[i, 0:half], out_d.at[0:half]),
        (far_later, lambda i: pack_d.at[i, half:whole_d], out_d.at[half:whole_d]),
        (far_first, lambda i: pack_e.at[i], out_e),
    )
    jobs = []
    for index, (order_of, pack, out) in enumerate(plans):
        room = pieces[4 * index : 4 * index + 4]
        jobs.append(Reduce(order_of, pack, *room, out, reduce_sems.at[index], t, f))
    job_a, job_b, job_c, job_d, job_dd, job_e = jobs
    blocks = []
    for index, (source, landed) in enumerate(((out_blocks, output), (glat_blocks, glat))):
        blocks.append(
            Exchange(
                lambda peer, source=source: source.at[peer],
                lambda peer, landed=landed: landed.at[rows_at(s * blk, blk)],
                source.at[f],
                landed.at[rows_at(s * blk, blk)],
                f,
                nf,
                block_sems.at[index],
            )
        )
    def rim_grads(c):
        part = pl.ds(chunk_at(c), CH)
        for side in range(2):
            beyond = pl.ds(pl.multiple_of(2 * side * px + chunk_at(c), CH), CH)
            value = mm_nt(dk[beyond], proj[2]) + mm_nt(dv[beyond], proj[3])
            rim_out[side, part] = value.astype(BF)

    loop(chunks, rim_grads)
    rim_swap = Swap(
        where, rim_out.at[0], rim_out.at[1], rim_got.at[0], rim_got.at[1], kv_sems.at[0]
    )
    rim_swap.start()
    job_a.advance()
    order[...] = chunk_order(nf)
    clear_ends(spot, count, from_left, from_right)
    clear_ends(spot, count, rim_got.at[0], rim_got.at[1])
    gmat[...] = group_matrix()
    row_masks(rowtab, prev_mask, next_mask, rows)
    clip = Clip(same, rowtab, edge, gmat)
    sums[...] = jnp.zeros_like(sums)

    def v(i):
        return vec[i : i + 1]

    def first(c):
        p0 = chunk_at(c)
        part = pl.ds(p0, CH)
        own = pl.ds(pl.multiple_of(px + p0, CH), CH)
        normed_low[part] = (zhat3[part] * v(7) + v(8)).astype(BF)
        grad = gafter[part] + mm_nt(dq[part], proj[1])
        gresid[part] = grad + mm_nt(dk[own], proj[2]) + mm_nt(dv[own], proj[3])

    loop(chunks, first)
    depth = C // nf

    def proj_grad(which, grad):
        low = grad.astype(BF)
        for k in range(nf):
            pack_b[k, which * depth : (which + 1) * depth] = low[k * depth : (k + 1) * depth]

    proj_grad(1, mm_tn(inext[px : 2 * px], dq[...]))
    job_a.advance()
    rim_swap.wait()

    def row_sums(c, grad3, hat3):
        rs[pl.ds(chunk_at(c, CR), CR)] = jnp.sum(grad3, axis=1)
        rq[pl.ds(chunk_at(c, CR), CR)] = jnp.sum(grad3 * hat3, axis=1)

    def second(c):
        p0 = chunk_at(c)
        part = pl.ds(p0, CH)
        grad = gresid[part] + rim_got[0, part].astype(F32) + rim_got[1, part].astype(F32)
        sums[9:10] += jnp.sum(grad, axis=0, keepdims=True)
        low = grad.astype(BF)
        grad_low[part] = low
        d3 = mm_nt(low, proj[0])
        dgrad[part] = d3
        row_sums(c, d3.reshape(CR, F, C), zhat3[part].reshape(CR, F, C))

    loop(chunks, second)

    def swap_step(step, rim_first, rim_last):
        clip.pack(rs, rq, to_left.at[step], to_right.at[step])
        if rim_first is not None:
            to_left[step, 8 : 8 + rim_first.shape[0]] = rim_first
            to_right[step, 8 : 8 + rim_last.shape[0]] = rim_last
        swap = Swap(
            where,
            to_left.at[step],
            to_right.at[step],
            from_left.at[step],
            from_right.at[step],
            msg_sems.at[step],
        )
        swap.start()
        return swap

    def set_means(step, gain):
        mean_e[...], mean_ez[...] = clip.means(
            rs, rq, gain, from_left.at[step], from_right.at[step]
        )

    def back_norm(grad3, hat3, rstd, gain, r0, size):
        value = grad3 * gain - spread(mean_e[pl.ds(r0, size)], size)
        value = value - hat3 * spread(mean_ez[pl.ds(r0, size)], size)
        return value * spread(rstd[pl.ds(r0, size)], size)

    def rim_grad(step, at):
        both = jnp.concatenate([from_left[step, at : at + 8], from_right[step, at : at + 8]], axis=0)
        return both.reshape(2, F, C)

    sums[7:8] = jnp.sum(rq[...], axis=0, keepdims=True)
    sums[8:9] = jnp.sum(rs[...], axis=0, keepdims=True)
    cot_first = cot[0:16].astype(F32)[0:8]
    cot_last = cot[px - 16 : px].astype(F32)[8:16]
    swap = swap_step(
        0,
        jnp.concatenate([dgrad[0:8], cot_first], axis=0),
        jnp.concatenate([dgrad[px - 8 : px], cot_last], axis=0),
    )
    proj_grad(2, mm_tn(inext[...], dk[...]))
    proj_grad(3, mm_tn(inext[...], dv[...]))
    proj_grad(0, mm_tn(normed_low[...], grad_low[...]))
    job_b.advance()
    job_a.advance()
    swap.wait()
    set_means(0, v(7))

    def set_rims(value):
        low = value.astype(BF).astype(F32)
        two[0:8] = low[0]
        two[px + 8 : px + 16] = low[1]

    rim = rim_grad(0, 8)
    rim_hat = zhat3[px : px + 16].reshape(2, F, C)
    set_rims(rim_grad(0, 16) + back_norm(rim, rim_hat, rstd3, v(7), rows, 2))

    def third(c):
        p0 = chunk_at(c)
        part = pl.ds(p0, CH)
        grad3 = dgrad[part].reshape(CR, F, C)
        hat3 = zhat3[part].reshape(CR, F, C)
        value = back_norm(grad3, hat3, rstd3, v(7), chunk_at(c, CR), CR).reshape(CH, C)
        value = cot[part].astype(F32) + value
        gresid[part] = value
        sums[6:7] += jnp.sum(value, axis=0, keepdims=True)
        two[pl.ds(pl.multiple_of(p0 + 8, 8), CH)] = value.astype(BF).astype(F32)

    loop(chunks, third)

    def conv_inputs(zhat, gain, shift, c):
        p0 = chunk_at(c)
        part = pl.ds(p0, CH)
        r0 = chunk_at(c, CR)
        keep_prev = spread(prev_mask[pl.ds(r0, CR)], CR).reshape(CH, C) > 0.0
        keep_next = spread(next_mask[pl.ds(r0, CR)], CR).reshape(CH, C) > 0.0
        after = two[pl.ds(pl.multiple_of(p0 + 16, 16), CH)]
        here = two[pl.ds(pl.multiple_of(p0 + 8, 8), CH)]
        shifted[part, 0:C] = jnp.where(keep_next, after, 0.0).astype(BF)
        shifted[part, C : 2 * C] = here.astype(BF)
        shifted[part, 2 * C : 3 * C] = jnp.where(keep_prev, two[part], 0.0).astype(BF)
        pre = zhat[part] * gain + shift
        act = (pre * jax.nn.sigmoid(pre)).astype(BF).astype(F32).reshape(CR, F, C)
        store_shifts(xc, p0, act, CR)

    def conv_back(kernel, zhat, gain, shift, c):
        part = pl.ds(chunk_at(c), CH)
        hat = zhat[part]
        pre = hat * gain + shift
        sig = jax.nn.sigmoid(pre)

        def columns(j):
            piece = slice(j * C, (j + 1) * C)
            value = mm_nt(shifted[part, 0:C], kernel[0 : 3 * C][piece])
            value = value + mm_nt(shifted[part, C : 2 * C], kernel[3 * C : 6 * C][piece])
            value = value + mm_nt(shifted[part, 2 * C : 3 * C], kernel[6 * C : 9 * C][piece])
            return value.reshape(CR, F, C)

        col = column_index(CR)
        back = columns(1)
        back = back + jnp.where(col == F - 1, 0.0, pltpu.roll(columns(0), F - 1, 1))
        back = back + jnp.where(col == 0, 0.0, pltpu.roll(columns(2), 1, 1))
        grad = back.reshape(CH, C) * sig * (1.0 + pre * (1.0 - sig))
        dgrad[part] = grad
        row_sums(c, grad.reshape(CR, F, C), hat.reshape(CR, F, C))

    share = TAPS * C // nf

    def kernel_grad(pack):
        for k in range(nf):
            if pack.shape[1] > share:
                pack[k, share:] = jnp.zeros((pack.shape[1] - share, C), BF)
        for d in range(3):
            for j in range(3):
                grad = mm_tn(xc[:, j * C : (j + 1) * C], shifted[:, d * C : (d + 1) * C])
                low = grad.astype(BF)
                start = (d * 3 + j) * C
                end = start + C
                at = start
                while at < end:
                    k = at // share
                    upto = min(end, (k + 1) * share)
                    pack[k, at - k * share : upto - k * share] = low[at - start : upto - start]
                    at = upto

    def step_two(c):
        conv_inputs(zhat2, v(4), v(5), c)
        conv_back(conv.at[1], zhat2, v(4), v(5), c)

    loop(chunks, step_two)
    sums[4:5] = jnp.sum(rq[...], axis=0, keepdims=True)
    sums[5:6] = jnp.sum(rs[...], axis=0, keepdims=True)
    swap = swap_step(1, dgrad[0:8], dgrad[px - 8 : px])
    job_a.advance()
    blocks[0].start()
    kernel_grad(pack_c)
    job_c.advance()
    job_b.advance()
    swap.wait()
    set_means(1, v(4))
    rim_hat = zhat2[px : px + 16].reshape(2, F, C)
    set_rims(back_norm(rim_grad(1, 8), rim_hat, rstd2, v(4), rows, 2))

    def fourth(c):
        p0 = chunk_at(c)
        part = pl.ds(p0, CH)
        grad3 = dgrad[part].reshape(CR, F, C)
        hat3 = zhat2[part].reshape(CR, F, C)
        value3 = back_norm(grad3, hat3, rstd2, v(4), chunk_at(c, CR), CR)
        film_rows[pl.ds(chunk_at(c, CR), CR)] = jnp.sum(value3, axis=1)
        low = value3.reshape(CH, C).astype(BF).astype(F32)
        two[pl.ds(pl.multiple_of(p0 + 8, 8), CH)] = low

    loop(chunks, fourth)
    total = jnp.sum(film_rows[...], axis=0, keepdims=True)
    sums[2:3] = total
    sums[3:4] = total
    loop(chunks, partial(conv_inputs, zhat1, v(0), v(1)))
    kernel_grad(pack_d)
    grad_film = hdot_tn(onehot[...], film_rows[...])
    gemb = hdot_tn(cond[...].astype(F32), grad_film).astype(BF)
    edepth = gemb.shape[0] // nf
    job_d.advance()
    job_dd.advance()

    def sums_one(c):
        conv_back(conv.at[0], zhat1, v(0), v(1), c)

    loop(chunks, sums_one)
    sums[0:1] = jnp.sum(rq[...], axis=0, keepdims=True)
    sums[1:2] = jnp.sum(rs[...], axis=0, keepdims=True)
    swap = swap_step(2, None, None)
    tail = jnp.concatenate(
        [
            sums[0:10],
            mid_sums[2:3],
            mid_sums[3 : 3 + FF // C],
            mid_sums[1:2],
            mid_sums[0:1],
            jnp.zeros((32 - 13 - FF // C, C), F32),
        ],
        axis=0,
    ).astype(BF)
    for k in range(nf):
        pack_e[k, 0:edepth] = gemb[k * edepth : (k + 1) * edepth]
        pack_e[k, edepth : edepth + 32] = tail
        pack_e[k, edepth + 32 :] = jnp.zeros((pack_e.shape[1] - edepth - 32, C), BF)
    job_e.advance()
    for job in (job_d, job_dd, job_c, job_a, job_b):
        job.advance()
    swap.wait()
    set_means(2, v(0))

    def fifth(c):
        p0 = chunk_at(c)
        part = pl.ds(p0, CH)
        grad3 = dgrad[part].reshape(CR, F, C)
        hat3 = zhat1[part].reshape(CR, F, C)
        value = back_norm(grad3, hat3, rstd1, v(0), chunk_at(c, CR), CR).reshape(CH, C)
        moved = mm_tn(order[...], (gresid[part] + value).astype(BF)).astype(BF)
        for k in range(nf):
            glat_blocks[k, rows_at(c * seg, seg)] = moved[k * seg : (k + 1) * seg]

    loop(chunks, fifth)
    blocks[1].start()
    while not all(job.done() for job in jobs):
        for job in (job_d, job_dd, job_e, job_c, job_a, job_b):
            job.advance()
    for block in blocks:
        block.wait()


def back(nt, nf, *args):
    px = args[0].shape[0]
    rows = px // F
    tab = args[-7].shape[0]
    pack_rows = args[-2].shape[1]
    edepth = args[-5].shape[1] // nf
    share = TAPS * C // nf
    heights = (pack_rows, 4 * C // nf, share, share, padded(edepth + 32))
    half = padded(share // 2)
    job_heights = heights[:3] + (half, share - half) + heights[4:]
    buffers = [pltpu.VMEM((nf, u, C), BF) for u in heights[1:]]
    for u in job_heights:
        buffers.extend(
            [
                pltpu.VMEM((2, u, C), BF),
                pltpu.VMEM((2, u, C), BF),
                pltpu.VMEM((u, C), BF),
                pltpu.VMEM((2, 2 * u, C), BF),
            ]
        )
    big = pltpu.VMEM((px, C), F32)
    low = pltpu.VMEM((px, C), BF)
    table = pltpu.VMEM((rows, C), F32)
    return pl.pallas_call(
        partial(back_kernel, nt, nf),
        out_shape=[
            jax.ShapeDtypeStruct((px, C), BF),
            jax.ShapeDtypeStruct((px, C), BF),
        ]
        + [jax.ShapeDtypeStruct((u, C), BF) for u in heights],
        in_specs=vmem(len(args)),
        out_specs=vmem(7),
        scratch_shapes=[
            pltpu.VMEM((16, C), F32),
            pltpu.VMEM((rows, C), F32),
            pltpu.VMEM((C, C), F32),
            table,
            table,
            pltpu.VMEM((tab, C), F32),
            pltpu.VMEM((tab, C), F32),
            table,
            table,
            low,
            low,
            big,
            big,
            pltpu.VMEM((px + 16, C), F32),
            pltpu.VMEM((px, 3 * C), BF),
            pltpu.VMEM((px, 3 * C), BF),
            pltpu.VMEM((2, px, C), BF),
            pltpu.VMEM((2, px, C), BF),
            pltpu.VMEM((3, 24, C), F32),
            pltpu.VMEM((3, 24, C), F32),
            pltpu.VMEM((3, 24, C), F32),
            pltpu.VMEM((3, 24, C), F32),
            pltpu.VMEM((CH, CH), BF),
            pltpu.VMEM((nf, px // nf, C), BF),
            *buffers,
            pltpu.SemaphoreType.DMA((3, 4)),
            pltpu.SemaphoreType.DMA((2, 4)),
            pltpu.SemaphoreType.DMA((2, nf - 1, 2)),
            pltpu.SemaphoreType.DMA((6, stage_count(nt), 2)),
        ],
        compiler_params=pltpu.CompilerParams(
            collective_id=2, has_side_effects=True, vmem_limit_bytes=VMEM_LIMIT
        ),
        name="back",
    )(*args)


def adamw_step(weight, moment, second, grad, decay_rate):
    moment_new = beta_first * moment + (1.0 - beta_first) * grad
    second_new = beta_second * second + (1.0 - beta_second) * grad * grad
    moment_hat = moment_new / (1.0 - beta_first**STEP)
    second_hat = second_new / (1.0 - beta_second**STEP)
    weight_new = weight - learn_rate * (
        moment_hat / (jnp.sqrt(second_hat) + adam_eps) + decay_rate * weight
    )
    return (weight_new, moment_new, second_new)


def layout_of(lengths, spot, count, rows):
    clips = lengths.shape[0]
    clip_index = jnp.arange(clips, dtype=jnp.int32)
    upto = clip_index[:, None] >= clip_index[None, :]
    clip_ends = jnp.sum(jnp.where(upto, lengths[None, :], 0), axis=1)
    first_row = spot * rows
    total_rows = count * rows
    row = first_row - rows + jnp.arange(3 * rows, dtype=jnp.int32)
    seg_ext = jnp.sum((clip_ends[None, :] <= row[:, None]).astype(jnp.int32), axis=1)
    seg_ext = jnp.where((row >= 0) & (row < total_rows), seg_ext, -1)
    seg = seg_ext[rows : 2 * rows]
    seg_left = seg_ext[rows - 1]
    seg_right = seg_ext[2 * rows]
    pad = jnp.full((6,), -2, jnp.int32)
    seg_tab = jnp.concatenate([seg, seg_ext[rows - 1 : rows], seg_ext[2 * rows : 2 * rows + 1], pad])
    onehot = (seg_tab[:, None] == clip_index[None, :]).astype(F32)
    row_len = jnp.sum(onehot * lengths[None, :].astype(F32), axis=1)
    inverse = 1.0 / jnp.maximum(row_len * (F * GW), 1.0)
    beside_prev = jnp.concatenate([(seg_ext[rows - 1 : 2 * rows - 1] == seg).astype(F32), jnp.zeros((8,), F32)])
    beside_next = jnp.concatenate([(seg_ext[rows + 1 : 2 * rows + 1] == seg).astype(F32), jnp.zeros((8,), F32)])
    fields = (
        inverse,
        (seg_tab == seg_left).astype(F32),
        (seg_tab == seg_right).astype(F32),
        beside_prev,
        beside_next,
    )
    lane = jnp.arange(128, dtype=jnp.int32)[None, :]
    rowtab = jnp.zeros((rows + 8, 128), F32)
    for index, field in enumerate(fields):
        rowtab = jnp.where(lane == index, field[:, None], rowtab)
    same = (seg_tab[:, None] == seg[None, :]).astype(F32)
    which = jnp.arange(8, dtype=jnp.int32)[:, None]
    edge = jnp.where(which == 0, seg[None, :] == seg[0], seg[None, :] == seg[rows - 1])
    edge = jnp.where(which < 2, edge, False).astype(F32)
    segk = jnp.broadcast_to(seg_ext.astype(F32)[:, None], (3 * rows, 128))
    segq = jnp.broadcast_to(jnp.repeat(seg.astype(F32), F)[None, :], (8, rows * F))
    tiles = rows // CR
    starts = clip_ends - lengths
    low_clip = seg[::CR]
    high_clip = seg[CR - 1 :: CR]
    low_row = jnp.sum(jnp.where(low_clip[:, None] == clip_index[None, :], starts[None, :], 0), axis=1)
    high_row = jnp.sum(
        jnp.where(high_clip[:, None] == clip_index[None, :], clip_ends[None, :], 0), axis=1
    )
    low_row = low_row - first_row + rows
    high_row = high_row - first_row + rows
    low = low_row // 16
    number = (high_row - low * 16 + CR - 1) // CR
    low = jnp.minimum(low, (3 * rows - number * CR) // 16)
    meta = jnp.stack([low, number]).astype(jnp.int32)
    return same, rowtab, edge, segk, segq, meta, onehot[:rows]


def on_device(
    nt,
    nf,
    latent,
    condition,
    lengths,
    cotangent,
    conv_weight,
    conv_moment,
    conv_second,
    proj_weight,
    proj_moment,
    proj_second,
    mlp_weight,
    mlp_moment,
    mlp_second,
    emb_weight,
    emb_moment,
    emb_second,
    small_weight,
    small_moment,
    small_second,
):
    masters = (conv_weight, proj_weight, mlp_weight, emb_weight, small_weight)
    nsmall, width = small_weight.shape
    t = lax.axis_index("tm")
    f = lax.axis_index("freq")
    lane_share = jnp.arange(C, dtype=jnp.int32)[None, :] // width
    wsmall = jnp.where(lane_share == f, jnp.tile(small_weight, (1, nf)), 0.0)
    wsmall = jnp.pad(wsmall, ((0, 32 - nsmall), (0, 0)))
    spot = t * nf + snake(f, t, nf)
    rows = latent.shape[0] // nf
    same, rowtab, edge, segk, segq, meta, onehot = layout_of(lengths, spot, nt * nf, rows)
    cond_low = jax.nn.silu(condition).astype(BF)
    (
        conv_full,
        proj_full,
        mlp_full,
        vec,
        cot,
        zhat1,
        zhat2,
        zhat3,
        rstd1,
        rstd2,
        rstd3,
        resid,
        inner,
        query,
        kext,
        vext,
        inext,
    ) = front(
        nt,
        nf,
        latent.reshape(-1, C),
        cotangent.reshape(-1, C),
        conv_weight,
        proj_weight,
        mlp_weight,
        emb_weight,
        wsmall,
        cond_low,
        onehot,
        same,
        rowtab,
        edge,
    )
    mixed, mixed_t, lse = attend(meta, query, kext, vext, segq, segk)
    out_blocks, gafter, gmix, pack_a, mid_sums = middle(
        nf, inner, mixed, resid, cot, proj_full, mlp_full, vec
    )
    dq, dk, dv = attend_back(
        meta, query, kext, vext, segq, segk, gmix, mixed_t, lse
    )
    output, glat, sum_a, sum_b, sum_c, sum_d, sum_e = back(
        nt,
        nf,
        dq,
        dk,
        dv,
        gafter,
        inext,
        zhat1,
        zhat2,
        zhat3,
        rstd1,
        rstd2,
        rstd3,
        cot,
        conv_full,
        proj_full,
        vec,
        same,
        rowtab,
        edge,
        cond_low,
        onehot,
        mid_sums,
        pack_a,
        out_blocks,
    )
    cdepth, pdepth, mdepth, edepth = (
        conv_weight.shape[1],
        proj_weight.shape[1],
        mlp_weight.shape[1],
        emb_weight.shape[0],
    )
    grad_conv = jnp.stack([sum_d[:cdepth], sum_c[:cdepth]])
    first_four = sum_b[: 4 * pdepth].reshape(4, pdepth, C)
    last_two = sum_a[2 * mdepth :].reshape(2, pdepth, C)
    grad_small = lax.dynamic_slice(sum_e, (edepth, f * width), (nsmall, width))
    shares = [
        grad_conv.astype(F32),
        jnp.concatenate([first_four, last_two], axis=0).astype(F32),
        sum_a[: 2 * mdepth].reshape(2, mdepth, C).astype(F32),
        sum_e[:edepth].astype(F32),
        grad_small.astype(F32),
    ]
    moments = (conv_moment, proj_moment, mlp_moment, emb_moment, small_moment)
    seconds = (conv_second, proj_second, mlp_second, emb_second, small_second)
    decays = (weight_decay, weight_decay, weight_decay, weight_decay, 0.0)
    updated = []
    for position in range(5):
        updated.extend(
            adamw_step(
                masters[position],
                moments[position],
                seconds[position],
                shares[position],
                decays[position],
            )
        )
    bias_share = shares[4][nsmall - 1]
    return (
        output.reshape(latent.shape),
        glat.reshape(latent.shape),
        *updated,
        bias_share,
    )


def solution(mesh):
    nt, nf = mesh.shape["tm"], mesh.shape["freq"]
    rows_spec = P("tm", "freq", None)
    middle_spec = P(None, "freq", None)
    params = (middle_spec,) * 9 + (P("freq", None),) * 3 + (P(None, "freq"),) * 3
    return jax.shard_map(
        partial(on_device, nt, nf),
        mesh=mesh,
        in_specs=(rows_spec, P(), P(), rows_spec) + params,
        out_specs=(rows_spec, rows_spec) + params + (P("freq"),),
        check_vma=False,
    )
```

```python
from functools import partial

import jax
import jax.numpy as jnp
from jax import lax
from jax.experimental import pallas as pl
from jax.experimental.pallas import tpu as pltpu
from jax.sharding import PartitionSpec as P

C = 256
G = 32
GW = C // G
HD = 32
H = C // HD
FF = 1024
F = 8
MAXLEN = 128
STEP = 10
TAPS = 9
CH = 256
CR = CH // F

HIGHEST = lax.Precision.HIGHEST
norm_eps = 1e-05
beta_first = 0.9
beta_second = 0.999
learn_rate = 0.5
weight_decay = 0.01
adam_eps = 1e-08
masked_score = -1e30
score_scale = HD**-0.5
LOG2E = 1.4426950408889634
MESH = pltpu.DeviceIdType.MESH if hasattr(pltpu, "DeviceIdType") else pl.DeviceIdType.MESH
VMEM_LIMIT = 64 * 1024 * 1024 - 65536
BF = jnp.bfloat16
F32 = jnp.float32


def mm(a, b):
    return jnp.dot(a, b, preferred_element_type=F32)


def mm_nt(a, b):
    return lax.dot_general(a, b, (((1,), (1,)), ((), ())), preferred_element_type=F32)


def mm_tn(a, b):
    return lax.dot_general(a, b, (((0,), (0,)), ((), ())), preferred_element_type=F32)


def hdot(a, b):
    return jnp.dot(a, b, precision=HIGHEST, preferred_element_type=F32)


def thirds(x):
    high = x.astype(BF)
    rest = x - high.astype(F32)
    middle = rest.astype(BF)
    low = (rest - middle.astype(F32)).astype(BF)
    return high, middle, low


def hdot_tn(a, b):
    return lax.dot_general(
        a, b, (((0,), (0,)), ((), ())), precision=HIGHEST, preferred_element_type=F32
    )


def place(nt, nf):
    t = lax.axis_index("tm")
    f = lax.axis_index("freq")
    odd = lax.rem(t, 2)
    s = f + odd * (nf - 1 - 2 * f)
    turn = 1 - 2 * odd
    at_end = (s + 1) // nf
    at_start = 1 - (s + nf - 1) // nf
    right = {"tm": t + at_end, "freq": f + (1 - at_end) * turn}
    left = {"tm": t - at_start, "freq": f - (1 - at_start) * turn}
    return t * nf + s, left, right


def flip(x, bit):
    return x + bit - 2 * bit * lax.rem(x // bit, 2)


def flip_by(x, mask):
    bit = 1
    while bit <= mask:
        if mask & bit:
            x = flip(x, bit)
        bit *= 2
    return x


def bits_of(count):
    bits = []
    bit = 1
    while bit < count:
        bits.append(bit)
        bit *= 2
    return bits


def snake(f, t, nf):
    return f + lax.rem(t, 2) * (nf - 1 - 2 * f)


def enter(spot, count, left, right, partners):
    barrier = pltpu.get_barrier_semaphore()
    for partner in partners:
        pl.semaphore_signal(barrier, inc=1, device_id=partner, device_id_type=MESH)

    @pl.when(spot > 0)
    def _():
        pl.semaphore_signal(barrier, inc=1, device_id=left, device_id_type=MESH)

    @pl.when(spot < count - 1)
    def _():
        pl.semaphore_signal(barrier, inc=1, device_id=right, device_id_type=MESH)

    inside = (spot > 0) & (spot < count - 1)

    @pl.when(inside)
    def _():
        pl.semaphore_wait(barrier, len(partners) + 2)

    @pl.when(jnp.logical_not(inside))
    def _():
        pl.semaphore_wait(barrier, len(partners) + 1)


class Swap:
    def __init__(self, where, to_left, to_right, from_left, from_right, sems):
        self.spot, self.count, left, right = where
        self.go_left = pltpu.make_async_remote_copy(
            src_ref=to_left,
            dst_ref=from_right,
            send_sem=sems.at[0],
            recv_sem=sems.at[1],
            device_id=left,
            device_id_type=MESH,
        )
        self.go_right = pltpu.make_async_remote_copy(
            src_ref=to_right,
            dst_ref=from_left,
            send_sem=sems.at[2],
            recv_sem=sems.at[3],
            device_id=right,
            device_id_type=MESH,
        )

    def start(self):
        @pl.when(self.spot > 0)
        def _():
            self.go_left.start()

        @pl.when(self.spot < self.count - 1)
        def _():
            self.go_right.start()

    def wait(self):
        @pl.when(self.spot > 0)
        def _():
            self.go_left.wait_send()
            self.go_right.wait_recv()

        @pl.when(self.spot < self.count - 1)
        def _():
            self.go_right.wait_send()
            self.go_left.wait_recv()


def remote(src, dst, sems, device):
    return pltpu.make_async_remote_copy(
        src_ref=src,
        dst_ref=dst,
        send_sem=sems.at[0],
        recv_sem=sems.at[1],
        device_id=device,
        device_id_type=MESH,
    )


class Exchange:
    def __init__(self, source, target, own_source, own_target, f, nf, sems):
        self.copies = []
        for mask in range(1, nf):
            peer = flip_by(f, mask)
            self.copies.append(
                remote(source(peer), target(peer), sems.at[mask - 1], {"freq": peer})
            )
        self.own_source, self.own_target = own_source, own_target

    def start(self):
        for copy in self.copies[::-1]:
            copy.start()
        self.own_target[...] = self.own_source[...]

    def wait(self):
        for copy in self.copies:
            copy.wait()


class Gather:
    def __init__(self, view, f, t, sems, size=None):
        near = {"freq": flip(f, 1)}
        far = flip(f, 2)
        self.halves = size is not None
        if self.halves:
            side = lax.rem(t, 2)
            mine, other = (side, size // 2), (1 - side, size // 2)
        else:
            mine = (0, None)
        beside = {"tm": flip(t, 1)}
        self.far = remote(view(f, mine), view(f, mine), sems.at[0], {"freq": far})
        self.near = remote(view(f, (0, None)), view(f, (0, None)), sems.at[1], near)
        self.forward = remote(view(far, mine), view(far, mine), sems.at[2], near)
        if self.halves:
            self.cross = remote(view(far, mine), view(far, mine), sems.at[3], beside)
            self.second = remote(view(far, other), view(far, other), sems.at[4], near)

    def start(self):
        self.far.start()
        self.near.start()

    def relay(self):
        self.far.wait_recv()
        if self.halves:
            self.cross.start()
        self.forward.start()

    def collect(self):
        if self.halves:
            self.cross.wait_recv()
            self.second.start()
        self.near.wait_recv()
        self.forward.wait_recv()
        if self.halves:
            self.second.wait_recv()

    def finish(self):
        self.far.wait_send()
        self.near.wait_send()
        self.forward.wait_send()
        if self.halves:
            self.cross.wait_send()
            self.second.wait_send()


def share_view(ref, depth, lead):
    def view(i, part):
        which, size = part
        start = i * depth if size is None else i * depth + which * size
        rows = rows_at(start, depth if size is None else size)
        return ref.at[lead, rows] if lead is not None else ref.at[rows]

    return view


def rows_at(start, size):
    return pl.ds(pl.multiple_of(start, 16), size)


def piece_of(n):
    for size in (128, 96, 80, 64, 48, 32):
        if n % size == 0:
            return size
    return 16


def add_rows(dst, to, a, a_at, b, b_at, n):
    size = piece_of(n)

    def step(i):
        left = a[rows_at(a_at + i * size, size)].astype(F32)
        right = b[rows_at(b_at + i * size, size)].astype(F32)
        dst[rows_at(to + i * size, size)] = (left + right).astype(BF)

    loop(n // size, step)


class Reduce:
    def __init__(self, order, pack, got, acc, far, rs, out, sems, t, f):
        u = far.shape[0]
        near = {"freq": flip(f, 1)}
        one = remote(pack(flip_by(f, 1)), got.at[0], sems.at[0], near)
        two = remote(pack(flip_by(f, 3)), got.at[1], sems.at[1], near)

        def add_near():
            add_rows(acc.at[1], 0, pack(flip(f, 2)), 0, got.at[1], 0, u)
            add_rows(acc.at[0], 0, pack(f), 0, got.at[0], 0, u)

        self.stages = [((two, one), add_near)]
        gathers = []
        n, at, base, place_at = u, 0, 0, 2
        slots = 2
        for bit in order:
            last = bit == order[-1]
            if bit == 0:
                rows = rows_at(at, n)
                copy = remote(
                    acc.at[1, rows], far.at[0:n], sems.at[place_at], {"freq": flip(f, 2)}
                )
                finish = partial(add_rows, acc.at[0], at, acc.at[0], at, far, 0, n)
                self.stages.append(((copy,), finish))
                slots, place_at = 1, place_at + 1
                continue
            peer = {"tm": flip(t, bit)}
            half = n % 32 == 0 and not last
            if half:
                upper = lax.rem(t // bit, 2)
                n = n // 2
                keep, give = at + upper * n, at + (1 - upper) * n
            else:
                keep, give = at, at
            copy = remote(
                acc.at[0:slots, rows_at(give, n)],
                rs.at[0:slots, base : base + n],
                sems.at[place_at],
                peer,
            )

            def finish(slots=slots, keep=keep, base=base, n=n, last=last):
                for slot in range(slots):
                    target = out if last else acc.at[slot]
                    add_rows(target, keep, acc.at[slot], keep, rs.at[slot], base, n)

            self.stages.append(((copy,), finish))
            if half:
                share = out.at[rows_at(keep, n)]
                gathers.append(((remote(share, share, sems.at[place_at + 1], peer),), None))
            at, base, place_at = keep, base + n, place_at + 2
        self.stages.extend(gathers[::-1])
        self.now = -1

    def done(self):
        return self.now >= len(self.stages)

    def advance(self):
        if self.done():
            return
        if self.now >= 0:
            copies, finish = self.stages[self.now]
            for copy in copies:
                copy.wait()
            if finish is not None:
                finish()
        self.now += 1
        if not self.done():
            for copy in self.stages[self.now][0]:
                copy.start()


def orders_of(nt):
    bits = bits_of(nt)
    far_first = [0] + bits
    if len(bits) < 2:
        return far_first, far_first
    return far_first, [bits[1], 0, bits[0]] + bits[2:]


def stage_count(nt):
    return 3 + 2 * len(bits_of(nt))


def padded(rows):
    return (rows + 63) // 64 * 64


def chunk_order(nf):
    width = F // nf
    row = lax.broadcasted_iota(jnp.int32, (CH, CH), 0)
    source = lax.broadcasted_iota(jnp.int32, (CH, CH), 1)
    col = lax.rem(row, F)
    wanted = (col // width) * (CR * width) + (row // F) * width + lax.rem(col, width)
    return jnp.where(source == wanted, 1.0, 0.0).astype(BF)


def clear_ends(spot, count, from_left, from_right):
    @pl.when(spot == 0)
    def _():
        from_left[...] = jnp.zeros_like(from_left)

    @pl.when(spot == count - 1)
    def _():
        from_right[...] = jnp.zeros_like(from_right)


def group_matrix():
    i = lax.broadcasted_iota(jnp.int32, (C, C), 0) // GW
    j = lax.broadcasted_iota(jnp.int32, (C, C), 1) // GW
    return (i == j).astype(BF)


def spread(rows, count):
    return jnp.broadcast_to(rows[:, None, :], (count, F, C))


def column_index(count):
    return lax.broadcasted_iota(jnp.int32, (count, F, C), 1)


def column_shifts(act, count):
    col = column_index(count)
    before = jnp.where(col == 0, 0.0, pltpu.roll(act, 1, 1))
    after = jnp.where(col == F - 1, 0.0, pltpu.roll(act, F - 1, 1))
    return before, after


def store_shifts(xc, at, act, count):
    before, after = column_shifts(act, count)
    size = count * F
    xc[pl.ds(at, size), 0:C] = before.reshape(size, C).astype(BF)
    xc[pl.ds(at, size), C : 2 * C] = act.reshape(size, C).astype(BF)
    xc[pl.ds(at, size), 2 * C : 3 * C] = after.reshape(size, C).astype(BF)


def loop(count, body):
    def step(i, carry):
        body(i)
        return carry

    lax.fori_loop(0, count, step, 0)


def chunk_at(i, size=CH):
    return pl.multiple_of(i * size, size)


class Clip:
    def __init__(self, same, rowtab, gmat, local):
        self.same, self.rowtab, self.gmat, self.local = same, rowtab, gmat, local

    def pack(self, rs, rq, to_left, to_right):
        tab = self.rowtab.shape[0]
        for index, table in ((0, rs), (1, rq)):
            total = 0.0
            for part in thirds(table[...])[::-1]:
                total = total + mm(self.same[...], part)
            self.local[index] = total[0:tab]
            to_left[index : index + 1] = total[tab : tab + 1]
            to_right[index : index + 1] = total[tab + 1 : tab + 2]

    def means(self, rs, rq, gain, from_left, from_right):
        at_left = self.rowtab[:, 1:2] > 0.0
        at_right = self.rowtab[:, 2:3] > 0.0
        inverse = self.rowtab[:, 0:1]
        tab = self.rowtab.shape[0]
        parts = []
        for index in range(2):
            total = self.local[index]
            total = total + jnp.where(at_left, from_left[index : index + 1], 0.0)
            total = total + jnp.where(at_right, from_right[index : index + 1], 0.0)
            total = total * inverse
            if gain is not None:
                total = total * gain
            parts.append(thirds(total))
        results = []
        for high, middle, low in parts:
            value = mm(low, self.gmat[...]) + mm(middle, self.gmat[...])
            results.append(value + mm(high, self.gmat[...]))
        return results


def row_masks(rowtab, prev_mask, next_mask, rows):
    prev_mask[...] = jnp.broadcast_to(rowtab[0:rows, 3:4], (rows, C))
    next_mask[...] = jnp.broadcast_to(rowtab[0:rows, 4:5], (rows, C))


def front_kernel(
    nt,
    nf,
    lat_local,
    cot_local,
    wconv,
    wproj,
    wmlp,
    wemb,
    wsmall,
    cond,
    onehot,
    same,
    rowtab,
    conv,
    proj,
    mlp,
    vec,
    cot,
    zhat1,
    zhat2,
    zhat3,
    rstd1,
    rstd2,
    rstd3,
    resid,
    inner,
    query,
    kext,
    vext,
    inext,
    gmat,
    own_sums,
    rs,
    rq,
    mean,
    prev_mask,
    next_mask,
    xc,
    z_prev,
    z_here,
    z_next,
    hidden,
    to_left,
    to_right,
    from_left,
    from_right,
    emb,
    small,
    lat,
    lat_in,
    cot_in,
    order,
    film,
    msg_sems,
    kv_sems,
    block_sems,
    gather_sems,
):
    px = lat.shape[0]
    rows = px // F
    chunks = px // CH
    blk = px // nf
    seg = CH // nf
    spot, left, right = place(nt, nf)
    count = nt * nf
    where = (spot, count, left, right)
    f = lax.axis_index("freq")
    t = lax.axis_index("tm")
    s = snake(f, t, nf)
    partners = [{"freq": flip_by(f, mask)} for mask in range(1, nf)] + [{"tm": flip(t, 1)}]
    enter(spot, count, left, right, partners)
    blocks = []
    for index, (local, landed) in enumerate(((lat_local, lat_in), (cot_local, cot_in))):
        blocks.append(
            Exchange(
                lambda peer, local=local: local.at[rows_at(snake(peer, t, nf) * blk, blk)],
                lambda peer, landed=landed: landed.at[f],
                local.at[rows_at(s * blk, blk)],
                landed.at[f],
                f,
                nf,
                block_sems.at[index],
            )
        )
    blocks[0].start()

    def cast(src, dst, base):
        size = 32 if src.shape[0] % 64 else 64

        def step(i):
            dst[rows_at(base + i * size, size)] = src[rows_at(i * size, size)].astype(BF)

        loop(src.shape[0] // size, step)

    cdepth, pdepth, mdepth, edepth = (
        wconv.shape[1],
        wproj.shape[1],
        wmlp.shape[1],
        wemb.shape[0],
    )
    views = (
        (share_view(conv, cdepth, 0), cdepth),
        (share_view(conv, cdepth, 1), cdepth),
        (share_view(proj, pdepth, slice(None)), pdepth),
        (share_view(mlp, mdepth, slice(None)), mdepth),
        (share_view(emb, edepth, None), edepth),
        (share_view(small, wsmall.shape[0], None), None),
    )
    gathers = []
    for i, (view, size) in enumerate(views):
        gathers.append(Gather(view, f, t, gather_sems.at[i], size))
    get_first, get_second, get_proj, get_mlp, get_emb, get_small = gathers
    cast(wsmall, small, f * wsmall.shape[0])
    cast(wconv.at[0], conv.at[0], f * cdepth)
    get_small.start()
    get_first.start()
    cast(wemb, emb, f * edepth)
    cast(wconv.at[1], conv.at[1], f * cdepth)
    for i in range(wproj.shape[0]):
        cast(wproj.at[i], proj.at[i], f * pdepth)
    for i in range(wmlp.shape[0]):
        cast(wmlp.at[i], mlp.at[i], f * mdepth)
    order[...] = chunk_order(nf)

    def arrange(landed, target):
        def step(c):
            parts = [landed[k, rows_at(c * seg, seg)] for k in range(nf)]
            moved = mm(order[...], jnp.concatenate(parts, axis=0))
            target[pl.ds(chunk_at(c), CH)] = moved.astype(BF)

        loop(chunks, step)

    clear_ends(spot, count, from_left, from_right)

    @pl.when(spot == 0)
    def _():
        inext[0:px] = jnp.zeros((px, C), BF)

    @pl.when(spot == count - 1)
    def _():
        inext[2 * px : 3 * px] = jnp.zeros((px, C), BF)

    gmat[...] = group_matrix()
    row_masks(rowtab, prev_mask, next_mask, rows)
    clip = Clip(same, rowtab, gmat, own_sums)

    def v(i):
        return vec[i : i + 1]

    def norm_stage(step, load, zhat, rstd, rim, beside):
        def sums(c):
            x3 = load(c).reshape(CR, F, C)
            rs[pl.ds(chunk_at(c, CR), CR)] = jnp.sum(x3, axis=1)
            rq[pl.ds(chunk_at(c, CR), CR)] = jnp.sum(x3 * x3, axis=1)

        loop(chunks, sums)
        clip.pack(rs, rq, to_left.at[step], to_right.at[step])
        first, last = rim()
        to_left[step, 8:16] = first
        to_right[step, 8:16] = last
        swap = Swap(
            where,
            to_left.at[step],
            to_right.at[step],
            from_left.at[step],
            from_right.at[step],
            msg_sems.at[step],
        )
        swap.start()
        beside()
        swap.wait()
        mean_rows, square_rows = clip.means(rs, rq, None, from_left.at[step], from_right.at[step])
        mean[...] = mean_rows
        rstd[...] = lax.rsqrt(square_rows - mean_rows * mean_rows + norm_eps)
        rim_raw = jnp.concatenate([from_left[step, 8:16], from_right[step, 8:16]], axis=0)
        rim3 = rim_raw.reshape(2, F, C)
        rim_hat = (rim3 - spread(mean[rows : rows + 2], 2)) * spread(rstd[rows : rows + 2], 2)
        if zhat.shape[0] > px:
            zhat[px : px + 16] = rim_hat.reshape(16, C)
        return rim_hat

    def normed(load, zhat, rstd, c):
        r0 = chunk_at(c, CR)
        x3 = load(c).reshape(CR, F, C)
        hat = (x3 - spread(mean[pl.ds(r0, CR)], CR)) * spread(rstd[pl.ds(r0, CR)], CR)
        zhat[pl.ds(chunk_at(c), CH)] = hat.reshape(CH, C)
        return hat

    def conv_stage(rim_hat, load, zhat, rstd, gain, shift, kernel, ready, finish):
        pre = rim_hat * gain + shift
        store_shifts(xc, px, (pre * jax.nn.sigmoid(pre)).astype(BF).astype(F32), 2)

        def build(c):
            pre = normed(load, zhat, rstd, c) * gain + shift
            act = (pre * jax.nn.sigmoid(pre)).astype(BF).astype(F32)
            store_shifts(xc, chunk_at(c), act, CR)

        loop(chunks, build)
        ready()

        def product(c):
            p0 = chunk_at(c)
            part = xc[pl.ds(p0, CH)]
            z_prev[pl.ds(pl.multiple_of(p0 + 8, 8), CH)] = mm(part, kernel[0 : 3 * C])
            z_here[pl.ds(p0, CH)] = mm(part, kernel[3 * C : 6 * C])
            z_next[pl.ds(p0, CH)] = mm(part, kernel[6 * C : 9 * C])

        loop(chunks, product)
        part = xc[px : px + 16]
        z_prev[0:8] = mm(part, kernel[0 : 3 * C])[0:8]
        z_next[px : px + 8] = mm(part, kernel[6 * C : 9 * C])[8:16]

        def join(c):
            p0 = chunk_at(c)
            r0 = chunk_at(c, CR)
            keep_prev = spread(prev_mask[pl.ds(r0, CR)], CR) > 0.0
            keep_next = spread(next_mask[pl.ds(r0, CR)], CR) > 0.0
            out = z_here[pl.ds(p0, CH)].reshape(CR, F, C)
            out = out + jnp.where(keep_prev, z_prev[pl.ds(p0, CH)].reshape(CR, F, C), 0.0)
            after = z_next[pl.ds(pl.multiple_of(p0 + 8, 8), CH)].reshape(CR, F, C)
            finish(c, out + jnp.where(keep_next, after, 0.0))

        loop(chunks, join)

    def load_latent(c):
        return lat[pl.ds(chunk_at(c), CH)].astype(F32)

    def load_hidden(c):
        return hidden[pl.ds(chunk_at(c), CH)]

    def load_resid(c):
        return resid[pl.ds(chunk_at(c), CH)]

    def send_second():
        get_emb.start()
        get_second.start()
        blocks[1].start()
        get_small.relay()
        get_small.collect()
        total = small[0 : wsmall.shape[0]].astype(F32)
        for k in range(1, nf):
            at = k * wsmall.shape[0]
            total = total + small[at : at + wsmall.shape[0]].astype(F32)
        vec[...] = total

    blocks[0].wait()
    arrange(lat_in, lat)
    rim_hat = norm_stage(
        0,
        load_latent,
        zhat1,
        rstd1,
        lambda: (lat[0:16].astype(F32)[0:8], lat[px - 16 : px].astype(F32)[8:16]),
        send_second,
    )

    def ready_first():
        get_first.relay()
        get_emb.relay()
        get_second.relay()
        get_first.collect()
        get_emb.collect()
        table = mm(cond[...], emb[...]) + v(3)
        film[...] = hdot(onehot[...], table)

    def finish_one(c, out):
        r0 = chunk_at(c, CR)
        out = out + v(2) + spread(film[pl.ds(r0, CR)], CR)
        hidden[pl.ds(chunk_at(c), CH)] = out.reshape(CH, C)

    conv_stage(rim_hat, load_latent, zhat1, rstd1, v(0), v(1), conv.at[0], ready_first, finish_one)

    def send_proj():
        get_proj.start()
        get_mlp.start()
        blocks[1].wait()
        arrange(cot_in, cot)

    def ready_second():
        get_second.collect()
        get_proj.relay()
        get_mlp.relay()

    rim_hat = norm_stage(
        1, load_hidden, zhat2, rstd2, lambda: (hidden[0:8], hidden[px - 8 : px]), send_proj
    )

    def finish_two(c, out):
        p0 = chunk_at(c)
        total = lat[pl.ds(p0, CH)].astype(F32) + out.reshape(CH, C) + v(6)
        resid[pl.ds(p0, CH)] = total

    conv_stage(rim_hat, load_hidden, zhat2, rstd2, v(4), v(5), conv.at[1], ready_second, finish_two)

    def ready_proj():
        get_proj.collect()
        get_mlp.collect()

    norm_stage(
        2, load_resid, zhat3, rstd3, lambda: (resid[0:8], resid[px - 8 : px]), ready_proj
    )

    def project(c):
        p0 = chunk_at(c)
        hat = normed(load_resid, zhat3, rstd3, c).reshape(CH, C)
        low = (hat * v(7) + v(8)).astype(BF)
        value = mm(low, proj[0]) + v(9)
        inner[pl.ds(p0, CH)] = value
        inext[pl.ds(pl.multiple_of(px + p0, CH), CH)] = value.astype(BF)

    loop(chunks, project)
    swap = Swap(
        where,
        inext.at[px : 2 * px],
        inext.at[px : 2 * px],
        inext.at[0:px],
        inext.at[2 * px : 3 * px],
        kv_sems.at[0],
    )
    swap.start()

    def keys_values(part):
        low = inext[part]
        kext[part] = mm(low, proj[2]).astype(BF)
        vext[part] = mm(low, proj[3]).astype(BF)

    def heads(c):
        part = pl.ds(pl.multiple_of(px + chunk_at(c), CH), CH)
        query[pl.ds(chunk_at(c), CH)] = mm(inext[part], proj[1]).astype(BF)
        keys_values(part)

    loop(chunks, heads)
    swap.wait()

    def rims(c):
        keys_values(pl.ds(chunk_at(c), CH))
        keys_values(pl.ds(pl.multiple_of(2 * px + chunk_at(c), CH), CH))

    loop(chunks, rims)
    for gather in gathers:
        gather.finish()


def vmem(count):
    return [pl.BlockSpec(memory_space=pltpu.VMEM)] * count


def front(nt, nf, lat, cot, wconv, wproj, wmlp, wemb, wsmall, cond, onehot, same, rowtab):
    px = lat.shape[0]
    rows = px // F
    tab = rowtab.shape[0]

    def whole(share, axis):
        shape = list(share.shape)
        shape[axis] *= nf
        return tuple(shape)

    shapes = (
        (whole(wconv, 1), BF),
        (whole(wproj, 1), BF),
        (whole(wmlp, 1), BF),
        (wsmall.shape, F32),
        ((px, C), BF),
        ((px, C), F32),
        ((px + 16, C), F32),
        ((px + 16, C), F32),
        ((tab, C), F32),
        ((tab, C), F32),
        ((tab, C), F32),
        ((px, C), F32),
        ((px, C), F32),
        ((px, C), BF),
        ((3 * px, C), BF),
        ((3 * px, C), BF),
        ((3 * px, C), BF),
    )
    return pl.pallas_call(
        partial(front_kernel, nt, nf),
        out_shape=[jax.ShapeDtypeStruct(s, d) for s, d in shapes],
        in_specs=vmem(11),
        out_specs=vmem(len(shapes)),
        scratch_shapes=[
            pltpu.VMEM((C, C), BF),
            pltpu.VMEM((2, tab, C), F32),
            pltpu.VMEM((rows, C), F32),
            pltpu.VMEM((rows, C), F32),
            pltpu.VMEM((tab, C), F32),
            pltpu.VMEM((rows, C), F32),
            pltpu.VMEM((rows, C), F32),
            pltpu.VMEM((px + 16, 3 * C), BF),
            pltpu.VMEM((px + 16, C), F32),
            pltpu.VMEM((px, C), F32),
            pltpu.VMEM((px + 16, C), F32),
            pltpu.VMEM((px, C), F32),
            pltpu.VMEM((3, 16, C), F32),
            pltpu.VMEM((3, 16, C), F32),
            pltpu.VMEM((3, 16, C), F32),
            pltpu.VMEM((3, 16, C), F32),
            pltpu.VMEM(whole(wemb, 0), BF),
            pltpu.VMEM((nf * wsmall.shape[0], C), BF),
            pltpu.VMEM((px, C), BF),
            pltpu.VMEM((nf, px // nf, C), BF),
            pltpu.VMEM((nf, px // nf, C), BF),
            pltpu.VMEM((CH, CH), BF),
            pltpu.VMEM((rows, C), F32),
            pltpu.SemaphoreType.DMA((3, 4)),
            pltpu.SemaphoreType.DMA((2, 4)),
            pltpu.SemaphoreType.DMA((2, nf - 1, 2)),
            pltpu.SemaphoreType.DMA((6, 5, 2)),
        ],
        compiler_params=pltpu.CompilerParams(
            collective_id=1, has_side_effects=True, vmem_limit_bytes=VMEM_LIMIT
        ),
        name="front",
    )(lat, cot, wconv, wproj, wmlp, wemb, wsmall, cond, onehot, same, rowtab)


def head_mask(h):
    lane = lax.broadcasted_iota(jnp.int32, (CH, C), 1)
    return (lane >= h * HD) & (lane < (h + 1) * HD)


def head_rows(h):
    return slice(h * HD, (h + 1) * HD)


def turned(block):
    return block.astype(F32).T


def score_bias(segk, segq, key_row, q0):
    keys = jnp.broadcast_to(segk[pl.ds(key_row, CR), 0:1], (CR, C))
    keys = spread(keys, CR).reshape(CH, C)
    return jnp.where(keys == segq[0:1, pl.ds(q0, CH)], 0.0, masked_score)


def attend_kernel(meta, query, kext, vext, segq, segk, mixed, mixed_t, lse, vt, qm, bias, top, tot, acc, scores, peak):
    px = query.shape[0]
    factor = score_scale * LOG2E

    def turn(i):
        k0 = chunk_at(i)
        vt[:, pl.ds(k0, CH)] = turned(vext[pl.ds(k0, CH)]).astype(BF)

    loop(vext.shape[0] // CH, turn)

    def tile(t):
        q0 = chunk_at(t)
        block = query[pl.ds(q0, CH)].astype(F32)
        for h in range(H):
            qm[h] = jnp.where(head_mask(h), block, 0.0).astype(BF)
        top[...] = jnp.full((H, CH), masked_score, F32)
        tot[...] = jnp.zeros((H, CH), F32)
        acc[...] = jnp.zeros((C, CH), F32)

        def keys(i):
            row = meta[t, 0] * 16 + i * CR
            base = pl.multiple_of(row * F, 128)
            bias[...] = score_bias(segk, segq, pl.multiple_of(row, 16), q0)
            key = kext[pl.ds(base, CH)]
            for h in range(H):
                raw = mm_nt(key, qm[h]) + bias[...]
                scores[h] = raw
                peak[h : h + 1] = jnp.maximum(top[h : h + 1], jnp.max(raw, axis=0, keepdims=True))
            for h in range(H):
                new = peak[h : h + 1]
                fade = jnp.exp2((top[h : h + 1] - new) * factor)
                weight = jnp.exp2((scores[h] - new) * factor)
                top[h : h + 1] = new
                tot[h : h + 1] = tot[h : h + 1] * fade + jnp.sum(weight, axis=0, keepdims=True)
                part = mm(vt[head_rows(h), pl.ds(base, CH)], weight.astype(BF))
                acc[head_rows(h)] = acc[head_rows(h)] * fade + part

        loop(meta[t, 1], keys)
        for h in range(H):
            acc[head_rows(h)] = acc[head_rows(h)] / tot[h : h + 1]
        lse[:, pl.ds(q0, CH)] = top[...] * factor + jnp.log2(tot[...])
        mixed_t[:, pl.ds(q0, CH)] = acc[...].astype(BF)
        mixed[pl.ds(q0, CH)] = acc[...].T.astype(BF)

    loop(px // CH, tile)


def attend(meta, query, kext, vext, segq, segk):
    px = query.shape[0]
    ext = kext.shape[0]
    return pl.pallas_call(
        attend_kernel,
        out_shape=[
            jax.ShapeDtypeStruct((px, C), BF),
            jax.ShapeDtypeStruct((C, px), BF),
            jax.ShapeDtypeStruct((H, px), F32),
        ],
        in_specs=[pl.BlockSpec(memory_space=pltpu.SMEM)] + vmem(5),
        out_specs=vmem(3),
        scratch_shapes=[
            pltpu.VMEM((C, ext), BF),
            pltpu.VMEM((H, CH, C), BF),
            pltpu.VMEM((CH, CH), F32),
            pltpu.VMEM((H, CH), F32),
            pltpu.VMEM((H, CH), F32),
            pltpu.VMEM((C, CH), F32),
            pltpu.VMEM((H, CH, CH), F32),
            pltpu.VMEM((H, CH), F32),
        ],
        compiler_params=pltpu.CompilerParams(vmem_limit_bytes=VMEM_LIMIT),
        name="attend",
    )(meta, query, kext, vext, segq, segk)


def attend_back_kernel(
    meta,
    query,
    kext,
    vext,
    segq,
    segk,
    gmix,
    mixed_t,
    lse,
    dq,
    dk,
    dv,
    kt,
    qm,
    gm,
    qt,
    gt,
    inner_rows,
    bias,
    dqt,
    dkt,
    dvt,
    kept,
    gscores,
):
    px = query.shape[0]
    ext = kext.shape[0]
    factor = score_scale * LOG2E

    def turn(i):
        k0 = chunk_at(i)
        kt[:, pl.ds(k0, CH)] = turned(kext[pl.ds(k0, CH)]).astype(BF)
        dkt[:, pl.ds(k0, CH)] = jnp.zeros((C, CH), F32)
        dvt[:, pl.ds(k0, CH)] = jnp.zeros((C, CH), F32)

    loop(ext // CH, turn)

    def tile(t):
        q0 = chunk_at(t)
        block = query[pl.ds(q0, CH)].astype(F32)
        grad = gmix[pl.ds(q0, CH)].astype(F32)
        for h in range(H):
            qm[h] = jnp.where(head_mask(h), block, 0.0).astype(BF)
            gm[h] = jnp.where(head_mask(h), grad, 0.0).astype(BF)
        qt[...] = block.T.astype(BF)
        grad_t = grad.T
        gt[...] = grad_t.astype(BF)
        crossed = grad_t * mixed_t[:, pl.ds(q0, CH)].astype(F32)
        inner_rows[...] = jnp.sum(crossed.reshape(H, HD, CH), axis=1)
        dqt[...] = jnp.zeros((C, CH), F32)

        def keys(i):
            row = meta[t, 0] * 16 + i * CR
            base = pl.multiple_of(row * F, 128)
            bias[...] = score_bias(segk, segq, pl.multiple_of(row, 16), q0)
            key = kext[pl.ds(base, CH)]
            val = vext[pl.ds(base, CH)]
            for h in range(H):
                raw = mm_nt(key, qm[h]) + bias[...]
                probs = jnp.exp2(raw * factor - lse[h : h + 1, pl.ds(q0, CH)])
                gprob = mm_nt(val, gm[h])
                kept[h] = probs.astype(BF)
                gscores[h] = (probs * (gprob - inner_rows[h : h + 1])).astype(BF)
            for h in range(H):
                dvt[head_rows(h), pl.ds(base, CH)] += mm_nt(gt[head_rows(h)], kept[h])
                dkt[head_rows(h), pl.ds(base, CH)] += mm_nt(qt[head_rows(h)], gscores[h])
                dqt[head_rows(h)] += mm(kt[head_rows(h), pl.ds(base, CH)], gscores[h])

        loop(meta[t, 1], keys)
        dq[pl.ds(q0, CH)] = (dqt[...] * score_scale).T.astype(BF)

    loop(px // CH, tile)

    def settle(i):
        k0 = chunk_at(i)
        dk[pl.ds(k0, CH)] = (dkt[:, pl.ds(k0, CH)] * score_scale).T.astype(BF)
        dv[pl.ds(k0, CH)] = dvt[:, pl.ds(k0, CH)].T.astype(BF)

    loop(ext // CH, settle)


def attend_back(meta, query, kext, vext, segq, segk, gmix, mixed_t, lse):
    px = query.shape[0]
    ext = kext.shape[0]
    return pl.pallas_call(
        attend_back_kernel,
        out_shape=[
            jax.ShapeDtypeStruct((px, C), BF),
            jax.ShapeDtypeStruct((ext, C), BF),
            jax.ShapeDtypeStruct((ext, C), BF),
        ],
        in_specs=[pl.BlockSpec(memory_space=pltpu.SMEM)] + vmem(8),
        out_specs=vmem(3),
        scratch_shapes=[
            pltpu.VMEM((C, ext), BF),
            pltpu.VMEM((H, CH, C), BF),
            pltpu.VMEM((H, CH, C), BF),
            pltpu.VMEM((C, CH), BF),
            pltpu.VMEM((C, CH), BF),
            pltpu.VMEM((H, CH), F32),
            pltpu.VMEM((CH, CH), F32),
            pltpu.VMEM((C, CH), F32),
            pltpu.VMEM((C, ext), F32),
            pltpu.VMEM((C, ext), F32),
            pltpu.VMEM((H, CH, CH), BF),
            pltpu.VMEM((H, CH, CH), BF),
        ],
        compiler_params=pltpu.CompilerParams(vmem_limit_bytes=VMEM_LIMIT),
        name="attend_back",
    )(meta, query, kext, vext, segq, segk, gmix, mixed_t, lse)


def middle_kernel(
    nf,
    inner,
    mixed,
    resid,
    cot,
    proj,
    mlp,
    vec,
    output,
    gafter,
    gmix,
    pack,
    sums,
    after_low,
    act_low,
    pre_low,
    down_low,
    mlp_low,
    after_grad_low,
    ubias,
    order,
):
    px = inner.shape[0]
    seg = CH // nf
    tail = 11 + FF // C
    order[...] = chunk_order(nf)
    sums[...] = jnp.zeros_like(sums)
    for j in range(FF // C):
        ubias[:, j * C : (j + 1) * C] = vec[11 + j : 12 + j]

    def step(c):
        p0 = chunk_at(c)
        after = inner[pl.ds(p0, CH)] + mm(mixed[pl.ds(p0, CH)], proj[4]) + vec[10:11]
        low = after.astype(BF)
        after_low[pl.ds(p0, CH)] = low
        grad_out = cot[pl.ds(p0, CH)]
        grad_mlp = mm_nt(grad_out, proj[5])
        down = grad_mlp.astype(BF)
        down_low[pl.ds(p0, CH)] = down
        total = after
        grad_after = grad_mlp
        for j in range(FF // C):
            part = slice(j * C, (j + 1) * C)
            pre = mm_nt(low, mlp[0, part]) + ubias[:, part]
            cdf = 0.5 + 0.5 * lax.erf(pre * (0.5**0.5))
            act = (pre * cdf).astype(BF)
            act_low[pl.ds(p0, CH), part] = act
            total = total + mm(act, mlp[1, part])
            density = jnp.exp(pre * pre * -0.5) * 0.3989422804014327
            grad_pre = mm_nt(down, mlp[1, part]) * (cdf + pre * density)
            sums[3 + j : 4 + j] += jnp.sum(grad_pre, axis=0, keepdims=True)
            grad_low = grad_pre.astype(BF)
            pre_low[pl.ds(p0, CH), part] = grad_low
            grad_after = grad_after + mm(grad_low, mlp[0, part])
        total = (total + vec[tail : tail + 1]).astype(BF)
        mlp_low[pl.ds(p0, CH)] = total
        branch = mm(total, proj[5]) + vec[tail + 1 : tail + 2]
        moved = mm_tn(order[...], (resid[pl.ds(p0, CH)] + branch).astype(BF)).astype(BF)
        for k in range(nf):
            output[k, rows_at(c * seg, seg)] = moved[k * seg : (k + 1) * seg]
        gafter[pl.ds(p0, CH)] = grad_after
        grad_low = grad_after.astype(BF)
        after_grad_low[pl.ds(p0, CH)] = grad_low
        gmix[pl.ds(p0, CH)] = mm_nt(grad_low, proj[4]).astype(BF)
        sums[0:1] += jnp.sum(grad_out.astype(F32), axis=0, keepdims=True)
        sums[1:2] += jnp.sum(grad_mlp, axis=0, keepdims=True)
        sums[2:3] += jnp.sum(grad_after, axis=0, keepdims=True)

    loop(px // CH, step)
    width = FF // nf
    for k in range(nf):
        part = slice(k * width, (k + 1) * width)
        pack[k, 0:width] = mm_tn(pre_low[:, part], after_low[...]).astype(BF)
        pack[k, width : 2 * width] = mm_tn(act_low[:, part], down_low[...]).astype(BF)
    depth = C // nf
    gw_attn = mm_tn(mixed[...], after_grad_low[...]).astype(BF)
    gw_out = mm_tn(mlp_low[...], cot[...]).astype(BF)
    for k in range(nf):
        part = slice(k * depth, (k + 1) * depth)
        pack[k, 2 * width : 2 * width + depth] = gw_attn[part]
        pack[k, 2 * width + depth : 2 * width + 2 * depth] = gw_out[part]


def middle(nf, inner, mixed, resid, cot, proj, mlp, vec):
    px = inner.shape[0]
    return pl.pallas_call(
        partial(middle_kernel, nf),
        out_shape=[
            jax.ShapeDtypeStruct((nf, px // nf, C), BF),
            jax.ShapeDtypeStruct((px, C), F32),
            jax.ShapeDtypeStruct((px, C), BF),
            jax.ShapeDtypeStruct((nf, 2 * (FF + C) // nf, C), BF),
            jax.ShapeDtypeStruct((8, C), F32),
        ],
        in_specs=vmem(7),
        out_specs=vmem(5),
        scratch_shapes=[
            pltpu.VMEM((px, C), BF),
            pltpu.VMEM((px, FF), BF),
            pltpu.VMEM((px, FF), BF),
            pltpu.VMEM((px, C), BF),
            pltpu.VMEM((px, C), BF),
            pltpu.VMEM((px, C), BF),
            pltpu.VMEM((1, FF), F32),
            pltpu.VMEM((CH, CH), BF),
        ],
        compiler_params=pltpu.CompilerParams(vmem_limit_bytes=VMEM_LIMIT),
        name="middle",
    )(inner, mixed, resid, cot, proj, mlp, vec)


def back_kernel(
    nt,
    nf,
    dq,
    dk,
    dv,
    gafter,
    inext,
    zhat1,
    zhat2,
    zhat3,
    rstd1,
    rstd2,
    rstd3,
    cot,
    conv,
    proj,
    vec,
    same,
    rowtab,
    cond,
    onehot,
    mid_sums,
    pack_a,
    out_blocks,
    output,
    glat,
    out_a,
    out_b,
    out_c,
    out_d,
    out_e,
    sums,
    film_rows,
    gmat,
    own_sums,
    rs,
    rq,
    mean_e,
    mean_ez,
    prev_mask,
    next_mask,
    normed_low,
    grad_low,
    gresid,
    dgrad,
    two,
    xc,
    shifted,
    rim_out,
    rim_got,
    to_left,
    to_right,
    from_left,
    from_right,
    order,
    glat_blocks,
    *rest,
):
    pack_b, pack_c, pack_d, pack_e = rest[:4]
    pieces = rest[4:28]
    msg_sems, kv_sems, block_sems, reduce_sems = rest[28:32]
    px = dq.shape[0]
    rows = px // F
    chunks = px // CH
    blk = px // nf
    seg = CH // nf
    spot, left, right = place(nt, nf)
    count = nt * nf
    where = (spot, count, left, right)
    f = lax.axis_index("freq")
    t = lax.axis_index("tm")
    s = snake(f, t, nf)
    partners = [{"freq": flip_by(f, mask)} for mask in range(1, nf)]
    partners = partners + [{"tm": flip(t, bit)} for bit in bits_of(nt)]
    enter(spot, count, left, right, partners)
    far_first, far_later = orders_of(nt)
    whole_d = out_d.shape[0]
    half = padded(whole_d // 2)
    plans = (
        (far_later, lambda i: pack_a.at[i], out_a),
        (far_first, lambda i: pack_b.at[i], out_b),
        (far_later, lambda i: pack_c.at[i], out_c),
        (far_first, lambda i: pack_d.at[i, 0:half], out_d.at[0:half]),
        (far_later, lambda i: pack_d.at[i, half:whole_d], out_d.at[half:whole_d]),
        (far_first, lambda i: pack_e.at[i], out_e),
    )
    jobs = []
    for index, (order_of, pack, out) in enumerate(plans):
        room = pieces[4 * index : 4 * index + 4]
        jobs.append(Reduce(order_of, pack, *room, out, reduce_sems.at[index], t, f))
    job_a, job_b, job_c, job_d, job_dd, job_e = jobs
    blocks = []
    for index, (source, landed) in enumerate(((out_blocks, output), (glat_blocks, glat))):
        blocks.append(
            Exchange(
                lambda peer, source=source: source.at[peer],
                lambda peer, landed=landed: landed.at[rows_at(s * blk, blk)],
                source.at[f],
                landed.at[rows_at(s * blk, blk)],
                f,
                nf,
                block_sems.at[index],
            )
        )
    def rim_grads(c):
        part = pl.ds(chunk_at(c), CH)
        for side in range(2):
            beyond = pl.ds(pl.multiple_of(2 * side * px + chunk_at(c), CH), CH)
            value = mm_nt(dk[beyond], proj[2]) + mm_nt(dv[beyond], proj[3])
            rim_out[side, part] = value.astype(BF)

    loop(chunks, rim_grads)
    rim_swap = Swap(
        where, rim_out.at[0], rim_out.at[1], rim_got.at[0], rim_got.at[1], kv_sems.at[0]
    )
    rim_swap.start()
    job_a.advance()
    order[...] = chunk_order(nf)
    clear_ends(spot, count, from_left, from_right)
    clear_ends(spot, count, rim_got.at[0], rim_got.at[1])
    gmat[...] = group_matrix()
    row_masks(rowtab, prev_mask, next_mask, rows)
    clip = Clip(same, rowtab, gmat, own_sums)
    sums[...] = jnp.zeros_like(sums)

    def v(i):
        return vec[i : i + 1]

    def first(c):
        p0 = chunk_at(c)
        part = pl.ds(p0, CH)
        own = pl.ds(pl.multiple_of(px + p0, CH), CH)
        normed_low[part] = (zhat3[part] * v(7) + v(8)).astype(BF)
        grad = gafter[part] + mm_nt(dq[part], proj[1])
        gresid[part] = grad + mm_nt(dk[own], proj[2]) + mm_nt(dv[own], proj[3])

    loop(chunks, first)
    depth = C // nf

    def proj_grad(which, grad):
        low = grad.astype(BF)
        for k in range(nf):
            pack_b[k, which * depth : (which + 1) * depth] = low[k * depth : (k + 1) * depth]

    proj_grad(1, mm_tn(inext[px : 2 * px], dq[...]))
    job_a.advance()
    rim_swap.wait()

    def row_sums(c, grad3, hat3):
        rs[pl.ds(chunk_at(c, CR), CR)] = jnp.sum(grad3, axis=1)
        rq[pl.ds(chunk_at(c, CR), CR)] = jnp.sum(grad3 * hat3, axis=1)

    def second(c):
        p0 = chunk_at(c)
        part = pl.ds(p0, CH)
        grad = gresid[part] + rim_got[0, part].astype(F32) + rim_got[1, part].astype(F32)
        sums[9:10] += jnp.sum(grad, axis=0, keepdims=True)
        low = grad.astype(BF)
        grad_low[part] = low
        d3 = mm_nt(low, proj[0])
        dgrad[part] = d3
        row_sums(c, d3.reshape(CR, F, C), zhat3[part].reshape(CR, F, C))

    loop(chunks, second)

    def swap_step(step, rim_first, rim_last):
        clip.pack(rs, rq, to_left.at[step], to_right.at[step])
        if rim_first is not None:
            to_left[step, 8 : 8 + rim_first.shape[0]] = rim_first
            to_right[step, 8 : 8 + rim_last.shape[0]] = rim_last
        swap = Swap(
            where,
            to_left.at[step],
            to_right.at[step],
            from_left.at[step],
            from_right.at[step],
            msg_sems.at[step],
        )
        swap.start()
        return swap

    def set_means(step, gain):
        mean_e[...], mean_ez[...] = clip.means(
            rs, rq, gain, from_left.at[step], from_right.at[step]
        )

    def back_norm(grad3, hat3, rstd, gain, r0, size):
        value = grad3 * gain - spread(mean_e[pl.ds(r0, size)], size)
        value = value - hat3 * spread(mean_ez[pl.ds(r0, size)], size)
        return value * spread(rstd[pl.ds(r0, size)], size)

    def rim_grad(step, at):
        both = jnp.concatenate([from_left[step, at : at + 8], from_right[step, at : at + 8]], axis=0)
        return both.reshape(2, F, C)

    sums[7:8] = jnp.sum(rq[...], axis=0, keepdims=True)
    sums[8:9] = jnp.sum(rs[...], axis=0, keepdims=True)
    cot_first = cot[0:16].astype(F32)[0:8]
    cot_last = cot[px - 16 : px].astype(F32)[8:16]
    swap = swap_step(
        0,
        jnp.concatenate([dgrad[0:8], cot_first], axis=0),
        jnp.concatenate([dgrad[px - 8 : px], cot_last], axis=0),
    )
    proj_grad(2, mm_tn(inext[...], dk[...]))
    proj_grad(3, mm_tn(inext[...], dv[...]))
    proj_grad(0, mm_tn(normed_low[...], grad_low[...]))
    job_b.advance()
    job_a.advance()
    swap.wait()
    set_means(0, v(7))

    def set_rims(value):
        low = value.astype(BF).astype(F32)
        two[0:8] = low[0]
        two[px + 8 : px + 16] = low[1]

    rim = rim_grad(0, 8)
    rim_hat = zhat3[px : px + 16].reshape(2, F, C)
    set_rims(rim_grad(0, 16) + back_norm(rim, rim_hat, rstd3, v(7), rows, 2))

    def third(c):
        p0 = chunk_at(c)
        part = pl.ds(p0, CH)
        grad3 = dgrad[part].reshape(CR, F, C)
        hat3 = zhat3[part].reshape(CR, F, C)
        value = back_norm(grad3, hat3, rstd3, v(7), chunk_at(c, CR), CR).reshape(CH, C)
        value = cot[part].astype(F32) + value
        gresid[part] = value
        sums[6:7] += jnp.sum(value, axis=0, keepdims=True)
        two[pl.ds(pl.multiple_of(p0 + 8, 8), CH)] = value.astype(BF).astype(F32)

    loop(chunks, third)

    def conv_inputs(zhat, gain, shift, c):
        p0 = chunk_at(c)
        part = pl.ds(p0, CH)
        r0 = chunk_at(c, CR)
        keep_prev = spread(prev_mask[pl.ds(r0, CR)], CR).reshape(CH, C) > 0.0
        keep_next = spread(next_mask[pl.ds(r0, CR)], CR).reshape(CH, C) > 0.0
        after = two[pl.ds(pl.multiple_of(p0 + 16, 16), CH)]
        here = two[pl.ds(pl.multiple_of(p0 + 8, 8), CH)]
        shifted[part, 0:C] = jnp.where(keep_next, after, 0.0).astype(BF)
        shifted[part, C : 2 * C] = here.astype(BF)
        shifted[part, 2 * C : 3 * C] = jnp.where(keep_prev, two[part], 0.0).astype(BF)
        pre = zhat[part] * gain + shift
        act = (pre * jax.nn.sigmoid(pre)).astype(BF).astype(F32).reshape(CR, F, C)
        store_shifts(xc, p0, act, CR)

    def conv_back(kernel, zhat, gain, shift, c):
        part = pl.ds(chunk_at(c), CH)
        hat = zhat[part]
        pre = hat * gain + shift
        sig = jax.nn.sigmoid(pre)

        def columns(j):
            piece = slice(j * C, (j + 1) * C)
            value = mm_nt(shifted[part, 0:C], kernel[0 : 3 * C][piece])
            value = value + mm_nt(shifted[part, C : 2 * C], kernel[3 * C : 6 * C][piece])
            value = value + mm_nt(shifted[part, 2 * C : 3 * C], kernel[6 * C : 9 * C][piece])
            return value.reshape(CR, F, C)

        col = column_index(CR)
        back = columns(1)
        back = back + jnp.where(col == F - 1, 0.0, pltpu.roll(columns(0), F - 1, 1))
        back = back + jnp.where(col == 0, 0.0, pltpu.roll(columns(2), 1, 1))
        grad = back.reshape(CH, C) * sig * (1.0 + pre * (1.0 - sig))
        dgrad[part] = grad
        row_sums(c, grad.reshape(CR, F, C), hat.reshape(CR, F, C))

    share = TAPS * C // nf

    def kernel_grad(pack):
        for k in range(nf):
            if pack.shape[1] > share:
                pack[k, share:] = jnp.zeros((pack.shape[1] - share, C), BF)
        for d in range(3):
            for j in range(3):
                grad = mm_tn(xc[:, j * C : (j + 1) * C], shifted[:, d * C : (d + 1) * C])
                low = grad.astype(BF)
                start = (d * 3 + j) * C
                end = start + C
                at = start
                while at < end:
                    k = at // share
                    upto = min(end, (k + 1) * share)
                    pack[k, at - k * share : upto - k * share] = low[at - start : upto - start]
                    at = upto

    def step_two(c):
        conv_inputs(zhat2, v(4), v(5), c)
        conv_back(conv.at[1], zhat2, v(4), v(5), c)

    loop(chunks, step_two)
    sums[4:5] = jnp.sum(rq[...], axis=0, keepdims=True)
    sums[5:6] = jnp.sum(rs[...], axis=0, keepdims=True)
    swap = swap_step(1, dgrad[0:8], dgrad[px - 8 : px])
    job_a.advance()
    blocks[0].start()
    kernel_grad(pack_c)
    job_c.advance()
    job_b.advance()
    swap.wait()
    set_means(1, v(4))
    rim_hat = zhat2[px : px + 16].reshape(2, F, C)
    set_rims(back_norm(rim_grad(1, 8), rim_hat, rstd2, v(4), rows, 2))

    def fourth(c):
        p0 = chunk_at(c)
        part = pl.ds(p0, CH)
        grad3 = dgrad[part].reshape(CR, F, C)
        hat3 = zhat2[part].reshape(CR, F, C)
        value3 = back_norm(grad3, hat3, rstd2, v(4), chunk_at(c, CR), CR)
        film_rows[pl.ds(chunk_at(c, CR), CR)] = jnp.sum(value3, axis=1)
        low = value3.reshape(CH, C).astype(BF).astype(F32)
        two[pl.ds(pl.multiple_of(p0 + 8, 8), CH)] = low

    loop(chunks, fourth)
    total = jnp.sum(film_rows[...], axis=0, keepdims=True)
    sums[2:3] = total
    sums[3:4] = total
    loop(chunks, partial(conv_inputs, zhat1, v(0), v(1)))
    kernel_grad(pack_d)
    grad_film = hdot_tn(onehot[...], film_rows[...])
    gemb = hdot_tn(cond[...].astype(F32), grad_film).astype(BF)
    edepth = gemb.shape[0] // nf
    job_d.advance()
    job_dd.advance()

    def sums_one(c):
        conv_back(conv.at[0], zhat1, v(0), v(1), c)

    loop(chunks, sums_one)
    sums[0:1] = jnp.sum(rq[...], axis=0, keepdims=True)
    sums[1:2] = jnp.sum(rs[...], axis=0, keepdims=True)
    swap = swap_step(2, None, None)
    tail = jnp.concatenate(
        [
            sums[0:10],
            mid_sums[2:3],
            mid_sums[3 : 3 + FF // C],
            mid_sums[1:2],
            mid_sums[0:1],
            jnp.zeros((32 - 13 - FF // C, C), F32),
        ],
        axis=0,
    ).astype(BF)
    for k in range(nf):
        pack_e[k, 0:edepth] = gemb[k * edepth : (k + 1) * edepth]
        pack_e[k, edepth : edepth + 32] = tail
        pack_e[k, edepth + 32 :] = jnp.zeros((pack_e.shape[1] - edepth - 32, C), BF)
    job_e.advance()
    for job in (job_d, job_dd, job_c, job_a, job_b):
        job.advance()
    swap.wait()
    set_means(2, v(0))

    def fifth(c):
        p0 = chunk_at(c)
        part = pl.ds(p0, CH)
        grad3 = dgrad[part].reshape(CR, F, C)
        hat3 = zhat1[part].reshape(CR, F, C)
        value = back_norm(grad3, hat3, rstd1, v(0), chunk_at(c, CR), CR).reshape(CH, C)
        moved = mm_tn(order[...], (gresid[part] + value).astype(BF)).astype(BF)
        for k in range(nf):
            glat_blocks[k, rows_at(c * seg, seg)] = moved[k * seg : (k + 1) * seg]

    loop(chunks, fifth)
    blocks[1].start()
    while not all(job.done() for job in jobs):
        for job in (job_d, job_dd, job_e, job_c, job_a, job_b):
            job.advance()
    for block in blocks:
        block.wait()


def back(nt, nf, *args):
    px = args[0].shape[0]
    rows = px // F
    tab = args[-6].shape[0]
    pack_rows = args[-2].shape[1]
    edepth = args[-5].shape[1] // nf
    share = TAPS * C // nf
    heights = (pack_rows, 4 * C // nf, share, share, padded(edepth + 32))
    half = padded(share // 2)
    job_heights = heights[:3] + (half, share - half) + heights[4:]
    buffers = [pltpu.VMEM((nf, u, C), BF) for u in heights[1:]]
    for u in job_heights:
        buffers.extend(
            [
                pltpu.VMEM((2, u, C), BF),
                pltpu.VMEM((2, u, C), BF),
                pltpu.VMEM((u, C), BF),
                pltpu.VMEM((2, 2 * u, C), BF),
            ]
        )
    big = pltpu.VMEM((px, C), F32)
    low = pltpu.VMEM((px, C), BF)
    table = pltpu.VMEM((rows, C), F32)
    return pl.pallas_call(
        partial(back_kernel, nt, nf),
        out_shape=[
            jax.ShapeDtypeStruct((px, C), BF),
            jax.ShapeDtypeStruct((px, C), BF),
        ]
        + [jax.ShapeDtypeStruct((u, C), BF) for u in heights],
        in_specs=vmem(len(args)),
        out_specs=vmem(7),
        scratch_shapes=[
            pltpu.VMEM((16, C), F32),
            pltpu.VMEM((rows, C), F32),
            pltpu.VMEM((C, C), BF),
            pltpu.VMEM((2, tab, C), F32),
            table,
            table,
            pltpu.VMEM((tab, C), F32),
            pltpu.VMEM((tab, C), F32),
            table,
            table,
            low,
            low,
            big,
            big,
            pltpu.VMEM((px + 16, C), F32),
            pltpu.VMEM((px, 3 * C), BF),
            pltpu.VMEM((px, 3 * C), BF),
            pltpu.VMEM((2, px, C), BF),
            pltpu.VMEM((2, px, C), BF),
            pltpu.VMEM((3, 24, C), F32),
            pltpu.VMEM((3, 24, C), F32),
            pltpu.VMEM((3, 24, C), F32),
            pltpu.VMEM((3, 24, C), F32),
            pltpu.VMEM((CH, CH), BF),
            pltpu.VMEM((nf, px // nf, C), BF),
            *buffers,
            pltpu.SemaphoreType.DMA((3, 4)),
            pltpu.SemaphoreType.DMA((2, 4)),
            pltpu.SemaphoreType.DMA((2, nf - 1, 2)),
            pltpu.SemaphoreType.DMA((6, stage_count(nt), 2)),
        ],
        compiler_params=pltpu.CompilerParams(
            collective_id=2, has_side_effects=True, vmem_limit_bytes=VMEM_LIMIT
        ),
        name="back",
    )(*args)


def adamw_step(weight, moment, second, grad, decay_rate):
    moment_new = beta_first * moment + (1.0 - beta_first) * grad
    second_new = beta_second * second + (1.0 - beta_second) * grad * grad
    moment_hat = moment_new / (1.0 - beta_first**STEP)
    second_hat = second_new / (1.0 - beta_second**STEP)
    weight_new = weight - learn_rate * (
        moment_hat / (jnp.sqrt(second_hat) + adam_eps) + decay_rate * weight
    )
    return (weight_new, moment_new, second_new)


def layout_kernel(
    nt,
    nf,
    len_row,
    len_col,
    condition,
    weight,
    same,
    rowtab,
    segk,
    segq,
    meta,
    onehot,
    cond,
    wsmall,
    wide,
):
    rows, clips = onehot.shape
    tab = rowtab.shape[0]
    f = lax.axis_index("freq")
    t = lax.axis_index("tm")
    total_rows = nt * nf * rows
    first_row = (t * nf + snake(f, t, nf)) * rows

    def iota(shape, dim):
        return lax.broadcasted_iota(jnp.int32, shape, dim)

    upto = (iota((clips, clips), 0) <= iota((clips, clips), 1)).astype(BF)
    from_low = (iota((clips, clips), 1) <= iota((clips, clips), 0)).astype(BF)
    lengths = len_row[...].astype(F32)
    ends = mm(lengths.astype(BF), upto)[0:1]
    lengths = lengths[0:1]
    ends_col = mm(from_low, len_col[...].astype(F32).astype(BF))[:, 0:1]

    def finished(row):
        return ends <= row.astype(F32)

    def seg_of(row):
        seg = jnp.sum(jnp.where(finished(row), 1.0, 0.0), axis=1, keepdims=True)
        return jnp.where((row >= 0) & (row < total_rows), seg, -1.0)

    def seg_lanes(row):
        return jnp.sum(jnp.where(ends_col <= row.astype(F32), 1.0, 0.0), axis=0, keepdims=True)

    ext_row = first_row - rows + iota((3 * rows, 1), 0)
    segk[...] = jnp.broadcast_to(seg_of(ext_row), segk.shape)
    pixel = iota((1, rows * F), 1)
    segq[...] = jnp.broadcast_to(seg_lanes(first_row + pixel // F), segq.shape)
    seg_row = seg_lanes(first_row + iota((1, rows), 1))
    index = iota((tab + 8, 1), 0)
    at = jnp.where(index < rows, first_row + index, first_row)
    at = jnp.where(index == rows, first_row - 1, at)
    at = jnp.where(index == rows + 1, first_row + rows, at)
    at = jnp.where(index == tab + 1, first_row + rows - 1, at)
    unused = ((index > rows + 1) & (index < tab)) | (index > tab + 1)
    seg_tab = jnp.where(unused, -2.0, seg_of(at))
    same[...] = (seg_tab == seg_row).astype(BF)
    clip_lane = iota((tab + 8, clips), 1).astype(F32)
    hot = jnp.where(seg_tab == clip_lane, 1.0, 0.0)
    onehot[...] = hot[0:rows]
    row_len = jnp.sum(hot * lengths, axis=1, keepdims=True)
    inner = index < rows
    fields = (
        1.0 / jnp.maximum(row_len * (F * GW), 1.0),
        jnp.where(seg_tab == seg_of(first_row - 1 + 0 * index), 1.0, 0.0),
        jnp.where(seg_tab == seg_of(first_row + rows + 0 * index), 1.0, 0.0),
        jnp.where(inner & (seg_tab == seg_of(at - 1)), 1.0, 0.0),
        jnp.where(inner & (seg_tab == seg_of(at + 1)), 1.0, 0.0),
    )
    lane = iota((tab + 8, 128), 1)
    values = jnp.zeros((tab + 8, 128), F32)
    for place_at, field in enumerate(fields):
        values = jnp.where(lane == place_at, field, values)
    rowtab[...] = values[0:tab]
    tile = iota((8, 1), 0)

    def bounds(row):
        low = jnp.sum(jnp.where(finished(row), lengths, 0.0), axis=1, keepdims=True)
        seg = jnp.sum(jnp.where(finished(row), 1.0, 0.0), axis=1, keepdims=True)
        here = iota((8, clips), 1).astype(F32) == seg
        return low, low + jnp.sum(jnp.where(here, lengths, 0.0), axis=1, keepdims=True)

    low_row = bounds(first_row + tile * CR)[0].astype(jnp.int32) - first_row + rows
    high_row = bounds(first_row + tile * CR + CR - 1)[1].astype(jnp.int32) - first_row + rows
    low = low_row // 16
    number = (high_row - low * 16 + CR - 1) // CR
    low = jnp.minimum(low, (3 * rows - number * CR) // 16)
    meta[...] = jnp.where(iota((8, 128), 1) == 0, low, number)
    value = condition[...]
    cond[...] = (value * jax.nn.sigmoid(value)).astype(BF)
    nsmall, width = weight.shape
    wide[...] = jnp.zeros_like(wide)
    wide[0:nsmall] = weight[...]
    chosen = iota((width, C), 1) == f * width + iota((width, C), 0)
    wsmall[...] = mm(wide[...].astype(BF), chosen.astype(BF))


def layout_of(nt, nf, lengths, condition, weight, rows):
    clips = lengths.shape[0]
    tab = rows + 8
    shapes = (
        ((tab + 8, rows), BF),
        ((tab, 128), F32),
        ((3 * rows, 128), F32),
        ((8, rows * F), F32),
        ((8, 128), jnp.int32),
        ((rows, clips), F32),
        (condition.shape, BF),
        ((32, C), F32),
    )
    return pl.pallas_call(
        partial(layout_kernel, nt, nf),
        out_shape=[jax.ShapeDtypeStruct(s, d) for s, d in shapes],
        in_specs=vmem(4),
        out_specs=vmem(len(shapes)),
        scratch_shapes=[pltpu.VMEM((32, weight.shape[1]), F32)],
        compiler_params=pltpu.CompilerParams(vmem_limit_bytes=VMEM_LIMIT),
        name="layout",
    )(
        jnp.broadcast_to(lengths[None, :], (8, clips)),
        jnp.broadcast_to(lengths[:, None], (clips, 128)),
        condition,
        weight,
    )


def on_device(
    nt,
    nf,
    latent,
    condition,
    lengths,
    cotangent,
    conv_weight,
    conv_moment,
    conv_second,
    proj_weight,
    proj_moment,
    proj_second,
    mlp_weight,
    mlp_moment,
    mlp_second,
    emb_weight,
    emb_moment,
    emb_second,
    small_weight,
    small_moment,
    small_second,
):
    masters = (conv_weight, proj_weight, mlp_weight, emb_weight, small_weight)
    nsmall, width = small_weight.shape
    f = lax.axis_index("freq")
    rows = latent.shape[0] // nf
    same, rowtab, segk, segq, meta, onehot, cond_low, wsmall = layout_of(
        nt, nf, lengths, condition, small_weight, rows
    )
    (
        conv_full,
        proj_full,
        mlp_full,
        vec,
        cot,
        zhat1,
        zhat2,
        zhat3,
        rstd1,
        rstd2,
        rstd3,
        resid,
        inner,
        query,
        kext,
        vext,
        inext,
    ) = front(
        nt,
        nf,
        latent.reshape(-1, C),
        cotangent.reshape(-1, C),
        conv_weight,
        proj_weight,
        mlp_weight,
        emb_weight,
        wsmall,
        cond_low,
        onehot,
        same,
        rowtab,
    )
    mixed, mixed_t, lse = attend(meta, query, kext, vext, segq, segk)
    out_blocks, gafter, gmix, pack_a, mid_sums = middle(
        nf, inner, mixed, resid, cot, proj_full, mlp_full, vec
    )
    dq, dk, dv = attend_back(
        meta, query, kext, vext, segq, segk, gmix, mixed_t, lse
    )
    output, glat, sum_a, sum_b, sum_c, sum_d, sum_e = back(
        nt,
        nf,
        dq,
        dk,
        dv,
        gafter,
        inext,
        zhat1,
        zhat2,
        zhat3,
        rstd1,
        rstd2,
        rstd3,
        cot,
        conv_full,
        proj_full,
        vec,
        same,
        rowtab,
        cond_low,
        onehot,
        mid_sums,
        pack_a,
        out_blocks,
    )
    cdepth, pdepth, mdepth, edepth = (
        conv_weight.shape[1],
        proj_weight.shape[1],
        mlp_weight.shape[1],
        emb_weight.shape[0],
    )
    grad_conv = jnp.stack([sum_d[:cdepth], sum_c[:cdepth]])
    first_four = sum_b[: 4 * pdepth].reshape(4, pdepth, C)
    last_two = sum_a[2 * mdepth :].reshape(2, pdepth, C)
    grad_small = lax.dynamic_slice(sum_e, (edepth, f * width), (nsmall, width))
    shares = [
        grad_conv.astype(F32),
        jnp.concatenate([first_four, last_two], axis=0).astype(F32),
        sum_a[: 2 * mdepth].reshape(2, mdepth, C).astype(F32),
        sum_e[:edepth].astype(F32),
        grad_small.astype(F32),
    ]
    moments = (conv_moment, proj_moment, mlp_moment, emb_moment, small_moment)
    seconds = (conv_second, proj_second, mlp_second, emb_second, small_second)
    decays = (weight_decay, weight_decay, weight_decay, weight_decay, 0.0)
    updated = []
    for position in range(5):
        updated.extend(
            adamw_step(
                masters[position],
                moments[position],
                seconds[position],
                shares[position],
                decays[position],
            )
        )
    bias_share = shares[4][nsmall - 1]
    return (
        output.reshape(latent.shape),
        glat.reshape(latent.shape),
        *updated,
        bias_share,
    )


def solution(mesh):
    nt, nf = mesh.shape["tm"], mesh.shape["freq"]
    rows_spec = P("tm", "freq", None)
    middle_spec = P(None, "freq", None)
    params = (middle_spec,) * 9 + (P("freq", None),) * 3 + (P(None, "freq"),) * 3
    return jax.shard_map(
        partial(on_device, nt, nf),
        mesh=mesh,
        in_specs=(rows_spec, P(), P(), rows_spec) + params,
        out_specs=(rows_spec, rows_spec) + params + (P("freq"),),
        check_vma=False,
    )
```

```python
from functools import partial

import jax
import jax.numpy as jnp
from jax import lax
from jax.experimental import pallas as pl
from jax.experimental.pallas import tpu as pltpu
from jax.sharding import PartitionSpec as P

C = 256
G = 32
GW = C // G
HD = 32
H = C // HD
FF = 1024
F = 8
MAXLEN = 128
STEP = 10
TAPS = 9
CH = 256
CR = CH // F

HIGHEST = lax.Precision.HIGHEST
norm_eps = 1e-05
beta_first = 0.9
beta_second = 0.999
learn_rate = 0.5
weight_decay = 0.01
adam_eps = 1e-08
masked_score = -1e30
score_scale = HD**-0.5
LOG2E = 1.4426950408889634
MESH = pltpu.DeviceIdType.MESH if hasattr(pltpu, "DeviceIdType") else pl.DeviceIdType.MESH
VMEM_LIMIT = 64 * 1024 * 1024 - 65536
BF = jnp.bfloat16
F32 = jnp.float32


def mm(a, b):
    return jnp.dot(a, b, preferred_element_type=F32)


def mm_nt(a, b):
    return lax.dot_general(a, b, (((1,), (1,)), ((), ())), preferred_element_type=F32)


def mm_tn(a, b):
    return lax.dot_general(a, b, (((0,), (0,)), ((), ())), preferred_element_type=F32)


def hdot(a, b):
    return jnp.dot(a, b, precision=HIGHEST, preferred_element_type=F32)


def thirds(x):
    high = x.astype(BF)
    rest = x - high.astype(F32)
    middle = rest.astype(BF)
    low = (rest - middle.astype(F32)).astype(BF)
    return high, middle, low


def hdot_tn(a, b):
    return lax.dot_general(
        a, b, (((0,), (0,)), ((), ())), precision=HIGHEST, preferred_element_type=F32
    )


def place(nt, nf):
    t = lax.axis_index("tm")
    f = lax.axis_index("freq")
    odd = lax.rem(t, 2)
    s = f + odd * (nf - 1 - 2 * f)
    turn = 1 - 2 * odd
    at_end = (s + 1) // nf
    at_start = 1 - (s + nf - 1) // nf
    right = {"tm": t + at_end, "freq": f + (1 - at_end) * turn}
    left = {"tm": t - at_start, "freq": f - (1 - at_start) * turn}
    return t * nf + s, left, right


def flip(x, bit):
    return x + bit - 2 * bit * lax.rem(x // bit, 2)


def flip_by(x, mask):
    bit = 1
    while bit <= mask:
        if mask & bit:
            x = flip(x, bit)
        bit *= 2
    return x


def bits_of(count):
    bits = []
    bit = 1
    while bit < count:
        bits.append(bit)
        bit *= 2
    return bits


def snake(f, t, nf):
    return f + lax.rem(t, 2) * (nf - 1 - 2 * f)


def enter(spot, count, left, right, partners):
    barrier = pltpu.get_barrier_semaphore()
    for partner in partners:
        pl.semaphore_signal(barrier, inc=1, device_id=partner, device_id_type=MESH)

    @pl.when(spot > 0)
    def _():
        pl.semaphore_signal(barrier, inc=1, device_id=left, device_id_type=MESH)

    @pl.when(spot < count - 1)
    def _():
        pl.semaphore_signal(barrier, inc=1, device_id=right, device_id_type=MESH)

    inside = (spot > 0) & (spot < count - 1)

    @pl.when(inside)
    def _():
        pl.semaphore_wait(barrier, len(partners) + 2)

    @pl.when(jnp.logical_not(inside))
    def _():
        pl.semaphore_wait(barrier, len(partners) + 1)


class Swap:
    def __init__(self, where, to_left, to_right, from_left, from_right, sems):
        self.spot, self.count, left, right = where
        self.go_left = pltpu.make_async_remote_copy(
            src_ref=to_left,
            dst_ref=from_right,
            send_sem=sems.at[0],
            recv_sem=sems.at[1],
            device_id=left,
            device_id_type=MESH,
        )
        self.go_right = pltpu.make_async_remote_copy(
            src_ref=to_right,
            dst_ref=from_left,
            send_sem=sems.at[2],
            recv_sem=sems.at[3],
            device_id=right,
            device_id_type=MESH,
        )

    def start(self):
        @pl.when(self.spot > 0)
        def _():
            self.go_left.start()

        @pl.when(self.spot < self.count - 1)
        def _():
            self.go_right.start()

    def wait(self):
        @pl.when(self.spot > 0)
        def _():
            self.go_left.wait_send()
            self.go_right.wait_recv()

        @pl.when(self.spot < self.count - 1)
        def _():
            self.go_right.wait_send()
            self.go_left.wait_recv()


def remote(src, dst, sems, device):
    return pltpu.make_async_remote_copy(
        src_ref=src,
        dst_ref=dst,
        send_sem=sems.at[0],
        recv_sem=sems.at[1],
        device_id=device,
        device_id_type=MESH,
    )


class Exchange:
    def __init__(self, source, target, own_source, own_target, f, nf, sems):
        self.copies = []
        for mask in range(1, nf):
            peer = flip_by(f, mask)
            self.copies.append(
                remote(source(peer), target(peer), sems.at[mask - 1], {"freq": peer})
            )
        self.own_source, self.own_target = own_source, own_target

    def start(self):
        for copy in self.copies[::-1]:
            copy.start()
        self.own_target[...] = self.own_source[...]

    def wait(self):
        for copy in self.copies:
            copy.wait()


class Gather:
    def __init__(self, view, f, t, sems, size=None):
        near = {"freq": flip(f, 1)}
        far = flip(f, 2)
        self.halves = size is not None
        if self.halves:
            side = lax.rem(t, 2)
            mine, other = (side, size // 2), (1 - side, size // 2)
        else:
            mine = (0, None)
        beside = {"tm": flip(t, 1)}
        self.far = remote(view(f, mine), view(f, mine), sems.at[0], {"freq": far})
        self.near = remote(view(f, (0, None)), view(f, (0, None)), sems.at[1], near)
        self.forward = remote(view(far, mine), view(far, mine), sems.at[2], near)
        if self.halves:
            self.cross = remote(view(far, mine), view(far, mine), sems.at[3], beside)
            self.second = remote(view(far, other), view(far, other), sems.at[4], near)

    def start(self):
        self.far.start()
        self.near.start()

    def relay(self):
        self.far.wait_recv()
        if self.halves:
            self.cross.start()
        self.forward.start()

    def collect(self):
        if self.halves:
            self.cross.wait_recv()
            self.second.start()
        self.near.wait_recv()
        self.forward.wait_recv()
        if self.halves:
            self.second.wait_recv()

    def finish(self):
        self.far.wait_send()
        self.near.wait_send()
        self.forward.wait_send()
        if self.halves:
            self.cross.wait_send()
            self.second.wait_send()


def share_view(ref, depth, lead):
    def view(i, part):
        which, size = part
        start = i * depth if size is None else i * depth + which * size
        rows = rows_at(start, depth if size is None else size)
        return ref.at[lead, rows] if lead is not None else ref.at[rows]

    return view


def rows_at(start, size):
    return pl.ds(pl.multiple_of(start, 16), size)


def piece_of(n):
    for size in (128, 96, 80, 64, 48, 32):
        if n % size == 0:
            return size
    return 16


def add_rows(dst, to, a, a_at, b, b_at, n):
    size = piece_of(n)

    def step(i):
        left = a[rows_at(a_at + i * size, size)].astype(F32)
        right = b[rows_at(b_at + i * size, size)].astype(F32)
        dst[rows_at(to + i * size, size)] = (left + right).astype(BF)

    loop(n // size, step)


class Reduce:
    def __init__(self, order, pack, got, acc, far, rs, out, sems, t, f):
        u = far.shape[0]
        near = {"freq": flip(f, 1)}
        one = remote(pack(flip_by(f, 1)), got.at[0], sems.at[0], near)
        two = remote(pack(flip_by(f, 3)), got.at[1], sems.at[1], near)

        def add_near():
            add_rows(acc.at[1], 0, pack(flip(f, 2)), 0, got.at[1], 0, u)
            add_rows(acc.at[0], 0, pack(f), 0, got.at[0], 0, u)

        self.stages = [((two, one), add_near)]
        gathers = []
        n, at, base, place_at = u, 0, 0, 2
        slots = 2
        for bit in order:
            last = bit == order[-1]
            if bit == 0:
                rows = rows_at(at, n)
                copy = remote(
                    acc.at[1, rows], far.at[0:n], sems.at[place_at], {"freq": flip(f, 2)}
                )
                finish = partial(add_rows, acc.at[0], at, acc.at[0], at, far, 0, n)
                self.stages.append(((copy,), finish))
                slots, place_at = 1, place_at + 1
                continue
            peer = {"tm": flip(t, bit)}
            half = n % 32 == 0 and not last
            if half:
                upper = lax.rem(t // bit, 2)
                n = n // 2
                keep, give = at + upper * n, at + (1 - upper) * n
            else:
                keep, give = at, at
            copy = remote(
                acc.at[0:slots, rows_at(give, n)],
                rs.at[0:slots, base : base + n],
                sems.at[place_at],
                peer,
            )

            def finish(slots=slots, keep=keep, base=base, n=n, last=last):
                for slot in range(slots):
                    target = out if last else acc.at[slot]
                    add_rows(target, keep, acc.at[slot], keep, rs.at[slot], base, n)

            self.stages.append(((copy,), finish))
            if half:
                share = out.at[rows_at(keep, n)]
                gathers.append(((remote(share, share, sems.at[place_at + 1], peer),), None))
            at, base, place_at = keep, base + n, place_at + 2
        self.stages.extend(gathers[::-1])
        self.now = -1

    def done(self):
        return self.now >= len(self.stages)

    def advance(self):
        if self.done():
            return
        if self.now >= 0:
            copies, finish = self.stages[self.now]
            for copy in copies:
                copy.wait()
            if finish is not None:
                finish()
        self.now += 1
        if not self.done():
            for copy in self.stages[self.now][0]:
                copy.start()


def orders_of(nt):
    bits = bits_of(nt)
    far_first = [0] + bits
    if len(bits) < 2:
        return far_first, far_first
    return far_first, [bits[1], 0, bits[0]] + bits[2:]


def stage_count(nt):
    return 3 + 2 * len(bits_of(nt))


def padded(rows):
    return (rows + 63) // 64 * 64


def chunk_order(nf):
    width = F // nf
    row = lax.broadcasted_iota(jnp.int32, (CH, CH), 0)
    source = lax.broadcasted_iota(jnp.int32, (CH, CH), 1)
    col = lax.rem(row, F)
    wanted = (col // width) * (CR * width) + (row // F) * width + lax.rem(col, width)
    return jnp.where(source == wanted, 1.0, 0.0).astype(BF)


def clear_ends(spot, count, from_left, from_right):
    @pl.when(spot == 0)
    def _():
        from_left[...] = jnp.zeros_like(from_left)

    @pl.when(spot == count - 1)
    def _():
        from_right[...] = jnp.zeros_like(from_right)


def group_matrix():
    i = lax.broadcasted_iota(jnp.int32, (C, C), 0) // GW
    j = lax.broadcasted_iota(jnp.int32, (C, C), 1) // GW
    return (i == j).astype(BF)


def spread(rows, count):
    return jnp.broadcast_to(rows[:, None, :], (count, F, C))


def column_index(count):
    return lax.broadcasted_iota(jnp.int32, (count, F, C), 1)


def column_shifts(act, count):
    col = column_index(count)
    before = jnp.where(col == 0, 0.0, pltpu.roll(act, 1, 1))
    after = jnp.where(col == F - 1, 0.0, pltpu.roll(act, F - 1, 1))
    return before, after


def store_shifts(xc, at, act, count):
    before, after = column_shifts(act, count)
    size = count * F
    xc[pl.ds(at, size), 0:C] = before.reshape(size, C).astype(BF)
    xc[pl.ds(at, size), C : 2 * C] = act.reshape(size, C).astype(BF)
    xc[pl.ds(at, size), 2 * C : 3 * C] = after.reshape(size, C).astype(BF)


def loop(count, body):
    def step(i, carry):
        body(i)
        return carry

    lax.fori_loop(0, count, step, 0)


def chunk_at(i, size=CH):
    return pl.multiple_of(i * size, size)


class Clip:
    def __init__(self, same, rowtab, gmat, local):
        self.same, self.rowtab, self.gmat, self.local = same, rowtab, gmat, local

    def pack(self, rs, rq, to_left, to_right):
        tab = self.rowtab.shape[0]
        for index, table in ((0, rs), (1, rq)):
            total = 0.0
            for part in thirds(table[...])[::-1]:
                total = total + mm(self.same[...], part)
            self.local[index] = total[0:tab]
            to_left[index : index + 1] = total[tab : tab + 1]
            to_right[index : index + 1] = total[tab + 1 : tab + 2]

    def means(self, rs, rq, gain, from_left, from_right):
        at_left = self.rowtab[:, 1:2] > 0.0
        at_right = self.rowtab[:, 2:3] > 0.0
        inverse = self.rowtab[:, 0:1]
        tab = self.rowtab.shape[0]
        parts = []
        for index in range(2):
            total = self.local[index]
            total = total + jnp.where(at_left, from_left[index : index + 1], 0.0)
            total = total + jnp.where(at_right, from_right[index : index + 1], 0.0)
            total = total * inverse
            if gain is not None:
                total = total * gain
            parts.append(thirds(total))
        results = []
        for high, middle, low in parts:
            value = mm(low, self.gmat[...]) + mm(middle, self.gmat[...])
            results.append(value + mm(high, self.gmat[...]))
        return results


def row_masks(rowtab, prev_mask, next_mask, rows):
    prev_mask[...] = jnp.broadcast_to(rowtab[0:rows, 3:4], (rows, C))
    next_mask[...] = jnp.broadcast_to(rowtab[0:rows, 4:5], (rows, C))


def front_kernel(
    nt,
    nf,
    lat_local,
    cot_local,
    wconv,
    wproj,
    wmlp,
    wemb,
    wsmall,
    cond,
    onehot,
    same,
    rowtab,
    conv,
    proj,
    mlp,
    vec,
    cot,
    zhat1,
    zhat2,
    zhat3,
    rstd1,
    rstd2,
    rstd3,
    resid,
    inner,
    query,
    kext,
    vext,
    inext,
    gmat,
    own_sums,
    rs,
    rq,
    mean,
    prev_mask,
    next_mask,
    xc,
    z_prev,
    z_here,
    z_next,
    hidden,
    to_left,
    to_right,
    from_left,
    from_right,
    emb,
    small,
    lat,
    lat_in,
    cot_in,
    order,
    film,
    msg_sems,
    kv_sems,
    block_sems,
    gather_sems,
):
    px = lat.shape[0]
    rows = px // F
    chunks = px // CH
    blk = px // nf
    seg = CH // nf
    spot, left, right = place(nt, nf)
    count = nt * nf
    where = (spot, count, left, right)
    f = lax.axis_index("freq")
    t = lax.axis_index("tm")
    s = snake(f, t, nf)
    partners = [{"freq": flip_by(f, mask)} for mask in range(1, nf)] + [{"tm": flip(t, 1)}]
    enter(spot, count, left, right, partners)
    blocks = []
    for index, (local, landed) in enumerate(((lat_local, lat_in), (cot_local, cot_in))):
        blocks.append(
            Exchange(
                lambda peer, local=local: local.at[rows_at(snake(peer, t, nf) * blk, blk)],
                lambda peer, landed=landed: landed.at[f],
                local.at[rows_at(s * blk, blk)],
                landed.at[f],
                f,
                nf,
                block_sems.at[index],
            )
        )
    blocks[0].start()

    def cast(src, dst, base):
        size = 32 if src.shape[0] % 64 else 64

        def step(i):
            dst[rows_at(base + i * size, size)] = src[rows_at(i * size, size)].astype(BF)

        loop(src.shape[0] // size, step)

    cdepth, pdepth, mdepth, edepth = (
        wconv.shape[1],
        wproj.shape[1],
        wmlp.shape[1],
        wemb.shape[0],
    )
    views = (
        (share_view(conv, cdepth, 0), cdepth),
        (share_view(conv, cdepth, 1), cdepth),
        (share_view(proj, pdepth, slice(None)), pdepth),
        (share_view(mlp, mdepth, slice(None)), mdepth),
        (share_view(emb, edepth, None), edepth),
        (share_view(small, wsmall.shape[0], None), None),
    )
    gathers = []
    for i, (view, size) in enumerate(views):
        gathers.append(Gather(view, f, t, gather_sems.at[i], size))
    get_first, get_second, get_proj, get_mlp, get_emb, get_small = gathers
    cast(wsmall, small, f * wsmall.shape[0])
    cast(wconv.at[0], conv.at[0], f * cdepth)
    get_small.start()
    get_first.start()
    cast(wemb, emb, f * edepth)
    cast(wconv.at[1], conv.at[1], f * cdepth)
    for i in range(wproj.shape[0]):
        cast(wproj.at[i], proj.at[i], f * pdepth)
    for i in range(wmlp.shape[0]):
        cast(wmlp.at[i], mlp.at[i], f * mdepth)
    order[...] = chunk_order(nf)

    def arrange(landed, target):
        def step(c):
            parts = [landed[k, rows_at(c * seg, seg)] for k in range(nf)]
            moved = mm(order[...], jnp.concatenate(parts, axis=0))
            target[pl.ds(chunk_at(c), CH)] = moved.astype(BF)

        loop(chunks, step)

    clear_ends(spot, count, from_left, from_right)

    @pl.when(spot == 0)
    def _():
        inext[0:px] = jnp.zeros((px, C), BF)

    @pl.when(spot == count - 1)
    def _():
        inext[2 * px : 3 * px] = jnp.zeros((px, C), BF)

    gmat[...] = group_matrix()
    row_masks(rowtab, prev_mask, next_mask, rows)
    clip = Clip(same, rowtab, gmat, own_sums)

    def v(i):
        return vec[i : i + 1]

    def norm_stage(step, load, zhat, rstd, rim, beside):
        def sums(c):
            x3 = load(c).reshape(CR, F, C)
            rs[pl.ds(chunk_at(c, CR), CR)] = jnp.sum(x3, axis=1)
            rq[pl.ds(chunk_at(c, CR), CR)] = jnp.sum(x3 * x3, axis=1)

        loop(chunks, sums)
        clip.pack(rs, rq, to_left.at[step], to_right.at[step])
        first, last = rim()
        to_left[step, 8:16] = first
        to_right[step, 8:16] = last
        swap = Swap(
            where,
            to_left.at[step],
            to_right.at[step],
            from_left.at[step],
            from_right.at[step],
            msg_sems.at[step],
        )
        swap.start()
        beside()
        swap.wait()
        mean_rows, square_rows = clip.means(rs, rq, None, from_left.at[step], from_right.at[step])
        mean[...] = mean_rows
        rstd[...] = lax.rsqrt(square_rows - mean_rows * mean_rows + norm_eps)
        rim_raw = jnp.concatenate([from_left[step, 8:16], from_right[step, 8:16]], axis=0)
        rim3 = rim_raw.reshape(2, F, C)
        rim_hat = (rim3 - spread(mean[rows : rows + 2], 2)) * spread(rstd[rows : rows + 2], 2)
        if zhat.shape[0] > px:
            zhat[px : px + 16] = rim_hat.reshape(16, C)
        return rim_hat

    def normed(load, zhat, rstd, c):
        r0 = chunk_at(c, CR)
        x3 = load(c).reshape(CR, F, C)
        hat = (x3 - spread(mean[pl.ds(r0, CR)], CR)) * spread(rstd[pl.ds(r0, CR)], CR)
        zhat[pl.ds(chunk_at(c), CH)] = hat.reshape(CH, C)
        return hat

    def conv_stage(rim_hat, load, zhat, rstd, gain, shift, kernel, ready, finish):
        pre = rim_hat * gain + shift
        store_shifts(xc, px, (pre * jax.nn.sigmoid(pre)).astype(BF).astype(F32), 2)

        def build(c):
            pre = normed(load, zhat, rstd, c) * gain + shift
            act = (pre * jax.nn.sigmoid(pre)).astype(BF).astype(F32)
            store_shifts(xc, chunk_at(c), act, CR)

        loop(chunks, build)
        ready()

        def product(c):
            p0 = chunk_at(c)
            part = xc[pl.ds(p0, CH)]
            z_prev[pl.ds(pl.multiple_of(p0 + 8, 8), CH)] = mm(part, kernel[0 : 3 * C])
            z_here[pl.ds(p0, CH)] = mm(part, kernel[3 * C : 6 * C])
            z_next[pl.ds(p0, CH)] = mm(part, kernel[6 * C : 9 * C])

        loop(chunks, product)
        part = xc[px : px + 16]
        z_prev[0:8] = mm(part, kernel[0 : 3 * C])[0:8]
        z_next[px : px + 8] = mm(part, kernel[6 * C : 9 * C])[8:16]

        def join(c):
            p0 = chunk_at(c)
            r0 = chunk_at(c, CR)
            keep_prev = spread(prev_mask[pl.ds(r0, CR)], CR) > 0.0
            keep_next = spread(next_mask[pl.ds(r0, CR)], CR) > 0.0
            out = z_here[pl.ds(p0, CH)].reshape(CR, F, C)
            out = out + jnp.where(keep_prev, z_prev[pl.ds(p0, CH)].reshape(CR, F, C), 0.0)
            after = z_next[pl.ds(pl.multiple_of(p0 + 8, 8), CH)].reshape(CR, F, C)
            finish(c, out + jnp.where(keep_next, after, 0.0))

        loop(chunks, join)

    def load_latent(c):
        return lat[pl.ds(chunk_at(c), CH)].astype(F32)

    def load_hidden(c):
        return hidden[pl.ds(chunk_at(c), CH)]

    def load_resid(c):
        return resid[pl.ds(chunk_at(c), CH)]

    def send_second():
        get_emb.start()
        get_second.start()
        blocks[1].start()
        get_small.relay()
        get_small.collect()
        total = small[0 : wsmall.shape[0]].astype(F32)
        for k in range(1, nf):
            at = k * wsmall.shape[0]
            total = total + small[at : at + wsmall.shape[0]].astype(F32)
        vec[...] = total

    blocks[0].wait()
    arrange(lat_in, lat)
    rim_hat = norm_stage(
        0,
        load_latent,
        zhat1,
        rstd1,
        lambda: (lat[0:16].astype(F32)[0:8], lat[px - 16 : px].astype(F32)[8:16]),
        send_second,
    )

    def ready_first():
        get_first.relay()
        get_emb.relay()
        get_second.relay()
        get_first.collect()
        get_emb.collect()
        table = mm(cond[...], emb[...]) + v(3)
        film[...] = hdot(onehot[...], table)

    def finish_one(c, out):
        r0 = chunk_at(c, CR)
        out = out + v(2) + spread(film[pl.ds(r0, CR)], CR)
        hidden[pl.ds(chunk_at(c), CH)] = out.reshape(CH, C)

    conv_stage(rim_hat, load_latent, zhat1, rstd1, v(0), v(1), conv.at[0], ready_first, finish_one)

    def send_proj():
        get_proj.start()
        get_mlp.start()
        blocks[1].wait()
        arrange(cot_in, cot)

    def ready_second():
        get_second.collect()
        get_proj.relay()
        get_mlp.relay()

    rim_hat = norm_stage(
        1, load_hidden, zhat2, rstd2, lambda: (hidden[0:8], hidden[px - 8 : px]), send_proj
    )

    def finish_two(c, out):
        p0 = chunk_at(c)
        total = lat[pl.ds(p0, CH)].astype(F32) + out.reshape(CH, C) + v(6)
        resid[pl.ds(p0, CH)] = total

    conv_stage(rim_hat, load_hidden, zhat2, rstd2, v(4), v(5), conv.at[1], ready_second, finish_two)

    def ready_proj():
        get_proj.collect()
        get_mlp.collect()

    norm_stage(
        2, load_resid, zhat3, rstd3, lambda: (resid[0:8], resid[px - 8 : px]), ready_proj
    )

    def project(c):
        p0 = chunk_at(c)
        hat = normed(load_resid, zhat3, rstd3, c).reshape(CH, C)
        low = (hat * v(7) + v(8)).astype(BF)
        value = mm(low, proj[0]) + v(9)
        inner[pl.ds(p0, CH)] = value
        inext[pl.ds(pl.multiple_of(px + p0, CH), CH)] = value.astype(BF)

    loop(chunks, project)
    swap = Swap(
        where,
        inext.at[px : 2 * px],
        inext.at[px : 2 * px],
        inext.at[0:px],
        inext.at[2 * px : 3 * px],
        kv_sems.at[0],
    )
    swap.start()

    def keys_values(part):
        low = inext[part]
        kext[part] = mm(low, proj[2]).astype(BF)
        vext[part] = mm(low, proj[3]).astype(BF)

    def heads(c):
        part = pl.ds(pl.multiple_of(px + chunk_at(c), CH), CH)
        query[pl.ds(chunk_at(c), CH)] = mm(inext[part], proj[1]).astype(BF)
        keys_values(part)

    loop(chunks, heads)
    swap.wait()

    def rims(c):
        keys_values(pl.ds(chunk_at(c), CH))
        keys_values(pl.ds(pl.multiple_of(2 * px + chunk_at(c), CH), CH))

    loop(chunks, rims)
    for gather in gathers:
        gather.finish()


def vmem(count):
    return [pl.BlockSpec(memory_space=pltpu.VMEM)] * count


def front(nt, nf, lat, cot, wconv, wproj, wmlp, wemb, wsmall, cond, onehot, same, rowtab):
    px = lat.shape[0]
    rows = px // F
    tab = rowtab.shape[0]

    def whole(share, axis):
        shape = list(share.shape)
        shape[axis] *= nf
        return tuple(shape)

    shapes = (
        (whole(wconv, 1), BF),
        (whole(wproj, 1), BF),
        (whole(wmlp, 1), BF),
        (wsmall.shape, F32),
        ((px, C), BF),
        ((px, C), F32),
        ((px + 16, C), F32),
        ((px + 16, C), F32),
        ((tab, C), F32),
        ((tab, C), F32),
        ((tab, C), F32),
        ((px, C), F32),
        ((px, C), F32),
        ((px, C), BF),
        ((3 * px, C), BF),
        ((3 * px, C), BF),
        ((3 * px, C), BF),
    )
    return pl.pallas_call(
        partial(front_kernel, nt, nf),
        out_shape=[jax.ShapeDtypeStruct(s, d) for s, d in shapes],
        in_specs=vmem(11),
        out_specs=vmem(len(shapes)),
        scratch_shapes=[
            pltpu.VMEM((C, C), BF),
            pltpu.VMEM((2, tab, C), F32),
            pltpu.VMEM((rows, C), F32),
            pltpu.VMEM((rows, C), F32),
            pltpu.VMEM((tab, C), F32),
            pltpu.VMEM((rows, C), F32),
            pltpu.VMEM((rows, C), F32),
            pltpu.VMEM((px + 16, 3 * C), BF),
            pltpu.VMEM((px + 16, C), F32),
            pltpu.VMEM((px, C), F32),
            pltpu.VMEM((px + 16, C), F32),
            pltpu.VMEM((px, C), F32),
            pltpu.VMEM((3, 16, C), F32),
            pltpu.VMEM((3, 16, C), F32),
            pltpu.VMEM((3, 16, C), F32),
            pltpu.VMEM((3, 16, C), F32),
            pltpu.VMEM(whole(wemb, 0), BF),
            pltpu.VMEM((nf * wsmall.shape[0], C), BF),
            pltpu.VMEM((px, C), BF),
            pltpu.VMEM((nf, px // nf, C), BF),
            pltpu.VMEM((nf, px // nf, C), BF),
            pltpu.VMEM((CH, CH), BF),
            pltpu.VMEM((rows, C), F32),
            pltpu.SemaphoreType.DMA((3, 4)),
            pltpu.SemaphoreType.DMA((2, 4)),
            pltpu.SemaphoreType.DMA((2, nf - 1, 2)),
            pltpu.SemaphoreType.DMA((6, 5, 2)),
        ],
        compiler_params=pltpu.CompilerParams(
            collective_id=1, has_side_effects=True, vmem_limit_bytes=VMEM_LIMIT
        ),
        name="front",
    )(lat, cot, wconv, wproj, wmlp, wemb, wsmall, cond, onehot, same, rowtab)


def head_mask(h):
    lane = lax.broadcasted_iota(jnp.int32, (CH, C), 1)
    return (lane >= h * HD) & (lane < (h + 1) * HD)


def head_rows(h):
    return slice(h * HD, (h + 1) * HD)


def turned(block):
    return block.astype(F32).T


def score_bias(segk, segq, key_row, q0):
    keys = jnp.broadcast_to(segk[pl.ds(key_row, CR), 0:1], (CR, C))
    keys = spread(keys, CR).reshape(CH, C)
    return jnp.where(keys == segq[0:1, pl.ds(q0, CH)], 0.0, masked_score)


def attend_kernel(meta, query, kext, vext, segq, segk, mixed, mixed_t, lse, vt, qm, bias, top, tot, acc, scores, peak):
    px = query.shape[0]
    factor = score_scale * LOG2E

    def turn(i):
        k0 = chunk_at(i)
        vt[:, pl.ds(k0, CH)] = turned(vext[pl.ds(k0, CH)]).astype(BF)

    loop(vext.shape[0] // CH, turn)

    def tile(t):
        q0 = chunk_at(t)
        block = query[pl.ds(q0, CH)].astype(F32)
        for h in range(H):
            qm[h] = jnp.where(head_mask(h), block, 0.0).astype(BF)
        top[...] = jnp.full((H, CH), masked_score, F32)
        tot[...] = jnp.zeros((H, CH), F32)
        acc[...] = jnp.zeros((C, CH), F32)

        def keys(i):
            row = meta[t, 0] * 16 + i * CR
            base = pl.multiple_of(row * F, 128)
            bias[...] = score_bias(segk, segq, pl.multiple_of(row, 16), q0)
            key = kext[pl.ds(base, CH)]
            for h in range(H):
                raw = mm_nt(key, qm[h]) + bias[...]
                scores[h] = raw
                peak[h : h + 1] = jnp.maximum(top[h : h + 1], jnp.max(raw, axis=0, keepdims=True))
            for h in range(H):
                new = peak[h : h + 1]
                fade = jnp.exp2((top[h : h + 1] - new) * factor)
                weight = jnp.exp2((scores[h] - new) * factor)
                top[h : h + 1] = new
                tot[h : h + 1] = tot[h : h + 1] * fade + jnp.sum(weight, axis=0, keepdims=True)
                part = mm(vt[head_rows(h), pl.ds(base, CH)], weight.astype(BF))
                acc[head_rows(h)] = acc[head_rows(h)] * fade + part

        loop(meta[t, 1], keys)
        for h in range(H):
            acc[head_rows(h)] = acc[head_rows(h)] / tot[h : h + 1]
        lse[:, pl.ds(q0, CH)] = top[...] * factor + jnp.log2(tot[...])
        mixed_t[:, pl.ds(q0, CH)] = acc[...].astype(BF)
        mixed[pl.ds(q0, CH)] = acc[...].T.astype(BF)

    loop(px // CH, tile)


def attend(meta, query, kext, vext, segq, segk):
    px = query.shape[0]
    ext = kext.shape[0]
    return pl.pallas_call(
        attend_kernel,
        out_shape=[
            jax.ShapeDtypeStruct((px, C), BF),
            jax.ShapeDtypeStruct((C, px), BF),
            jax.ShapeDtypeStruct((H, px), F32),
        ],
        in_specs=[pl.BlockSpec(memory_space=pltpu.SMEM)] + vmem(5),
        out_specs=vmem(3),
        scratch_shapes=[
            pltpu.VMEM((C, ext), BF),
            pltpu.VMEM((H, CH, C), BF),
            pltpu.VMEM((CH, CH), F32),
            pltpu.VMEM((H, CH), F32),
            pltpu.VMEM((H, CH), F32),
            pltpu.VMEM((C, CH), F32),
            pltpu.VMEM((H, CH, CH), F32),
            pltpu.VMEM((H, CH), F32),
        ],
        compiler_params=pltpu.CompilerParams(vmem_limit_bytes=VMEM_LIMIT),
        name="attend",
    )(meta, query, kext, vext, segq, segk)


def attend_back_kernel(
    meta,
    query,
    kext,
    vext,
    segq,
    segk,
    gmix,
    mixed_t,
    lse,
    dq,
    dk,
    dv,
    kt,
    qm,
    gm,
    qt,
    gt,
    inner_rows,
    bias,
    dqt,
    dkt,
    dvt,
    kept,
    gscores,
):
    px = query.shape[0]
    ext = kext.shape[0]
    factor = score_scale * LOG2E

    def turn(i):
        k0 = chunk_at(i)
        kt[:, pl.ds(k0, CH)] = turned(kext[pl.ds(k0, CH)]).astype(BF)
        dkt[:, pl.ds(k0, CH)] = jnp.zeros((C, CH), F32)
        dvt[:, pl.ds(k0, CH)] = jnp.zeros((C, CH), F32)

    loop(ext // CH, turn)

    def tile(t):
        q0 = chunk_at(t)
        block = query[pl.ds(q0, CH)].astype(F32)
        grad = gmix[pl.ds(q0, CH)].astype(F32)
        for h in range(H):
            qm[h] = jnp.where(head_mask(h), block, 0.0).astype(BF)
            gm[h] = jnp.where(head_mask(h), grad, 0.0).astype(BF)
        qt[...] = block.T.astype(BF)
        grad_t = grad.T
        gt[...] = grad_t.astype(BF)
        crossed = grad_t * mixed_t[:, pl.ds(q0, CH)].astype(F32)
        inner_rows[...] = jnp.sum(crossed.reshape(H, HD, CH), axis=1)
        dqt[...] = jnp.zeros((C, CH), F32)

        def keys(i):
            row = meta[t, 0] * 16 + i * CR
            base = pl.multiple_of(row * F, 128)
            bias[...] = score_bias(segk, segq, pl.multiple_of(row, 16), q0)
            key = kext[pl.ds(base, CH)]
            val = vext[pl.ds(base, CH)]
            for h in range(H):
                raw = mm_nt(key, qm[h]) + bias[...]
                probs = jnp.exp2(raw * factor - lse[h : h + 1, pl.ds(q0, CH)])
                gprob = mm_nt(val, gm[h])
                kept[h] = probs.astype(BF)
                gscores[h] = (probs * (gprob - inner_rows[h : h + 1])).astype(BF)
            for h in range(H):
                dvt[head_rows(h), pl.ds(base, CH)] += mm_nt(gt[head_rows(h)], kept[h])
                dkt[head_rows(h), pl.ds(base, CH)] += mm_nt(qt[head_rows(h)], gscores[h])
                dqt[head_rows(h)] += mm(kt[head_rows(h), pl.ds(base, CH)], gscores[h])

        loop(meta[t, 1], keys)
        dq[pl.ds(q0, CH)] = (dqt[...] * score_scale).T.astype(BF)

    loop(px // CH, tile)

    def settle(i):
        k0 = chunk_at(i)
        dk[pl.ds(k0, CH)] = (dkt[:, pl.ds(k0, CH)] * score_scale).T.astype(BF)
        dv[pl.ds(k0, CH)] = dvt[:, pl.ds(k0, CH)].T.astype(BF)

    loop(ext // CH, settle)


def attend_back(meta, query, kext, vext, segq, segk, gmix, mixed_t, lse):
    px = query.shape[0]
    ext = kext.shape[0]
    return pl.pallas_call(
        attend_back_kernel,
        out_shape=[
            jax.ShapeDtypeStruct((px, C), BF),
            jax.ShapeDtypeStruct((ext, C), BF),
            jax.ShapeDtypeStruct((ext, C), BF),
        ],
        in_specs=[pl.BlockSpec(memory_space=pltpu.SMEM)] + vmem(8),
        out_specs=vmem(3),
        scratch_shapes=[
            pltpu.VMEM((C, ext), BF),
            pltpu.VMEM((H, CH, C), BF),
            pltpu.VMEM((H, CH, C), BF),
            pltpu.VMEM((C, CH), BF),
            pltpu.VMEM((C, CH), BF),
            pltpu.VMEM((H, CH), F32),
            pltpu.VMEM((CH, CH), F32),
            pltpu.VMEM((C, CH), F32),
            pltpu.VMEM((C, ext), F32),
            pltpu.VMEM((C, ext), F32),
            pltpu.VMEM((H, CH, CH), BF),
            pltpu.VMEM((H, CH, CH), BF),
        ],
        compiler_params=pltpu.CompilerParams(vmem_limit_bytes=VMEM_LIMIT),
        name="attend_back",
    )(meta, query, kext, vext, segq, segk, gmix, mixed_t, lse)


def middle_kernel(
    nf,
    inner,
    mixed,
    resid,
    cot,
    proj,
    mlp,
    vec,
    output,
    gafter,
    gmix,
    pack,
    sums,
    after_low,
    act_low,
    pre_low,
    down_low,
    mlp_low,
    after_grad_low,
    ubias,
    order,
):
    px = inner.shape[0]
    seg = CH // nf
    tail = 11 + FF // C
    order[...] = chunk_order(nf)
    sums[...] = jnp.zeros_like(sums)
    for j in range(FF // C):
        ubias[:, j * C : (j + 1) * C] = vec[11 + j : 12 + j]

    def step(c):
        p0 = chunk_at(c)
        after = inner[pl.ds(p0, CH)] + mm(mixed[pl.ds(p0, CH)], proj[4]) + vec[10:11]
        low = after.astype(BF)
        after_low[pl.ds(p0, CH)] = low
        grad_out = cot[pl.ds(p0, CH)]
        grad_mlp = mm_nt(grad_out, proj[5])
        down = grad_mlp.astype(BF)
        down_low[pl.ds(p0, CH)] = down
        total = after
        grad_after = grad_mlp
        for j in range(FF // C):
            part = slice(j * C, (j + 1) * C)
            pre = mm_nt(low, mlp[0, part]) + ubias[:, part]
            cdf = 0.5 + 0.5 * lax.erf(pre * (0.5**0.5))
            act = (pre * cdf).astype(BF)
            act_low[pl.ds(p0, CH), part] = act
            total = total + mm(act, mlp[1, part])
            density = jnp.exp(pre * pre * -0.5) * 0.3989422804014327
            grad_pre = mm_nt(down, mlp[1, part]) * (cdf + pre * density)
            sums[3 + j : 4 + j] += jnp.sum(grad_pre, axis=0, keepdims=True)
            grad_low = grad_pre.astype(BF)
            pre_low[pl.ds(p0, CH), part] = grad_low
            grad_after = grad_after + mm(grad_low, mlp[0, part])
        total = (total + vec[tail : tail + 1]).astype(BF)
        mlp_low[pl.ds(p0, CH)] = total
        branch = mm(total, proj[5]) + vec[tail + 1 : tail + 2]
        moved = mm_tn(order[...], (resid[pl.ds(p0, CH)] + branch).astype(BF)).astype(BF)
        for k in range(nf):
            output[k, rows_at(c * seg, seg)] = moved[k * seg : (k + 1) * seg]
        gafter[pl.ds(p0, CH)] = grad_after
        grad_low = grad_after.astype(BF)
        after_grad_low[pl.ds(p0, CH)] = grad_low
        gmix[pl.ds(p0, CH)] = mm_nt(grad_low, proj[4]).astype(BF)
        sums[0:1] += jnp.sum(grad_out.astype(F32), axis=0, keepdims=True)
        sums[1:2] += jnp.sum(grad_mlp, axis=0, keepdims=True)
        sums[2:3] += jnp.sum(grad_after, axis=0, keepdims=True)

    loop(px // CH, step)
    width = FF // nf
    for k in range(nf):
        part = slice(k * width, (k + 1) * width)
        pack[k, 0:width] = mm_tn(pre_low[:, part], after_low[...]).astype(BF)
        pack[k, width : 2 * width] = mm_tn(act_low[:, part], down_low[...]).astype(BF)
    depth = C // nf
    gw_attn = mm_tn(mixed[...], after_grad_low[...]).astype(BF)
    gw_out = mm_tn(mlp_low[...], cot[...]).astype(BF)
    for k in range(nf):
        part = slice(k * depth, (k + 1) * depth)
        pack[k, 2 * width : 2 * width + depth] = gw_attn[part]
        pack[k, 2 * width + depth : 2 * width + 2 * depth] = gw_out[part]


def middle(nf, inner, mixed, resid, cot, proj, mlp, vec):
    px = inner.shape[0]
    return pl.pallas_call(
        partial(middle_kernel, nf),
        out_shape=[
            jax.ShapeDtypeStruct((nf, px // nf, C), BF),
            jax.ShapeDtypeStruct((px, C), F32),
            jax.ShapeDtypeStruct((px, C), BF),
            jax.ShapeDtypeStruct((nf, 2 * (FF + C) // nf, C), BF),
            jax.ShapeDtypeStruct((8, C), F32),
        ],
        in_specs=vmem(7),
        out_specs=vmem(5),
        scratch_shapes=[
            pltpu.VMEM((px, C), BF),
            pltpu.VMEM((px, FF), BF),
            pltpu.VMEM((px, FF), BF),
            pltpu.VMEM((px, C), BF),
            pltpu.VMEM((px, C), BF),
            pltpu.VMEM((px, C), BF),
            pltpu.VMEM((1, FF), F32),
            pltpu.VMEM((CH, CH), BF),
        ],
        compiler_params=pltpu.CompilerParams(vmem_limit_bytes=VMEM_LIMIT),
        name="middle",
    )(inner, mixed, resid, cot, proj, mlp, vec)


def back_kernel(
    nt,
    nf,
    dq,
    dk,
    dv,
    gafter,
    inext,
    zhat1,
    zhat2,
    zhat3,
    rstd1,
    rstd2,
    rstd3,
    cot,
    conv,
    proj,
    vec,
    same,
    rowtab,
    cond,
    onehot,
    mid_sums,
    pack_a,
    out_blocks,
    output,
    glat,
    out_a,
    out_b,
    out_c,
    out_d,
    out_e,
    sums,
    film_rows,
    gmat,
    own_sums,
    rs,
    rq,
    mean_e,
    mean_ez,
    prev_mask,
    next_mask,
    normed_low,
    grad_low,
    gresid,
    dgrad,
    two,
    xc,
    shifted,
    rim_out,
    rim_got,
    to_left,
    to_right,
    from_left,
    from_right,
    order,
    glat_blocks,
    *rest,
):
    pack_b, pack_c, pack_d, pack_e = rest[:4]
    pieces = rest[4:28]
    msg_sems, kv_sems, block_sems, reduce_sems = rest[28:32]
    px = dq.shape[0]
    rows = px // F
    chunks = px // CH
    blk = px // nf
    seg = CH // nf
    spot, left, right = place(nt, nf)
    count = nt * nf
    where = (spot, count, left, right)
    f = lax.axis_index("freq")
    t = lax.axis_index("tm")
    s = snake(f, t, nf)
    partners = [{"freq": flip_by(f, mask)} for mask in range(1, nf)]
    partners = partners + [{"tm": flip(t, bit)} for bit in bits_of(nt)]
    enter(spot, count, left, right, partners)
    far_first, far_later = orders_of(nt)
    whole_d = out_d.shape[0]
    half = padded(whole_d // 2)
    plans = (
        (far_later, lambda i: pack_a.at[i], out_a),
        (far_first, lambda i: pack_b.at[i], out_b),
        (far_later, lambda i: pack_c.at[i], out_c),
        (far_first, lambda i: pack_d.at[i, 0:half], out_d.at[0:half]),
        (far_later, lambda i: pack_d.at[i, half:whole_d], out_d.at[half:whole_d]),
        (far_first, lambda i: pack_e.at[i], out_e),
    )
    jobs = []
    for index, (order_of, pack, out) in enumerate(plans):
        room = pieces[4 * index : 4 * index + 4]
        jobs.append(Reduce(order_of, pack, *room, out, reduce_sems.at[index], t, f))
    job_a, job_b, job_c, job_d, job_dd, job_e = jobs
    blocks = []
    for index, (source, landed) in enumerate(((out_blocks, output), (glat_blocks, glat))):
        blocks.append(
            Exchange(
                lambda peer, source=source: source.at[peer],
                lambda peer, landed=landed: landed.at[rows_at(s * blk, blk)],
                source.at[f],
                landed.at[rows_at(s * blk, blk)],
                f,
                nf,
                block_sems.at[index],
            )
        )
    def rim_grads(c):
        part = pl.ds(chunk_at(c), CH)
        for side in range(2):
            beyond = pl.ds(pl.multiple_of(2 * side * px + chunk_at(c), CH), CH)
            value = mm_nt(dk[beyond], proj[2]) + mm_nt(dv[beyond], proj[3])
            rim_out[side, part] = value.astype(BF)

    loop(chunks, rim_grads)
    rim_swap = Swap(
        where, rim_out.at[0], rim_out.at[1], rim_got.at[0], rim_got.at[1], kv_sems.at[0]
    )
    rim_swap.start()
    job_a.advance()
    order[...] = chunk_order(nf)
    clear_ends(spot, count, from_left, from_right)
    clear_ends(spot, count, rim_got.at[0], rim_got.at[1])
    gmat[...] = group_matrix()
    row_masks(rowtab, prev_mask, next_mask, rows)
    clip = Clip(same, rowtab, gmat, own_sums)
    sums[...] = jnp.zeros_like(sums)

    def v(i):
        return vec[i : i + 1]

    def first(c):
        p0 = chunk_at(c)
        part = pl.ds(p0, CH)
        own = pl.ds(pl.multiple_of(px + p0, CH), CH)
        normed_low[part] = (zhat3[part] * v(7) + v(8)).astype(BF)
        grad = gafter[part] + mm_nt(dq[part], proj[1])
        gresid[part] = grad + mm_nt(dk[own], proj[2]) + mm_nt(dv[own], proj[3])

    loop(chunks, first)
    depth = C // nf

    def proj_grad(which, grad):
        low = grad.astype(BF)
        for k in range(nf):
            pack_b[k, which * depth : (which + 1) * depth] = low[k * depth : (k + 1) * depth]

    proj_grad(1, mm_tn(inext[px : 2 * px], dq[...]))
    job_a.advance()
    rim_swap.wait()

    def row_sums(c, grad3, hat3):
        rs[pl.ds(chunk_at(c, CR), CR)] = jnp.sum(grad3, axis=1)
        rq[pl.ds(chunk_at(c, CR), CR)] = jnp.sum(grad3 * hat3, axis=1)

    def second(c):
        p0 = chunk_at(c)
        part = pl.ds(p0, CH)
        grad = gresid[part] + rim_got[0, part].astype(F32) + rim_got[1, part].astype(F32)
        sums[9:10] += jnp.sum(grad, axis=0, keepdims=True)
        low = grad.astype(BF)
        grad_low[part] = low
        d3 = mm_nt(low, proj[0])
        dgrad[part] = d3
        row_sums(c, d3.reshape(CR, F, C), zhat3[part].reshape(CR, F, C))

    loop(chunks, second)

    def swap_step(step, rim_first, rim_last):
        clip.pack(rs, rq, to_left.at[step], to_right.at[step])
        if rim_first is not None:
            to_left[step, 8 : 8 + rim_first.shape[0]] = rim_first
            to_right[step, 8 : 8 + rim_last.shape[0]] = rim_last
        swap = Swap(
            where,
            to_left.at[step],
            to_right.at[step],
            from_left.at[step],
            from_right.at[step],
            msg_sems.at[step],
        )
        swap.start()
        return swap

    def set_means(step, gain):
        mean_e[...], mean_ez[...] = clip.means(
            rs, rq, gain, from_left.at[step], from_right.at[step]
        )

    def back_norm(grad3, hat3, rstd, gain, r0, size):
        value = grad3 * gain - spread(mean_e[pl.ds(r0, size)], size)
        value = value - hat3 * spread(mean_ez[pl.ds(r0, size)], size)
        return value * spread(rstd[pl.ds(r0, size)], size)

    def rim_grad(step, at):
        both = jnp.concatenate([from_left[step, at : at + 8], from_right[step, at : at + 8]], axis=0)
        return both.reshape(2, F, C)

    sums[7:8] = jnp.sum(rq[...], axis=0, keepdims=True)
    sums[8:9] = jnp.sum(rs[...], axis=0, keepdims=True)
    cot_first = cot[0:16].astype(F32)[0:8]
    cot_last = cot[px - 16 : px].astype(F32)[8:16]
    swap = swap_step(
        0,
        jnp.concatenate([dgrad[0:8], cot_first], axis=0),
        jnp.concatenate([dgrad[px - 8 : px], cot_last], axis=0),
    )
    proj_grad(2, mm_tn(inext[...], dk[...]))
    proj_grad(3, mm_tn(inext[...], dv[...]))
    proj_grad(0, mm_tn(normed_low[...], grad_low[...]))
    job_b.advance()
    job_a.advance()
    swap.wait()
    set_means(0, v(7))

    def set_rims(value):
        low = value.astype(BF).astype(F32)
        two[0:8] = low[0]
        two[px + 8 : px + 16] = low[1]

    rim = rim_grad(0, 8)
    rim_hat = zhat3[px : px + 16].reshape(2, F, C)
    set_rims(rim_grad(0, 16) + back_norm(rim, rim_hat, rstd3, v(7), rows, 2))

    def third(c):
        p0 = chunk_at(c)
        part = pl.ds(p0, CH)
        grad3 = dgrad[part].reshape(CR, F, C)
        hat3 = zhat3[part].reshape(CR, F, C)
        value = back_norm(grad3, hat3, rstd3, v(7), chunk_at(c, CR), CR).reshape(CH, C)
        value = cot[part].astype(F32) + value
        gresid[part] = value
        sums[6:7] += jnp.sum(value, axis=0, keepdims=True)
        two[pl.ds(pl.multiple_of(p0 + 8, 8), CH)] = value.astype(BF).astype(F32)

    loop(chunks, third)

    def conv_inputs(zhat, gain, shift, c):
        p0 = chunk_at(c)
        part = pl.ds(p0, CH)
        r0 = chunk_at(c, CR)
        keep_prev = spread(prev_mask[pl.ds(r0, CR)], CR).reshape(CH, C) > 0.0
        keep_next = spread(next_mask[pl.ds(r0, CR)], CR).reshape(CH, C) > 0.0
        after = two[pl.ds(pl.multiple_of(p0 + 16, 16), CH)]
        here = two[pl.ds(pl.multiple_of(p0 + 8, 8), CH)]
        shifted[part, 0:C] = jnp.where(keep_next, after, 0.0).astype(BF)
        shifted[part, C : 2 * C] = here.astype(BF)
        shifted[part, 2 * C : 3 * C] = jnp.where(keep_prev, two[part], 0.0).astype(BF)
        pre = zhat[part] * gain + shift
        act = (pre * jax.nn.sigmoid(pre)).astype(BF).astype(F32).reshape(CR, F, C)
        store_shifts(xc, p0, act, CR)

    def conv_back(kernel, zhat, gain, shift, c):
        part = pl.ds(chunk_at(c), CH)
        hat = zhat[part]
        pre = hat * gain + shift
        sig = jax.nn.sigmoid(pre)

        def columns(j):
            piece = slice(j * C, (j + 1) * C)
            value = mm_nt(shifted[part, 0:C], kernel[0 : 3 * C][piece])
            value = value + mm_nt(shifted[part, C : 2 * C], kernel[3 * C : 6 * C][piece])
            value = value + mm_nt(shifted[part, 2 * C : 3 * C], kernel[6 * C : 9 * C][piece])
            return value.reshape(CR, F, C)

        col = column_index(CR)
        back = columns(1)
        back = back + jnp.where(col == F - 1, 0.0, pltpu.roll(columns(0), F - 1, 1))
        back = back + jnp.where(col == 0, 0.0, pltpu.roll(columns(2), 1, 1))
        grad = back.reshape(CH, C) * sig * (1.0 + pre * (1.0 - sig))
        dgrad[part] = grad
        row_sums(c, grad.reshape(CR, F, C), hat.reshape(CR, F, C))

    share = TAPS * C // nf

    def kernel_grad(pack):
        for k in range(nf):
            if pack.shape[1] > share:
                pack[k, share:] = jnp.zeros((pack.shape[1] - share, C), BF)
        for d in range(3):
            for j in range(3):
                grad = mm_tn(xc[:, j * C : (j + 1) * C], shifted[:, d * C : (d + 1) * C])
                low = grad.astype(BF)
                start = (d * 3 + j) * C
                end = start + C
                at = start
                while at < end:
                    k = at // share
                    upto = min(end, (k + 1) * share)
                    pack[k, at - k * share : upto - k * share] = low[at - start : upto - start]
                    at = upto

    def step_two(c):
        conv_inputs(zhat2, v(4), v(5), c)
        conv_back(conv.at[1], zhat2, v(4), v(5), c)

    loop(chunks, step_two)
    sums[4:5] = jnp.sum(rq[...], axis=0, keepdims=True)
    sums[5:6] = jnp.sum(rs[...], axis=0, keepdims=True)
    swap = swap_step(1, dgrad[0:8], dgrad[px - 8 : px])
    job_a.advance()
    blocks[0].start()
    kernel_grad(pack_c)
    job_c.advance()
    job_b.advance()
    swap.wait()
    set_means(1, v(4))
    rim_hat = zhat2[px : px + 16].reshape(2, F, C)
    set_rims(back_norm(rim_grad(1, 8), rim_hat, rstd2, v(4), rows, 2))

    def fourth(c):
        p0 = chunk_at(c)
        part = pl.ds(p0, CH)
        grad3 = dgrad[part].reshape(CR, F, C)
        hat3 = zhat2[part].reshape(CR, F, C)
        value3 = back_norm(grad3, hat3, rstd2, v(4), chunk_at(c, CR), CR)
        film_rows[pl.ds(chunk_at(c, CR), CR)] = jnp.sum(value3, axis=1)
        low = value3.reshape(CH, C).astype(BF).astype(F32)
        two[pl.ds(pl.multiple_of(p0 + 8, 8), CH)] = low

    loop(chunks, fourth)
    total = jnp.sum(film_rows[...], axis=0, keepdims=True)
    sums[2:3] = total
    sums[3:4] = total
    loop(chunks, partial(conv_inputs, zhat1, v(0), v(1)))
    kernel_grad(pack_d)
    grad_film = hdot_tn(onehot[...], film_rows[...])
    gemb = hdot_tn(cond[...].astype(F32), grad_film).astype(BF)
    edepth = gemb.shape[0] // nf
    job_d.advance()
    job_dd.advance()

    def sums_one(c):
        conv_back(conv.at[0], zhat1, v(0), v(1), c)

    loop(chunks, sums_one)
    sums[0:1] = jnp.sum(rq[...], axis=0, keepdims=True)
    sums[1:2] = jnp.sum(rs[...], axis=0, keepdims=True)
    swap = swap_step(2, None, None)
    tail = jnp.concatenate(
        [
            sums[0:10],
            mid_sums[2:3],
            mid_sums[3 : 3 + FF // C],
            mid_sums[1:2],
            mid_sums[0:1],
            jnp.zeros((32 - 13 - FF // C, C), F32),
        ],
        axis=0,
    ).astype(BF)
    for k in range(nf):
        pack_e[k, 0:edepth] = gemb[k * edepth : (k + 1) * edepth]
        pack_e[k, edepth : edepth + 32] = tail
        pack_e[k, edepth + 32 :] = jnp.zeros((pack_e.shape[1] - edepth - 32, C), BF)
    job_e.advance()
    for job in (job_d, job_dd, job_c, job_a, job_b):
        job.advance()
    swap.wait()
    set_means(2, v(0))

    def fifth(c):
        p0 = chunk_at(c)
        part = pl.ds(p0, CH)
        grad3 = dgrad[part].reshape(CR, F, C)
        hat3 = zhat1[part].reshape(CR, F, C)
        value = back_norm(grad3, hat3, rstd1, v(0), chunk_at(c, CR), CR).reshape(CH, C)
        moved = mm_tn(order[...], (gresid[part] + value).astype(BF)).astype(BF)
        for k in range(nf):
            glat_blocks[k, rows_at(c * seg, seg)] = moved[k * seg : (k + 1) * seg]

    loop(chunks, fifth)
    turns = 0
    while turns <= 3 or not all(job.done() for job in jobs):
        if turns == 3:
            blocks[1].start()
        for job in (job_e, job_d, job_dd, job_c, job_a, job_b):
            job.advance()
        turns += 1
    for block in blocks:
        block.wait()


def back(nt, nf, *args):
    px = args[0].shape[0]
    rows = px // F
    tab = args[-6].shape[0]
    pack_rows = args[-2].shape[1]
    edepth = args[-5].shape[1] // nf
    share = TAPS * C // nf
    heights = (pack_rows, 4 * C // nf, share, share, padded(edepth + 32))
    half = padded(share // 2)
    job_heights = heights[:3] + (half, share - half) + heights[4:]
    buffers = [pltpu.VMEM((nf, u, C), BF) for u in heights[1:]]
    for u in job_heights:
        buffers.extend(
            [
                pltpu.VMEM((2, u, C), BF),
                pltpu.VMEM((2, u, C), BF),
                pltpu.VMEM((u, C), BF),
                pltpu.VMEM((2, 2 * u, C), BF),
            ]
        )
    big = pltpu.VMEM((px, C), F32)
    low = pltpu.VMEM((px, C), BF)
    table = pltpu.VMEM((rows, C), F32)
    return pl.pallas_call(
        partial(back_kernel, nt, nf),
        out_shape=[
            jax.ShapeDtypeStruct((px, C), BF),
            jax.ShapeDtypeStruct((px, C), BF),
        ]
        + [jax.ShapeDtypeStruct((u, C), BF) for u in heights],
        in_specs=vmem(len(args)),
        out_specs=vmem(7),
        scratch_shapes=[
            pltpu.VMEM((16, C), F32),
            pltpu.VMEM((rows, C), F32),
            pltpu.VMEM((C, C), BF),
            pltpu.VMEM((2, tab, C), F32),
            table,
            table,
            pltpu.VMEM((tab, C), F32),
            pltpu.VMEM((tab, C), F32),
            table,
            table,
            low,
            low,
            big,
            big,
            pltpu.VMEM((px + 16, C), F32),
            pltpu.VMEM((px, 3 * C), BF),
            pltpu.VMEM((px, 3 * C), BF),
            pltpu.VMEM((2, px, C), BF),
            pltpu.VMEM((2, px, C), BF),
            pltpu.VMEM((3, 24, C), F32),
            pltpu.VMEM((3, 24, C), F32),
            pltpu.VMEM((3, 24, C), F32),
            pltpu.VMEM((3, 24, C), F32),
            pltpu.VMEM((CH, CH), BF),
            pltpu.VMEM((nf, px // nf, C), BF),
            *buffers,
            pltpu.SemaphoreType.DMA((3, 4)),
            pltpu.SemaphoreType.DMA((2, 4)),
            pltpu.SemaphoreType.DMA((2, nf - 1, 2)),
            pltpu.SemaphoreType.DMA((6, stage_count(nt), 2)),
        ],
        compiler_params=pltpu.CompilerParams(
            collective_id=2, has_side_effects=True, vmem_limit_bytes=VMEM_LIMIT
        ),
        name="back",
    )(*args)


def adamw_step(weight, moment, second, grad, decay_rate):
    moment_new = beta_first * moment + (1.0 - beta_first) * grad
    second_new = beta_second * second + (1.0 - beta_second) * grad * grad
    moment_hat = moment_new / (1.0 - beta_first**STEP)
    second_hat = second_new / (1.0 - beta_second**STEP)
    weight_new = weight - learn_rate * (
        moment_hat / (jnp.sqrt(second_hat) + adam_eps) + decay_rate * weight
    )
    return (weight_new, moment_new, second_new)


def adam_kernel(sum_a, sum_b, sum_c, sum_d, sum_e, *refs):
    masters, moments, seconds = refs[0:5], refs[5:10], refs[10:15]
    news, bias = refs[15:30], refs[30]
    i = pl.program_id(0)

    def update(kind, at, grad, decay):
        values = adamw_step(
            masters[kind][at], moments[kind][at], seconds[kind][at], grad.astype(F32), decay
        )
        for k, value in enumerate(values):
            news[3 * kind + k][at] = value

    def block(total, start, size):
        return total[rows_at(start + i * size, size)]

    cdepth, pdepth, mdepth, edepth = (
        masters[0].shape[1],
        masters[1].shape[1],
        masters[2].shape[1],
        masters[3].shape[0],
    )
    steps = sum_d.shape[0] // cdepth
    update(0, 0, block(sum_d, 0, cdepth), weight_decay)
    update(0, 1, block(sum_c, 0, cdepth), weight_decay)
    whole_p, whole_m, whole_e = pdepth * steps, mdepth * steps, edepth * steps
    for k in range(4):
        update(1, k, block(sum_b, k * whole_p, pdepth), weight_decay)
    for k in range(2):
        update(1, 4 + k, block(sum_a, 2 * whole_m + k * whole_p, pdepth), weight_decay)
        update(2, k, block(sum_a, k * whole_m, mdepth), weight_decay)
    update(3, slice(None), block(sum_e, 0, edepth), weight_decay)

    @pl.when(i == 0)
    def _():
        nsmall, width = masters[4].shape
        first = lax.axis_index("freq") * width
        source = lax.broadcasted_iota(jnp.int32, (C, width), 0)
        chosen = source == first + lax.broadcasted_iota(jnp.int32, (C, width), 1)
        grad = mm(sum_e[whole_e : whole_e + 32], chosen.astype(BF))
        update(4, slice(None), grad[0:nsmall], 0.0)
        bias[...] = grad[nsmall - 1 : nsmall]


def adam(sums, masters, moments, seconds):
    steps = 4

    def whole(array):
        return pl.BlockSpec(array.shape, lambda i: (0,) * array.ndim)

    def piece(array):
        if array.ndim == 3:
            shape = (array.shape[0], array.shape[1] // steps, C)
            return pl.BlockSpec(shape, lambda i: (0, i, 0))
        if array.shape[1] == C:
            return pl.BlockSpec((array.shape[0] // steps, C), lambda i: (i, 0))
        return whole(array)

    specs = [piece(array) for array in masters]
    out_shapes, out_specs = [], []
    for array, spec in zip(masters, specs):
        out_shapes.extend([jax.ShapeDtypeStruct(array.shape, F32)] * 3)
        out_specs.extend([spec] * 3)
    width = masters[4].shape[1]
    out_shapes.append(jax.ShapeDtypeStruct((1, width), F32))
    out_specs.append(pl.BlockSpec((1, width), lambda i: (0, 0)))
    return pl.pallas_call(
        adam_kernel,
        grid=(steps,),
        out_shape=out_shapes,
        in_specs=[whole(array) for array in sums] + specs * 3,
        out_specs=out_specs,
        compiler_params=pltpu.CompilerParams(vmem_limit_bytes=VMEM_LIMIT),
        name="adam",
    )(*sums, *masters, *moments, *seconds)


def layout_kernel(
    nt,
    nf,
    len_row,
    condition,
    weight,
    same,
    rowtab,
    segk,
    segq,
    meta,
    onehot,
    cond,
    wsmall,
    wide,
):
    rows, clips = onehot.shape
    tab = rowtab.shape[0]
    f = lax.axis_index("freq")
    t = lax.axis_index("tm")
    total_rows = nt * nf * rows
    first_row = (t * nf + snake(f, t, nf)) * rows

    def iota(shape, dim):
        return lax.broadcasted_iota(jnp.int32, shape, dim)

    down = iota((clips, clips), 0)
    across = iota((clips, clips), 1)
    lengths = len_row[...].astype(F32)
    len_col = jnp.sum(jnp.where(down == across, lengths, 0.0), axis=1, keepdims=True)
    ends_col = jnp.sum(jnp.where(across <= down, lengths, 0.0), axis=1, keepdims=True)
    ends = jnp.sum(jnp.where(down <= across, len_col, 0.0), axis=0, keepdims=True)

    def finished(row):
        return ends <= row.astype(F32)

    def seg_of(row):
        seg = jnp.sum(jnp.where(finished(row), 1.0, 0.0), axis=1, keepdims=True)
        return jnp.where((row >= 0) & (row < total_rows), seg, -1.0)

    def seg_lanes(row):
        return jnp.sum(jnp.where(ends_col <= row.astype(F32), 1.0, 0.0), axis=0, keepdims=True)

    ext_row = first_row - rows + iota((3 * rows, 1), 0)
    segk[...] = jnp.broadcast_to(seg_of(ext_row), segk.shape)
    pixel = iota((1, rows * F), 1)
    segq[...] = jnp.broadcast_to(seg_lanes(first_row + pixel // F), segq.shape)
    seg_row = seg_lanes(first_row + iota((1, rows), 1))
    index = iota((tab + 8, 1), 0)
    at = jnp.where(index < rows, first_row + index, first_row)
    at = jnp.where(index == rows, first_row - 1, at)
    at = jnp.where(index == rows + 1, first_row + rows, at)
    at = jnp.where(index == tab + 1, first_row + rows - 1, at)
    unused = ((index > rows + 1) & (index < tab)) | (index > tab + 1)
    seg_tab = jnp.where(unused, -2.0, seg_of(at))
    same[...] = (seg_tab == seg_row).astype(BF)
    clip_lane = iota((tab + 8, clips), 1).astype(F32)
    hot = jnp.where(seg_tab == clip_lane, 1.0, 0.0)
    onehot[...] = hot[0:rows]
    row_len = jnp.sum(hot * lengths, axis=1, keepdims=True)
    inner = index < rows
    fields = (
        1.0 / jnp.maximum(row_len * (F * GW), 1.0),
        jnp.where(seg_tab == seg_of(first_row - 1 + 0 * index), 1.0, 0.0),
        jnp.where(seg_tab == seg_of(first_row + rows + 0 * index), 1.0, 0.0),
        jnp.where(inner & (seg_tab == seg_of(at - 1)), 1.0, 0.0),
        jnp.where(inner & (seg_tab == seg_of(at + 1)), 1.0, 0.0),
    )
    lane = iota((tab + 8, 128), 1)
    values = jnp.zeros((tab + 8, 128), F32)
    for place_at, field in enumerate(fields):
        values = jnp.where(lane == place_at, field, values)
    rowtab[...] = values[0:tab]
    tile = iota((8, 1), 0)

    def bounds(row):
        low = jnp.sum(jnp.where(finished(row), lengths, 0.0), axis=1, keepdims=True)
        seg = jnp.sum(jnp.where(finished(row), 1.0, 0.0), axis=1, keepdims=True)
        here = iota((8, clips), 1).astype(F32) == seg
        return low, low + jnp.sum(jnp.where(here, lengths, 0.0), axis=1, keepdims=True)

    low_row = bounds(first_row + tile * CR)[0].astype(jnp.int32) - first_row + rows
    high_row = bounds(first_row + tile * CR + CR - 1)[1].astype(jnp.int32) - first_row + rows
    low = low_row // 16
    number = (high_row - low * 16 + CR - 1) // CR
    low = jnp.minimum(low, (3 * rows - number * CR) // 16)
    meta[...] = jnp.where(iota((8, 128), 1) == 0, low, number)
    value = condition[...]
    cond[...] = (value * jax.nn.sigmoid(value)).astype(BF)
    nsmall, width = weight.shape
    wide[...] = jnp.zeros_like(wide)
    wide[0:nsmall] = weight[...]
    chosen = iota((width, C), 1) == f * width + iota((width, C), 0)
    wsmall[...] = mm(wide[...].astype(BF), chosen.astype(BF))


def layout_of(nt, nf, lengths, condition, weight, rows):
    clips = lengths.shape[0]
    tab = rows + 8
    shapes = (
        ((tab + 8, rows), BF),
        ((tab, 128), F32),
        ((3 * rows, 128), F32),
        ((8, rows * F), F32),
        ((8, 128), jnp.int32),
        ((rows, clips), F32),
        (condition.shape, BF),
        ((32, C), F32),
    )
    return pl.pallas_call(
        partial(layout_kernel, nt, nf),
        out_shape=[jax.ShapeDtypeStruct(s, d) for s, d in shapes],
        in_specs=vmem(3),
        out_specs=vmem(len(shapes)),
        scratch_shapes=[pltpu.VMEM((32, weight.shape[1]), F32)],
        compiler_params=pltpu.CompilerParams(vmem_limit_bytes=VMEM_LIMIT),
        name="layout",
    )(
        lengths.reshape(1, clips),
        condition,
        weight,
    )


def on_device(
    nt,
    nf,
    latent,
    condition,
    lengths,
    cotangent,
    conv_weight,
    conv_moment,
    conv_second,
    proj_weight,
    proj_moment,
    proj_second,
    mlp_weight,
    mlp_moment,
    mlp_second,
    emb_weight,
    emb_moment,
    emb_second,
    small_weight,
    small_moment,
    small_second,
):
    rows = latent.shape[0] // nf
    same, rowtab, segk, segq, meta, onehot, cond_low, wsmall = layout_of(
        nt, nf, lengths, condition, small_weight, rows
    )
    (
        conv_full,
        proj_full,
        mlp_full,
        vec,
        cot,
        zhat1,
        zhat2,
        zhat3,
        rstd1,
        rstd2,
        rstd3,
        resid,
        inner,
        query,
        kext,
        vext,
        inext,
    ) = front(
        nt,
        nf,
        latent.reshape(-1, C),
        cotangent.reshape(-1, C),
        conv_weight,
        proj_weight,
        mlp_weight,
        emb_weight,
        wsmall,
        cond_low,
        onehot,
        same,
        rowtab,
    )
    mixed, mixed_t, lse = attend(meta, query, kext, vext, segq, segk)
    out_blocks, gafter, gmix, pack_a, mid_sums = middle(
        nf, inner, mixed, resid, cot, proj_full, mlp_full, vec
    )
    dq, dk, dv = attend_back(
        meta, query, kext, vext, segq, segk, gmix, mixed_t, lse
    )
    output, glat, sum_a, sum_b, sum_c, sum_d, sum_e = back(
        nt,
        nf,
        dq,
        dk,
        dv,
        gafter,
        inext,
        zhat1,
        zhat2,
        zhat3,
        rstd1,
        rstd2,
        rstd3,
        cot,
        conv_full,
        proj_full,
        vec,
        same,
        rowtab,
        cond_low,
        onehot,
        mid_sums,
        pack_a,
        out_blocks,
    )
    masters = (conv_weight, proj_weight, mlp_weight, emb_weight, small_weight)
    moments = (conv_moment, proj_moment, mlp_moment, emb_moment, small_moment)
    seconds = (conv_second, proj_second, mlp_second, emb_second, small_second)
    *updated, bias = adam((sum_a, sum_b, sum_c, sum_d, sum_e), masters, moments, seconds)
    return (
        output.reshape(latent.shape),
        glat.reshape(latent.shape),
        *updated,
        bias.reshape(-1),
    )


def solution(mesh):
    nt, nf = mesh.shape["tm"], mesh.shape["freq"]
    rows_spec = P("tm", "freq", None)
    middle_spec = P(None, "freq", None)
    params = (middle_spec,) * 9 + (P("freq", None),) * 3 + (P(None, "freq"),) * 3
    return jax.shard_map(
        partial(on_device, nt, nf),
        mesh=mesh,
        in_specs=(rows_spec, P(), P(), rows_spec) + params,
        out_specs=(rows_spec, rows_spec) + params + (P("freq"),),
        check_vma=False,
    )
```

```python
from functools import partial

import jax
import jax.numpy as jnp
from jax import lax
from jax.experimental import pallas as pl
from jax.experimental.pallas import tpu as pltpu
from jax.sharding import PartitionSpec as P

C = 256
G = 32
GW = C // G
HD = 32
H = C // HD
FF = 1024
F = 8
MAXLEN = 128
STEP = 10
TAPS = 9
CH = 256
CR = CH // F

HIGHEST = lax.Precision.HIGHEST
norm_eps = 1e-05
beta_first = 0.9
beta_second = 0.999
learn_rate = 0.5
weight_decay = 0.01
adam_eps = 1e-08
masked_score = -1e30
score_scale = HD**-0.5
LOG2E = 1.4426950408889634
MESH = pltpu.DeviceIdType.MESH if hasattr(pltpu, "DeviceIdType") else pl.DeviceIdType.MESH
VMEM_LIMIT = 64 * 1024 * 1024 - 65536
BF = jnp.bfloat16
F32 = jnp.float32


def mm(a, b):
    return jnp.dot(a, b, preferred_element_type=F32)


def mm_nt(a, b):
    return lax.dot_general(a, b, (((1,), (1,)), ((), ())), preferred_element_type=F32)


def mm_tn(a, b):
    return lax.dot_general(a, b, (((0,), (0,)), ((), ())), preferred_element_type=F32)


def hdot(a, b):
    return jnp.dot(a, b, precision=HIGHEST, preferred_element_type=F32)


def thirds(x):
    high = x.astype(BF)
    rest = x - high.astype(F32)
    middle = rest.astype(BF)
    low = (rest - middle.astype(F32)).astype(BF)
    return high, middle, low


def hdot_tn(a, b):
    return lax.dot_general(
        a, b, (((0,), (0,)), ((), ())), precision=HIGHEST, preferred_element_type=F32
    )


def place(nt, nf):
    t = lax.axis_index("tm")
    f = lax.axis_index("freq")
    odd = lax.rem(t, 2)
    s = f + odd * (nf - 1 - 2 * f)
    turn = 1 - 2 * odd
    at_end = (s + 1) // nf
    at_start = 1 - (s + nf - 1) // nf
    right = {"tm": t + at_end, "freq": f + (1 - at_end) * turn}
    left = {"tm": t - at_start, "freq": f - (1 - at_start) * turn}
    return t * nf + s, left, right


def flip(x, bit):
    return x + bit - 2 * bit * lax.rem(x // bit, 2)


def flip_by(x, mask):
    bit = 1
    while bit <= mask:
        if mask & bit:
            x = flip(x, bit)
        bit *= 2
    return x


def bits_of(count):
    bits = []
    bit = 1
    while bit < count:
        bits.append(bit)
        bit *= 2
    return bits


def snake(f, t, nf):
    return f + lax.rem(t, 2) * (nf - 1 - 2 * f)


def enter(spot, count, left, right, partners):
    barrier = pltpu.get_barrier_semaphore()
    for partner in partners:
        pl.semaphore_signal(barrier, inc=1, device_id=partner, device_id_type=MESH)

    @pl.when(spot > 0)
    def _():
        pl.semaphore_signal(barrier, inc=1, device_id=left, device_id_type=MESH)

    @pl.when(spot < count - 1)
    def _():
        pl.semaphore_signal(barrier, inc=1, device_id=right, device_id_type=MESH)

    inside = (spot > 0) & (spot < count - 1)

    @pl.when(inside)
    def _():
        pl.semaphore_wait(barrier, len(partners) + 2)

    @pl.when(jnp.logical_not(inside))
    def _():
        pl.semaphore_wait(barrier, len(partners) + 1)


class Swap:
    def __init__(self, where, to_left, to_right, from_left, from_right, sems):
        self.spot, self.count, left, right = where
        self.go_left = pltpu.make_async_remote_copy(
            src_ref=to_left,
            dst_ref=from_right,
            send_sem=sems.at[0],
            recv_sem=sems.at[1],
            device_id=left,
            device_id_type=MESH,
        )
        self.go_right = pltpu.make_async_remote_copy(
            src_ref=to_right,
            dst_ref=from_left,
            send_sem=sems.at[2],
            recv_sem=sems.at[3],
            device_id=right,
            device_id_type=MESH,
        )

    def start(self):
        @pl.when(self.spot > 0)
        def _():
            self.go_left.start()

        @pl.when(self.spot < self.count - 1)
        def _():
            self.go_right.start()

    def wait(self):
        @pl.when(self.spot > 0)
        def _():
            self.go_left.wait_send()
            self.go_right.wait_recv()

        @pl.when(self.spot < self.count - 1)
        def _():
            self.go_right.wait_send()
            self.go_left.wait_recv()


def remote(src, dst, sems, device):
    return pltpu.make_async_remote_copy(
        src_ref=src,
        dst_ref=dst,
        send_sem=sems.at[0],
        recv_sem=sems.at[1],
        device_id=device,
        device_id_type=MESH,
    )


class Exchange:
    def __init__(self, source, target, own_source, own_target, f, nf, sems):
        self.copies = []
        for mask in range(1, nf):
            peer = flip_by(f, mask)
            self.copies.append(
                remote(source(peer), target(peer), sems.at[mask - 1], {"freq": peer})
            )
        self.own_source, self.own_target = own_source, own_target

    def start(self):
        for copy in self.copies[::-1]:
            copy.start()
        self.own_target[...] = self.own_source[...]

    def wait(self):
        for copy in self.copies:
            copy.wait()


class Gather:
    def __init__(self, view, f, t, sems, size=None):
        near = {"freq": flip(f, 1)}
        far = flip(f, 2)
        self.halves = size is not None
        if self.halves:
            side = lax.rem(t, 2)
            mine, other = (side, size // 2), (1 - side, size // 2)
        else:
            mine = (0, None)
        beside = {"tm": flip(t, 1)}
        self.far = remote(view(f, mine), view(f, mine), sems.at[0], {"freq": far})
        self.near = remote(view(f, (0, None)), view(f, (0, None)), sems.at[1], near)
        self.forward = remote(view(far, mine), view(far, mine), sems.at[2], near)
        if self.halves:
            self.cross = remote(view(far, mine), view(far, mine), sems.at[3], beside)
            self.second = remote(view(far, other), view(far, other), sems.at[4], near)

    def start(self):
        self.far.start()
        self.near.start()

    def relay(self):
        self.far.wait_recv()
        if self.halves:
            self.cross.start()
        self.forward.start()

    def collect(self):
        if self.halves:
            self.cross.wait_recv()
            self.second.start()
        self.near.wait_recv()
        self.forward.wait_recv()
        if self.halves:
            self.second.wait_recv()

    def finish(self):
        self.far.wait_send()
        self.near.wait_send()
        self.forward.wait_send()
        if self.halves:
            self.cross.wait_send()
            self.second.wait_send()


def share_view(ref, depth, lead):
    def view(i, part):
        which, size = part
        start = i * depth if size is None else i * depth + which * size
        rows = rows_at(start, depth if size is None else size)
        return ref.at[lead, rows] if lead is not None else ref.at[rows]

    return view


def rows_at(start, size):
    return pl.ds(pl.multiple_of(start, 16), size)


def piece_of(n):
    for size in (128, 96, 80, 64, 48, 32):
        if n % size == 0:
            return size
    return 16


def add_rows(dst, to, a, a_at, b, b_at, n):
    size = piece_of(n)

    def step(i):
        left = a[rows_at(a_at + i * size, size)].astype(F32)
        right = b[rows_at(b_at + i * size, size)].astype(F32)
        dst[rows_at(to + i * size, size)] = (left + right).astype(BF)

    loop(n // size, step)


class Reduce:
    def __init__(self, order, pack, got, acc, far, rs, out, sems, t, f):
        u = far.shape[0]
        near = {"freq": flip(f, 1)}
        one = remote(pack(flip_by(f, 1)), got.at[0], sems.at[0], near)
        two = remote(pack(flip_by(f, 3)), got.at[1], sems.at[1], near)

        def add_near():
            add_rows(acc.at[1], 0, pack(flip(f, 2)), 0, got.at[1], 0, u)
            add_rows(acc.at[0], 0, pack(f), 0, got.at[0], 0, u)

        self.stages = [((two, one), add_near)]
        gathers = []
        n, at, base, place_at = u, 0, 0, 2
        slots = 2
        for bit in order:
            last = bit == order[-1]
            if bit == 0:
                rows = rows_at(at, n)
                copy = remote(
                    acc.at[1, rows], far.at[0:n], sems.at[place_at], {"freq": flip(f, 2)}
                )
                finish = partial(add_rows, acc.at[0], at, acc.at[0], at, far, 0, n)
                self.stages.append(((copy,), finish))
                slots, place_at = 1, place_at + 1
                continue
            peer = {"tm": flip(t, bit)}
            half = n % 32 == 0 and not last
            if half:
                upper = lax.rem(t // bit, 2)
                n = n // 2
                keep, give = at + upper * n, at + (1 - upper) * n
            else:
                keep, give = at, at
            copy = remote(
                acc.at[0:slots, rows_at(give, n)],
                rs.at[0:slots, base : base + n],
                sems.at[place_at],
                peer,
            )

            def finish(slots=slots, keep=keep, base=base, n=n, last=last):
                for slot in range(slots):
                    target = out if last else acc.at[slot]
                    add_rows(target, keep, acc.at[slot], keep, rs.at[slot], base, n)

            self.stages.append(((copy,), finish))
            if half:
                share = out.at[rows_at(keep, n)]
                gathers.append(((remote(share, share, sems.at[place_at + 1], peer),), None))
            at, base, place_at = keep, base + n, place_at + 2
        self.stages.extend(gathers[::-1])
        self.now = -1

    def done(self):
        return self.now >= len(self.stages)

    def advance(self):
        if self.done():
            return
        if self.now >= 0:
            copies, finish = self.stages[self.now]
            for copy in copies:
                copy.wait()
            if finish is not None:
                finish()
        self.now += 1
        if not self.done():
            for copy in self.stages[self.now][0]:
                copy.start()


def orders_of(nt):
    bits = bits_of(nt)
    far_first = [0] + bits
    if len(bits) < 2:
        return far_first, far_first
    return far_first, [bits[1], 0, bits[0]] + bits[2:]


def stage_count(nt):
    return 3 + 2 * len(bits_of(nt))


def padded(rows):
    return (rows + 63) // 64 * 64


def chunk_order(nf):
    width = F // nf
    row = lax.broadcasted_iota(jnp.int32, (CH, CH), 0)
    source = lax.broadcasted_iota(jnp.int32, (CH, CH), 1)
    col = lax.rem(row, F)
    wanted = (col // width) * (CR * width) + (row // F) * width + lax.rem(col, width)
    return jnp.where(source == wanted, 1.0, 0.0).astype(BF)


def clear_ends(spot, count, from_left, from_right):
    @pl.when(spot == 0)
    def _():
        from_left[...] = jnp.zeros_like(from_left)

    @pl.when(spot == count - 1)
    def _():
        from_right[...] = jnp.zeros_like(from_right)


def group_matrix():
    i = lax.broadcasted_iota(jnp.int32, (C, C), 0) // GW
    j = lax.broadcasted_iota(jnp.int32, (C, C), 1) // GW
    return (i == j).astype(BF)


def spread(rows, count):
    return jnp.broadcast_to(rows[:, None, :], (count, F, C))


def column_index(count):
    return lax.broadcasted_iota(jnp.int32, (count, F, C), 1)


def column_shifts(act, count):
    col = column_index(count)
    before = jnp.where(col == 0, 0.0, pltpu.roll(act, 1, 1))
    after = jnp.where(col == F - 1, 0.0, pltpu.roll(act, F - 1, 1))
    return before, after


def store_shifts(xc, at, act, count):
    before, after = column_shifts(act, count)
    size = count * F
    xc[pl.ds(at, size), 0:C] = before.reshape(size, C).astype(BF)
    xc[pl.ds(at, size), C : 2 * C] = act.reshape(size, C).astype(BF)
    xc[pl.ds(at, size), 2 * C : 3 * C] = after.reshape(size, C).astype(BF)


def loop(count, body):
    def step(i, carry):
        body(i)
        return carry

    lax.fori_loop(0, count, step, 0)


def chunk_at(i, size=CH):
    return pl.multiple_of(i * size, size)


class Clip:
    def __init__(self, same, rowtab, gmat, local):
        self.same, self.rowtab, self.gmat, self.local = same, rowtab, gmat, local

    def pack(self, rs, rq, to_left, to_right):
        tab = self.rowtab.shape[0]
        for index, table in ((0, rs), (1, rq)):
            total = 0.0
            for part in thirds(table[...])[::-1]:
                total = total + mm(self.same[...], part)
            self.local[index] = total[0:tab]
            to_left[index : index + 1] = total[tab : tab + 1]
            to_right[index : index + 1] = total[tab + 1 : tab + 2]

    def means(self, rs, rq, gain, from_left, from_right):
        at_left = self.rowtab[:, 1:2] > 0.0
        at_right = self.rowtab[:, 2:3] > 0.0
        inverse = self.rowtab[:, 0:1]
        tab = self.rowtab.shape[0]
        parts = []
        for index in range(2):
            total = self.local[index]
            total = total + jnp.where(at_left, from_left[index : index + 1], 0.0)
            total = total + jnp.where(at_right, from_right[index : index + 1], 0.0)
            total = total * inverse
            if gain is not None:
                total = total * gain
            parts.append(thirds(total))
        results = []
        for high, middle, low in parts:
            value = mm(low, self.gmat[...]) + mm(middle, self.gmat[...])
            results.append(value + mm(high, self.gmat[...]))
        return results


def row_masks(rowtab, prev_mask, next_mask, rows):
    prev_mask[...] = jnp.broadcast_to(rowtab[0:rows, 3:4], (rows, C))
    next_mask[...] = jnp.broadcast_to(rowtab[0:rows, 4:5], (rows, C))


def front_kernel(
    nt,
    nf,
    lat_local,
    cot_local,
    wconv,
    wproj,
    wmlp,
    wemb,
    wsmall,
    cond,
    onehot,
    same,
    rowtab,
    conv,
    proj,
    mlp,
    vec,
    cot,
    zhat1,
    zhat2,
    zhat3,
    rstd1,
    rstd2,
    rstd3,
    resid,
    inner,
    query,
    kext,
    vext,
    inext,
    gmat,
    own_sums,
    rs,
    rq,
    mean,
    prev_mask,
    next_mask,
    xc,
    z_prev,
    z_here,
    z_next,
    hidden,
    to_left,
    to_right,
    from_left,
    from_right,
    emb,
    small,
    lat,
    lat_in,
    cot_in,
    order,
    film,
    msg_sems,
    kv_sems,
    block_sems,
    gather_sems,
):
    px = lat.shape[0]
    rows = px // F
    chunks = px // CH
    blk = px // nf
    seg = CH // nf
    spot, left, right = place(nt, nf)
    count = nt * nf
    where = (spot, count, left, right)
    f = lax.axis_index("freq")
    t = lax.axis_index("tm")
    s = snake(f, t, nf)
    partners = [{"freq": flip_by(f, mask)} for mask in range(1, nf)] + [{"tm": flip(t, 1)}]
    enter(spot, count, left, right, partners)
    blocks = []
    for index, (local, landed) in enumerate(((lat_local, lat_in), (cot_local, cot_in))):
        blocks.append(
            Exchange(
                lambda peer, local=local: local.at[rows_at(snake(peer, t, nf) * blk, blk)],
                lambda peer, landed=landed: landed.at[f],
                local.at[rows_at(s * blk, blk)],
                landed.at[f],
                f,
                nf,
                block_sems.at[index],
            )
        )
    blocks[0].start()

    def cast(src, dst, base):
        size = 32 if src.shape[0] % 64 else 64

        def step(i):
            dst[rows_at(base + i * size, size)] = src[rows_at(i * size, size)].astype(BF)

        loop(src.shape[0] // size, step)

    cdepth, pdepth, mdepth, edepth = (
        wconv.shape[1],
        wproj.shape[1],
        wmlp.shape[1],
        wemb.shape[0],
    )
    views = (
        (share_view(conv, cdepth, 0), None),
        (share_view(conv, cdepth, 1), cdepth),
        (share_view(proj, pdepth, slice(None)), pdepth),
        (share_view(mlp, mdepth, slice(None)), mdepth),
        (share_view(emb, edepth, None), edepth),
        (share_view(small, wsmall.shape[0], None), None),
    )
    gathers = []
    for i, (view, size) in enumerate(views):
        gathers.append(Gather(view, f, t, gather_sems.at[i], size))
    get_first, get_second, get_proj, get_mlp, get_emb, get_small = gathers
    cast(wsmall, small, f * wsmall.shape[0])
    cast(wconv.at[0], conv.at[0], f * cdepth)
    get_small.start()
    get_first.start()
    cast(wemb, emb, f * edepth)
    cast(wconv.at[1], conv.at[1], f * cdepth)
    for i in range(wproj.shape[0]):
        cast(wproj.at[i], proj.at[i], f * pdepth)
    for i in range(wmlp.shape[0]):
        cast(wmlp.at[i], mlp.at[i], f * mdepth)
    order[...] = chunk_order(nf)

    def arrange(landed, target):
        def step(c):
            parts = [landed[k, rows_at(c * seg, seg)] for k in range(nf)]
            moved = mm(order[...], jnp.concatenate(parts, axis=0))
            target[pl.ds(chunk_at(c), CH)] = moved.astype(BF)

        loop(chunks, step)

    clear_ends(spot, count, from_left, from_right)

    @pl.when(spot == 0)
    def _():
        inext[0:px] = jnp.zeros((px, C), BF)

    @pl.when(spot == count - 1)
    def _():
        inext[2 * px : 3 * px] = jnp.zeros((px, C), BF)

    gmat[...] = group_matrix()
    row_masks(rowtab, prev_mask, next_mask, rows)
    clip = Clip(same, rowtab, gmat, own_sums)

    def v(i):
        return vec[i : i + 1]

    def norm_stage(step, load, zhat, rstd, rim, beside):
        def sums(c):
            x3 = load(c).reshape(CR, F, C)
            rs[pl.ds(chunk_at(c, CR), CR)] = jnp.sum(x3, axis=1)
            rq[pl.ds(chunk_at(c, CR), CR)] = jnp.sum(x3 * x3, axis=1)

        loop(chunks, sums)
        clip.pack(rs, rq, to_left.at[step], to_right.at[step])
        first, last = rim()
        to_left[step, 8:16] = first
        to_right[step, 8:16] = last
        swap = Swap(
            where,
            to_left.at[step],
            to_right.at[step],
            from_left.at[step],
            from_right.at[step],
            msg_sems.at[step],
        )
        swap.start()
        beside()
        swap.wait()
        mean_rows, square_rows = clip.means(rs, rq, None, from_left.at[step], from_right.at[step])
        mean[...] = mean_rows
        rstd[...] = lax.rsqrt(square_rows - mean_rows * mean_rows + norm_eps)
        rim_raw = jnp.concatenate([from_left[step, 8:16], from_right[step, 8:16]], axis=0)
        rim3 = rim_raw.reshape(2, F, C)
        rim_hat = (rim3 - spread(mean[rows : rows + 2], 2)) * spread(rstd[rows : rows + 2], 2)
        if zhat.shape[0] > px:
            zhat[px : px + 16] = rim_hat.reshape(16, C)
        return rim_hat

    def normed(load, zhat, rstd, c):
        r0 = chunk_at(c, CR)
        x3 = load(c).reshape(CR, F, C)
        hat = (x3 - spread(mean[pl.ds(r0, CR)], CR)) * spread(rstd[pl.ds(r0, CR)], CR)
        zhat[pl.ds(chunk_at(c), CH)] = hat.reshape(CH, C)
        return hat

    def conv_stage(rim_hat, load, zhat, rstd, gain, shift, kernel, ready, finish):
        pre = rim_hat * gain + shift
        store_shifts(xc, px, (pre * jax.nn.sigmoid(pre)).astype(BF).astype(F32), 2)

        def build(c):
            pre = normed(load, zhat, rstd, c) * gain + shift
            act = (pre * jax.nn.sigmoid(pre)).astype(BF).astype(F32)
            store_shifts(xc, chunk_at(c), act, CR)

        loop(chunks, build)
        ready()

        def product(c):
            p0 = chunk_at(c)
            part = xc[pl.ds(p0, CH)]
            z_prev[pl.ds(pl.multiple_of(p0 + 8, 8), CH)] = mm(part, kernel[0 : 3 * C])
            z_here[pl.ds(p0, CH)] = mm(part, kernel[3 * C : 6 * C])
            z_next[pl.ds(p0, CH)] = mm(part, kernel[6 * C : 9 * C])

        loop(chunks, product)
        part = xc[px : px + 16]
        z_prev[0:8] = mm(part, kernel[0 : 3 * C])[0:8]
        z_next[px : px + 8] = mm(part, kernel[6 * C : 9 * C])[8:16]

        def join(c):
            p0 = chunk_at(c)
            r0 = chunk_at(c, CR)
            keep_prev = spread(prev_mask[pl.ds(r0, CR)], CR) > 0.0
            keep_next = spread(next_mask[pl.ds(r0, CR)], CR) > 0.0
            out = z_here[pl.ds(p0, CH)].reshape(CR, F, C)
            out = out + jnp.where(keep_prev, z_prev[pl.ds(p0, CH)].reshape(CR, F, C), 0.0)
            after = z_next[pl.ds(pl.multiple_of(p0 + 8, 8), CH)].reshape(CR, F, C)
            finish(c, out + jnp.where(keep_next, after, 0.0))

        loop(chunks, join)

    def load_latent(c):
        return lat[pl.ds(chunk_at(c), CH)].astype(F32)

    def load_hidden(c):
        return hidden[pl.ds(chunk_at(c), CH)]

    def load_resid(c):
        return resid[pl.ds(chunk_at(c), CH)]

    def send_second():
        get_emb.start()
        get_second.start()
        blocks[1].start()
        get_small.relay()
        get_small.collect()
        total = small[0 : wsmall.shape[0]].astype(F32)
        for k in range(1, nf):
            at = k * wsmall.shape[0]
            total = total + small[at : at + wsmall.shape[0]].astype(F32)
        vec[...] = total

    blocks[0].wait()
    arrange(lat_in, lat)
    rim_hat = norm_stage(
        0,
        load_latent,
        zhat1,
        rstd1,
        lambda: (lat[0:16].astype(F32)[0:8], lat[px - 16 : px].astype(F32)[8:16]),
        send_second,
    )

    def ready_first():
        get_first.relay()
        get_emb.relay()
        get_first.collect()
        get_emb.collect()
        table = mm(cond[...], emb[...]) + v(3)
        film[...] = hdot(onehot[...], table)

    def finish_one(c, out):
        r0 = chunk_at(c, CR)
        out = out + v(2) + spread(film[pl.ds(r0, CR)], CR)
        hidden[pl.ds(chunk_at(c), CH)] = out.reshape(CH, C)

    conv_stage(rim_hat, load_latent, zhat1, rstd1, v(0), v(1), conv.at[0], ready_first, finish_one)

    def send_proj():
        get_second.relay()
        get_proj.start()
        get_mlp.start()
        blocks[1].wait()
        arrange(cot_in, cot)

    def ready_second():
        get_second.collect()
        get_proj.relay()
        get_mlp.relay()

    rim_hat = norm_stage(
        1, load_hidden, zhat2, rstd2, lambda: (hidden[0:8], hidden[px - 8 : px]), send_proj
    )

    def finish_two(c, out):
        p0 = chunk_at(c)
        total = lat[pl.ds(p0, CH)].astype(F32) + out.reshape(CH, C) + v(6)
        resid[pl.ds(p0, CH)] = total

    conv_stage(rim_hat, load_hidden, zhat2, rstd2, v(4), v(5), conv.at[1], ready_second, finish_two)

    def ready_proj():
        get_proj.collect()
        get_mlp.collect()

    norm_stage(
        2, load_resid, zhat3, rstd3, lambda: (resid[0:8], resid[px - 8 : px]), ready_proj
    )

    def project(c):
        p0 = chunk_at(c)
        hat = normed(load_resid, zhat3, rstd3, c).reshape(CH, C)
        low = (hat * v(7) + v(8)).astype(BF)
        value = mm(low, proj[0]) + v(9)
        inner[pl.ds(p0, CH)] = value
        inext[pl.ds(pl.multiple_of(px + p0, CH), CH)] = value.astype(BF)

    loop(chunks, project)
    swap = Swap(
        where,
        inext.at[px : 2 * px],
        inext.at[px : 2 * px],
        inext.at[0:px],
        inext.at[2 * px : 3 * px],
        kv_sems.at[0],
    )
    swap.start()

    def keys_values(part):
        low = inext[part]
        kext[part] = mm(low, proj[2]).astype(BF)
        vext[part] = mm(low, proj[3]).astype(BF)

    def heads(c):
        part = pl.ds(pl.multiple_of(px + chunk_at(c), CH), CH)
        query[pl.ds(chunk_at(c), CH)] = mm(inext[part], proj[1]).astype(BF)
        keys_values(part)

    loop(chunks, heads)
    swap.wait()

    def rims(c):
        keys_values(pl.ds(chunk_at(c), CH))
        keys_values(pl.ds(pl.multiple_of(2 * px + chunk_at(c), CH), CH))

    loop(chunks, rims)
    for gather in gathers:
        gather.finish()


def vmem(count):
    return [pl.BlockSpec(memory_space=pltpu.VMEM)] * count


def front(nt, nf, lat, cot, wconv, wproj, wmlp, wemb, wsmall, cond, onehot, same, rowtab):
    px = lat.shape[0]
    rows = px // F
    tab = rowtab.shape[0]

    def whole(share, axis):
        shape = list(share.shape)
        shape[axis] *= nf
        return tuple(shape)

    shapes = (
        (whole(wconv, 1), BF),
        (whole(wproj, 1), BF),
        (whole(wmlp, 1), BF),
        (wsmall.shape, F32),
        ((px, C), BF),
        ((px, C), F32),
        ((px + 16, C), F32),
        ((px + 16, C), F32),
        ((tab, C), F32),
        ((tab, C), F32),
        ((tab, C), F32),
        ((px, C), F32),
        ((px, C), F32),
        ((px, C), BF),
        ((3 * px, C), BF),
        ((3 * px, C), BF),
        ((3 * px, C), BF),
    )
    return pl.pallas_call(
        partial(front_kernel, nt, nf),
        out_shape=[jax.ShapeDtypeStruct(s, d) for s, d in shapes],
        in_specs=vmem(11),
        out_specs=vmem(len(shapes)),
        scratch_shapes=[
            pltpu.VMEM((C, C), BF),
            pltpu.VMEM((2, tab, C), F32),
            pltpu.VMEM((rows, C), F32),
            pltpu.VMEM((rows, C), F32),
            pltpu.VMEM((tab, C), F32),
            pltpu.VMEM((rows, C), F32),
            pltpu.VMEM((rows, C), F32),
            pltpu.VMEM((px + 16, 3 * C), BF),
            pltpu.VMEM((px + 16, C), F32),
            pltpu.VMEM((px, C), F32),
            pltpu.VMEM((px + 16, C), F32),
            pltpu.VMEM((px, C), F32),
            pltpu.VMEM((3, 16, C), F32),
            pltpu.VMEM((3, 16, C), F32),
            pltpu.VMEM((3, 16, C), F32),
            pltpu.VMEM((3, 16, C), F32),
            pltpu.VMEM(whole(wemb, 0), BF),
            pltpu.VMEM((nf * wsmall.shape[0], C), BF),
            pltpu.VMEM((px, C), BF),
            pltpu.VMEM((nf, px // nf, C), BF),
            pltpu.VMEM((nf, px // nf, C), BF),
            pltpu.VMEM((CH, CH), BF),
            pltpu.VMEM((rows, C), F32),
            pltpu.SemaphoreType.DMA((3, 4)),
            pltpu.SemaphoreType.DMA((2, 4)),
            pltpu.SemaphoreType.DMA((2, nf - 1, 2)),
            pltpu.SemaphoreType.DMA((6, 5, 2)),
        ],
        compiler_params=pltpu.CompilerParams(
            collective_id=1, has_side_effects=True, vmem_limit_bytes=VMEM_LIMIT
        ),
        name="front",
    )(lat, cot, wconv, wproj, wmlp, wemb, wsmall, cond, onehot, same, rowtab)


def head_mask(h):
    lane = lax.broadcasted_iota(jnp.int32, (CH, C), 1)
    return (lane >= h * HD) & (lane < (h + 1) * HD)


def head_rows(h):
    return slice(h * HD, (h + 1) * HD)


def turned(block):
    return block.astype(F32).T


def score_bias(segk, segq, key_row, q0, key_rows):
    keys = jnp.broadcast_to(segk[pl.ds(key_row, key_rows), 0:1], (key_rows, C))
    keys = spread(keys, key_rows).reshape(key_rows * F, C)
    return jnp.where(keys == segq[0:1, pl.ds(q0, CH)], 0.0, masked_score)


def attend_kernel(meta, query, kext, vext, segq, segk, mixed, mixed_t, lse, vt, qm, bias, top, tot, acc, scores, peak):
    px = query.shape[0]
    factor = score_scale * LOG2E

    def turn(i):
        k0 = chunk_at(i)
        vt[:, pl.ds(k0, CH)] = turned(vext[pl.ds(k0, CH)]).astype(BF)

    loop(vext.shape[0] // CH, turn)

    def tile(t):
        q0 = chunk_at(t)
        block = query[pl.ds(q0, CH)].astype(F32)
        for h in range(H):
            qm[h] = jnp.where(head_mask(h), block, 0.0).astype(BF)
        top[...] = jnp.full((H, CH), masked_score, F32)
        tot[...] = jnp.zeros((H, CH), F32)
        acc[...] = jnp.zeros((C, CH), F32)

        def keys(row, key_rows):
            size = key_rows * F
            base = pl.multiple_of(row * F, 128)
            bias[0:size] = score_bias(segk, segq, pl.multiple_of(row, 16), q0, key_rows)
            key = kext[pl.ds(base, size)]
            for h in range(H):
                raw = mm_nt(key, qm[h]) + bias[0:size]
                scores[h, 0:size] = raw
                peak[h : h + 1] = jnp.maximum(top[h : h + 1], jnp.max(raw, axis=0, keepdims=True))
            for h in range(H):
                new = peak[h : h + 1]
                fade = jnp.exp2((top[h : h + 1] - new) * factor)
                weight = jnp.exp2((scores[h, 0:size] - new) * factor)
                top[h : h + 1] = new
                tot[h : h + 1] = tot[h : h + 1] * fade + jnp.sum(weight, axis=0, keepdims=True)
                part = mm(vt[head_rows(h), pl.ds(base, size)], weight.astype(BF))
                acc[head_rows(h)] = acc[head_rows(h)] * fade + part

        first = meta[t, 0] * 16
        loop(meta[t, 1], lambda i: keys(first + i * CR, CR))

        @pl.when(meta[t, 2] > 0)
        def _():
            keys(first + meta[t, 1] * CR, CR // 2)

        for h in range(H):
            acc[head_rows(h)] = acc[head_rows(h)] / tot[h : h + 1]
        lse[:, pl.ds(q0, CH)] = top[...] * factor + jnp.log2(tot[...])
        mixed_t[:, pl.ds(q0, CH)] = acc[...].astype(BF)
        mixed[pl.ds(q0, CH)] = acc[...].T.astype(BF)

    loop(px // CH, tile)


def attend(meta, query, kext, vext, segq, segk):
    px = query.shape[0]
    ext = kext.shape[0]
    return pl.pallas_call(
        attend_kernel,
        out_shape=[
            jax.ShapeDtypeStruct((px, C), BF),
            jax.ShapeDtypeStruct((C, px), BF),
            jax.ShapeDtypeStruct((H, px), F32),
        ],
        in_specs=[pl.BlockSpec(memory_space=pltpu.SMEM)] + vmem(5),
        out_specs=vmem(3),
        scratch_shapes=[
            pltpu.VMEM((C, ext), BF),
            pltpu.VMEM((H, CH, C), BF),
            pltpu.VMEM((CH, CH), F32),
            pltpu.VMEM((H, CH), F32),
            pltpu.VMEM((H, CH), F32),
            pltpu.VMEM((C, CH), F32),
            pltpu.VMEM((H, CH, CH), F32),
            pltpu.VMEM((H, CH), F32),
        ],
        compiler_params=pltpu.CompilerParams(vmem_limit_bytes=VMEM_LIMIT),
        name="attend",
    )(meta, query, kext, vext, segq, segk)


def attend_back_kernel(
    meta,
    query,
    kext,
    vext,
    segq,
    segk,
    gmix,
    mixed_t,
    lse,
    dq,
    dk,
    dv,
    kt,
    qm,
    gm,
    qt,
    gt,
    inner_rows,
    bias,
    dqt,
    dkt,
    dvt,
    kept,
    gscores,
):
    px = query.shape[0]
    ext = kext.shape[0]
    factor = score_scale * LOG2E

    def turn(i):
        k0 = chunk_at(i)
        kt[:, pl.ds(k0, CH)] = turned(kext[pl.ds(k0, CH)]).astype(BF)
        dkt[:, pl.ds(k0, CH)] = jnp.zeros((C, CH), F32)
        dvt[:, pl.ds(k0, CH)] = jnp.zeros((C, CH), F32)

    loop(ext // CH, turn)

    def tile(t):
        q0 = chunk_at(t)
        block = query[pl.ds(q0, CH)].astype(F32)
        grad = gmix[pl.ds(q0, CH)].astype(F32)
        for h in range(H):
            qm[h] = jnp.where(head_mask(h), block, 0.0).astype(BF)
            gm[h] = jnp.where(head_mask(h), grad, 0.0).astype(BF)
        qt[...] = block.T.astype(BF)
        grad_t = grad.T
        gt[...] = grad_t.astype(BF)
        crossed = grad_t * mixed_t[:, pl.ds(q0, CH)].astype(F32)
        inner_rows[...] = jnp.sum(crossed.reshape(H, HD, CH), axis=1)
        dqt[...] = jnp.zeros((C, CH), F32)

        def keys(row, key_rows):
            size = key_rows * F
            base = pl.multiple_of(row * F, 128)
            bias[0:size] = score_bias(segk, segq, pl.multiple_of(row, 16), q0, key_rows)
            key = kext[pl.ds(base, size)]
            val = vext[pl.ds(base, size)]
            for h in range(H):
                raw = mm_nt(key, qm[h]) + bias[0:size]
                probs = jnp.exp2(raw * factor - lse[h : h + 1, pl.ds(q0, CH)])
                gprob = mm_nt(val, gm[h])
                kept[h, 0:size] = probs.astype(BF)
                gscores[h, 0:size] = (probs * (gprob - inner_rows[h : h + 1])).astype(BF)
            for h in range(H):
                low_score = gscores[h, 0:size]
                dvt[head_rows(h), pl.ds(base, size)] += mm_nt(gt[head_rows(h)], kept[h, 0:size])
                dkt[head_rows(h), pl.ds(base, size)] += mm_nt(qt[head_rows(h)], low_score)
                dqt[head_rows(h)] += mm(kt[head_rows(h), pl.ds(base, size)], low_score)

        first = meta[t, 0] * 16
        loop(meta[t, 1], lambda i: keys(first + i * CR, CR))

        @pl.when(meta[t, 2] > 0)
        def _():
            keys(first + meta[t, 1] * CR, CR // 2)

        dq[pl.ds(q0, CH)] = (dqt[...] * score_scale).T.astype(BF)

    loop(px // CH, tile)

    def settle(i):
        k0 = chunk_at(i)
        dk[pl.ds(k0, CH)] = (dkt[:, pl.ds(k0, CH)] * score_scale).T.astype(BF)
        dv[pl.ds(k0, CH)] = dvt[:, pl.ds(k0, CH)].T.astype(BF)

    loop(ext // CH, settle)


def attend_back(meta, query, kext, vext, segq, segk, gmix, mixed_t, lse):
    px = query.shape[0]
    ext = kext.shape[0]
    return pl.pallas_call(
        attend_back_kernel,
        out_shape=[
            jax.ShapeDtypeStruct((px, C), BF),
            jax.ShapeDtypeStruct((ext, C), BF),
            jax.ShapeDtypeStruct((ext, C), BF),
        ],
        in_specs=[pl.BlockSpec(memory_space=pltpu.SMEM)] + vmem(8),
        out_specs=vmem(3),
        scratch_shapes=[
            pltpu.VMEM((C, ext), BF),
            pltpu.VMEM((H, CH, C), BF),
            pltpu.VMEM((H, CH, C), BF),
            pltpu.VMEM((C, CH), BF),
            pltpu.VMEM((C, CH), BF),
            pltpu.VMEM((H, CH), F32),
            pltpu.VMEM((CH, CH), F32),
            pltpu.VMEM((C, CH), F32),
            pltpu.VMEM((C, ext), F32),
            pltpu.VMEM((C, ext), F32),
            pltpu.VMEM((H, CH, CH), BF),
            pltpu.VMEM((H, CH, CH), BF),
        ],
        compiler_params=pltpu.CompilerParams(vmem_limit_bytes=VMEM_LIMIT),
        name="attend_back",
    )(meta, query, kext, vext, segq, segk, gmix, mixed_t, lse)


def middle_kernel(
    nf,
    inner,
    mixed,
    resid,
    cot,
    proj,
    mlp,
    vec,
    output,
    gafter,
    gmix,
    pack,
    sums,
    after_low,
    act_low,
    pre_low,
    down_low,
    mlp_low,
    after_grad_low,
    ubias,
    order,
):
    px = inner.shape[0]
    seg = CH // nf
    tail = 11 + FF // C
    order[...] = chunk_order(nf)
    sums[...] = jnp.zeros_like(sums)
    for j in range(FF // C):
        ubias[:, j * C : (j + 1) * C] = vec[11 + j : 12 + j]

    def step(c):
        p0 = chunk_at(c)
        after = inner[pl.ds(p0, CH)] + mm(mixed[pl.ds(p0, CH)], proj[4]) + vec[10:11]
        low = after.astype(BF)
        after_low[pl.ds(p0, CH)] = low
        grad_out = cot[pl.ds(p0, CH)]
        grad_mlp = mm_nt(grad_out, proj[5])
        down = grad_mlp.astype(BF)
        down_low[pl.ds(p0, CH)] = down
        total = after
        grad_after = grad_mlp
        for j in range(FF // C):
            part = slice(j * C, (j + 1) * C)
            pre = mm_nt(low, mlp[0, part]) + ubias[:, part]
            cdf = 0.5 + 0.5 * lax.erf(pre * (0.5**0.5))
            act = (pre * cdf).astype(BF)
            act_low[pl.ds(p0, CH), part] = act
            total = total + mm(act, mlp[1, part])
            density = jnp.exp(pre * pre * -0.5) * 0.3989422804014327
            grad_pre = mm_nt(down, mlp[1, part]) * (cdf + pre * density)
            sums[3 + j : 4 + j] += jnp.sum(grad_pre, axis=0, keepdims=True)
            grad_low = grad_pre.astype(BF)
            pre_low[pl.ds(p0, CH), part] = grad_low
            grad_after = grad_after + mm(grad_low, mlp[0, part])
        total = (total + vec[tail : tail + 1]).astype(BF)
        mlp_low[pl.ds(p0, CH)] = total
        branch = mm(total, proj[5]) + vec[tail + 1 : tail + 2]
        moved = mm_tn(order[...], (resid[pl.ds(p0, CH)] + branch).astype(BF)).astype(BF)
        for k in range(nf):
            output[k, rows_at(c * seg, seg)] = moved[k * seg : (k + 1) * seg]
        gafter[pl.ds(p0, CH)] = grad_after
        grad_low = grad_after.astype(BF)
        after_grad_low[pl.ds(p0, CH)] = grad_low
        gmix[pl.ds(p0, CH)] = mm_nt(grad_low, proj[4]).astype(BF)
        sums[0:1] += jnp.sum(grad_out.astype(F32), axis=0, keepdims=True)
        sums[1:2] += jnp.sum(grad_mlp, axis=0, keepdims=True)
        sums[2:3] += jnp.sum(grad_after, axis=0, keepdims=True)

    loop(px // CH, step)
    width = FF // nf
    for k in range(nf):
        part = slice(k * width, (k + 1) * width)
        pack[k, 0:width] = mm_tn(pre_low[:, part], after_low[...]).astype(BF)
        pack[k, width : 2 * width] = mm_tn(act_low[:, part], down_low[...]).astype(BF)
    depth = C // nf
    gw_attn = mm_tn(mixed[...], after_grad_low[...]).astype(BF)
    gw_out = mm_tn(mlp_low[...], cot[...]).astype(BF)
    for k in range(nf):
        part = slice(k * depth, (k + 1) * depth)
        pack[k, 2 * width : 2 * width + depth] = gw_attn[part]
        pack[k, 2 * width + depth : 2 * width + 2 * depth] = gw_out[part]


def middle(nf, inner, mixed, resid, cot, proj, mlp, vec):
    px = inner.shape[0]
    return pl.pallas_call(
        partial(middle_kernel, nf),
        out_shape=[
            jax.ShapeDtypeStruct((nf, px // nf, C), BF),
            jax.ShapeDtypeStruct((px, C), F32),
            jax.ShapeDtypeStruct((px, C), BF),
            jax.ShapeDtypeStruct((nf, 2 * (FF + C) // nf, C), BF),
            jax.ShapeDtypeStruct((8, C), F32),
        ],
        in_specs=vmem(7),
        out_specs=vmem(5),
        scratch_shapes=[
            pltpu.VMEM((px, C), BF),
            pltpu.VMEM((px, FF), BF),
            pltpu.VMEM((px, FF), BF),
            pltpu.VMEM((px, C), BF),
            pltpu.VMEM((px, C), BF),
            pltpu.VMEM((px, C), BF),
            pltpu.VMEM((1, FF), F32),
            pltpu.VMEM((CH, CH), BF),
        ],
        compiler_params=pltpu.CompilerParams(vmem_limit_bytes=VMEM_LIMIT),
        name="middle",
    )(inner, mixed, resid, cot, proj, mlp, vec)


def back_kernel(
    nt,
    nf,
    dq,
    dk,
    dv,
    gafter,
    inext,
    zhat1,
    zhat2,
    zhat3,
    rstd1,
    rstd2,
    rstd3,
    cot,
    conv,
    proj,
    vec,
    same,
    rowtab,
    cond,
    onehot,
    mid_sums,
    pack_a,
    out_blocks,
    output,
    glat,
    out_a,
    out_b,
    out_c,
    out_d,
    out_e,
    sums,
    film_rows,
    gmat,
    own_sums,
    rs,
    rq,
    mean_e,
    mean_ez,
    prev_mask,
    next_mask,
    normed_low,
    grad_low,
    gresid,
    dgrad,
    two,
    xc,
    shifted,
    rim_out,
    rim_got,
    to_left,
    to_right,
    from_left,
    from_right,
    order,
    glat_blocks,
    *rest,
):
    pack_b, pack_c, pack_d, pack_e = rest[:4]
    pieces = rest[4:28]
    msg_sems, kv_sems, block_sems, reduce_sems = rest[28:32]
    px = dq.shape[0]
    rows = px // F
    chunks = px // CH
    blk = px // nf
    seg = CH // nf
    spot, left, right = place(nt, nf)
    count = nt * nf
    where = (spot, count, left, right)
    f = lax.axis_index("freq")
    t = lax.axis_index("tm")
    s = snake(f, t, nf)
    partners = [{"freq": flip_by(f, mask)} for mask in range(1, nf)]
    partners = partners + [{"tm": flip(t, bit)} for bit in bits_of(nt)]
    enter(spot, count, left, right, partners)
    far_first, far_later = orders_of(nt)
    whole_d = out_d.shape[0]
    half = padded(whole_d // 2)
    plans = (
        (far_later, lambda i: pack_a.at[i], out_a),
        (far_first, lambda i: pack_b.at[i], out_b),
        (far_later, lambda i: pack_c.at[i], out_c),
        (far_first, lambda i: pack_d.at[i, 0:half], out_d.at[0:half]),
        (far_later, lambda i: pack_d.at[i, half:whole_d], out_d.at[half:whole_d]),
        (far_first, lambda i: pack_e.at[i], out_e),
    )
    jobs = []
    for index, (order_of, pack, out) in enumerate(plans):
        room = pieces[4 * index : 4 * index + 4]
        jobs.append(Reduce(order_of, pack, *room, out, reduce_sems.at[index], t, f))
    job_a, job_b, job_c, job_d, job_dd, job_e = jobs
    blocks = []
    for index, (source, landed) in enumerate(((out_blocks, output), (glat_blocks, glat))):
        blocks.append(
            Exchange(
                lambda peer, source=source: source.at[peer],
                lambda peer, landed=landed: landed.at[rows_at(s * blk, blk)],
                source.at[f],
                landed.at[rows_at(s * blk, blk)],
                f,
                nf,
                block_sems.at[index],
            )
        )
    def rim_grads(c):
        part = pl.ds(chunk_at(c), CH)
        for side in range(2):
            beyond = pl.ds(pl.multiple_of(2 * side * px + chunk_at(c), CH), CH)
            value = mm_nt(dk[beyond], proj[2]) + mm_nt(dv[beyond], proj[3])
            rim_out[side, part] = value.astype(BF)

    loop(chunks, rim_grads)
    rim_swap = Swap(
        where, rim_out.at[0], rim_out.at[1], rim_got.at[0], rim_got.at[1], kv_sems.at[0]
    )
    rim_swap.start()
    job_a.advance()
    order[...] = chunk_order(nf)
    clear_ends(spot, count, from_left, from_right)
    clear_ends(spot, count, rim_got.at[0], rim_got.at[1])
    gmat[...] = group_matrix()
    row_masks(rowtab, prev_mask, next_mask, rows)
    clip = Clip(same, rowtab, gmat, own_sums)
    sums[...] = jnp.zeros_like(sums)

    def v(i):
        return vec[i : i + 1]

    def first(c):
        p0 = chunk_at(c)
        part = pl.ds(p0, CH)
        own = pl.ds(pl.multiple_of(px + p0, CH), CH)
        normed_low[part] = (zhat3[part] * v(7) + v(8)).astype(BF)
        grad = gafter[part] + mm_nt(dq[part], proj[1])
        gresid[part] = grad + mm_nt(dk[own], proj[2]) + mm_nt(dv[own], proj[3])

    loop(chunks, first)
    depth = C // nf

    def proj_grad(which, grad):
        low = grad.astype(BF)
        for k in range(nf):
            pack_b[k, which * depth : (which + 1) * depth] = low[k * depth : (k + 1) * depth]

    proj_grad(1, mm_tn(inext[px : 2 * px], dq[...]))
    job_a.advance()
    rim_swap.wait()

    def row_sums(c, grad3, hat3):
        rs[pl.ds(chunk_at(c, CR), CR)] = jnp.sum(grad3, axis=1)
        rq[pl.ds(chunk_at(c, CR), CR)] = jnp.sum(grad3 * hat3, axis=1)

    def second(c):
        p0 = chunk_at(c)
        part = pl.ds(p0, CH)
        grad = gresid[part] + rim_got[0, part].astype(F32) + rim_got[1, part].astype(F32)
        sums[9:10] += jnp.sum(grad, axis=0, keepdims=True)
        low = grad.astype(BF)
        grad_low[part] = low
        d3 = mm_nt(low, proj[0])
        dgrad[part] = d3
        row_sums(c, d3.reshape(CR, F, C), zhat3[part].reshape(CR, F, C))

    loop(chunks, second)

    def swap_step(step, rim_first, rim_last):
        clip.pack(rs, rq, to_left.at[step], to_right.at[step])
        if rim_first is not None:
            to_left[step, 8 : 8 + rim_first.shape[0]] = rim_first
            to_right[step, 8 : 8 + rim_last.shape[0]] = rim_last
        swap = Swap(
            where,
            to_left.at[step],
            to_right.at[step],
            from_left.at[step],
            from_right.at[step],
            msg_sems.at[step],
        )
        swap.start()
        return swap

    def set_means(step, gain):
        mean_e[...], mean_ez[...] = clip.means(
            rs, rq, gain, from_left.at[step], from_right.at[step]
        )

    def back_norm(grad3, hat3, rstd, gain, r0, size):
        value = grad3 * gain - spread(mean_e[pl.ds(r0, size)], size)
        value = value - hat3 * spread(mean_ez[pl.ds(r0, size)], size)
        return value * spread(rstd[pl.ds(r0, size)], size)

    def rim_grad(step, at):
        both = jnp.concatenate([from_left[step, at : at + 8], from_right[step, at : at + 8]], axis=0)
        return both.reshape(2, F, C)

    sums[7:8] = jnp.sum(rq[...], axis=0, keepdims=True)
    sums[8:9] = jnp.sum(rs[...], axis=0, keepdims=True)
    cot_first = cot[0:16].astype(F32)[0:8]
    cot_last = cot[px - 16 : px].astype(F32)[8:16]
    swap = swap_step(
        0,
        jnp.concatenate([dgrad[0:8], cot_first], axis=0),
        jnp.concatenate([dgrad[px - 8 : px], cot_last], axis=0),
    )
    proj_grad(2, mm_tn(inext[...], dk[...]))
    proj_grad(3, mm_tn(inext[...], dv[...]))
    proj_grad(0, mm_tn(normed_low[...], grad_low[...]))
    job_b.advance()
    job_a.advance()
    swap.wait()
    set_means(0, v(7))

    def set_rims(value):
        low = value.astype(BF).astype(F32)
        two[0:8] = low[0]
        two[px + 8 : px + 16] = low[1]

    rim = rim_grad(0, 8)
    rim_hat = zhat3[px : px + 16].reshape(2, F, C)
    set_rims(rim_grad(0, 16) + back_norm(rim, rim_hat, rstd3, v(7), rows, 2))

    def third(c):
        p0 = chunk_at(c)
        part = pl.ds(p0, CH)
        grad3 = dgrad[part].reshape(CR, F, C)
        hat3 = zhat3[part].reshape(CR, F, C)
        value = back_norm(grad3, hat3, rstd3, v(7), chunk_at(c, CR), CR).reshape(CH, C)
        value = cot[part].astype(F32) + value
        gresid[part] = value
        sums[6:7] += jnp.sum(value, axis=0, keepdims=True)
        two[pl.ds(pl.multiple_of(p0 + 8, 8), CH)] = value.astype(BF).astype(F32)

    loop(chunks, third)

    def conv_inputs(zhat, gain, shift, c):
        p0 = chunk_at(c)
        part = pl.ds(p0, CH)
        r0 = chunk_at(c, CR)
        keep_prev = spread(prev_mask[pl.ds(r0, CR)], CR).reshape(CH, C) > 0.0
        keep_next = spread(next_mask[pl.ds(r0, CR)], CR).reshape(CH, C) > 0.0
        after = two[pl.ds(pl.multiple_of(p0 + 16, 16), CH)]
        here = two[pl.ds(pl.multiple_of(p0 + 8, 8), CH)]
        shifted[part, 0:C] = jnp.where(keep_next, after, 0.0).astype(BF)
        shifted[part, C : 2 * C] = here.astype(BF)
        shifted[part, 2 * C : 3 * C] = jnp.where(keep_prev, two[part], 0.0).astype(BF)
        pre = zhat[part] * gain + shift
        act = (pre * jax.nn.sigmoid(pre)).astype(BF).astype(F32).reshape(CR, F, C)
        store_shifts(xc, p0, act, CR)

    def conv_back(kernel, zhat, gain, shift, c):
        part = pl.ds(chunk_at(c), CH)
        hat = zhat[part]
        pre = hat * gain + shift
        sig = jax.nn.sigmoid(pre)

        def columns(j):
            piece = slice(j * C, (j + 1) * C)
            value = mm_nt(shifted[part, 0:C], kernel[0 : 3 * C][piece])
            value = value + mm_nt(shifted[part, C : 2 * C], kernel[3 * C : 6 * C][piece])
            value = value + mm_nt(shifted[part, 2 * C : 3 * C], kernel[6 * C : 9 * C][piece])
            return value.reshape(CR, F, C)

        col = column_index(CR)
        back = columns(1)
        back = back + jnp.where(col == F - 1, 0.0, pltpu.roll(columns(0), F - 1, 1))
        back = back + jnp.where(col == 0, 0.0, pltpu.roll(columns(2), 1, 1))
        grad = back.reshape(CH, C) * sig * (1.0 + pre * (1.0 - sig))
        dgrad[part] = grad
        row_sums(c, grad.reshape(CR, F, C), hat.reshape(CR, F, C))

    share = TAPS * C // nf

    def kernel_grad(pack):
        for k in range(nf):
            if pack.shape[1] > share:
                pack[k, share:] = jnp.zeros((pack.shape[1] - share, C), BF)
        for d in range(3):
            for j in range(3):
                grad = mm_tn(xc[:, j * C : (j + 1) * C], shifted[:, d * C : (d + 1) * C])
                low = grad.astype(BF)
                start = (d * 3 + j) * C
                end = start + C
                at = start
                while at < end:
                    k = at // share
                    upto = min(end, (k + 1) * share)
                    pack[k, at - k * share : upto - k * share] = low[at - start : upto - start]
                    at = upto

    def step_two(c):
        conv_inputs(zhat2, v(4), v(5), c)
        conv_back(conv.at[1], zhat2, v(4), v(5), c)

    loop(chunks, step_two)
    sums[4:5] = jnp.sum(rq[...], axis=0, keepdims=True)
    sums[5:6] = jnp.sum(rs[...], axis=0, keepdims=True)
    swap = swap_step(1, dgrad[0:8], dgrad[px - 8 : px])
    job_a.advance()
    blocks[0].start()
    kernel_grad(pack_c)
    job_c.advance()
    job_b.advance()
    swap.wait()
    set_means(1, v(4))
    rim_hat = zhat2[px : px + 16].reshape(2, F, C)
    set_rims(back_norm(rim_grad(1, 8), rim_hat, rstd2, v(4), rows, 2))

    def fourth(c):
        p0 = chunk_at(c)
        part = pl.ds(p0, CH)
        grad3 = dgrad[part].reshape(CR, F, C)
        hat3 = zhat2[part].reshape(CR, F, C)
        value3 = back_norm(grad3, hat3, rstd2, v(4), chunk_at(c, CR), CR)
        film_rows[pl.ds(chunk_at(c, CR), CR)] = jnp.sum(value3, axis=1)
        low = value3.reshape(CH, C).astype(BF).astype(F32)
        two[pl.ds(pl.multiple_of(p0 + 8, 8), CH)] = low

    loop(chunks, fourth)
    total = jnp.sum(film_rows[...], axis=0, keepdims=True)
    sums[2:3] = total
    sums[3:4] = total
    loop(chunks, partial(conv_inputs, zhat1, v(0), v(1)))
    kernel_grad(pack_d)
    grad_film = hdot_tn(onehot[...], film_rows[...])
    gemb = hdot_tn(cond[...].astype(F32), grad_film).astype(BF)
    edepth = gemb.shape[0] // nf
    job_d.advance()
    job_dd.advance()

    def sums_one(c):
        conv_back(conv.at[0], zhat1, v(0), v(1), c)

    loop(chunks, sums_one)
    sums[0:1] = jnp.sum(rq[...], axis=0, keepdims=True)
    sums[1:2] = jnp.sum(rs[...], axis=0, keepdims=True)
    swap = swap_step(2, None, None)
    tail = jnp.concatenate(
        [
            sums[0:10],
            mid_sums[2:3],
            mid_sums[3 : 3 + FF // C],
            mid_sums[1:2],
            mid_sums[0:1],
            jnp.zeros((32 - 13 - FF // C, C), F32),
        ],
        axis=0,
    ).astype(BF)
    for k in range(nf):
        pack_e[k, 0:edepth] = gemb[k * edepth : (k + 1) * edepth]
        pack_e[k, edepth : edepth + 32] = tail
        pack_e[k, edepth + 32 :] = jnp.zeros((pack_e.shape[1] - edepth - 32, C), BF)
    job_e.advance()
    for job in (job_d, job_dd, job_c, job_a, job_b):
        job.advance()
    swap.wait()
    set_means(2, v(0))

    def fifth(c):
        p0 = chunk_at(c)
        part = pl.ds(p0, CH)
        grad3 = dgrad[part].reshape(CR, F, C)
        hat3 = zhat1[part].reshape(CR, F, C)
        value = back_norm(grad3, hat3, rstd1, v(0), chunk_at(c, CR), CR).reshape(CH, C)
        moved = mm_tn(order[...], (gresid[part] + value).astype(BF)).astype(BF)
        for k in range(nf):
            glat_blocks[k, rows_at(c * seg, seg)] = moved[k * seg : (k + 1) * seg]

    loop(chunks, fifth)
    turns = 0
    while turns <= 3 or not all(job.done() for job in jobs):
        if turns == 3:
            blocks[1].start()
        for job in (job_e, job_d, job_dd, job_c, job_a, job_b):
            job.advance()
        turns += 1
    for block in blocks:
        block.wait()


def back(nt, nf, *args):
    px = args[0].shape[0]
    rows = px // F
    tab = args[-6].shape[0]
    pack_rows = args[-2].shape[1]
    edepth = args[-5].shape[1] // nf
    share = TAPS * C // nf
    heights = (pack_rows, 4 * C // nf, share, share, padded(edepth + 32))
    half = padded(share // 2)
    job_heights = heights[:3] + (half, share - half) + heights[4:]
    buffers = [pltpu.VMEM((nf, u, C), BF) for u in heights[1:]]
    for u in job_heights:
        buffers.extend(
            [
                pltpu.VMEM((2, u, C), BF),
                pltpu.VMEM((2, u, C), BF),
                pltpu.VMEM((u, C), BF),
                pltpu.VMEM((2, 2 * u, C), BF),
            ]
        )
    big = pltpu.VMEM((px, C), F32)
    low = pltpu.VMEM((px, C), BF)
    table = pltpu.VMEM((rows, C), F32)
    return pl.pallas_call(
        partial(back_kernel, nt, nf),
        out_shape=[
            jax.ShapeDtypeStruct((px, C), BF),
            jax.ShapeDtypeStruct((px, C), BF),
        ]
        + [jax.ShapeDtypeStruct((u, C), BF) for u in heights],
        in_specs=vmem(len(args)),
        out_specs=vmem(7),
        scratch_shapes=[
            pltpu.VMEM((16, C), F32),
            pltpu.VMEM((rows, C), F32),
            pltpu.VMEM((C, C), BF),
            pltpu.VMEM((2, tab, C), F32),
            table,
            table,
            pltpu.VMEM((tab, C), F32),
            pltpu.VMEM((tab, C), F32),
            table,
            table,
            low,
            low,
            big,
            big,
            pltpu.VMEM((px + 16, C), F32),
            pltpu.VMEM((px, 3 * C), BF),
            pltpu.VMEM((px, 3 * C), BF),
            pltpu.VMEM((2, px, C), BF),
            pltpu.VMEM((2, px, C), BF),
            pltpu.VMEM((3, 24, C), F32),
            pltpu.VMEM((3, 24, C), F32),
            pltpu.VMEM((3, 24, C), F32),
            pltpu.VMEM((3, 24, C), F32),
            pltpu.VMEM((CH, CH), BF),
            pltpu.VMEM((nf, px // nf, C), BF),
            *buffers,
            pltpu.SemaphoreType.DMA((3, 4)),
            pltpu.SemaphoreType.DMA((2, 4)),
            pltpu.SemaphoreType.DMA((2, nf - 1, 2)),
            pltpu.SemaphoreType.DMA((6, stage_count(nt), 2)),
        ],
        compiler_params=pltpu.CompilerParams(
            collective_id=2, has_side_effects=True, vmem_limit_bytes=VMEM_LIMIT
        ),
        name="back",
    )(*args)


def adamw_step(weight, moment, second, grad, decay_rate):
    moment_new = beta_first * moment + (1.0 - beta_first) * grad
    second_new = beta_second * second + (1.0 - beta_second) * grad * grad
    moment_hat = moment_new / (1.0 - beta_first**STEP)
    second_hat = second_new / (1.0 - beta_second**STEP)
    weight_new = weight - learn_rate * (
        moment_hat / (jnp.sqrt(second_hat) + adam_eps) + decay_rate * weight
    )
    return (weight_new, moment_new, second_new)


def adam_kernel(sum_a, sum_b, sum_c, sum_d, sum_e, *refs):
    masters, moments, seconds = refs[0:5], refs[5:10], refs[10:15]
    news, bias = refs[15:30], refs[30]
    i = pl.program_id(0)

    def update(kind, at, grad, decay):
        values = adamw_step(
            masters[kind][at], moments[kind][at], seconds[kind][at], grad.astype(F32), decay
        )
        for k, value in enumerate(values):
            news[3 * kind + k][at] = value

    def block(total, start, size):
        return total[rows_at(start + i * size, size)]

    cdepth, pdepth, mdepth, edepth = (
        masters[0].shape[1],
        masters[1].shape[1],
        masters[2].shape[1],
        masters[3].shape[0],
    )
    steps = sum_d.shape[0] // cdepth
    update(0, 0, block(sum_d, 0, cdepth), weight_decay)
    update(0, 1, block(sum_c, 0, cdepth), weight_decay)
    whole_p, whole_m, whole_e = pdepth * steps, mdepth * steps, edepth * steps
    for k in range(4):
        update(1, k, block(sum_b, k * whole_p, pdepth), weight_decay)
    for k in range(2):
        update(1, 4 + k, block(sum_a, 2 * whole_m + k * whole_p, pdepth), weight_decay)
        update(2, k, block(sum_a, k * whole_m, mdepth), weight_decay)
    update(3, slice(None), block(sum_e, 0, edepth), weight_decay)

    @pl.when(i == 0)
    def _():
        nsmall, width = masters[4].shape
        first = lax.axis_index("freq") * width
        source = lax.broadcasted_iota(jnp.int32, (C, width), 0)
        chosen = source == first + lax.broadcasted_iota(jnp.int32, (C, width), 1)
        grad = mm(sum_e[whole_e : whole_e + 32], chosen.astype(BF))
        update(4, slice(None), grad[0:nsmall], 0.0)
        bias[...] = grad[nsmall - 1 : nsmall]


def adam(sums, masters, moments, seconds):
    steps = 4

    def whole(array):
        return pl.BlockSpec(array.shape, lambda i: (0,) * array.ndim)

    def piece(array):
        if array.ndim == 3:
            shape = (array.shape[0], array.shape[1] // steps, C)
            return pl.BlockSpec(shape, lambda i: (0, i, 0))
        if array.shape[1] == C:
            return pl.BlockSpec((array.shape[0] // steps, C), lambda i: (i, 0))
        return whole(array)

    specs = [piece(array) for array in masters]
    out_shapes, out_specs = [], []
    for array, spec in zip(masters, specs):
        out_shapes.extend([jax.ShapeDtypeStruct(array.shape, F32)] * 3)
        out_specs.extend([spec] * 3)
    width = masters[4].shape[1]
    out_shapes.append(jax.ShapeDtypeStruct((1, width), F32))
    out_specs.append(pl.BlockSpec((1, width), lambda i: (0, 0)))
    return pl.pallas_call(
        adam_kernel,
        grid=(steps,),
        out_shape=out_shapes,
        in_specs=[whole(array) for array in sums] + specs * 3,
        out_specs=out_specs,
        compiler_params=pltpu.CompilerParams(vmem_limit_bytes=VMEM_LIMIT),
        name="adam",
    )(*sums, *masters, *moments, *seconds)


def layout_kernel(
    nt,
    nf,
    len_row,
    condition,
    weight,
    same,
    rowtab,
    segk,
    segq,
    meta,
    onehot,
    cond,
    wsmall,
    wide,
):
    rows, clips = onehot.shape
    tab = rowtab.shape[0]
    f = lax.axis_index("freq")
    t = lax.axis_index("tm")
    total_rows = nt * nf * rows
    first_row = (t * nf + snake(f, t, nf)) * rows

    def iota(shape, dim):
        return lax.broadcasted_iota(jnp.int32, shape, dim)

    down = iota((clips, clips), 0)
    across = iota((clips, clips), 1)
    lengths = len_row[...].astype(F32)
    len_col = jnp.sum(jnp.where(down == across, lengths, 0.0), axis=1, keepdims=True)
    ends_col = jnp.sum(jnp.where(across <= down, lengths, 0.0), axis=1, keepdims=True)
    ends = jnp.sum(jnp.where(down <= across, len_col, 0.0), axis=0, keepdims=True)

    def finished(row):
        return ends <= row.astype(F32)

    def seg_of(row):
        seg = jnp.sum(jnp.where(finished(row), 1.0, 0.0), axis=1, keepdims=True)
        return jnp.where((row >= 0) & (row < total_rows), seg, -1.0)

    def seg_lanes(row):
        return jnp.sum(jnp.where(ends_col <= row.astype(F32), 1.0, 0.0), axis=0, keepdims=True)

    ext_row = first_row - rows + iota((3 * rows, 1), 0)
    segk[...] = jnp.broadcast_to(seg_of(ext_row), segk.shape)
    pixel = iota((1, rows * F), 1)
    segq[...] = jnp.broadcast_to(seg_lanes(first_row + pixel // F), segq.shape)
    seg_row = seg_lanes(first_row + iota((1, rows), 1))
    index = iota((tab + 8, 1), 0)
    at = jnp.where(index < rows, first_row + index, first_row)
    at = jnp.where(index == rows, first_row - 1, at)
    at = jnp.where(index == rows + 1, first_row + rows, at)
    at = jnp.where(index == tab + 1, first_row + rows - 1, at)
    unused = ((index > rows + 1) & (index < tab)) | (index > tab + 1)
    seg_tab = jnp.where(unused, -2.0, seg_of(at))
    same[...] = (seg_tab == seg_row).astype(BF)
    clip_lane = iota((tab + 8, clips), 1).astype(F32)
    hot = jnp.where(seg_tab == clip_lane, 1.0, 0.0)
    onehot[...] = hot[0:rows]
    row_len = jnp.sum(hot * lengths, axis=1, keepdims=True)
    inner = index < rows
    fields = (
        1.0 / jnp.maximum(row_len * (F * GW), 1.0),
        jnp.where(seg_tab == seg_of(first_row - 1 + 0 * index), 1.0, 0.0),
        jnp.where(seg_tab == seg_of(first_row + rows + 0 * index), 1.0, 0.0),
        jnp.where(inner & (seg_tab == seg_of(at - 1)), 1.0, 0.0),
        jnp.where(inner & (seg_tab == seg_of(at + 1)), 1.0, 0.0),
    )
    lane = iota((tab + 8, 128), 1)
    values = jnp.zeros((tab + 8, 128), F32)
    for place_at, field in enumerate(fields):
        values = jnp.where(lane == place_at, field, values)
    rowtab[...] = values[0:tab]
    tile = iota((8, 1), 0)

    def bounds(row):
        low = jnp.sum(jnp.where(finished(row), lengths, 0.0), axis=1, keepdims=True)
        seg = jnp.sum(jnp.where(finished(row), 1.0, 0.0), axis=1, keepdims=True)
        here = iota((8, clips), 1).astype(F32) == seg
        return low, low + jnp.sum(jnp.where(here, lengths, 0.0), axis=1, keepdims=True)

    low_row = bounds(first_row + tile * CR)[0].astype(jnp.int32) - first_row + rows
    high_row = bounds(first_row + tile * CR + CR - 1)[1].astype(jnp.int32) - first_row + rows
    low = low_row // 16
    number = (high_row - low * 16 + 15) // 16
    full = number // 2
    spot = iota((8, 128), 1)
    meta[...] = jnp.where(spot == 0, low, jnp.where(spot == 1, full, number - 2 * full))
    value = condition[...]
    cond[...] = (value * jax.nn.sigmoid(value)).astype(BF)
    nsmall, width = weight.shape
    wide[...] = jnp.zeros_like(wide)
    wide[0:nsmall] = weight[...]
    chosen = iota((width, C), 1) == f * width + iota((width, C), 0)
    wsmall[...] = mm(wide[...].astype(BF), chosen.astype(BF))


def layout_of(nt, nf, lengths, condition, weight, rows):
    clips = lengths.shape[0]
    tab = rows + 8
    shapes = (
        ((tab + 8, rows), BF),
        ((tab, 128), F32),
        ((3 * rows, 128), F32),
        ((8, rows * F), F32),
        ((8, 128), jnp.int32),
        ((rows, clips), F32),
        (condition.shape, BF),
        ((32, C), F32),
    )
    return pl.pallas_call(
        partial(layout_kernel, nt, nf),
        out_shape=[jax.ShapeDtypeStruct(s, d) for s, d in shapes],
        in_specs=vmem(3),
        out_specs=vmem(len(shapes)),
        scratch_shapes=[pltpu.VMEM((32, weight.shape[1]), F32)],
        compiler_params=pltpu.CompilerParams(vmem_limit_bytes=VMEM_LIMIT),
        name="layout",
    )(
        lengths.reshape(1, clips),
        condition,
        weight,
    )


def on_device(
    nt,
    nf,
    latent,
    condition,
    lengths,
    cotangent,
    conv_weight,
    conv_moment,
    conv_second,
    proj_weight,
    proj_moment,
    proj_second,
    mlp_weight,
    mlp_moment,
    mlp_second,
    emb_weight,
    emb_moment,
    emb_second,
    small_weight,
    small_moment,
    small_second,
):
    rows = latent.shape[0] // nf
    same, rowtab, segk, segq, meta, onehot, cond_low, wsmall = layout_of(
        nt, nf, lengths, condition, small_weight, rows
    )
    (
        conv_full,
        proj_full,
        mlp_full,
        vec,
        cot,
        zhat1,
        zhat2,
        zhat3,
        rstd1,
        rstd2,
        rstd3,
        resid,
        inner,
        query,
        kext,
        vext,
        inext,
    ) = front(
        nt,
        nf,
        latent.reshape(-1, C),
        cotangent.reshape(-1, C),
        conv_weight,
        proj_weight,
        mlp_weight,
        emb_weight,
        wsmall,
        cond_low,
        onehot,
        same,
        rowtab,
    )
    mixed, mixed_t, lse = attend(meta, query, kext, vext, segq, segk)
    out_blocks, gafter, gmix, pack_a, mid_sums = middle(
        nf, inner, mixed, resid, cot, proj_full, mlp_full, vec
    )
    dq, dk, dv = attend_back(
        meta, query, kext, vext, segq, segk, gmix, mixed_t, lse
    )
    output, glat, sum_a, sum_b, sum_c, sum_d, sum_e = back(
        nt,
        nf,
        dq,
        dk,
        dv,
        gafter,
        inext,
        zhat1,
        zhat2,
        zhat3,
        rstd1,
        rstd2,
        rstd3,
        cot,
        conv_full,
        proj_full,
        vec,
        same,
        rowtab,
        cond_low,
        onehot,
        mid_sums,
        pack_a,
        out_blocks,
    )
    masters = (conv_weight, proj_weight, mlp_weight, emb_weight, small_weight)
    moments = (conv_moment, proj_moment, mlp_moment, emb_moment, small_moment)
    seconds = (conv_second, proj_second, mlp_second, emb_second, small_second)
    *updated, bias = adam((sum_a, sum_b, sum_c, sum_d, sum_e), masters, moments, seconds)
    return (
        output.reshape(latent.shape),
        glat.reshape(latent.shape),
        *updated,
        bias.reshape(-1),
    )


def solution(mesh):
    nt, nf = mesh.shape["tm"], mesh.shape["freq"]
    rows_spec = P("tm", "freq", None)
    middle_spec = P(None, "freq", None)
    params = (middle_spec,) * 9 + (P("freq", None),) * 3 + (P(None, "freq"),) * 3
    return jax.shard_map(
        partial(on_device, nt, nf),
        mesh=mesh,
        in_specs=(rows_spec, P(), P(), rows_spec) + params,
        out_specs=(rows_spec, rows_spec) + params + (P("freq"),),
        check_vma=False,
    )
```

```python
from functools import partial

import jax
import jax.numpy as jnp
from jax import lax
from jax.experimental import pallas as pl
from jax.experimental.pallas import tpu as pltpu
from jax.sharding import PartitionSpec as P

C = 256
G = 32
GW = C // G
HD = 32
H = C // HD
FF = 1024
F = 8
MAXLEN = 128
STEP = 10
TAPS = 9
CH = 256
CR = CH // F

HIGHEST = lax.Precision.HIGHEST
norm_eps = 1e-05
beta_first = 0.9
beta_second = 0.999
learn_rate = 0.5
weight_decay = 0.01
adam_eps = 1e-08
masked_score = -1e30
score_scale = HD**-0.5
LOG2E = 1.4426950408889634
MESH = pltpu.DeviceIdType.MESH if hasattr(pltpu, "DeviceIdType") else pl.DeviceIdType.MESH
VMEM_LIMIT = 64 * 1024 * 1024 - 65536
BF = jnp.bfloat16
F32 = jnp.float32


def mm(a, b):
    return jnp.dot(a, b, preferred_element_type=F32)


def mm_nt(a, b):
    return lax.dot_general(a, b, (((1,), (1,)), ((), ())), preferred_element_type=F32)


def mm_tn(a, b):
    return lax.dot_general(a, b, (((0,), (0,)), ((), ())), preferred_element_type=F32)


def hdot(a, b):
    return jnp.dot(a, b, precision=HIGHEST, preferred_element_type=F32)


def thirds(x):
    high = x.astype(BF)
    rest = x - high.astype(F32)
    middle = rest.astype(BF)
    low = (rest - middle.astype(F32)).astype(BF)
    return high, middle, low


def hdot_tn(a, b):
    return lax.dot_general(
        a, b, (((0,), (0,)), ((), ())), precision=HIGHEST, preferred_element_type=F32
    )


def place(nt, nf):
    t = lax.axis_index("tm")
    f = lax.axis_index("freq")
    odd = lax.rem(t, 2)
    s = f + odd * (nf - 1 - 2 * f)
    turn = 1 - 2 * odd
    at_end = (s + 1) // nf
    at_start = 1 - (s + nf - 1) // nf
    right = {"tm": t + at_end, "freq": f + (1 - at_end) * turn}
    left = {"tm": t - at_start, "freq": f - (1 - at_start) * turn}
    return t * nf + s, left, right


def flip(x, bit):
    return x + bit - 2 * bit * lax.rem(x // bit, 2)


def flip_by(x, mask):
    bit = 1
    while bit <= mask:
        if mask & bit:
            x = flip(x, bit)
        bit *= 2
    return x


def bits_of(count):
    bits = []
    bit = 1
    while bit < count:
        bits.append(bit)
        bit *= 2
    return bits


def snake(f, t, nf):
    return f + lax.rem(t, 2) * (nf - 1 - 2 * f)


def enter(spot, count, left, right, partners):
    barrier = pltpu.get_barrier_semaphore()
    for partner in partners:
        pl.semaphore_signal(barrier, inc=1, device_id=partner, device_id_type=MESH)

    @pl.when(spot > 0)
    def _():
        pl.semaphore_signal(barrier, inc=1, device_id=left, device_id_type=MESH)

    @pl.when(spot < count - 1)
    def _():
        pl.semaphore_signal(barrier, inc=1, device_id=right, device_id_type=MESH)

    inside = (spot > 0) & (spot < count - 1)

    @pl.when(inside)
    def _():
        pl.semaphore_wait(barrier, len(partners) + 2)

    @pl.when(jnp.logical_not(inside))
    def _():
        pl.semaphore_wait(barrier, len(partners) + 1)


class Swap:
    def __init__(self, where, to_left, to_right, from_left, from_right, sems):
        self.spot, self.count, left, right = where
        self.go_left = pltpu.make_async_remote_copy(
            src_ref=to_left,
            dst_ref=from_right,
            send_sem=sems.at[0],
            recv_sem=sems.at[1],
            device_id=left,
            device_id_type=MESH,
        )
        self.go_right = pltpu.make_async_remote_copy(
            src_ref=to_right,
            dst_ref=from_left,
            send_sem=sems.at[2],
            recv_sem=sems.at[3],
            device_id=right,
            device_id_type=MESH,
        )

    def start(self):
        @pl.when(self.spot > 0)
        def _():
            self.go_left.start()

        @pl.when(self.spot < self.count - 1)
        def _():
            self.go_right.start()

    def wait(self):
        @pl.when(self.spot > 0)
        def _():
            self.go_left.wait_send()
            self.go_right.wait_recv()

        @pl.when(self.spot < self.count - 1)
        def _():
            self.go_right.wait_send()
            self.go_left.wait_recv()


def remote(src, dst, sems, device):
    return pltpu.make_async_remote_copy(
        src_ref=src,
        dst_ref=dst,
        send_sem=sems.at[0],
        recv_sem=sems.at[1],
        device_id=device,
        device_id_type=MESH,
    )


class Exchange:
    def __init__(self, source, target, own_source, own_target, f, nf, sems):
        self.copies = []
        for mask in range(1, nf):
            peer = flip_by(f, mask)
            self.copies.append(
                remote(source(peer), target(peer), sems.at[mask - 1], {"freq": peer})
            )
        self.own_source, self.own_target = own_source, own_target

    def start(self):
        for copy in self.copies[::-1]:
            copy.start()
        self.own_target[...] = self.own_source[...]

    def wait(self):
        for copy in self.copies:
            copy.wait()


class Gather:
    def __init__(self, view, f, t, sems, size=None):
        near = {"freq": flip(f, 1)}
        far = flip(f, 2)
        self.halves = size is not None
        if self.halves:
            side = lax.rem(t, 2)
            mine, other = (side, size // 2), (1 - side, size // 2)
        else:
            mine = (0, None)
        beside = {"tm": flip(t, 1)}
        self.far = remote(view(f, mine), view(f, mine), sems.at[0], {"freq": far})
        self.near = remote(view(f, (0, None)), view(f, (0, None)), sems.at[1], near)
        self.forward = remote(view(far, mine), view(far, mine), sems.at[2], near)
        if self.halves:
            self.cross = remote(view(far, mine), view(far, mine), sems.at[3], beside)
            self.second = remote(view(far, other), view(far, other), sems.at[4], near)

    def start(self):
        self.far.start()
        self.near.start()

    def relay(self):
        self.far.wait_recv()
        if self.halves:
            self.cross.start()
        self.forward.start()

    def collect(self):
        if self.halves:
            self.cross.wait_recv()
            self.second.start()
        self.near.wait_recv()
        self.forward.wait_recv()
        if self.halves:
            self.second.wait_recv()

    def finish(self):
        self.far.wait_send()
        self.near.wait_send()
        self.forward.wait_send()
        if self.halves:
            self.cross.wait_send()
            self.second.wait_send()


def share_view(ref, depth, lead):
    def view(i, part):
        which, size = part
        start = i * depth if size is None else i * depth + which * size
        rows = rows_at(start, depth if size is None else size)
        return ref.at[lead, rows] if lead is not None else ref.at[rows]

    return view


def rows_at(start, size):
    return pl.ds(pl.multiple_of(start, 16), size)


def piece_of(n):
    for size in (128, 96, 80, 64, 48, 32):
        if n % size == 0:
            return size
    return 16


def add_rows(dst, to, a, a_at, b, b_at, n):
    size = piece_of(n)

    def step(i):
        left = a[rows_at(a_at + i * size, size)].astype(F32)
        right = b[rows_at(b_at + i * size, size)].astype(F32)
        dst[rows_at(to + i * size, size)] = (left + right).astype(BF)

    loop(n // size, step)


class Reduce:
    def __init__(self, order, pack, got, acc, far, rs, out, sems, t, f):
        u = far.shape[0]
        near = {"freq": flip(f, 1)}
        one = remote(pack(flip_by(f, 1)), got.at[0], sems.at[0], near)
        two = remote(pack(flip_by(f, 3)), got.at[1], sems.at[1], near)

        def add_near():
            add_rows(acc.at[1], 0, pack(flip(f, 2)), 0, got.at[1], 0, u)
            add_rows(acc.at[0], 0, pack(f), 0, got.at[0], 0, u)

        self.stages = [((two, one), add_near)]
        gathers = []
        n, at, base, place_at = u, 0, 0, 2
        slots = 2
        for bit in order:
            last = bit == order[-1]
            if bit == 0:
                rows = rows_at(at, n)
                copy = remote(
                    acc.at[1, rows], far.at[0:n], sems.at[place_at], {"freq": flip(f, 2)}
                )
                finish = partial(add_rows, acc.at[0], at, acc.at[0], at, far, 0, n)
                self.stages.append(((copy,), finish))
                slots, place_at = 1, place_at + 1
                continue
            peer = {"tm": flip(t, bit)}
            half = n % 32 == 0 and not last
            if half:
                upper = lax.rem(t // bit, 2)
                n = n // 2
                keep, give = at + upper * n, at + (1 - upper) * n
            else:
                keep, give = at, at
            copy = remote(
                acc.at[0:slots, rows_at(give, n)],
                rs.at[0:slots, base : base + n],
                sems.at[place_at],
                peer,
            )

            def finish(slots=slots, keep=keep, base=base, n=n, last=last):
                for slot in range(slots):
                    target = out if last else acc.at[slot]
                    add_rows(target, keep, acc.at[slot], keep, rs.at[slot], base, n)

            self.stages.append(((copy,), finish))
            if half:
                share = out.at[rows_at(keep, n)]
                gathers.append(((remote(share, share, sems.at[place_at + 1], peer),), None))
            at, base, place_at = keep, base + n, place_at + 2
        self.stages.extend(gathers[::-1])
        self.now = -1

    def done(self):
        return self.now >= len(self.stages)

    def advance(self):
        if self.done():
            return
        if self.now >= 0:
            copies, finish = self.stages[self.now]
            for copy in copies:
                copy.wait()
            if finish is not None:
                finish()
        self.now += 1
        if not self.done():
            for copy in self.stages[self.now][0]:
                copy.start()


def orders_of(nt):
    bits = bits_of(nt)
    far_first = [0] + bits
    if len(bits) < 2:
        return far_first, far_first
    return far_first, [bits[1], 0, bits[0]] + bits[2:]


def stage_count(nt):
    return 3 + 2 * len(bits_of(nt))


def padded(rows):
    return (rows + 63) // 64 * 64


def chunk_order(nf):
    width = F // nf
    row = lax.broadcasted_iota(jnp.int32, (CH, CH), 0)
    source = lax.broadcasted_iota(jnp.int32, (CH, CH), 1)
    col = lax.rem(row, F)
    wanted = (col // width) * (CR * width) + (row // F) * width + lax.rem(col, width)
    return jnp.where(source == wanted, 1.0, 0.0).astype(BF)


def clear_ends(spot, count, from_left, from_right):
    @pl.when(spot == 0)
    def _():
        from_left[...] = jnp.zeros_like(from_left)

    @pl.when(spot == count - 1)
    def _():
        from_right[...] = jnp.zeros_like(from_right)


def group_matrix():
    i = lax.broadcasted_iota(jnp.int32, (C, C), 0) // GW
    j = lax.broadcasted_iota(jnp.int32, (C, C), 1) // GW
    return (i == j).astype(BF)


def spread(rows, count):
    return jnp.broadcast_to(rows[:, None, :], (count, F, C))


def column_index(count):
    return lax.broadcasted_iota(jnp.int32, (count, F, C), 1)


def column_shifts(act, count):
    col = column_index(count)
    before = jnp.where(col == 0, 0.0, pltpu.roll(act, 1, 1))
    after = jnp.where(col == F - 1, 0.0, pltpu.roll(act, F - 1, 1))
    return before, after


def store_shifts(xc, at, act, count):
    before, after = column_shifts(act, count)
    size = count * F
    xc[pl.ds(at, size), 0:C] = before.reshape(size, C).astype(BF)
    xc[pl.ds(at, size), C : 2 * C] = act.reshape(size, C).astype(BF)
    xc[pl.ds(at, size), 2 * C : 3 * C] = after.reshape(size, C).astype(BF)


def loop(count, body):
    def step(i, carry):
        body(i)
        return carry

    lax.fori_loop(0, count, step, 0)


def chunk_at(i, size=CH):
    return pl.multiple_of(i * size, size)


class Clip:
    def __init__(self, same, rowtab, gmat, local):
        self.same, self.rowtab, self.gmat, self.local = same, rowtab, gmat, local

    def pack(self, rs, rq, to_left, to_right):
        tab = self.rowtab.shape[0]
        for index, table in ((0, rs), (1, rq)):
            total = 0.0
            for part in thirds(table[...])[::-1]:
                total = total + mm(self.same[...], part)
            self.local[index] = total[0:tab]
            to_left[index : index + 1] = total[tab : tab + 1]
            to_right[index : index + 1] = total[tab + 1 : tab + 2]

    def means(self, rs, rq, gain, from_left, from_right):
        at_left = self.rowtab[:, 1:2] > 0.0
        at_right = self.rowtab[:, 2:3] > 0.0
        inverse = self.rowtab[:, 0:1]
        tab = self.rowtab.shape[0]
        parts = []
        for index in range(2):
            total = self.local[index]
            total = total + jnp.where(at_left, from_left[index : index + 1], 0.0)
            total = total + jnp.where(at_right, from_right[index : index + 1], 0.0)
            total = total * inverse
            if gain is not None:
                total = total * gain
            parts.append(thirds(total))
        results = []
        for high, middle, low in parts:
            value = mm(low, self.gmat[...]) + mm(middle, self.gmat[...])
            results.append(value + mm(high, self.gmat[...]))
        return results


def row_masks(rowtab, prev_mask, next_mask, rows):
    prev_mask[...] = jnp.broadcast_to(rowtab[0:rows, 3:4], (rows, C))
    next_mask[...] = jnp.broadcast_to(rowtab[0:rows, 4:5], (rows, C))


def front_kernel(
    nt,
    nf,
    lat_local,
    cot_local,
    wconv,
    wproj,
    wmlp,
    wemb,
    wsmall,
    cond,
    onehot,
    same,
    rowtab,
    conv,
    proj,
    mlp,
    vec,
    cot,
    zhat1,
    zhat2,
    zhat3,
    rstd1,
    rstd2,
    rstd3,
    resid,
    inner,
    query,
    kext,
    vext,
    inext,
    gmat,
    own_sums,
    rs,
    rq,
    mean,
    prev_mask,
    next_mask,
    xc,
    z_prev,
    z_here,
    z_next,
    hidden,
    to_left,
    to_right,
    from_left,
    from_right,
    emb,
    small,
    lat,
    lat_in,
    cot_in,
    order,
    film,
    msg_sems,
    kv_sems,
    block_sems,
    gather_sems,
):
    px = lat.shape[0]
    rows = px // F
    chunks = px // CH
    blk = px // nf
    seg = CH // nf
    spot, left, right = place(nt, nf)
    count = nt * nf
    where = (spot, count, left, right)
    f = lax.axis_index("freq")
    t = lax.axis_index("tm")
    s = snake(f, t, nf)
    partners = [{"freq": flip_by(f, mask)} for mask in range(1, nf)] + [{"tm": flip(t, 1)}]
    enter(spot, count, left, right, partners)
    blocks = []
    for index, (local, landed) in enumerate(((lat_local, lat_in), (cot_local, cot_in))):
        blocks.append(
            Exchange(
                lambda peer, local=local: local.at[rows_at(snake(peer, t, nf) * blk, blk)],
                lambda peer, landed=landed: landed.at[f],
                local.at[rows_at(s * blk, blk)],
                landed.at[f],
                f,
                nf,
                block_sems.at[index],
            )
        )
    blocks[0].start()

    def cast(src, dst, base):
        size = 32 if src.shape[0] % 64 else 64

        def step(i):
            dst[rows_at(base + i * size, size)] = src[rows_at(i * size, size)].astype(BF)

        loop(src.shape[0] // size, step)

    cdepth, pdepth, mdepth, edepth = (
        wconv.shape[1],
        wproj.shape[1],
        wmlp.shape[1],
        wemb.shape[0],
    )
    views = (
        (share_view(conv, cdepth, 0), None),
        (share_view(conv, cdepth, 1), cdepth),
        (share_view(proj, pdepth, slice(None)), pdepth),
        (share_view(mlp, mdepth, slice(None)), mdepth),
        (share_view(emb, edepth, None), edepth),
        (share_view(small, wsmall.shape[0], None), None),
    )
    gathers = []
    for i, (view, size) in enumerate(views):
        gathers.append(Gather(view, f, t, gather_sems.at[i], size))
    get_first, get_second, get_proj, get_mlp, get_emb, get_small = gathers
    cast(wsmall, small, f * wsmall.shape[0])
    cast(wconv.at[0], conv.at[0], f * cdepth)
    get_small.start()
    get_first.start()
    cast(wemb, emb, f * edepth)
    cast(wconv.at[1], conv.at[1], f * cdepth)
    for i in range(wproj.shape[0]):
        cast(wproj.at[i], proj.at[i], f * pdepth)
    for i in range(wmlp.shape[0]):
        cast(wmlp.at[i], mlp.at[i], f * mdepth)
    order[...] = chunk_order(nf)

    def arrange(landed, target):
        def step(c):
            parts = [landed[k, rows_at(c * seg, seg)] for k in range(nf)]
            moved = mm(order[...], jnp.concatenate(parts, axis=0))
            target[pl.ds(chunk_at(c), CH)] = moved.astype(BF)

        loop(chunks, step)

    clear_ends(spot, count, from_left, from_right)

    @pl.when(spot == 0)
    def _():
        inext[0:px] = jnp.zeros((px, C), BF)

    @pl.when(spot == count - 1)
    def _():
        inext[2 * px : 3 * px] = jnp.zeros((px, C), BF)

    gmat[...] = group_matrix()
    row_masks(rowtab, prev_mask, next_mask, rows)
    clip = Clip(same, rowtab, gmat, own_sums)

    def v(i):
        return vec[i : i + 1]

    def norm_stage(step, load, zhat, rstd, rim, beside):
        def sums(c):
            x3 = load(c).reshape(CR, F, C)
            rs[pl.ds(chunk_at(c, CR), CR)] = jnp.sum(x3, axis=1)
            rq[pl.ds(chunk_at(c, CR), CR)] = jnp.sum(x3 * x3, axis=1)

        loop(chunks, sums)
        clip.pack(rs, rq, to_left.at[step], to_right.at[step])
        first, last = rim()
        to_left[step, 8:16] = first
        to_right[step, 8:16] = last
        swap = Swap(
            where,
            to_left.at[step],
            to_right.at[step],
            from_left.at[step],
            from_right.at[step],
            msg_sems.at[step],
        )
        swap.start()
        beside()
        swap.wait()
        mean_rows, square_rows = clip.means(rs, rq, None, from_left.at[step], from_right.at[step])
        mean[...] = mean_rows
        rstd[...] = lax.rsqrt(square_rows - mean_rows * mean_rows + norm_eps)
        rim_raw = jnp.concatenate([from_left[step, 8:16], from_right[step, 8:16]], axis=0)
        rim3 = rim_raw.reshape(2, F, C)
        rim_hat = (rim3 - spread(mean[rows : rows + 2], 2)) * spread(rstd[rows : rows + 2], 2)
        if zhat.shape[0] > px:
            zhat[px : px + 16] = rim_hat.reshape(16, C)
        return rim_hat

    def normed(load, zhat, rstd, c):
        r0 = chunk_at(c, CR)
        x3 = load(c).reshape(CR, F, C)
        hat = (x3 - spread(mean[pl.ds(r0, CR)], CR)) * spread(rstd[pl.ds(r0, CR)], CR)
        zhat[pl.ds(chunk_at(c), CH)] = hat.reshape(CH, C)
        return hat

    def conv_stage(rim_hat, load, zhat, rstd, gain, shift, kernel, ready, finish):
        pre = rim_hat * gain + shift
        store_shifts(xc, px, (pre * jax.nn.sigmoid(pre)).astype(BF).astype(F32), 2)

        def build(c):
            pre = normed(load, zhat, rstd, c) * gain + shift
            act = (pre * jax.nn.sigmoid(pre)).astype(BF).astype(F32)
            store_shifts(xc, chunk_at(c), act, CR)

        loop(chunks, build)
        ready()

        def product(c):
            p0 = chunk_at(c)
            part = xc[pl.ds(p0, CH)]
            z_prev[pl.ds(pl.multiple_of(p0 + 8, 8), CH)] = mm(part, kernel[0 : 3 * C])
            z_here[pl.ds(p0, CH)] = mm(part, kernel[3 * C : 6 * C])
            z_next[pl.ds(p0, CH)] = mm(part, kernel[6 * C : 9 * C])

        loop(chunks, product)
        part = xc[px : px + 16]
        z_prev[0:8] = mm(part, kernel[0 : 3 * C])[0:8]
        z_next[px : px + 8] = mm(part, kernel[6 * C : 9 * C])[8:16]

        def join(c):
            p0 = chunk_at(c)
            r0 = chunk_at(c, CR)
            keep_prev = spread(prev_mask[pl.ds(r0, CR)], CR) > 0.0
            keep_next = spread(next_mask[pl.ds(r0, CR)], CR) > 0.0
            out = z_here[pl.ds(p0, CH)].reshape(CR, F, C)
            out = out + jnp.where(keep_prev, z_prev[pl.ds(p0, CH)].reshape(CR, F, C), 0.0)
            after = z_next[pl.ds(pl.multiple_of(p0 + 8, 8), CH)].reshape(CR, F, C)
            finish(c, out + jnp.where(keep_next, after, 0.0))

        loop(chunks, join)

    def load_latent(c):
        return lat[pl.ds(chunk_at(c), CH)].astype(F32)

    def load_hidden(c):
        return hidden[pl.ds(chunk_at(c), CH)]

    def load_resid(c):
        return resid[pl.ds(chunk_at(c), CH)]

    def send_second():
        get_emb.start()
        get_second.start()
        blocks[1].start()
        get_small.relay()
        get_small.collect()
        total = small[0 : wsmall.shape[0]].astype(F32)
        for k in range(1, nf):
            at = k * wsmall.shape[0]
            total = total + small[at : at + wsmall.shape[0]].astype(F32)
        vec[...] = total

    blocks[0].wait()
    arrange(lat_in, lat)
    rim_hat = norm_stage(
        0,
        load_latent,
        zhat1,
        rstd1,
        lambda: (lat[0:16].astype(F32)[0:8], lat[px - 16 : px].astype(F32)[8:16]),
        send_second,
    )

    def ready_first():
        get_first.relay()
        get_emb.relay()
        get_first.collect()
        get_emb.collect()
        table = mm(cond[...], emb[...]) + v(3)
        film[...] = hdot(onehot[...], table)

    def finish_one(c, out):
        r0 = chunk_at(c, CR)
        out = out + v(2) + spread(film[pl.ds(r0, CR)], CR)
        hidden[pl.ds(chunk_at(c), CH)] = out.reshape(CH, C)

    conv_stage(rim_hat, load_latent, zhat1, rstd1, v(0), v(1), conv.at[0], ready_first, finish_one)

    def send_proj():
        get_second.relay()
        get_proj.start()
        get_mlp.start()
        blocks[1].wait()
        arrange(cot_in, cot)

    def ready_second():
        get_second.collect()
        get_proj.relay()
        get_mlp.relay()

    rim_hat = norm_stage(
        1, load_hidden, zhat2, rstd2, lambda: (hidden[0:8], hidden[px - 8 : px]), send_proj
    )

    def finish_two(c, out):
        p0 = chunk_at(c)
        total = lat[pl.ds(p0, CH)].astype(F32) + out.reshape(CH, C) + v(6)
        resid[pl.ds(p0, CH)] = total

    conv_stage(rim_hat, load_hidden, zhat2, rstd2, v(4), v(5), conv.at[1], ready_second, finish_two)

    def ready_proj():
        get_proj.collect()
        get_mlp.collect()

    norm_stage(
        2, load_resid, zhat3, rstd3, lambda: (resid[0:8], resid[px - 8 : px]), ready_proj
    )

    def rim_copy(c):
        at = chunk_at(c)
        own = inext.at[pl.ds(pl.multiple_of(px + at, CH), CH)]
        return Swap(
            where,
            own,
            own,
            inext.at[pl.ds(at, CH)],
            inext.at[pl.ds(pl.multiple_of(2 * px + at, CH), CH)],
            kv_sems.at[c],
        )

    def project(c):
        p0 = chunk_at(c)
        hat = normed(load_resid, zhat3, rstd3, c).reshape(CH, C)
        low = (hat * v(7) + v(8)).astype(BF)
        value = mm(low, proj[0]) + v(9)
        inner[pl.ds(p0, CH)] = value
        inext[pl.ds(pl.multiple_of(px + p0, CH), CH)] = value.astype(BF)

        @pl.when(c > 0)
        def _():
            rim_copy(c - 1).start()

    loop(chunks, project)
    rim_copy(chunks - 1).start()

    def keys_values(part):
        low = inext[part]
        kext[part] = mm(low, proj[2]).astype(BF)
        vext[part] = mm(low, proj[3]).astype(BF)

    def heads(c):
        part = pl.ds(pl.multiple_of(px + chunk_at(c), CH), CH)
        query[pl.ds(chunk_at(c), CH)] = mm(inext[part], proj[1]).astype(BF)
        keys_values(part)

    loop(chunks, heads)

    def rims(c):
        rim_copy(c).wait()
        keys_values(pl.ds(chunk_at(c), CH))
        keys_values(pl.ds(pl.multiple_of(2 * px + chunk_at(c), CH), CH))

    loop(chunks, rims)
    for gather in gathers:
        gather.finish()


def vmem(count):
    return [pl.BlockSpec(memory_space=pltpu.VMEM)] * count


def front(nt, nf, lat, cot, wconv, wproj, wmlp, wemb, wsmall, cond, onehot, same, rowtab):
    px = lat.shape[0]
    rows = px // F
    tab = rowtab.shape[0]

    def whole(share, axis):
        shape = list(share.shape)
        shape[axis] *= nf
        return tuple(shape)

    shapes = (
        (whole(wconv, 1), BF),
        (whole(wproj, 1), BF),
        (whole(wmlp, 1), BF),
        (wsmall.shape, F32),
        ((px, C), BF),
        ((px, C), F32),
        ((px + 16, C), F32),
        ((px + 16, C), F32),
        ((tab, C), F32),
        ((tab, C), F32),
        ((tab, C), F32),
        ((px, C), F32),
        ((px, C), F32),
        ((px, C), BF),
        ((3 * px, C), BF),
        ((3 * px, C), BF),
        ((3 * px, C), BF),
    )
    return pl.pallas_call(
        partial(front_kernel, nt, nf),
        out_shape=[jax.ShapeDtypeStruct(s, d) for s, d in shapes],
        in_specs=vmem(11),
        out_specs=vmem(len(shapes)),
        scratch_shapes=[
            pltpu.VMEM((C, C), BF),
            pltpu.VMEM((2, tab, C), F32),
            pltpu.VMEM((rows, C), F32),
            pltpu.VMEM((rows, C), F32),
            pltpu.VMEM((tab, C), F32),
            pltpu.VMEM((rows, C), F32),
            pltpu.VMEM((rows, C), F32),
            pltpu.VMEM((px + 16, 3 * C), BF),
            pltpu.VMEM((px + 16, C), F32),
            pltpu.VMEM((px, C), F32),
            pltpu.VMEM((px + 16, C), F32),
            pltpu.VMEM((px, C), F32),
            pltpu.VMEM((3, 16, C), F32),
            pltpu.VMEM((3, 16, C), F32),
            pltpu.VMEM((3, 16, C), F32),
            pltpu.VMEM((3, 16, C), F32),
            pltpu.VMEM(whole(wemb, 0), BF),
            pltpu.VMEM((nf * wsmall.shape[0], C), BF),
            pltpu.VMEM((px, C), BF),
            pltpu.VMEM((nf, px // nf, C), BF),
            pltpu.VMEM((nf, px // nf, C), BF),
            pltpu.VMEM((CH, CH), BF),
            pltpu.VMEM((rows, C), F32),
            pltpu.SemaphoreType.DMA((3, 4)),
            pltpu.SemaphoreType.DMA((px // CH, 4)),
            pltpu.SemaphoreType.DMA((2, nf - 1, 2)),
            pltpu.SemaphoreType.DMA((6, 5, 2)),
        ],
        compiler_params=pltpu.CompilerParams(
            collective_id=1, has_side_effects=True, vmem_limit_bytes=VMEM_LIMIT
        ),
        name="front",
    )(lat, cot, wconv, wproj, wmlp, wemb, wsmall, cond, onehot, same, rowtab)


def head_mask(h):
    lane = lax.broadcasted_iota(jnp.int32, (CH, C), 1)
    return (lane >= h * HD) & (lane < (h + 1) * HD)


def head_rows(h):
    return slice(h * HD, (h + 1) * HD)


def turned(block):
    return block.astype(F32).T


def score_bias(segk, segq, key_row, q0, key_rows):
    keys = jnp.broadcast_to(segk[pl.ds(key_row, key_rows), 0:1], (key_rows, C))
    keys = spread(keys, key_rows).reshape(key_rows * F, C)
    return jnp.where(keys == segq[0:1, pl.ds(q0, CH)], 0.0, masked_score)


def attend_kernel(meta, query, kext, vext, segq, segk, mixed, mixed_t, lse, vt, qm, bias, top, tot, acc, scores, peak):
    px = query.shape[0]
    factor = score_scale * LOG2E

    def turn(i):
        k0 = chunk_at(i)
        vt[:, pl.ds(k0, CH)] = turned(vext[pl.ds(k0, CH)]).astype(BF)

    loop(vext.shape[0] // CH, turn)

    def tile(t):
        q0 = chunk_at(t)
        block = query[pl.ds(q0, CH)].astype(F32)
        for h in range(H):
            qm[h] = jnp.where(head_mask(h), block, 0.0).astype(BF)
        top[...] = jnp.full((H, CH), masked_score, F32)
        tot[...] = jnp.zeros((H, CH), F32)
        acc[...] = jnp.zeros((C, CH), F32)

        def keys(row, key_rows):
            size = key_rows * F
            base = pl.multiple_of(row * F, 128)
            bias[0:size] = score_bias(segk, segq, pl.multiple_of(row, 16), q0, key_rows)
            key = kext[pl.ds(base, size)]
            for h in range(H):
                raw = mm_nt(key, qm[h]) + bias[0:size]
                scores[h, 0:size] = raw
                peak[h : h + 1] = jnp.maximum(top[h : h + 1], jnp.max(raw, axis=0, keepdims=True))
            for h in range(H):
                new = peak[h : h + 1]
                fade = jnp.exp2((top[h : h + 1] - new) * factor)
                weight = jnp.exp2((scores[h, 0:size] - new) * factor)
                top[h : h + 1] = new
                tot[h : h + 1] = tot[h : h + 1] * fade + jnp.sum(weight, axis=0, keepdims=True)
                part = mm(vt[head_rows(h), pl.ds(base, size)], weight.astype(BF))
                acc[head_rows(h)] = acc[head_rows(h)] * fade + part

        first = meta[t, 0] * 16
        loop(meta[t, 1], lambda i: keys(first + i * CR, CR))

        @pl.when(meta[t, 2] > 0)
        def _():
            keys(first + meta[t, 1] * CR, CR // 2)

        for h in range(H):
            acc[head_rows(h)] = acc[head_rows(h)] / tot[h : h + 1]
        lse[:, pl.ds(q0, CH)] = top[...] * factor + jnp.log2(tot[...])
        mixed_t[:, pl.ds(q0, CH)] = acc[...].astype(BF)
        mixed[pl.ds(q0, CH)] = acc[...].T.astype(BF)

    loop(px // CH, tile)


def attend(meta, query, kext, vext, segq, segk):
    px = query.shape[0]
    ext = kext.shape[0]
    return pl.pallas_call(
        attend_kernel,
        out_shape=[
            jax.ShapeDtypeStruct((px, C), BF),
            jax.ShapeDtypeStruct((C, px), BF),
            jax.ShapeDtypeStruct((H, px), F32),
        ],
        in_specs=[pl.BlockSpec(memory_space=pltpu.SMEM)] + vmem(5),
        out_specs=vmem(3),
        scratch_shapes=[
            pltpu.VMEM((C, ext), BF),
            pltpu.VMEM((H, CH, C), BF),
            pltpu.VMEM((CH, CH), F32),
            pltpu.VMEM((H, CH), F32),
            pltpu.VMEM((H, CH), F32),
            pltpu.VMEM((C, CH), F32),
            pltpu.VMEM((H, CH, CH), F32),
            pltpu.VMEM((H, CH), F32),
        ],
        compiler_params=pltpu.CompilerParams(vmem_limit_bytes=VMEM_LIMIT),
        name="attend",
    )(meta, query, kext, vext, segq, segk)


def attend_back_kernel(
    meta,
    query,
    kext,
    vext,
    segq,
    segk,
    gmix,
    mixed_t,
    lse,
    dq,
    dk,
    dv,
    kt,
    qm,
    gm,
    qt,
    gt,
    inner_rows,
    bias,
    dqt,
    dkt,
    dvt,
    kept,
    gscores,
):
    px = query.shape[0]
    ext = kext.shape[0]
    factor = score_scale * LOG2E

    def turn(i):
        k0 = chunk_at(i)
        kt[:, pl.ds(k0, CH)] = turned(kext[pl.ds(k0, CH)]).astype(BF)
        dkt[:, pl.ds(k0, CH)] = jnp.zeros((C, CH), F32)
        dvt[:, pl.ds(k0, CH)] = jnp.zeros((C, CH), F32)

    loop(ext // CH, turn)

    def tile(t):
        q0 = chunk_at(t)
        block = query[pl.ds(q0, CH)].astype(F32)
        grad = gmix[pl.ds(q0, CH)].astype(F32)
        for h in range(H):
            qm[h] = jnp.where(head_mask(h), block, 0.0).astype(BF)
            gm[h] = jnp.where(head_mask(h), grad, 0.0).astype(BF)
        qt[...] = block.T.astype(BF)
        grad_t = grad.T
        gt[...] = grad_t.astype(BF)
        crossed = grad_t * mixed_t[:, pl.ds(q0, CH)].astype(F32)
        inner_rows[...] = jnp.sum(crossed.reshape(H, HD, CH), axis=1)
        dqt[...] = jnp.zeros((C, CH), F32)

        def keys(row, key_rows):
            size = key_rows * F
            base = pl.multiple_of(row * F, 128)
            bias[0:size] = score_bias(segk, segq, pl.multiple_of(row, 16), q0, key_rows)
            key = kext[pl.ds(base, size)]
            val = vext[pl.ds(base, size)]
            for h in range(H):
                raw = mm_nt(key, qm[h]) + bias[0:size]
                probs = jnp.exp2(raw * factor - lse[h : h + 1, pl.ds(q0, CH)])
                gprob = mm_nt(val, gm[h])
                kept[h, 0:size] = probs.astype(BF)
                gscores[h, 0:size] = (probs * (gprob - inner_rows[h : h + 1])).astype(BF)
            for h in range(H):
                low_score = gscores[h, 0:size]
                dvt[head_rows(h), pl.ds(base, size)] += mm_nt(gt[head_rows(h)], kept[h, 0:size])
                dkt[head_rows(h), pl.ds(base, size)] += mm_nt(qt[head_rows(h)], low_score)
                dqt[head_rows(h)] += mm(kt[head_rows(h), pl.ds(base, size)], low_score)

        first = meta[t, 0] * 16
        loop(meta[t, 1], lambda i: keys(first + i * CR, CR))

        @pl.when(meta[t, 2] > 0)
        def _():
            keys(first + meta[t, 1] * CR, CR // 2)

        dq[pl.ds(q0, CH)] = (dqt[...] * score_scale).T.astype(BF)

    loop(px // CH, tile)

    def settle(i):
        k0 = chunk_at(i)
        dk[pl.ds(k0, CH)] = (dkt[:, pl.ds(k0, CH)] * score_scale).T.astype(BF)
        dv[pl.ds(k0, CH)] = dvt[:, pl.ds(k0, CH)].T.astype(BF)

    loop(ext // CH, settle)


def attend_back(meta, query, kext, vext, segq, segk, gmix, mixed_t, lse):
    px = query.shape[0]
    ext = kext.shape[0]
    return pl.pallas_call(
        attend_back_kernel,
        out_shape=[
            jax.ShapeDtypeStruct((px, C), BF),
            jax.ShapeDtypeStruct((ext, C), BF),
            jax.ShapeDtypeStruct((ext, C), BF),
        ],
        in_specs=[pl.BlockSpec(memory_space=pltpu.SMEM)] + vmem(8),
        out_specs=vmem(3),
        scratch_shapes=[
            pltpu.VMEM((C, ext), BF),
            pltpu.VMEM((H, CH, C), BF),
            pltpu.VMEM((H, CH, C), BF),
            pltpu.VMEM((C, CH), BF),
            pltpu.VMEM((C, CH), BF),
            pltpu.VMEM((H, CH), F32),
            pltpu.VMEM((CH, CH), F32),
            pltpu.VMEM((C, CH), F32),
            pltpu.VMEM((C, ext), F32),
            pltpu.VMEM((C, ext), F32),
            pltpu.VMEM((H, CH, CH), BF),
            pltpu.VMEM((H, CH, CH), BF),
        ],
        compiler_params=pltpu.CompilerParams(vmem_limit_bytes=VMEM_LIMIT),
        name="attend_back",
    )(meta, query, kext, vext, segq, segk, gmix, mixed_t, lse)


def middle_kernel(
    nf,
    inner,
    mixed,
    resid,
    cot,
    proj,
    mlp,
    vec,
    output,
    gafter,
    gmix,
    pack,
    sums,
    after_low,
    act_low,
    pre_low,
    down_low,
    mlp_low,
    after_grad_low,
    ubias,
    order,
):
    px = inner.shape[0]
    seg = CH // nf
    tail = 11 + FF // C
    order[...] = chunk_order(nf)
    sums[...] = jnp.zeros_like(sums)
    for j in range(FF // C):
        ubias[:, j * C : (j + 1) * C] = vec[11 + j : 12 + j]

    def step(c):
        p0 = chunk_at(c)
        after = inner[pl.ds(p0, CH)] + mm(mixed[pl.ds(p0, CH)], proj[4]) + vec[10:11]
        low = after.astype(BF)
        after_low[pl.ds(p0, CH)] = low
        grad_out = cot[pl.ds(p0, CH)]
        grad_mlp = mm_nt(grad_out, proj[5])
        down = grad_mlp.astype(BF)
        down_low[pl.ds(p0, CH)] = down
        total = after
        grad_after = grad_mlp
        for j in range(FF // C):
            part = slice(j * C, (j + 1) * C)
            pre = mm_nt(low, mlp[0, part]) + ubias[:, part]
            cdf = 0.5 + 0.5 * lax.erf(pre * (0.5**0.5))
            act = (pre * cdf).astype(BF)
            act_low[pl.ds(p0, CH), part] = act
            total = total + mm(act, mlp[1, part])
            density = jnp.exp(pre * pre * -0.5) * 0.3989422804014327
            grad_pre = mm_nt(down, mlp[1, part]) * (cdf + pre * density)
            sums[3 + j : 4 + j] += jnp.sum(grad_pre, axis=0, keepdims=True)
            grad_low = grad_pre.astype(BF)
            pre_low[pl.ds(p0, CH), part] = grad_low
            grad_after = grad_after + mm(grad_low, mlp[0, part])
        total = (total + vec[tail : tail + 1]).astype(BF)
        mlp_low[pl.ds(p0, CH)] = total
        branch = mm(total, proj[5]) + vec[tail + 1 : tail + 2]
        moved = mm_tn(order[...], (resid[pl.ds(p0, CH)] + branch).astype(BF)).astype(BF)
        for k in range(nf):
            output[k, rows_at(c * seg, seg)] = moved[k * seg : (k + 1) * seg]
        gafter[pl.ds(p0, CH)] = grad_after
        grad_low = grad_after.astype(BF)
        after_grad_low[pl.ds(p0, CH)] = grad_low
        gmix[pl.ds(p0, CH)] = mm_nt(grad_low, proj[4]).astype(BF)
        sums[0:1] += jnp.sum(grad_out.astype(F32), axis=0, keepdims=True)
        sums[1:2] += jnp.sum(grad_mlp, axis=0, keepdims=True)
        sums[2:3] += jnp.sum(grad_after, axis=0, keepdims=True)

    loop(px // CH, step)
    width = FF // nf
    for k in range(nf):
        part = slice(k * width, (k + 1) * width)
        pack[k, 0:width] = mm_tn(pre_low[:, part], after_low[...]).astype(BF)
        pack[k, width : 2 * width] = mm_tn(act_low[:, part], down_low[...]).astype(BF)
    depth = C // nf
    gw_attn = mm_tn(mixed[...], after_grad_low[...]).astype(BF)
    gw_out = mm_tn(mlp_low[...], cot[...]).astype(BF)
    for k in range(nf):
        part = slice(k * depth, (k + 1) * depth)
        pack[k, 2 * width : 2 * width + depth] = gw_attn[part]
        pack[k, 2 * width + depth : 2 * width + 2 * depth] = gw_out[part]


def middle(nf, inner, mixed, resid, cot, proj, mlp, vec):
    px = inner.shape[0]
    return pl.pallas_call(
        partial(middle_kernel, nf),
        out_shape=[
            jax.ShapeDtypeStruct((nf, px // nf, C), BF),
            jax.ShapeDtypeStruct((px, C), F32),
            jax.ShapeDtypeStruct((px, C), BF),
            jax.ShapeDtypeStruct((nf, 2 * (FF + C) // nf, C), BF),
            jax.ShapeDtypeStruct((8, C), F32),
        ],
        in_specs=vmem(7),
        out_specs=vmem(5),
        scratch_shapes=[
            pltpu.VMEM((px, C), BF),
            pltpu.VMEM((px, FF), BF),
            pltpu.VMEM((px, FF), BF),
            pltpu.VMEM((px, C), BF),
            pltpu.VMEM((px, C), BF),
            pltpu.VMEM((px, C), BF),
            pltpu.VMEM((1, FF), F32),
            pltpu.VMEM((CH, CH), BF),
        ],
        compiler_params=pltpu.CompilerParams(vmem_limit_bytes=VMEM_LIMIT),
        name="middle",
    )(inner, mixed, resid, cot, proj, mlp, vec)


def back_kernel(
    nt,
    nf,
    dq,
    dk,
    dv,
    gafter,
    inext,
    zhat1,
    zhat2,
    zhat3,
    rstd1,
    rstd2,
    rstd3,
    cot,
    conv,
    proj,
    vec,
    same,
    rowtab,
    cond,
    onehot,
    mid_sums,
    pack_a,
    out_blocks,
    output,
    glat,
    out_a,
    out_b,
    out_c,
    out_d,
    out_e,
    sums,
    film_rows,
    gmat,
    own_sums,
    rs,
    rq,
    mean_e,
    mean_ez,
    prev_mask,
    next_mask,
    normed_low,
    grad_low,
    gresid,
    dgrad,
    two,
    xc,
    shifted,
    rim_out,
    rim_got,
    to_left,
    to_right,
    from_left,
    from_right,
    order,
    glat_blocks,
    *rest,
):
    pack_b, pack_c, pack_d, pack_e = rest[:4]
    pieces = rest[4:28]
    msg_sems, kv_sems, block_sems, reduce_sems = rest[28:32]
    px = dq.shape[0]
    rows = px // F
    chunks = px // CH
    blk = px // nf
    seg = CH // nf
    spot, left, right = place(nt, nf)
    count = nt * nf
    where = (spot, count, left, right)
    f = lax.axis_index("freq")
    t = lax.axis_index("tm")
    s = snake(f, t, nf)
    partners = [{"freq": flip_by(f, mask)} for mask in range(1, nf)]
    partners = partners + [{"tm": flip(t, bit)} for bit in bits_of(nt)]
    enter(spot, count, left, right, partners)
    far_first, far_later = orders_of(nt)
    whole_d = out_d.shape[0]
    half = padded(whole_d // 2)
    plans = (
        (far_later, lambda i: pack_a.at[i], out_a),
        (far_first, lambda i: pack_b.at[i], out_b),
        (far_later, lambda i: pack_c.at[i], out_c),
        (far_first, lambda i: pack_d.at[i, 0:half], out_d.at[0:half]),
        (far_later, lambda i: pack_d.at[i, half:whole_d], out_d.at[half:whole_d]),
        (far_first, lambda i: pack_e.at[i], out_e),
    )
    jobs = []
    for index, (order_of, pack, out) in enumerate(plans):
        room = pieces[4 * index : 4 * index + 4]
        jobs.append(Reduce(order_of, pack, *room, out, reduce_sems.at[index], t, f))
    job_a, job_b, job_c, job_d, job_dd, job_e = jobs
    blocks = []
    for index, (source, landed) in enumerate(((out_blocks, output), (glat_blocks, glat))):
        blocks.append(
            Exchange(
                lambda peer, source=source: source.at[peer],
                lambda peer, landed=landed: landed.at[rows_at(s * blk, blk)],
                source.at[f],
                landed.at[rows_at(s * blk, blk)],
                f,
                nf,
                block_sems.at[index],
            )
        )
    def rim_copy(c):
        part = pl.ds(chunk_at(c), CH)
        return Swap(
            where,
            rim_out.at[0, part],
            rim_out.at[1, part],
            rim_got.at[0, part],
            rim_got.at[1, part],
            kv_sems.at[c],
        )

    def rim_grads(c):
        part = pl.ds(chunk_at(c), CH)
        for side in range(2):
            beyond = pl.ds(pl.multiple_of(2 * side * px + chunk_at(c), CH), CH)
            value = mm_nt(dk[beyond], proj[2]) + mm_nt(dv[beyond], proj[3])
            rim_out[side, part] = value.astype(BF)

        @pl.when(c > 0)
        def _():
            rim_copy(c - 1).start()

    loop(chunks, rim_grads)
    rim_copy(chunks - 1).start()
    job_a.advance()
    order[...] = chunk_order(nf)
    clear_ends(spot, count, from_left, from_right)
    clear_ends(spot, count, rim_got.at[0], rim_got.at[1])
    gmat[...] = group_matrix()
    row_masks(rowtab, prev_mask, next_mask, rows)
    clip = Clip(same, rowtab, gmat, own_sums)
    sums[...] = jnp.zeros_like(sums)

    def v(i):
        return vec[i : i + 1]

    def first(c):
        p0 = chunk_at(c)
        part = pl.ds(p0, CH)
        own = pl.ds(pl.multiple_of(px + p0, CH), CH)
        normed_low[part] = (zhat3[part] * v(7) + v(8)).astype(BF)
        grad = gafter[part] + mm_nt(dq[part], proj[1])
        gresid[part] = grad + mm_nt(dk[own], proj[2]) + mm_nt(dv[own], proj[3])

    loop(chunks, first)
    depth = C // nf

    def proj_grad(which, grad):
        low = grad.astype(BF)
        for k in range(nf):
            pack_b[k, which * depth : (which + 1) * depth] = low[k * depth : (k + 1) * depth]

    proj_grad(1, mm_tn(inext[px : 2 * px], dq[...]))
    job_a.advance()
    loop(chunks, lambda c: rim_copy(c).wait())

    def row_sums(c, grad3, hat3):
        rs[pl.ds(chunk_at(c, CR), CR)] = jnp.sum(grad3, axis=1)
        rq[pl.ds(chunk_at(c, CR), CR)] = jnp.sum(grad3 * hat3, axis=1)

    def second(c):
        p0 = chunk_at(c)
        part = pl.ds(p0, CH)
        grad = gresid[part] + rim_got[0, part].astype(F32) + rim_got[1, part].astype(F32)
        sums[9:10] += jnp.sum(grad, axis=0, keepdims=True)
        low = grad.astype(BF)
        grad_low[part] = low
        d3 = mm_nt(low, proj[0])
        dgrad[part] = d3
        row_sums(c, d3.reshape(CR, F, C), zhat3[part].reshape(CR, F, C))

    loop(chunks, second)

    def swap_step(step, rim_first, rim_last):
        clip.pack(rs, rq, to_left.at[step], to_right.at[step])
        if rim_first is not None:
            to_left[step, 8 : 8 + rim_first.shape[0]] = rim_first
            to_right[step, 8 : 8 + rim_last.shape[0]] = rim_last
        swap = Swap(
            where,
            to_left.at[step],
            to_right.at[step],
            from_left.at[step],
            from_right.at[step],
            msg_sems.at[step],
        )
        swap.start()
        return swap

    def set_means(step, gain):
        mean_e[...], mean_ez[...] = clip.means(
            rs, rq, gain, from_left.at[step], from_right.at[step]
        )

    def back_norm(grad3, hat3, rstd, gain, r0, size):
        value = grad3 * gain - spread(mean_e[pl.ds(r0, size)], size)
        value = value - hat3 * spread(mean_ez[pl.ds(r0, size)], size)
        return value * spread(rstd[pl.ds(r0, size)], size)

    def rim_grad(step, at):
        both = jnp.concatenate([from_left[step, at : at + 8], from_right[step, at : at + 8]], axis=0)
        return both.reshape(2, F, C)

    sums[7:8] = jnp.sum(rq[...], axis=0, keepdims=True)
    sums[8:9] = jnp.sum(rs[...], axis=0, keepdims=True)
    cot_first = cot[0:16].astype(F32)[0:8]
    cot_last = cot[px - 16 : px].astype(F32)[8:16]
    swap = swap_step(
        0,
        jnp.concatenate([dgrad[0:8], cot_first], axis=0),
        jnp.concatenate([dgrad[px - 8 : px], cot_last], axis=0),
    )
    proj_grad(2, mm_tn(inext[...], dk[...]))
    proj_grad(3, mm_tn(inext[...], dv[...]))
    proj_grad(0, mm_tn(normed_low[...], grad_low[...]))
    job_b.advance()
    job_a.advance()
    swap.wait()
    set_means(0, v(7))

    def set_rims(value):
        low = value.astype(BF).astype(F32)
        two[0:8] = low[0]
        two[px + 8 : px + 16] = low[1]

    rim = rim_grad(0, 8)
    rim_hat = zhat3[px : px + 16].reshape(2, F, C)
    set_rims(rim_grad(0, 16) + back_norm(rim, rim_hat, rstd3, v(7), rows, 2))

    def third(c):
        p0 = chunk_at(c)
        part = pl.ds(p0, CH)
        grad3 = dgrad[part].reshape(CR, F, C)
        hat3 = zhat3[part].reshape(CR, F, C)
        value = back_norm(grad3, hat3, rstd3, v(7), chunk_at(c, CR), CR).reshape(CH, C)
        value = cot[part].astype(F32) + value
        gresid[part] = value
        sums[6:7] += jnp.sum(value, axis=0, keepdims=True)
        two[pl.ds(pl.multiple_of(p0 + 8, 8), CH)] = value.astype(BF).astype(F32)

    loop(chunks, third)

    def conv_inputs(zhat, gain, shift, c):
        p0 = chunk_at(c)
        part = pl.ds(p0, CH)
        r0 = chunk_at(c, CR)
        keep_prev = spread(prev_mask[pl.ds(r0, CR)], CR).reshape(CH, C) > 0.0
        keep_next = spread(next_mask[pl.ds(r0, CR)], CR).reshape(CH, C) > 0.0
        after = two[pl.ds(pl.multiple_of(p0 + 16, 16), CH)]
        here = two[pl.ds(pl.multiple_of(p0 + 8, 8), CH)]
        shifted[part, 0:C] = jnp.where(keep_next, after, 0.0).astype(BF)
        shifted[part, C : 2 * C] = here.astype(BF)
        shifted[part, 2 * C : 3 * C] = jnp.where(keep_prev, two[part], 0.0).astype(BF)
        pre = zhat[part] * gain + shift
        act = (pre * jax.nn.sigmoid(pre)).astype(BF).astype(F32).reshape(CR, F, C)
        store_shifts(xc, p0, act, CR)

    def conv_back(kernel, zhat, gain, shift, c):
        part = pl.ds(chunk_at(c), CH)
        hat = zhat[part]
        pre = hat * gain + shift
        sig = jax.nn.sigmoid(pre)

        def columns(j):
            piece = slice(j * C, (j + 1) * C)
            value = mm_nt(shifted[part, 0:C], kernel[0 : 3 * C][piece])
            value = value + mm_nt(shifted[part, C : 2 * C], kernel[3 * C : 6 * C][piece])
            value = value + mm_nt(shifted[part, 2 * C : 3 * C], kernel[6 * C : 9 * C][piece])
            return value.reshape(CR, F, C)

        col = column_index(CR)
        back = columns(1)
        back = back + jnp.where(col == F - 1, 0.0, pltpu.roll(columns(0), F - 1, 1))
        back = back + jnp.where(col == 0, 0.0, pltpu.roll(columns(2), 1, 1))
        grad = back.reshape(CH, C) * sig * (1.0 + pre * (1.0 - sig))
        dgrad[part] = grad
        row_sums(c, grad.reshape(CR, F, C), hat.reshape(CR, F, C))

    share = TAPS * C // nf

    def kernel_grad(pack):
        for k in range(nf):
            if pack.shape[1] > share:
                pack[k, share:] = jnp.zeros((pack.shape[1] - share, C), BF)
        for d in range(3):
            for j in range(3):
                grad = mm_tn(xc[:, j * C : (j + 1) * C], shifted[:, d * C : (d + 1) * C])
                low = grad.astype(BF)
                start = (d * 3 + j) * C
                end = start + C
                at = start
                while at < end:
                    k = at // share
                    upto = min(end, (k + 1) * share)
                    pack[k, at - k * share : upto - k * share] = low[at - start : upto - start]
                    at = upto

    def step_two(c):
        conv_inputs(zhat2, v(4), v(5), c)
        conv_back(conv.at[1], zhat2, v(4), v(5), c)

    loop(chunks, step_two)
    sums[4:5] = jnp.sum(rq[...], axis=0, keepdims=True)
    sums[5:6] = jnp.sum(rs[...], axis=0, keepdims=True)
    swap = swap_step(1, dgrad[0:8], dgrad[px - 8 : px])
    job_a.advance()
    blocks[0].start()
    kernel_grad(pack_c)
    job_c.advance()
    job_b.advance()
    swap.wait()
    set_means(1, v(4))
    rim_hat = zhat2[px : px + 16].reshape(2, F, C)
    set_rims(back_norm(rim_grad(1, 8), rim_hat, rstd2, v(4), rows, 2))

    def fourth(c):
        p0 = chunk_at(c)
        part = pl.ds(p0, CH)
        grad3 = dgrad[part].reshape(CR, F, C)
        hat3 = zhat2[part].reshape(CR, F, C)
        value3 = back_norm(grad3, hat3, rstd2, v(4), chunk_at(c, CR), CR)
        film_rows[pl.ds(chunk_at(c, CR), CR)] = jnp.sum(value3, axis=1)
        low = value3.reshape(CH, C).astype(BF).astype(F32)
        two[pl.ds(pl.multiple_of(p0 + 8, 8), CH)] = low

    loop(chunks, fourth)
    total = jnp.sum(film_rows[...], axis=0, keepdims=True)
    sums[2:3] = total
    sums[3:4] = total
    loop(chunks, partial(conv_inputs, zhat1, v(0), v(1)))
    kernel_grad(pack_d)
    grad_film = hdot_tn(onehot[...], film_rows[...])
    gemb = hdot_tn(cond[...].astype(F32), grad_film).astype(BF)
    edepth = gemb.shape[0] // nf
    job_d.advance()
    job_dd.advance()

    def sums_one(c):
        conv_back(conv.at[0], zhat1, v(0), v(1), c)

    loop(chunks, sums_one)
    sums[0:1] = jnp.sum(rq[...], axis=0, keepdims=True)
    sums[1:2] = jnp.sum(rs[...], axis=0, keepdims=True)
    swap = swap_step(2, None, None)
    tail = jnp.concatenate(
        [
            sums[0:10],
            mid_sums[2:3],
            mid_sums[3 : 3 + FF // C],
            mid_sums[1:2],
            mid_sums[0:1],
            jnp.zeros((32 - 13 - FF // C, C), F32),
        ],
        axis=0,
    ).astype(BF)
    for k in range(nf):
        pack_e[k, 0:edepth] = gemb[k * edepth : (k + 1) * edepth]
        pack_e[k, edepth : edepth + 32] = tail
        pack_e[k, edepth + 32 :] = jnp.zeros((pack_e.shape[1] - edepth - 32, C), BF)
    job_e.advance()
    for job in (job_d, job_dd, job_c, job_a, job_b):
        job.advance()
    swap.wait()
    set_means(2, v(0))

    def fifth(c):
        p0 = chunk_at(c)
        part = pl.ds(p0, CH)
        grad3 = dgrad[part].reshape(CR, F, C)
        hat3 = zhat1[part].reshape(CR, F, C)
        value = back_norm(grad3, hat3, rstd1, v(0), chunk_at(c, CR), CR).reshape(CH, C)
        moved = mm_tn(order[...], (gresid[part] + value).astype(BF)).astype(BF)
        for k in range(nf):
            glat_blocks[k, rows_at(c * seg, seg)] = moved[k * seg : (k + 1) * seg]

    loop(chunks, fifth)
    turns = 0
    while turns <= 3 or not all(job.done() for job in jobs):
        if turns == 3:
            blocks[1].start()
        for job in (job_e, job_d, job_dd, job_c, job_a, job_b):
            job.advance()
        turns += 1
    for block in blocks:
        block.wait()


def back(nt, nf, *args):
    px = args[0].shape[0]
    rows = px // F
    tab = args[-6].shape[0]
    pack_rows = args[-2].shape[1]
    edepth = args[-5].shape[1] // nf
    share = TAPS * C // nf
    heights = (pack_rows, 4 * C // nf, share, share, padded(edepth + 32))
    half = padded(share // 2)
    job_heights = heights[:3] + (half, share - half) + heights[4:]
    buffers = [pltpu.VMEM((nf, u, C), BF) for u in heights[1:]]
    for u in job_heights:
        buffers.extend(
            [
                pltpu.VMEM((2, u, C), BF),
                pltpu.VMEM((2, u, C), BF),
                pltpu.VMEM((u, C), BF),
                pltpu.VMEM((2, 2 * u, C), BF),
            ]
        )
    big = pltpu.VMEM((px, C), F32)
    low = pltpu.VMEM((px, C), BF)
    table = pltpu.VMEM((rows, C), F32)
    return pl.pallas_call(
        partial(back_kernel, nt, nf),
        out_shape=[
            jax.ShapeDtypeStruct((px, C), BF),
            jax.ShapeDtypeStruct((px, C), BF),
        ]
        + [jax.ShapeDtypeStruct((u, C), BF) for u in heights],
        in_specs=vmem(len(args)),
        out_specs=vmem(7),
        scratch_shapes=[
            pltpu.VMEM((16, C), F32),
            pltpu.VMEM((rows, C), F32),
            pltpu.VMEM((C, C), BF),
            pltpu.VMEM((2, tab, C), F32),
            table,
            table,
            pltpu.VMEM((tab, C), F32),
            pltpu.VMEM((tab, C), F32),
            table,
            table,
            low,
            low,
            big,
            big,
            pltpu.VMEM((px + 16, C), F32),
            pltpu.VMEM((px, 3 * C), BF),
            pltpu.VMEM((px, 3 * C), BF),
            pltpu.VMEM((2, px, C), BF),
            pltpu.VMEM((2, px, C), BF),
            pltpu.VMEM((3, 24, C), F32),
            pltpu.VMEM((3, 24, C), F32),
            pltpu.VMEM((3, 24, C), F32),
            pltpu.VMEM((3, 24, C), F32),
            pltpu.VMEM((CH, CH), BF),
            pltpu.VMEM((nf, px // nf, C), BF),
            *buffers,
            pltpu.SemaphoreType.DMA((3, 4)),
            pltpu.SemaphoreType.DMA((px // CH, 4)),
            pltpu.SemaphoreType.DMA((2, nf - 1, 2)),
            pltpu.SemaphoreType.DMA((6, stage_count(nt), 2)),
        ],
        compiler_params=pltpu.CompilerParams(
            collective_id=2, has_side_effects=True, vmem_limit_bytes=VMEM_LIMIT
        ),
        name="back",
    )(*args)


def adamw_step(weight, moment, second, grad, decay_rate):
    moment_new = beta_first * moment + (1.0 - beta_first) * grad
    second_new = beta_second * second + (1.0 - beta_second) * grad * grad
    moment_hat = moment_new / (1.0 - beta_first**STEP)
    second_hat = second_new / (1.0 - beta_second**STEP)
    weight_new = weight - learn_rate * (
        moment_hat / (jnp.sqrt(second_hat) + adam_eps) + decay_rate * weight
    )
    return (weight_new, moment_new, second_new)


def adam_kernel(sum_a, sum_b, sum_c, sum_d, sum_e, *refs):
    masters, moments, seconds = refs[0:5], refs[5:10], refs[10:15]
    news, bias = refs[15:30], refs[30]
    i = pl.program_id(0)

    def update(kind, at, grad, decay):
        values = adamw_step(
            masters[kind][at], moments[kind][at], seconds[kind][at], grad.astype(F32), decay
        )
        for k, value in enumerate(values):
            news[3 * kind + k][at] = value

    def block(total, start, size):
        return total[rows_at(start + i * size, size)]

    cdepth, pdepth, mdepth, edepth = (
        masters[0].shape[1],
        masters[1].shape[1],
        masters[2].shape[1],
        masters[3].shape[0],
    )
    steps = sum_d.shape[0] // cdepth
    update(0, 0, block(sum_d, 0, cdepth), weight_decay)
    update(0, 1, block(sum_c, 0, cdepth), weight_decay)
    whole_p, whole_m, whole_e = pdepth * steps, mdepth * steps, edepth * steps
    for k in range(4):
        update(1, k, block(sum_b, k * whole_p, pdepth), weight_decay)
    for k in range(2):
        update(1, 4 + k, block(sum_a, 2 * whole_m + k * whole_p, pdepth), weight_decay)
        update(2, k, block(sum_a, k * whole_m, mdepth), weight_decay)
    update(3, slice(None), block(sum_e, 0, edepth), weight_decay)

    @pl.when(i == 0)
    def _():
        nsmall, width = masters[4].shape
        first = lax.axis_index("freq") * width
        source = lax.broadcasted_iota(jnp.int32, (C, width), 0)
        chosen = source == first + lax.broadcasted_iota(jnp.int32, (C, width), 1)
        grad = mm(sum_e[whole_e : whole_e + 32], chosen.astype(BF))
        update(4, slice(None), grad[0:nsmall], 0.0)
        bias[...] = grad[nsmall - 1 : nsmall]


def adam(sums, masters, moments, seconds):
    steps = 4

    def whole(array):
        return pl.BlockSpec(array.shape, lambda i: (0,) * array.ndim)

    def piece(array):
        if array.ndim == 3:
            shape = (array.shape[0], array.shape[1] // steps, C)
            return pl.BlockSpec(shape, lambda i: (0, i, 0))
        if array.shape[1] == C:
            return pl.BlockSpec((array.shape[0] // steps, C), lambda i: (i, 0))
        return whole(array)

    specs = [piece(array) for array in masters]
    out_shapes, out_specs = [], []
    for array, spec in zip(masters, specs):
        out_shapes.extend([jax.ShapeDtypeStruct(array.shape, F32)] * 3)
        out_specs.extend([spec] * 3)
    width = masters[4].shape[1]
    out_shapes.append(jax.ShapeDtypeStruct((1, width), F32))
    out_specs.append(pl.BlockSpec((1, width), lambda i: (0, 0)))
    return pl.pallas_call(
        adam_kernel,
        grid=(steps,),
        out_shape=out_shapes,
        in_specs=[whole(array) for array in sums] + specs * 3,
        out_specs=out_specs,
        compiler_params=pltpu.CompilerParams(vmem_limit_bytes=VMEM_LIMIT),
        name="adam",
    )(*sums, *masters, *moments, *seconds)


def layout_kernel(
    nt,
    nf,
    len_row,
    condition,
    weight,
    same,
    rowtab,
    segk,
    segq,
    meta,
    onehot,
    cond,
    wsmall,
    wide,
):
    rows, clips = onehot.shape
    tab = rowtab.shape[0]
    f = lax.axis_index("freq")
    t = lax.axis_index("tm")
    total_rows = nt * nf * rows
    first_row = (t * nf + snake(f, t, nf)) * rows

    def iota(shape, dim):
        return lax.broadcasted_iota(jnp.int32, shape, dim)

    down = iota((clips, clips), 0)
    across = iota((clips, clips), 1)
    lengths = len_row[...].astype(F32)
    len_col = jnp.sum(jnp.where(down == across, lengths, 0.0), axis=1, keepdims=True)
    ends_col = jnp.sum(jnp.where(across <= down, lengths, 0.0), axis=1, keepdims=True)
    ends = jnp.sum(jnp.where(down <= across, len_col, 0.0), axis=0, keepdims=True)

    def finished(row):
        return ends <= row.astype(F32)

    def seg_of(row):
        seg = jnp.sum(jnp.where(finished(row), 1.0, 0.0), axis=1, keepdims=True)
        return jnp.where((row >= 0) & (row < total_rows), seg, -1.0)

    def seg_lanes(row):
        return jnp.sum(jnp.where(ends_col <= row.astype(F32), 1.0, 0.0), axis=0, keepdims=True)

    ext_row = first_row - rows + iota((3 * rows, 1), 0)
    segk[...] = jnp.broadcast_to(seg_of(ext_row), segk.shape)
    pixel = iota((1, rows * F), 1)
    segq[...] = jnp.broadcast_to(seg_lanes(first_row + pixel // F), segq.shape)
    seg_row = seg_lanes(first_row + iota((1, rows), 1))
    index = iota((tab + 8, 1), 0)
    at = jnp.where(index < rows, first_row + index, first_row)
    at = jnp.where(index == rows, first_row - 1, at)
    at = jnp.where(index == rows + 1, first_row + rows, at)
    at = jnp.where(index == tab + 1, first_row + rows - 1, at)
    unused = ((index > rows + 1) & (index < tab)) | (index > tab + 1)
    seg_tab = jnp.where(unused, -2.0, seg_of(at))
    same[...] = (seg_tab == seg_row).astype(BF)
    clip_lane = iota((tab + 8, clips), 1).astype(F32)
    hot = jnp.where(seg_tab == clip_lane, 1.0, 0.0)
    onehot[...] = hot[0:rows]
    row_len = jnp.sum(hot * lengths, axis=1, keepdims=True)
    inner = index < rows
    fields = (
        1.0 / jnp.maximum(row_len * (F * GW), 1.0),
        jnp.where(seg_tab == seg_of(first_row - 1 + 0 * index), 1.0, 0.0),
        jnp.where(seg_tab == seg_of(first_row + rows + 0 * index), 1.0, 0.0),
        jnp.where(inner & (seg_tab == seg_of(at - 1)), 1.0, 0.0),
        jnp.where(inner & (seg_tab == seg_of(at + 1)), 1.0, 0.0),
    )
    lane = iota((tab + 8, 128), 1)
    values = jnp.zeros((tab + 8, 128), F32)
    for place_at, field in enumerate(fields):
        values = jnp.where(lane == place_at, field, values)
    rowtab[...] = values[0:tab]
    tile = iota((8, 1), 0)

    def bounds(row):
        low = jnp.sum(jnp.where(finished(row), lengths, 0.0), axis=1, keepdims=True)
        seg = jnp.sum(jnp.where(finished(row), 1.0, 0.0), axis=1, keepdims=True)
        here = iota((8, clips), 1).astype(F32) == seg
        return low, low + jnp.sum(jnp.where(here, lengths, 0.0), axis=1, keepdims=True)

    low_row = bounds(first_row + tile * CR)[0].astype(jnp.int32) - first_row + rows
    high_row = bounds(first_row + tile * CR + CR - 1)[1].astype(jnp.int32) - first_row + rows
    low = low_row // 16
    number = (high_row - low * 16 + 15) // 16
    full = number // 2
    spot = iota((8, 128), 1)
    meta[...] = jnp.where(spot == 0, low, jnp.where(spot == 1, full, number - 2 * full))
    value = condition[...]
    cond[...] = (value * jax.nn.sigmoid(value)).astype(BF)
    nsmall, width = weight.shape
    wide[...] = jnp.zeros_like(wide)
    wide[0:nsmall] = weight[...]
    chosen = iota((width, C), 1) == f * width + iota((width, C), 0)
    wsmall[...] = mm(wide[...].astype(BF), chosen.astype(BF))


def layout_of(nt, nf, lengths, condition, weight, rows):
    clips = lengths.shape[0]
    tab = rows + 8
    shapes = (
        ((tab + 8, rows), BF),
        ((tab, 128), F32),
        ((3 * rows, 128), F32),
        ((8, rows * F), F32),
        ((8, 128), jnp.int32),
        ((rows, clips), F32),
        (condition.shape, BF),
        ((32, C), F32),
    )
    return pl.pallas_call(
        partial(layout_kernel, nt, nf),
        out_shape=[jax.ShapeDtypeStruct(s, d) for s, d in shapes],
        in_specs=vmem(3),
        out_specs=vmem(len(shapes)),
        scratch_shapes=[pltpu.VMEM((32, weight.shape[1]), F32)],
        compiler_params=pltpu.CompilerParams(vmem_limit_bytes=VMEM_LIMIT),
        name="layout",
    )(
        lengths.reshape(1, clips),
        condition,
        weight,
    )


def on_device(
    nt,
    nf,
    latent,
    condition,
    lengths,
    cotangent,
    conv_weight,
    conv_moment,
    conv_second,
    proj_weight,
    proj_moment,
    proj_second,
    mlp_weight,
    mlp_moment,
    mlp_second,
    emb_weight,
    emb_moment,
    emb_second,
    small_weight,
    small_moment,
    small_second,
):
    rows = latent.shape[0] // nf
    same, rowtab, segk, segq, meta, onehot, cond_low, wsmall = layout_of(
        nt, nf, lengths, condition, small_weight, rows
    )
    (
        conv_full,
        proj_full,
        mlp_full,
        vec,
        cot,
        zhat1,
        zhat2,
        zhat3,
        rstd1,
        rstd2,
        rstd3,
        resid,
        inner,
        query,
        kext,
        vext,
        inext,
    ) = front(
        nt,
        nf,
        latent.reshape(-1, C),
        cotangent.reshape(-1, C),
        conv_weight,
        proj_weight,
        mlp_weight,
        emb_weight,
        wsmall,
        cond_low,
        onehot,
        same,
        rowtab,
    )
    mixed, mixed_t, lse = attend(meta, query, kext, vext, segq, segk)
    out_blocks, gafter, gmix, pack_a, mid_sums = middle(
        nf, inner, mixed, resid, cot, proj_full, mlp_full, vec
    )
    dq, dk, dv = attend_back(
        meta, query, kext, vext, segq, segk, gmix, mixed_t, lse
    )
    output, glat, sum_a, sum_b, sum_c, sum_d, sum_e = back(
        nt,
        nf,
        dq,
        dk,
        dv,
        gafter,
        inext,
        zhat1,
        zhat2,
        zhat3,
        rstd1,
        rstd2,
        rstd3,
        cot,
        conv_full,
        proj_full,
        vec,
        same,
        rowtab,
        cond_low,
        onehot,
        mid_sums,
        pack_a,
        out_blocks,
    )
    masters = (conv_weight, proj_weight, mlp_weight, emb_weight, small_weight)
    moments = (conv_moment, proj_moment, mlp_moment, emb_moment, small_moment)
    seconds = (conv_second, proj_second, mlp_second, emb_second, small_second)
    *updated, bias = adam((sum_a, sum_b, sum_c, sum_d, sum_e), masters, moments, seconds)
    return (
        output.reshape(latent.shape),
        glat.reshape(latent.shape),
        *updated,
        bias.reshape(-1),
    )


def solution(mesh):
    nt, nf = mesh.shape["tm"], mesh.shape["freq"]
    rows_spec = P("tm", "freq", None)
    middle_spec = P(None, "freq", None)
    params = (middle_spec,) * 9 + (P("freq", None),) * 3 + (P(None, "freq"),) * 3
    return jax.shard_map(
        partial(on_device, nt, nf),
        mesh=mesh,
        in_specs=(rows_spec, P(), P(), rows_spec) + params,
        out_specs=(rows_spec, rows_spec) + params + (P("freq"),),
        check_vma=False,
    )
```
